32 devices in a mesh: img: 8 (over z, y), band: 4 (over x, core).
Axes of the slice: x: 2, y: 2, z: 4, core: 2. Of those that a mesh axis runs over, the one named last changes fastest.
Arguments:
- tokens: bfloat16 [8, 1024, 2, 768], P('img', 'band'), may hold values from -6 to 6
- slot_kind: int32 [8, 2], P('img'), may hold values from 0 to 2
- w_qkv: bfloat16 [768, 2304], P('band', 'img'), may hold values from -0.3125 to 0.3125
- w_out: bfloat16 [768, 768], P('band', 'img'), may hold values from -1.75 to 1.75
- w_up: bfloat16 [768, 3072], P('band', 'img'), may hold values from -0.21875 to 0.21875
- w_down: bfloat16 [3072, 768], P('band', 'img'), may hold values from -0.109375 to 0.109375
- bias_qv: bfloat16 [1536], P('img'), may hold values from -2 to 2
- bias_out: bfloat16 [768], P('img'), may hold values from -2 to 2
- bias_up: bfloat16 [3072], P('img'), may hold values from -2 to 2
- bias_down: bfloat16 [768], P('img'), may hold values from -2 to 2
- gain_one: bfloat16 [768], P('img'), may hold values from 0.25 to 1.75
- shift_one: bfloat16 [768], P('img'), may hold values from -2 to 2
- gain_two: bfloat16 [768], P('img'), may hold values from 0.25 to 1.75
- shift_two: bfloat16 [768], P('img'), may hold values from -2 to 2
- cotangent: bfloat16 [8, 1024, 2, 768], P('img', 'band'), may hold values from -6 to 6
Outputs:
- out_tokens: bfloat16 [8, 1024, 2, 768], P('img', 'band')
- grad_tokens: bfloat16 [8, 1024, 2, 768], P('img', 'band')
- grad_w_qkv: float32 [768, 2304], P('band', 'img')
- grad_w_out: float32 [768, 768], P('band', 'img')
- grad_w_up: float32 [768, 3072], P('band', 'img')
- grad_w_down: float32 [3072, 768], P('band', 'img')
- grad_bias_qv: float32 [1536], P('img')
- grad_bias_out: float32 [768], P('img')
- grad_bias_up: float32 [3072], P('img')
- grad_bias_down: float32 [768], P('img')
- grad_gain_one: float32 [768], P('img')
- grad_shift_one: float32 [768], P('img')
- grad_gain_two: float32 [768], P('img')
- grad_shift_two: float32 [768], P('img')
The draws below stay inside these ranges and needn't reach their ends.
Inputs may be any that keep to these rules, and one draw needn't show every extreme that they name: `slot_kind`: 0: an empty slot. 1: one image of 32 x 32 tokens. 2: four images of (16) x (16) tokens, as image_of gives them.
All inputs are finite; a program needn't handle non-finite values.
Results may differ from the reference program's by a relative error of at most 0.015.
Values may be sent and summed in bfloat16 or wider, within the bound.
A program may use at most 256 MiB of HBM per device.

```python
import jax
import jax.numpy as jnp
from jax import lax

D = 768
HEADS = 16
HEAD_DIM = 48
FF = 3072
SLOTS = 2
GROUPS = 8
GRID = 1024
ROWS = 256


def touch_ends(array, own_key, low, top_value):
    extent = array.shape
    index_at = [jax.random.randint(jax.random.fold_in(own_key, axis), (), 0, extent[axis]) for axis in range(len(extent))]
    array = array.at[tuple(index_at)].set(low)
    longest = extent.index(max(extent))
    index_at[longest] = (index_at[longest] + 1) % extent[longest]
    return array.at[tuple(index_at)].set(top_value)


def with_spikes(array, key, source, target, blocks, factor):
    def block_of(position):
        return (jnp.arange(array.shape[position]) // (array.shape[position] // blocks)).reshape((-1,) + (1,) * (array.ndim - 1 - position))

    near = jax.random.permutation(key, blocks)[block_of(target)]
    other_side = (block_of(target) + blocks // 2) % blocks
    return jnp.where((block_of(source) == near) | (block_of(source) == other_side), factor * array, array)


def shard_levels(rng, extent, pieces, least, high):
    def one(position, parts):
        heights = jax.random.uniform(jax.random.fold_in(jax.random.fold_in(rng, 6), position), (parts,), jnp.float32, least / len(pieces), high / len(pieces))
        return jnp.repeat(jnp.exp(heights), extent[position] // parts).reshape((-1,) + (1,) * (len(extent) - position - 1))

    gain = one(*pieces[0])
    for cut in pieces[1:]:
        gain = gain * one(*cut)
    return gain


def scatter_about(key, extent, spread, reach, cuts=(), held_as=jnp.bfloat16):
    level = shard_levels(key, extent, cuts, -0.22, 0.18) if cuts else 1.0
    values = jax.random.normal(key, extent, jnp.float32) * spread * level
    return jnp.minimum(jnp.maximum(values, -reach), reach).astype(held_as)


def heavy_noise(own_key, extent, scale, limit, cuts, heavy, held_as=jnp.bfloat16):
    drawn = scale * jax.random.normal(own_key, extent, jnp.float32)
    if cuts:
        drawn = drawn * shard_levels(own_key, extent, cuts, -0.22, 0.18)
    return jnp.clip(with_spikes(drawn, jax.random.fold_in(own_key, 3), *heavy), -limit, limit).astype(held_as)


def setup_inputs(seed: int = 0) -> dict:
    splits = jax.random.split(jax.random.key(seed), 16)
    return {
        "tokens": scatter_about(splits[0], (GROUPS, GRID, SLOTS, D), 1.0, 6.0, ((0, 8), (1, 4))),
        "slot_kind": touch_ends(jax.random.randint(splits[1], (GROUPS, SLOTS), 0, 3), jax.random.fold_in(splits[1], 1), 0, 2).astype(jnp.int32),
        "w_qkv": scatter_about(splits[2], (D, 3 * D), (D // 2) ** -0.5, 0.3125, ((0, 4), (1, 8))),
        "w_out": scatter_about(splits[3], (D, D), (D // 64) ** -0.5, 1.75, ((0, 4), (1, 8))),
        "w_up": scatter_about(splits[4], (D, FF), D ** -0.5, 0.21875, ((0, 4), (1, 8))),
        "w_down": scatter_about(splits[5], (FF, D), FF ** -0.5, 0.109375, ((0, 4), (1, 8))),
        "bias_qv": scatter_about(splits[6], (2 * D,), 0.3, 2.0, ((0, 8),)),
        "bias_out": scatter_about(splits[7], (D,), 0.3, 2.0, ((0, 8),)),
        "bias_up": scatter_about(splits[8], (FF,), 0.3, 2.0, ((0, 8),)),
        "bias_down": scatter_about(splits[9], (D,), 0.3, 2.0, ((0, 8),)),
        "gain_one": jnp.clip(1.0 + 0.15 * jax.random.normal(splits[10], (D,), jnp.float32), 0.25, 1.75).astype(jnp.bfloat16),
        "shift_one": scatter_about(splits[11], (D,), 0.3, 2.0, ((0, 8),)),
        "gain_two": jnp.clip(1.0 + 0.15 * jax.random.normal(splits[12], (D,), jnp.float32), 0.25, 1.75).astype(jnp.bfloat16),
        "shift_two": scatter_about(splits[13], (D,), 0.3, 2.0, ((0, 8),)),
        "cotangent": heavy_noise(splits[14], (GROUPS, GRID, SLOTS, D), 1.0, 6.0, ((0, 8), (1, 4)), (0, 3, 8, 2.0)),
    }


@jax.custom_vjp
def low(v):
    return lax.optimization_barrier(v.astype(jnp.bfloat16)).astype(jnp.float32)

@jax.custom_vjp
def low_back(v):
    return v

def low_keep(v):
    return (low(v), None)

def low_pass(kept, grad):
    return (grad,)

def back_keep(v):
    return (v, None)

def back_low(kept, grad):
    return (low(grad),)
low.defvjp(low_keep, low_pass)
low_back.defvjp(back_keep, back_low)
EPSILON = 1e-06
MASKED = -1e+30

def layer_norm(values, gain_vec, shift_vec):
    average = lax.optimization_barrier(jnp.mean(values, axis=-1, keepdims=True))
    centered = values - average
    variance = lax.optimization_barrier(jnp.mean(centered * centered, axis=-1, keepdims=True))
    return centered * lax.rsqrt(variance + EPSILON) * gain_vec + shift_vec

def mixed_dot(left_side, right_side):
    return jnp.dot(left_side, right_side, precision=lax.Precision.HIGHEST, preferred_element_type=jnp.float32)

def image_ids(kind_values, positions, band_rows):
    small_id = 2 * (positions % band_rows // (band_rows // 2)) + positions // band_rows // 2
    return jnp.where(kind_values == 2, small_id, 0)

def one_group(weights, tokens_grp, kinds_grp):
    w_qkv, w_out, w_up, w_down, bias_qv, bias_out, bias_up, bias_down, gain_one, shift_one, gain_two, shift_two = weights
    seq_count = tokens_grp.shape[0]
    flat_tokens = tokens_grp.reshape(-1, D)
    score_scale = 1.0 / HEAD_DIM ** 0.5
    normed_low = low(layer_norm(flat_tokens, gain_one, shift_one))
    projected = mixed_dot(normed_low, w_qkv)
    query_low = low(low_back(projected[:, :D] + bias_qv[:D]) * score_scale)
    key_low = low(low_back(projected[:, D:2 * D]))
    value_low = low(low_back(projected[:, 2 * D:] + bias_qv[D:]))
    query_low = query_low.reshape(seq_count, GRID, HEADS, HEAD_DIM)
    key_low = key_low.reshape(seq_count, GRID, HEADS, HEAD_DIM)
    value_low = value_low.reshape(seq_count, GRID, HEADS, HEAD_DIM)
    scores = low_back(jnp.einsum('gqhd,gkhd->ghqk', query_low, key_low, precision=lax.Precision.HIGHEST))
    positions = jnp.arange(GRID, dtype=jnp.int32)
    identity = image_ids(kinds_grp[:, None], positions[None, :], ROWS)
    allowed = identity[:, None, :, None] == identity[:, None, None, :]
    scores = jnp.where(allowed, scores, MASKED)
    maximum = lax.optimization_barrier(jnp.max(scores, axis=-1, keepdims=True))
    exponent = jnp.exp(scores - maximum)
    attention_p = low(exponent / lax.optimization_barrier(jnp.sum(exponent, axis=-1, keepdims=True)))
    attended = jnp.einsum('ghqk,gkhd->gqhd', attention_p, value_low, precision=lax.Precision.HIGHEST)
    attended = low(low_back(attended.reshape(-1, D)))
    branch = low_back(mixed_dot(attended, w_out) + bias_out)
    middle = flat_tokens + branch
    normed_two = low(layer_norm(middle, gain_two, shift_two))
    hidden_pre = low_back(mixed_dot(normed_two, w_up) + bias_up)
    activated = low(jax.nn.gelu(hidden_pre, approximate=False))
    mlp_out = low_back(mixed_dot(activated, w_down) + bias_down)
    result = (middle + mlp_out).reshape(seq_count, GRID, D)
    valid_rows = (kinds_grp > 0).astype(jnp.float32)
    return result * valid_rows[:, None, None]

def reference(tokens, slot_kind, w_qkv, w_out, w_up, w_down, bias_qv, bias_out, bias_up, bias_down, gain_one, shift_one, gain_two, shift_two, cotangent):
    params = tuple((parameter.astype(jnp.float32) for parameter in (w_qkv, w_out, w_up, w_down, bias_qv, bias_out, bias_up, bias_down, gain_one, shift_one, gain_two, shift_two)))
    slot_pairs = slot_kind.reshape(-1, 2)
    inputs = tokens.astype(jnp.float32).transpose(0, 2, 1, 3).reshape(-1, 2, GRID, D)

    def forward(weights, sequences):

        def one_pair(pair_data):
            return one_group(weights, pair_data[0], pair_data[1])
        return lax.map(jax.checkpoint(one_pair), (sequences, slot_pairs))
    result, pullback = jax.vjp(forward, params, inputs)
    cot_seqs = cotangent.astype(jnp.float32).transpose(0, 2, 1, 3).reshape(-1, 2, GRID, D)
    grad_params, grad_inputs = pullback(cot_seqs)

    def restore(values):
        return values.reshape(GROUPS, SLOTS, GRID, D).transpose(0, 2, 1, 3)
    return (restore(result).astype(jnp.bfloat16), restore(grad_inputs).astype(jnp.bfloat16), grad_params[0], grad_params[1], grad_params[2], grad_params[3], grad_params[4], grad_params[5], grad_params[6], grad_params[7], grad_params[8], grad_params[9], grad_params[10], grad_params[11])
```

```python
import functools
import math

import jax
import jax.numpy as jnp
from jax import lax
from jax.experimental import pallas as pl
from jax.experimental.pallas import tpu as pltpu
from jax.sharding import PartitionSpec as P

HEADS = 16
HEAD_DIM = 48
EPSILON = 1e-06
MASKED = -1e30
BF = jnp.bfloat16
F = jnp.float32
MESH = pl.DeviceIdType.MESH
VM = pl.BlockSpec(memory_space=pltpu.VMEM)
SM = pl.BlockSpec(memory_space=pltpu.SMEM)
ANY = pl.BlockSpec(memory_space=pl.ANY)
LIMIT = 67043328


def dg(left, right, left_dim, right_dim):
    return lax.dot_general(
        left, right, (((left_dim,), (right_dim,)), ((), ())), preferred_element_type=F
    )


def shape(dims, dtype):
    return jax.ShapeDtypeStruct(tuple(dims), dtype)


def row_sums(values):
    ones = jnp.ones((8, values.shape[1]), BF)
    if values.dtype == BF:
        return dg(ones, values, 1, 1)
    high = values.astype(BF)
    low = (values - high.astype(F)).astype(BF)
    return dg(ones, high, 1, 1) + dg(ones, low, 1, 1)


def normalize(values):
    average = jnp.mean(values, axis=0, keepdims=True)
    centered = values - average
    variance = jnp.mean(centered * centered, axis=0, keepdims=True)
    inverse = lax.rsqrt(variance + EPSILON)
    return centered * inverse, inverse


def norm_back(error, normed, inverse, gain):
    f = gain * error
    mean_f = jnp.mean(f, axis=0, keepdims=True)
    mean_fn = jnp.mean(f * normed, axis=0, keepdims=True)
    return (f - mean_f - normed * mean_fn) * inverse


def project_kernel(x_ref, w_ref, gain_ref, shift_ref, bias_ref, h_ref, qkv_ref):
    width = x_ref.shape[0]
    normed, _ = normalize(x_ref[...].astype(F))
    h_ref[...] = (normed * gain_ref[...] + shift_ref[...]).astype(BF)
    scale = 1.0 / math.sqrt(HEAD_DIM)
    step = 256

    @pl.loop(0, 3 * width // step)
    def _(j):
        rows = pl.ds(pl.multiple_of(j * step, step), step)
        out = dg(w_ref[rows, :], h_ref[...], 1, 0) + bias_ref[rows, :]
        qkv_ref[rows, :] = (out * jnp.where(j < width // step, scale, 1.0)).astype(BF)


def project(x, w, gain, shift, bias):
    width, tokens = x.shape
    return pl.pallas_call(
        project_kernel,
        name="project",
        out_shape=(shape((width, tokens), BF), shape((3 * width, tokens), BF)),
        in_specs=[VM] * 5,
        out_specs=(VM, VM),
        compiler_params=pltpu.CompilerParams(vmem_limit_bytes=LIMIT),
    )(x, w, gain, shift, bias)


def fill_bias(scalars_ref, bias_ref, rows):
    lane_half = lax.broadcasted_iota(jnp.int32, (1, rows), 1) // (rows // 2)
    for s in range(2):
        small = scalars_ref[s] == 2
        for other in range(2):
            for half in range(2):
                keep = jnp.logical_and(other == 0, lane_half == half)
                masked = jnp.where(small, MASKED, 0.0)
                bias_ref[pl.ds(4 * s + 2 * other + half, 1), :] = jnp.where(
                    keep, jnp.zeros((1, rows), F), jnp.full((1, rows), masked, F)
                )


def add_bias(scores, bias_ref, s, other):
    rows = scores.shape[0]
    at = 4 * s + 2 * other
    return jnp.concatenate(
        [
            scores[: rows // 2] + bias_ref[pl.ds(at, 1), :],
            scores[rows // 2 :] + bias_ref[pl.ds(at + 1, 1), :],
        ],
        axis=0,
    )


def head_slices(i, rows):
    s, h = i // HEADS, i % HEADS
    lanes = pl.ds(pl.multiple_of(s * rows, rows), rows)
    first = pl.ds(pl.multiple_of(h * HEAD_DIM, 16), HEAD_DIM)
    second = pl.ds(pl.multiple_of(HEADS * HEAD_DIM + h * HEAD_DIM, 16), HEAD_DIM)
    return s, lanes, first, second


def attend_step(i, chip_x, q_ref, kv_ref, bias_ref, out_ref, lse_ref):
    bands = kv_ref.shape[0]
    rows = q_ref.shape[1] // 2
    s, lanes, first, second = head_slices(i, rows)
    q = q_ref[first, lanes]
    scores = []
    maximum = None
    for b in range(bands):
        other = jnp.where(chip_x == b // 2, 0, 1)
        part = add_bias(dg(kv_ref[b, first, lanes], q, 0, 0), bias_ref, s, other)
        scores.append(part)
        top = jnp.max(part, axis=0, keepdims=True)
        maximum = top if maximum is None else jnp.maximum(maximum, top)
    total, acc = 0.0, 0.0
    for b in range(bands):
        weight = jnp.exp(scores[b] - maximum)
        total = total + jnp.sum(weight, axis=0, keepdims=True)
        acc = acc + dg(kv_ref[b, second, lanes], weight.astype(BF), 1, 0)
    out_ref[first, lanes] = acc / total
    lse_ref[pl.ds(i, 1), :] = maximum + jnp.log(total)


def attend_kernel(unroll, scalars_ref, q_ref, kv_ref, out_ref, lse_ref, bias_ref):
    fill_bias(scalars_ref, bias_ref, q_ref.shape[1] // 2)

    @pl.loop(0, 2 * HEADS // unroll)
    def _(j):
        for k in range(unroll):
            attend_step(
                j * unroll + k, scalars_ref[2], q_ref, kv_ref, bias_ref, out_ref, lse_ref
            )


def attend(scalars, q, kv):
    width, tokens = q.shape
    return pl.pallas_call(
        functools.partial(attend_kernel, 4),
        name="attend",
        out_shape=(shape((width, tokens), F), shape((2 * HEADS, tokens // 2), F)),
        in_specs=[SM, VM, VM],
        out_specs=(VM, VM),
        scratch_shapes=[pltpu.VMEM((8, tokens // 2), F)],
        compiler_params=pltpu.CompilerParams(vmem_limit_bytes=LIMIT),
    )(scalars, q, kv)


def attend_back_step(
    i, chip_x, q_ref, kv_ref, out_ref, lse_ref, dout_ref, bias_ref, dq_ref, dkv_ref
):
    bands = kv_ref.shape[0]
    rows = q_ref.shape[1] // 2
    s, lanes, first, second = head_slices(i, rows)
    q = q_ref[first, lanes]
    dout = dout_ref[first, lanes]
    delta = jnp.sum(out_ref[first, lanes] * dout.astype(F), axis=0, keepdims=True)
    lse = lse_ref[pl.ds(i, 1), :]
    dq = 0.0
    for b in range(bands):
        other = jnp.where(chip_x == b // 2, 0, 1)
        k, v = kv_ref[b, first, lanes], kv_ref[b, second, lanes]
        scores = add_bias(dg(k, q, 0, 0), bias_ref, s, other)
        dweight = dg(v, dout, 0, 0)
        weight = jnp.exp(scores - lse)
        dscores = (weight * (dweight - delta)).astype(BF)
        dq = dq + dg(k, dscores, 1, 0)
        dkv_ref[b, first, lanes] = dg(q, dscores, 1, 1).astype(BF)
        dkv_ref[b, second, lanes] = dg(dout, weight.astype(BF), 1, 1).astype(BF)
    dq_ref[first, lanes] = (dq * (1.0 / math.sqrt(HEAD_DIM))).astype(BF)


def attend_back_kernel(
    unroll, scalars_ref, q_ref, kv_ref, out_ref, lse_ref, dout_ref, dq_ref, dkv_ref, bias_ref
):
    fill_bias(scalars_ref, bias_ref, q_ref.shape[1] // 2)

    @pl.loop(0, 2 * HEADS // unroll)
    def _(j):
        for k in range(unroll):
            attend_back_step(
                j * unroll + k,
                scalars_ref[2],
                q_ref,
                kv_ref,
                out_ref,
                lse_ref,
                dout_ref,
                bias_ref,
                dq_ref,
                dkv_ref,
            )


def attend_back(scalars, q, kv, out, lse, dout):
    return pl.pallas_call(
        functools.partial(attend_back_kernel, 4),
        name="attend_back",
        out_shape=(shape(q.shape, BF), shape(kv.shape, BF)),
        in_specs=[SM] + [VM] * 5,
        out_specs=(VM, VM),
        scratch_shapes=[pltpu.VMEM((8, q.shape[1] // 2), F)],
        compiler_params=pltpu.CompilerParams(vmem_limit_bytes=LIMIT),
    )(scalars, q, kv, out, lse, dout)


def middle_kernel(
    x_ref,
    cot_ref,
    valid_ref,
    att_ref,
    w_out_ref,
    w_up_ref,
    w_down_ref,
    bias_out_ref,
    gain_ref,
    shift_ref,
    bias_up_ref,
    bias_down_ref,
    out_ref,
    dmid_ref,
    datt_ref,
    g_out_ref,
    g_up_ref,
    g_down_ref,
    sum_up_ref,
    sums_ref,
    mid_ref,
    norm_ref,
    h_ref,
    dmlp_ref,
    mlp_ref,
    err_ref,
    attb_ref,
    dbranch_ref,
):
    width, tokens = x_ref.shape
    hidden = w_up_ref.shape[0]
    step = 256
    attb_ref[...] = att_ref[...].astype(BF)

    @pl.loop(0, width // step)
    def _(j):
        rows = pl.ds(pl.multiple_of(j * step, step), step)
        mid_ref[rows, :] = (
            dg(w_out_ref[rows, :], attb_ref[...], 1, 0)
            + bias_out_ref[rows, :]
            + x_ref[rows, :].astype(F)
        )

    normed, inverse = normalize(mid_ref[...])
    norm_ref[...] = normed
    h_ref[...] = (normed * gain_ref[...] + shift_ref[...]).astype(BF)
    dmlp_ref[...] = (cot_ref[...].astype(F) * valid_ref[...]).astype(BF)
    mlp_ref[...] = jnp.zeros_like(mlp_ref)
    err_ref[...] = jnp.zeros_like(err_ref)

    @pl.loop(0, hidden // step)
    def _(j):
        rows = pl.ds(pl.multiple_of(j * step, step), step)
        pre = dg(w_up_ref[rows, :], h_ref[...], 1, 0) + bias_up_ref[rows, :]
        phi = 0.5 + 0.5 * lax.erf(pre * math.sqrt(0.5))
        act = (pre * phi).astype(BF)
        slope = phi + pre * jnp.exp(pre * pre * -0.5) * (1.0 / math.sqrt(2.0 * math.pi))
        mlp_ref[...] += dg(w_down_ref[:, rows], act, 1, 0)
        dact = dg(w_down_ref[:, rows], dmlp_ref[...], 0, 0)
        dhid = (slope * dact).astype(BF)
        g_down_ref[:, rows] = dg(dmlp_ref[...], act, 1, 1).astype(BF)
        g_up_ref[rows, :] = dg(dhid, h_ref[...], 1, 1).astype(BF)
        sum_up_ref[:, rows] = row_sums(dhid)
        err_ref[...] += dg(w_up_ref[rows, :], dhid, 0, 0)

    out_ref[...] = ((mid_ref[...] + mlp_ref[...] + bias_down_ref[...]) * valid_ref[...]).astype(BF)
    err = err_ref[...]
    sums_ref[0] = row_sums(dmlp_ref[...])
    sums_ref[1] = row_sums(err * norm_ref[...])
    sums_ref[2] = row_sums(err)
    dmid = cot_ref[...].astype(F) * valid_ref[...] + norm_back(
        err, norm_ref[...], inverse, gain_ref[...]
    )
    dmid_ref[...] = dmid
    dbranch_ref[...] = dmid.astype(BF)
    sums_ref[3] = row_sums(dbranch_ref[...])
    datt_ref[...] = dg(w_out_ref[...], dbranch_ref[...], 0, 0).astype(BF)

    @pl.loop(0, width // step)
    def _(j):
        rows = pl.ds(pl.multiple_of(j * step, step), step)
        g_out_ref[rows, :] = dg(dbranch_ref[rows, :], attb_ref[...], 1, 1).astype(BF)


def middle(x, cot, valid, att, w_out, w_up, w_down, bias_out, gain, shift, bias_up, bias_down):
    width, tokens = x.shape
    hidden = w_up.shape[0]
    full = (width, tokens)
    return pl.pallas_call(
        middle_kernel,
        name="middle",
        out_shape=(
            shape(full, BF),
            shape(full, F),
            shape(full, BF),
            shape(w_out.shape, BF),
            shape(w_up.shape, BF),
            shape(w_down.shape, BF),
            shape((8, hidden), F),
            shape((4, 8, width), F),
        ),
        in_specs=[VM] * 12,
        out_specs=tuple([VM] * 8),
        scratch_shapes=[
            pltpu.VMEM(full, F),
            pltpu.VMEM(full, F),
            pltpu.VMEM(full, BF),
            pltpu.VMEM(full, BF),
            pltpu.VMEM(full, F),
            pltpu.VMEM(full, F),
            pltpu.VMEM(full, BF),
            pltpu.VMEM(full, BF),
        ],
        compiler_params=pltpu.CompilerParams(vmem_limit_bytes=LIMIT),
    )(x, cot, valid, att, w_out, w_up, w_down, bias_out, gain, shift, bias_up, bias_down)


def finish_kernel(
    x_ref, h_ref, dq_ref, dkv_ref, w_ref, gain_ref, dmid_ref, gx_ref, g_ref, sums_ref, err_ref
):
    width, tokens = x_ref.shape
    step = 256
    blocks = width // step
    err_ref[...] = jnp.zeros_like(err_ref)
    for ref, count, base in ((dq_ref, blocks, 0), (dkv_ref, 2 * blocks, blocks)):

        @pl.loop(0, count)
        def _(j):
            rows = pl.ds(pl.multiple_of(j * step, step), step)
            to = pl.ds(pl.multiple_of((j + base) * step, step), step)
            g_ref[to, :] = dg(ref[rows, :], h_ref[...], 1, 1).astype(BF)
            err_ref[...] += dg(w_ref[to, :], ref[rows, :], 0, 0)

    normed, inverse = normalize(x_ref[...].astype(F))
    err = err_ref[...]
    sums_ref[0] = row_sums(dq_ref[...])
    sums_ref[1] = row_sums(dkv_ref[pl.ds(width, width), :])
    sums_ref[2] = row_sums(err * normed)
    sums_ref[3] = row_sums(err)
    gx_ref[...] = (dmid_ref[...] + norm_back(err, normed, inverse, gain_ref[...])).astype(BF)


def finish(x, h, dq, dkv, w, gain, dmid):
    width, tokens = x.shape
    return pl.pallas_call(
        finish_kernel,
        name="finish",
        out_shape=(shape(x.shape, BF), shape(w.shape, BF), shape((4, 8, width), F)),
        in_specs=[VM] * 7,
        out_specs=(VM, VM, VM),
        scratch_shapes=[pltpu.VMEM(x.shape, F)],
        compiler_params=pltpu.CompilerParams(vmem_limit_bytes=LIMIT),
    )(x, h, dq, dkv, w, gain, dmid)


class Place:
    def __init__(self, images):
        self.images = images
        self.depth = images // 2
        self.img = lax.axis_index("img")
        self.band = lax.axis_index("band")
        self.z, self.y = self.img // 2, self.img % 2
        self.x, self.c = self.band // 2, self.band % 2
        self.partner = (self.img, self.band + 1 - 2 * self.c)
        self.across_x = (self.img, self.band + 2 - 4 * self.x)
        self.across_y = (self.img + 1 - 2 * self.y, self.band)

    def along_z(self, k):
        z = lax.rem(self.z + k, self.depth)
        return (2 * z + self.y, self.band), z


def greet(peers):
    barrier = pltpu.get_barrier_semaphore()
    for peer in peers:
        pl.semaphore_signal(barrier, inc=1, device_id=peer, device_id_type=MESH)
    pl.semaphore_wait(barrier, len(peers))


def send(src, dst, send_sem, recv_sem, peer):
    copy = pltpu.make_async_remote_copy(
        src_ref=src,
        dst_ref=dst,
        send_sem=send_sem,
        recv_sem=recv_sem,
        device_id=peer,
        device_id_type=MESH,
    )
    copy.start()
    return copy


def comm_params(collective_id):
    return pltpu.CompilerParams(
        collective_id=collective_id, has_side_effects=True, vmem_limit_bytes=LIMIT
    )


def split_rows(shards, parts):
    return jnp.concatenate(
        [item.reshape(parts, item.shape[0] // parts, item.shape[1]) for item in shards], axis=1
    )


def gather_kernel(
    images, narrow_ref, wide_ref, small_ref, qkv_ref, out_ref, up_ref, down_ref, smalls_ref,
    theirs_ref, mine_ref, mine_wide_ref, local_sem, send_sem, recv_sem, small_send, small_recv,
):
    at = Place(images)
    depth, near = at.depth, at.depth // 2
    peers = [at.partner, at.across_x, at.across_y]
    peers += [at.along_z(k)[0] for k in range(1, depth)]
    others = [(lax.rem(at.img + k, images), at.band) for k in range(1, images)]
    others = peers[:2] + others
    greet(others)
    c = at.c

    first = [
        send(narrow_ref.at[1 - c], theirs_ref, send_sem.at[16], recv_sem.at[16], at.partner)
    ]
    half = wide_ref.shape[0] // 2
    wide = wide_ref.shape[1]
    lanes = pl.ds(pl.multiple_of(c * wide, 128), wide)
    own = pltpu.make_async_copy(
        wide_ref.at[pl.ds(pl.multiple_of(c * half, 8), half), :],
        mine_wide_ref.at[:, lanes],
        local_sem.at[0],
    )
    own.start()
    first.append(
        send(
            wide_ref.at[pl.ds(pl.multiple_of((1 - c) * half, 8), half), :],
            mine_wide_ref.at[:, lanes],
            send_sem.at[17],
            recv_sem.at[17],
            at.partner,
        )
    )
    small_copies = []
    keep = pltpu.make_async_copy(small_ref, smalls_ref.at[at.img], local_sem.at[1])
    keep.start()
    for k in range(1, images):
        small_copies.append(
            send(
                small_ref,
                smalls_ref.at[at.img],
                small_send.at[k - 1],
                small_recv.at[k - 1],
                others[k + 1],
            )
        )
    first[0].wait_recv()
    mine, theirs = narrow_ref[c], theirs_ref[...]
    width = mine.shape[1]
    mine_ref[:, pl.ds(0, width)] = jnp.where(c == 0, mine, theirs)
    mine_ref[:, pl.ds(width, width)] = jnp.where(c == 0, theirs, mine)
    own.wait()
    first[1].wait_recv()

    refs = (qkv_ref, out_ref, up_ref, down_ref)
    views, sources = [], []
    row = 0
    for ref in refs[:3]:
        rows = ref.shape[2] // 2
        sources.append(mine_ref.at[pl.ds(row, rows), :])
        row += rows
    sources.append(mine_wide_ref)

    sends = list(first) + small_copies
    stage = [[None] * 4 for _ in refs]
    locals_ = [keep]

    def rows_of(m):
        rows = refs[m].shape[2] // 2
        return pl.ds(pl.multiple_of(c * rows, 8), rows)

    def lanes_of(m):
        half_lanes = refs[m].shape[3] // 2
        return pl.ds(pl.multiple_of(at.x * half_lanes, 128), half_lanes)

    for m, ref in enumerate(refs):
        piece = ref.at[at.z, at.y, rows_of(m), lanes_of(m)]
        copy = pltpu.make_async_copy(sources[m], piece, local_sem.at[2 + m])
        copy.start()
        stage[m][0] = [copy]
        for k in range(1, depth):
            index = 18 + m * (depth - 1) + k - 1
            stage[m][0].append(
                send(sources[m], piece, send_sem.at[index], recv_sem.at[index], at.along_z(k)[0])
            )

    def second(m):
        stage[m][0][0].wait()
        for copy in stage[m][0][1:]:
            copy.wait_recv()
        region = (pl.ds(0, near), at.y, rows_of(m), lanes_of(m))
        to_x = refs[m].at[region]
        region = (pl.ds(near, depth - near), at.y, rows_of(m), lanes_of(m))
        to_y = refs[m].at[region]
        stage[m][1] = [
            send(to_x, to_x, send_sem.at[4 * m], recv_sem.at[4 * m], at.across_x),
            send(to_y, to_y, send_sem.at[4 * m + 1], recv_sem.at[4 * m + 1], at.across_y),
        ]

    def third(m):
        for copy in stage[m][1]:
            copy.wait_recv()
        to_y = refs[m].at[pl.ds(0, near), at.y, rows_of(m), :]
        to_x = refs[m].at[pl.ds(near, depth - near), :, rows_of(m), lanes_of(m)]
        stage[m][2] = [
            send(to_y, to_y, send_sem.at[4 * m + 2], recv_sem.at[4 * m + 2], at.across_y),
            send(to_x, to_x, send_sem.at[4 * m + 3], recv_sem.at[4 * m + 3], at.across_x),
        ]

    last = 18 + 4 * (depth - 1)

    def fourth(m):
        for copy in stage[m][2]:
            copy.wait_recv()
        part = refs[m].at[:, :, rows_of(m), :]
        stage[m][3] = [
            send(part, part, send_sem.at[last + m], recv_sem.at[last + m], at.partner)
        ]

    second(0)
    second(1)
    third(0)
    second(2)
    third(1)
    fourth(0)
    second(3)
    third(2)
    fourth(1)
    third(3)
    fourth(2)
    fourth(3)
    for m in range(4):
        stage[m][3][0].wait_recv()
        for copy in stage[m][0][1:] + stage[m][1] + stage[m][2] + stage[m][3]:
            copy.wait_send()
    for copy in first:
        copy.wait_send()
    for copy in small_copies:
        copy.wait()
    keep.wait()


def gather(images, narrow, wide, small, widths):
    depth = images // 2
    full = 4 * narrow.shape[2]
    outs = [shape((depth, 2, w, full), BF) for w in widths]
    outs.append(shape((depth, 2, wide.shape[0], 4 * wide.shape[1]), BF))
    outs.append(shape((images,) + small.shape, F))
    count = 18 + 4 * (depth - 1) + 4
    return pl.pallas_call(
        functools.partial(gather_kernel, images),
        name="gather",
        out_shape=tuple(outs),
        in_specs=[VM, VM, VM],
        out_specs=(ANY, ANY, ANY, ANY, VM),
        scratch_shapes=[
            pltpu.VMEM(narrow.shape[1:], BF),
            pltpu.VMEM((narrow.shape[1], 2 * narrow.shape[2]), BF),
            pltpu.VMEM((wide.shape[0] // 2, 2 * wide.shape[1]), BF),
            pltpu.SemaphoreType.DMA((6,)),
            pltpu.SemaphoreType.DMA((count,)),
            pltpu.SemaphoreType.DMA((count,)),
            pltpu.SemaphoreType.DMA((images - 1,)),
            pltpu.SemaphoreType.DMA((images - 1,)),
        ],
        compiler_params=comm_params(0),
    )(narrow, wide, small)


def share_kernel(images, kv_ref, all_ref, local_sem, send_sem, recv_sem):
    at = Place(images)
    greet([at.partner, at.across_x])
    rows = kv_ref.shape[1] // 2
    mine = pltpu.make_async_copy(kv_ref, all_ref.at[at.band], local_sem)
    mine.start()
    copies = []
    for s in range(2):
        lanes = pl.ds(s * rows, rows)
        copies.append(
            send(
                kv_ref.at[:, lanes],
                all_ref.at[at.band, :, lanes],
                send_sem.at[s],
                recv_sem.at[s],
                at.across_x,
            )
        )
    near = send(kv_ref, all_ref.at[at.band], send_sem.at[2], recv_sem.at[2], at.partner)
    passed = []
    for s in range(2):
        copies[s].wait_recv()
        part = all_ref.at[at.across_x[1], :, pl.ds(s * rows, rows)]
        passed.append(send(part, part, send_sem.at[3 + s], recv_sem.at[3 + s], at.partner))
    for copy in passed + [near]:
        copy.wait()
    for copy in copies:
        copy.wait_send()
    mine.wait()


def share(images, bands, kv):
    return pl.pallas_call(
        functools.partial(share_kernel, images),
        name="share",
        out_shape=shape((bands,) + kv.shape, BF),
        in_specs=[VM],
        out_specs=ANY,
        scratch_shapes=[
            pltpu.SemaphoreType.DMA,
            pltpu.SemaphoreType.DMA((5,)),
            pltpu.SemaphoreType.DMA((5,)),
        ],
        compiler_params=comm_params(1),
    )(kv)


def add_rows(total_ref, other_ref, step):
    @pl.loop(0, total_ref.shape[0] // step)
    def _(j):
        rows = pl.ds(pl.multiple_of(j * step, step), step)
        total_ref[rows, :] = (
            total_ref[rows, :].astype(F) + other_ref[rows, :].astype(F)
        ).astype(total_ref.dtype)


def unshare_kernel(images, dkv_ref, sum_ref, near_ref, far_ref, send_sem, recv_sem):
    at = Place(images)
    greet([at.partner, at.across_x])
    mate, far = at.partner[1], at.across_x[1]
    far_mate = at.band + 2 - 4 * at.x + 1 - 2 * at.c
    one = send(dkv_ref.at[far_mate], near_ref.at[0], send_sem.at[0], recv_sem.at[0], at.partner)
    two = send(dkv_ref.at[mate], near_ref.at[1], send_sem.at[1], recv_sem.at[1], at.partner)
    one.wait_recv()
    add_rows(near_ref.at[0], dkv_ref.at[far], 64)
    three = send(near_ref.at[0], far_ref, send_sem.at[2], recv_sem.at[2], at.across_x)
    two.wait_recv()
    add_rows(near_ref.at[1], dkv_ref.at[at.band], 64)
    three.wait_recv()
    sum_ref[...] = near_ref[1]
    add_rows(sum_ref, far_ref, 64)
    for copy in (one, two, three):
        copy.wait_send()


def unshare(images, dkv):
    block = dkv.shape[1:]
    return pl.pallas_call(
        functools.partial(unshare_kernel, images),
        name="unshare",
        out_shape=shape(block, BF),
        in_specs=[VM],
        out_specs=VM,
        scratch_shapes=[
            pltpu.VMEM((2,) + block, BF),
            pltpu.VMEM(block, BF),
            pltpu.SemaphoreType.DMA((3,)),
            pltpu.SemaphoreType.DMA((3,)),
        ],
        compiler_params=comm_params(2),
    )(dkv)


def scatter_kernel(
    images, bands, qkv_ref, out_ref, up_ref, down_ref, small_ref,
    narrow_ref, wide_ref, small_out_ref, *rest,
):
    at = Place(images)
    depth, near = at.depth, at.depth // 2
    c = at.c
    refs = (down_ref, up_ref, out_ref, qkv_ref)
    count = len(refs)
    one, two_x, two_y, three, four = (rest[count * k : count * k + count] for k in range(5))
    away_ref, away_wide_ref, small_in, small_band = rest[5 * count : 5 * count + 4]
    send_sem, recv_sem, small_send, small_recv = rest[5 * count + 4 :]
    others = [(lax.rem(at.img + k, images), at.band) for k in range(1, images)]
    mates = [(at.img, lax.rem(at.band + k, bands)) for k in range(1, bands)]
    greet(others + mates)

    small_copies = []
    for k in range(1, images):
        small_copies.append(
            send(
                small_ref.at[others[k - 1][0]],
                small_in.at[k - 1],
                small_send.at[k - 1],
                small_recv.at[k - 1],
                others[k - 1],
            )
        )

    def rows_of(m, core):
        rows = refs[m].shape[2] // 2
        return pl.ds(pl.multiple_of(core * rows, 8), rows)

    def lanes_of(m, x):
        half_lanes = refs[m].shape[3] // 2
        return pl.ds(pl.multiple_of(x * half_lanes, 128), half_lanes)

    stage = [[] for _ in refs]
    per = 6 + depth - 1
    for m, ref in enumerate(refs):
        stage[m].append(
            [
                send(
                    ref.at[:, :, rows_of(m, 1 - c), :],
                    one[m],
                    send_sem.at[per * m],
                    recv_sem.at[per * m],
                    at.partner,
                )
            ]
        )

    def add(total, other):
        total[...] = (total[...].astype(F) + other[...].astype(F)).astype(BF)

    def first(m):
        stage[m][0][0].wait_recv()

        @pl.loop(0, images)
        def _(j):
            add(one[m].at[j // 2, j % 2], refs[m].at[j // 2, j % 2, rows_of(m, c), :])

        stage[m].append(
            [
                send(
                    one[m].at[pl.ds(0, near), :, :, lanes_of(m, 1 - at.x)],
                    two_x[m],
                    send_sem.at[per * m + 1],
                    recv_sem.at[per * m + 1],
                    at.across_x,
                ),
                send(
                    one[m].at[pl.ds(near, depth - near), 1 - at.y],
                    two_y[m],
                    send_sem.at[per * m + 2],
                    recv_sem.at[per * m + 2],
                    at.across_y,
                ),
            ]
        )

    def second(m):
        stage[m][1][0].wait_recv()

        @pl.loop(0, 2 * near)
        def _(j):
            add(two_x[m].at[j // 2, j % 2], one[m].at[j // 2, j % 2, :, lanes_of(m, at.x)])

        copies = [
            send(
                two_x[m].at[:, 1 - at.y],
                three[m].at[pl.ds(0, near)],
                send_sem.at[per * m + 3],
                recv_sem.at[per * m + 3],
                at.across_y,
            )
        ]
        stage[m][1][1].wait_recv()

        @pl.loop(0, depth - near)
        def _(j):
            add(two_y[m].at[j], one[m].at[near + j, at.y])

        copies.append(
            send(
                two_y[m].at[:, :, lanes_of(m, 1 - at.x)],
                three[m].at[pl.ds(near, depth - near)],
                send_sem.at[per * m + 4],
                recv_sem.at[per * m + 4],
                at.across_x,
            )
        )
        stage[m].append(copies)

    def third(m):
        for copy in stage[m][2]:
            copy.wait_recv()

        @pl.loop(0, near)
        def _(j):
            add(three[m].at[j], two_x[m].at[j, at.y])

        @pl.loop(0, depth - near)
        def _(j):
            add(three[m].at[near + j], two_y[m].at[j, :, lanes_of(m, at.x)])

        copies = []
        for k in range(1, depth):
            peer, z = at.along_z(k)
            copies.append(
                send(
                    three[m].at[z],
                    four[m].at[k - 1],
                    send_sem.at[per * m + 5 + k],
                    recv_sem.at[per * m + 5 + k],
                    peer,
                )
            )
        stage[m].append(copies)

    width = narrow_ref.shape[2]
    starts = {}
    row = 0
    for m in (3, 2, 1):
        starts[m] = row
        row += refs[m].shape[2] // 2

    def fourth(m):
        for copy in stage[m][3]:
            copy.wait_recv()
        total = three[m][at.z].astype(F)
        for k in range(1, depth):
            total = total + four[m][k - 1].astype(F)
        if m == 0:
            lanes = wide_ref.shape[2]
            low, high = total[:, :lanes], total[:, lanes:]
            wide_ref[c] = jnp.where(c == 0, low, high)
            away_wide_ref[...] = jnp.where(c == 0, high, low)
            source, target = away_wide_ref, wide_ref.at[c]
        else:
            rows = pl.ds(starts[m], total.shape[0])
            low, high = total[:, :width], total[:, width:]
            narrow_ref[c, rows, :] = jnp.where(c == 0, low, high)
            away_ref[rows, :] = jnp.where(c == 0, high, low)
            source, target = away_ref.at[rows, :], narrow_ref.at[c, rows, :]
        stage[m].append(
            [send(source, target, send_sem.at[per * m + 5], recv_sem.at[per * m + 5], at.partner)]
        )

    def small_one():
        for copy in small_copies:
            copy.wait_recv()
        total = small_ref[at.img]
        for k in range(1, images):
            total = total + small_in[k - 1]
        small_band[at.band] = total
        copies = []
        for k in range(1, bands):
            slot = images - 2 + k
            copies.append(
                send(
                    small_band.at[at.band],
                    small_band.at[at.band],
                    small_send.at[slot],
                    small_recv.at[slot],
                    mates[k - 1],
                )
            )
        return copies

    first(0)
    first(1)
    second(0)
    first(2)
    second(1)
    third(0)
    first(3)
    second(2)
    third(1)
    fourth(0)
    small_mates = small_one()
    second(3)
    third(2)
    fourth(1)
    third(3)
    fourth(2)
    fourth(3)
    for copy in small_mates:
        copy.wait_recv()
    total = small_band[0]
    for k in range(1, bands):
        total = total + small_band[k]
    small_out_ref[...] = total
    for m in range(count):
        stage[m][4][0].wait_recv()
        for copies in stage[m]:
            for copy in copies:
                copy.wait_send()
    for copy in small_copies + small_mates:
        copy.wait_send()


def scatter(images, bands, qkv, out, up, down, small):
    depth = images // 2
    near = depth // 2
    refs = (down, up, out, qkv)
    full = qkv.shape[3]
    one, two_x, two_y, three, four = [], [], [], [], []
    for ref in refs:
        rows, lanes = ref.shape[2] // 2, ref.shape[3]
        one.append(pltpu.VMEM((depth, 2, rows, lanes), BF))
        two_x.append(pltpu.VMEM((near, 2, rows, lanes // 2), BF))
        two_y.append(pltpu.VMEM((depth - near, rows, lanes), BF))
        three.append(pltpu.VMEM((depth, rows, lanes // 2), BF))
        four.append(pltpu.VMEM((depth - 1, rows, lanes // 2), BF))
    rows = sum(ref.shape[2] // 2 for ref in refs[1:])
    wide_rows, wide = down.shape[2] // 2, down.shape[3] // 4
    count = len(refs) * (6 + depth)
    smalls = images + bands - 2
    return pl.pallas_call(
        functools.partial(scatter_kernel, images, bands),
        name="scatter",
        out_shape=(
            shape((2, rows, full // 4), F),
            shape((2, wide_rows, wide), F),
            shape(small.shape[1:], F),
        ),
        in_specs=[VM] * 5,
        out_specs=(VM, VM, VM),
        scratch_shapes=one
        + two_x
        + two_y
        + three
        + four
        + [
            pltpu.VMEM((rows, full // 4), F),
            pltpu.VMEM((wide_rows, wide), F),
            pltpu.VMEM((images - 1,) + small.shape[1:], F),
            pltpu.VMEM((bands,) + small.shape[1:], F),
            pltpu.SemaphoreType.DMA((count,)),
            pltpu.SemaphoreType.DMA((count,)),
            pltpu.SemaphoreType.DMA((smalls,)),
            pltpu.SemaphoreType.DMA((smalls,)),
        ],
        compiler_params=comm_params(3),
    )(qkv, out, up, down, small)


def pack_small(parts):
    flat = jnp.concatenate([p.reshape(p.shape[0], -1).astype(F) for p in parts], axis=1)
    size = flat.shape[1]
    lines = -(-size // 1024) * 8
    flat = jnp.pad(flat, ((0, 0), (0, lines * 128 - size)))
    return flat.reshape(flat.shape[0], lines, 128)


def unpack_small(packed, sizes):
    flat = packed.reshape(packed.shape[0], -1)
    pieces, start = [], 0
    for size in sizes:
        pieces.append(flat[:, start : start + size].reshape(-1))
        start += size
    return pieces


def body(
    tokens,
    slot_kind,
    w_qkv,
    w_out,
    w_up,
    w_down,
    bias_qv,
    bias_out,
    bias_up,
    bias_down,
    gain_one,
    shift_one,
    gain_two,
    shift_two,
    cotangent,
):
    rows, slots, width = tokens.shape[1:]
    count = rows * slots
    images, bands = lax.axis_size("img"), lax.axis_size("band")
    band = lax.axis_index("band")
    smalls = (bias_qv, bias_out, bias_up, bias_down, gain_one, shift_one, gain_two, shift_two)
    sizes = [item.shape[0] for item in smalls]
    own = (w_qkv, w_out, w_up)
    widths = [item.shape[1] for item in own]
    direct = images % 4 == 0 and all(w % 16 == 0 for w in widths + [w_down.shape[1]])

    def turn(values):
        return values[0].transpose(2, 1, 0).reshape(width, count)

    def turn_back(values):
        return values.reshape(width, slots, rows).transpose(2, 1, 0)[None]

    x, cot = turn(tokens), turn(cotangent)
    kinds = slot_kind[0].astype(jnp.int32)
    valid = jnp.repeat((kinds > 0).astype(F), rows)[None, :]
    scalars = jnp.concatenate([kinds, (band // 2).astype(jnp.int32)[None]])

    small = pack_small([item[None] for item in smalls])[0]
    if direct:
        narrow = split_rows([item.T for item in own], 2)
        *full, small_all = gather(images, narrow, w_down.T, small, widths)
        full = [item.reshape(-1, item.shape[3]) for item in full]
    else:
        full = [
            lax.all_gather(lax.all_gather(item, "band", axis=0, tiled=True).T, "img", tiled=True)
            for item in (*own, w_down)
        ]
        small_all = lax.all_gather(small, "img")
    full_qkv, full_out, full_up, full_down = full
    columns = [item[:, None] for item in unpack_small(small_all, sizes)]
    c_qv, c_out, c_up, c_down, c_gain_one, c_shift_one, c_gain_two, c_shift_two = columns
    bias = jnp.concatenate([c_qv[:width], jnp.zeros((width, 1), F), c_qv[width:]])

    h, qkv = project(x, full_qkv, c_gain_one, c_shift_one, bias)
    q, kv = qkv[:width], qkv[width:]
    all_kv = share(images, bands, kv)
    att, lse = attend(scalars, q, all_kv)
    out, dmid, datt, g_out, g_up, g_down, sum_up, sums_two = middle(
        x, cot, valid, att, full_out, full_up, full_down,
        c_out, c_gain_two, c_shift_two, c_up, c_down,
    )
    dq, dkv = attend_back(scalars, q, all_kv, att, lse, datt)
    dkv = unshare(images, dkv)
    gx, g_qkv, sums_one = finish(x, h, dq, dkv, full_qkv, c_gain_one, dmid)

    small_sums = [
        jnp.concatenate([sums_one[0, 0], sums_one[1, 0]]),
        sums_two[3, 0],
        sum_up[0],
        sums_two[0, 0],
        sums_one[2, 0],
        sums_one[3, 0],
        sums_two[1, 0],
        sums_two[2, 0],
    ]
    packed = pack_small([item.reshape(images, -1) for item in small_sums])
    grads = (g_qkv, g_out, g_up, g_down)
    if direct:
        grads = [item.reshape(images // 2, 2, -1, item.shape[1]) for item in grads]
        narrow, wide, small = scatter(images, bands, *grads, packed)
        matrices, start = [], 0
        for w in widths:
            part = narrow[:, start : start + w // 2].reshape(w, -1)
            matrices.append(part.T)
            start += w // 2
        matrices.append(wide.reshape(-1, wide.shape[2]).T)
    else:
        matrices = [
            lax.psum_scatter(
                lax.psum_scatter(item, "img", scatter_dimension=0, tiled=True),
                "band",
                scatter_dimension=1,
                tiled=True,
            )
            .astype(F)
            .T
            for item in grads
        ]
        small = lax.psum(lax.psum_scatter(packed, "img", scatter_dimension=0), "band")
    return (
        turn_back(out),
        turn_back(gx),
        *matrices,
        *unpack_small(small[None], sizes),
    )


def solution(mesh):
    data, weight, vector = P("img", "band", None, None), P("band", "img"), P("img")
    return jax.shard_map(
        body,
        mesh=mesh,
        in_specs=(data, P("img", None)) + (weight,) * 4 + (vector,) * 8 + (data,),
        out_specs=(data, data) + (weight,) * 4 + (vector,) * 8,
        check_vma=False,
    )
```

```python
import functools
import math

import jax
import jax.numpy as jnp
from jax import lax
from jax.experimental import pallas as pl
from jax.experimental.pallas import tpu as pltpu
from jax.sharding import PartitionSpec as P

HEADS = 16
HEAD_DIM = 48
EPSILON = 1e-06
MASKED = -1e30
BF = jnp.bfloat16
F = jnp.float32
MESH = pl.DeviceIdType.MESH
VM = pl.BlockSpec(memory_space=pltpu.VMEM)
SM = pl.BlockSpec(memory_space=pltpu.SMEM)
ANY = pl.BlockSpec(memory_space=pl.ANY)
LIMIT = 67043328
SUM_ROWS, UP_ROW = 16, 8


def dg(left, right, left_dim, right_dim):
    return lax.dot_general(
        left, right, (((left_dim,), (right_dim,)), ((), ())), preferred_element_type=F
    )


def shape(dims, dtype):
    return jax.ShapeDtypeStruct(tuple(dims), dtype)


def row_sums(values):
    ones = jnp.ones((8, values.shape[1]), BF)
    if values.dtype == BF:
        return dg(ones, values, 1, 1)
    high = values.astype(BF)
    low = (values - high.astype(F)).astype(BF)
    return dg(ones, high, 1, 1) + dg(ones, low, 1, 1)


def normalize(values):
    average = jnp.mean(values, axis=0, keepdims=True)
    centered = values - average
    variance = jnp.mean(centered * centered, axis=0, keepdims=True)
    inverse = lax.rsqrt(variance + EPSILON)
    return centered * inverse, inverse


def norm_back(error, normed, inverse, gain):
    f = gain * error
    mean_f = jnp.mean(f, axis=0, keepdims=True)
    mean_fn = jnp.mean(f * normed, axis=0, keepdims=True)
    return (f - mean_f - normed * mean_fn) * inverse


def project_kernel(x_ref, w_ref, gain_ref, shift_ref, bias_ref, h_ref, qkv_ref):
    width = x_ref.shape[0]
    normed, _ = normalize(x_ref[...].astype(F))
    h_ref[...] = (normed * gain_ref[...] + shift_ref[...]).astype(BF)
    scale = 1.0 / math.sqrt(HEAD_DIM)
    step = 256

    @pl.loop(0, 3 * width // step)
    def _(j):
        rows = pl.ds(pl.multiple_of(j * step, step), step)
        out = dg(w_ref[rows, :], h_ref[...], 1, 0) + bias_ref[rows, :]
        qkv_ref[rows, :] = (out * jnp.where(j < width // step, scale, 1.0)).astype(BF)


def project(x, w, gain, shift, bias):
    width, tokens = x.shape
    return pl.pallas_call(
        project_kernel,
        name="project",
        out_shape=(shape((width, tokens), BF), shape((3 * width, tokens), BF)),
        in_specs=[VM] * 5,
        out_specs=(VM, VM),
        compiler_params=pltpu.CompilerParams(vmem_limit_bytes=LIMIT),
    )(x, w, gain, shift, bias)


def fill_bias(scalars_ref, bias_ref, rows):
    lane_half = lax.broadcasted_iota(jnp.int32, (1, rows), 1) // (rows // 2)
    for s in range(2):
        small = scalars_ref[s] == 2
        for other in range(2):
            for half in range(2):
                keep = jnp.logical_and(other == 0, lane_half == half)
                masked = jnp.where(small, MASKED, 0.0)
                bias_ref[pl.ds(4 * s + 2 * other + half, 1), :] = jnp.where(
                    keep, jnp.zeros((1, rows), F), jnp.full((1, rows), masked, F)
                )


def add_bias(scores, bias_ref, s, other):
    rows = scores.shape[0]
    at = 4 * s + 2 * other
    return jnp.concatenate(
        [
            scores[: rows // 2] + bias_ref[pl.ds(at, 1), :],
            scores[rows // 2 :] + bias_ref[pl.ds(at + 1, 1), :],
        ],
        axis=0,
    )


def head_slices(i, rows):
    s, h = i // HEADS, i % HEADS
    lanes = pl.ds(pl.multiple_of(s * rows, rows), rows)
    first = pl.ds(pl.multiple_of(h * HEAD_DIM, 16), HEAD_DIM)
    second = pl.ds(pl.multiple_of(HEADS * HEAD_DIM + h * HEAD_DIM, 16), HEAD_DIM)
    return s, lanes, first, second


def attend_step(i, chip_x, q_ref, kv_ref, bias_ref, out_ref, lse_ref):
    bands = kv_ref.shape[0]
    rows = q_ref.shape[1] // 2
    s, lanes, first, second = head_slices(i, rows)
    q = q_ref[first, lanes]
    scores = []
    maximum = None
    for b in range(bands):
        other = jnp.where(chip_x == b // 2, 0, 1)
        part = add_bias(dg(kv_ref[b, first, lanes], q, 0, 0), bias_ref, s, other)
        scores.append(part)
        top = jnp.max(part, axis=0, keepdims=True)
        maximum = top if maximum is None else jnp.maximum(maximum, top)
    total, acc = 0.0, 0.0
    for b in range(bands):
        weight = jnp.exp(scores[b] - maximum)
        total = total + jnp.sum(weight, axis=0, keepdims=True)
        acc = acc + dg(kv_ref[b, second, lanes], weight.astype(BF), 1, 0)
    out_ref[first, lanes] = acc / total
    lse_ref[pl.ds(i, 1), :] = maximum + jnp.log(total)


def attend_kernel(unroll, scalars_ref, q_ref, kv_ref, out_ref, lse_ref, bias_ref):
    fill_bias(scalars_ref, bias_ref, q_ref.shape[1] // 2)

    @pl.loop(0, 2 * HEADS // unroll)
    def _(j):
        for k in range(unroll):
            attend_step(
                j * unroll + k, scalars_ref[2], q_ref, kv_ref, bias_ref, out_ref, lse_ref
            )


def attend(scalars, q, kv):
    width, tokens = q.shape
    return pl.pallas_call(
        functools.partial(attend_kernel, 4),
        name="attend",
        out_shape=(shape((width, tokens), F), shape((2 * HEADS, tokens // 2), F)),
        in_specs=[SM, VM, VM],
        out_specs=(VM, VM),
        scratch_shapes=[pltpu.VMEM((8, tokens // 2), F)],
        compiler_params=pltpu.CompilerParams(vmem_limit_bytes=LIMIT),
    )(scalars, q, kv)


def attend_back_step(
    i, chip_x, q_ref, kv_ref, out_ref, lse_ref, dout_ref, bias_ref, dq_ref, put_key, put_value
):
    bands = kv_ref.shape[0]
    rows = q_ref.shape[1] // 2
    s, lanes, first, second = head_slices(i, rows)
    q = q_ref[first, lanes]
    dout = dout_ref[first, lanes]
    delta = jnp.sum(out_ref[first, lanes] * dout.astype(F), axis=0, keepdims=True)
    lse = lse_ref[pl.ds(i, 1), :]
    dq = 0.0
    for b in range(bands):
        other = jnp.where(chip_x == b // 2, 0, 1)
        k, v = kv_ref[b, first, lanes], kv_ref[b, second, lanes]
        scores = add_bias(dg(k, q, 0, 0), bias_ref, s, other)
        dweight = dg(v, dout, 0, 0)
        weight = jnp.exp(scores - lse)
        dscores = (weight * (dweight - delta)).astype(BF)
        dq = dq + dg(k, dscores, 1, 0)
        put_key(b, dg(q, dscores, 1, 1).astype(BF))
        put_value(b, dg(dout, weight.astype(BF), 1, 1).astype(BF))
    dq_ref[first, lanes] = (dq * (1.0 / math.sqrt(HEAD_DIM))).astype(BF)


def attend_back_kernel(
    unroll, scalars_ref, q_ref, kv_ref, out_ref, lse_ref, dout_ref, dq_ref, dkv_ref, bias_ref
):
    fill_bias(scalars_ref, bias_ref, q_ref.shape[1] // 2)

    @pl.loop(0, 2 * HEADS // unroll)
    def _(j):
        for k in range(unroll):
            i = j * unroll + k
            _, lanes, first, second = head_slices(i, q_ref.shape[1] // 2)

            def put_key(b, values):
                dkv_ref[b, first, lanes] = values

            def put_value(b, values):
                dkv_ref[b, second, lanes] = values

            attend_back_step(
                i, scalars_ref[2], q_ref, kv_ref, out_ref, lse_ref, dout_ref, bias_ref, dq_ref,
                put_key, put_value,
            )


def attend_back(scalars, q, kv, out, lse, dout):
    return pl.pallas_call(
        functools.partial(attend_back_kernel, 4),
        name="attend_back",
        out_shape=(shape(q.shape, BF), shape(kv.shape, BF)),
        in_specs=[SM] + [VM] * 5,
        out_specs=(VM, VM),
        scratch_shapes=[pltpu.VMEM((8, q.shape[1] // 2), F)],
        compiler_params=pltpu.CompilerParams(vmem_limit_bytes=LIMIT),
    )(scalars, q, kv, out, lse, dout)


def middle_kernel(
    x_ref,
    cot_ref,
    valid_ref,
    att_ref,
    w_out_ref,
    w_up_ref,
    w_down_ref,
    bias_out_ref,
    gain_ref,
    shift_ref,
    bias_up_ref,
    bias_down_ref,
    out_ref,
    dmid_ref,
    datt_ref,
    g_out_ref,
    g_up_ref,
    g_down_ref,
    sums_ref,
    mid_ref,
    norm_ref,
    h_ref,
    dmlp_ref,
    mlp_ref,
    err_ref,
    attb_ref,
    dbranch_ref,
):
    width, tokens = x_ref.shape
    hidden = w_up_ref.shape[0]
    step = 256
    attb_ref[...] = att_ref[...].astype(BF)
    sums_ref[...] = jnp.zeros_like(sums_ref)

    @pl.loop(0, width // step)
    def _(j):
        rows = pl.ds(pl.multiple_of(j * step, step), step)
        mid_ref[rows, :] = (
            dg(w_out_ref[rows, :], attb_ref[...], 1, 0)
            + bias_out_ref[rows, :]
            + x_ref[rows, :].astype(F)
        )

    normed, inverse = normalize(mid_ref[...])
    norm_ref[...] = normed
    h_ref[...] = (normed * gain_ref[...] + shift_ref[...]).astype(BF)
    dmlp_ref[...] = (cot_ref[...].astype(F) * valid_ref[...]).astype(BF)
    mlp_ref[...] = jnp.zeros_like(mlp_ref)
    err_ref[...] = jnp.zeros_like(err_ref)

    @pl.loop(0, hidden // step)
    def _(j):
        rows = pl.ds(pl.multiple_of(j * step, step), step)
        pre = dg(w_up_ref[rows, :], h_ref[...], 1, 0) + bias_up_ref[rows, :]
        phi = 0.5 + 0.5 * lax.erf(pre * math.sqrt(0.5))
        act = (pre * phi).astype(BF)
        slope = phi + pre * jnp.exp(pre * pre * -0.5) * (1.0 / math.sqrt(2.0 * math.pi))
        mlp_ref[...] += dg(w_down_ref[:, rows], act, 1, 0)
        dact = dg(w_down_ref[:, rows], dmlp_ref[...], 0, 0)
        dhid = (slope * dact).astype(BF)
        g_down_ref[:, rows] = dg(dmlp_ref[...], act, 1, 1).astype(BF)
        g_up_ref[rows, :] = dg(dhid, h_ref[...], 1, 1).astype(BF)
        per = width // step
        lanes = pl.ds(pl.multiple_of(j % per * step, step), step)
        sums_ref[pl.ds(UP_ROW + j // per, 1), lanes] = row_sums(dhid)[:1]
        err_ref[...] += dg(w_up_ref[rows, :], dhid, 0, 0)

    out_ref[...] = ((mid_ref[...] + mlp_ref[...] + bias_down_ref[...]) * valid_ref[...]).astype(BF)
    err = err_ref[...]
    sums_ref[3:4] = row_sums(dmlp_ref[...])[:1]
    sums_ref[6:7] = row_sums(err * norm_ref[...])[:1]
    sums_ref[7:8] = row_sums(err)[:1]
    dmid = cot_ref[...].astype(F) * valid_ref[...] + norm_back(
        err, norm_ref[...], inverse, gain_ref[...]
    )
    dmid_ref[...] = dmid
    dbranch_ref[...] = dmid.astype(BF)
    sums_ref[2:3] = row_sums(dbranch_ref[...])[:1]
    datt_ref[...] = dg(w_out_ref[...], dbranch_ref[...], 0, 0).astype(BF)

    @pl.loop(0, width // step)
    def _(j):
        rows = pl.ds(pl.multiple_of(j * step, step), step)
        g_out_ref[rows, :] = dg(dbranch_ref[rows, :], attb_ref[...], 1, 1).astype(BF)


def middle(x, cot, valid, att, w_out, w_up, w_down, bias_out, gain, shift, bias_up, bias_down):
    width, tokens = x.shape
    hidden = w_up.shape[0]
    full = (width, tokens)
    return pl.pallas_call(
        middle_kernel,
        name="middle",
        out_shape=(
            shape(full, BF),
            shape(full, F),
            shape(full, BF),
            shape(w_out.shape, BF),
            shape(w_up.shape, BF),
            shape(w_down.shape, BF),
            shape((SUM_ROWS, width), F),
        ),
        in_specs=[VM] * 12,
        out_specs=tuple([VM] * 7),
        scratch_shapes=[
            pltpu.VMEM(full, F),
            pltpu.VMEM(full, F),
            pltpu.VMEM(full, BF),
            pltpu.VMEM(full, BF),
            pltpu.VMEM(full, F),
            pltpu.VMEM(full, F),
            pltpu.VMEM(full, BF),
            pltpu.VMEM(full, BF),
        ],
        compiler_params=pltpu.CompilerParams(vmem_limit_bytes=LIMIT),
    )(x, cot, valid, att, w_out, w_up, w_down, bias_out, gain, shift, bias_up, bias_down)


def finish_kernel(
    x_ref, h_ref, dq_ref, dkv_ref, w_ref, gain_ref, dmid_ref, gx_ref, g_ref, sums_ref, err_ref
):
    width, tokens = x_ref.shape
    step = 256
    blocks = width // step
    err_ref[...] = jnp.zeros_like(err_ref)
    for ref, count, base in ((dq_ref, blocks, 0), (dkv_ref, 2 * blocks, blocks)):

        @pl.loop(0, count)
        def _(j):
            rows = pl.ds(pl.multiple_of(j * step, step), step)
            to = pl.ds(pl.multiple_of((j + base) * step, step), step)
            g_ref[to, :] = dg(ref[rows, :], h_ref[...], 1, 1).astype(BF)
            err_ref[...] += dg(w_ref[to, :], ref[rows, :], 0, 0)

    normed, inverse = normalize(x_ref[...].astype(F))
    err = err_ref[...]
    sums_ref[...] = jnp.zeros_like(sums_ref)
    sums_ref[0:1] = row_sums(dq_ref[...])[:1]
    sums_ref[1:2] = row_sums(dkv_ref[pl.ds(width, width), :])[:1]
    sums_ref[4:5] = row_sums(err * normed)[:1]
    sums_ref[5:6] = row_sums(err)[:1]
    gx_ref[...] = (dmid_ref[...] + norm_back(err, normed, inverse, gain_ref[...])).astype(BF)


def finish(x, h, dq, dkv, w, gain, dmid):
    width, tokens = x.shape
    return pl.pallas_call(
        finish_kernel,
        name="finish",
        out_shape=(shape(x.shape, BF), shape(w.shape, BF), shape((SUM_ROWS, width), F)),
        in_specs=[VM] * 7,
        out_specs=(VM, VM, VM),
        scratch_shapes=[pltpu.VMEM(x.shape, F)],
        compiler_params=pltpu.CompilerParams(vmem_limit_bytes=LIMIT),
    )(x, h, dq, dkv, w, gain, dmid)


class Place:
    def __init__(self, images):
        self.images = images
        self.depth = images // 2
        self.img = lax.axis_index("img")
        self.band = lax.axis_index("band")
        self.z, self.y = self.img // 2, self.img % 2
        self.x, self.c = self.band // 2, self.band % 2
        self.partner = (self.img, self.band + 1 - 2 * self.c)
        self.across_x = (self.img, self.band + 2 - 4 * self.x)
        self.across_y = (self.img + 1 - 2 * self.y, self.band)
        self.z_peers = [self.along_z(k) for k in range(1, self.depth)]

    def along_z(self, k):
        z = lax.rem(self.z + k, self.depth)
        return (2 * z + self.y, self.band), z


def greet(peers):
    barrier = pltpu.get_barrier_semaphore()
    for peer in peers:
        pl.semaphore_signal(barrier, inc=1, device_id=peer, device_id_type=MESH)
    pl.semaphore_wait(barrier, len(peers))


def send(src, dst, send_sem, recv_sem, peer):
    copy = pltpu.make_async_remote_copy(
        src_ref=src,
        dst_ref=dst,
        send_sem=send_sem,
        recv_sem=recv_sem,
        device_id=peer,
        device_id_type=MESH,
    )
    copy.start()
    return copy


def comm_params(collective_id):
    return pltpu.CompilerParams(
        collective_id=collective_id, has_side_effects=True, vmem_limit_bytes=LIMIT
    )


def split_rows(shards, parts):
    return jnp.concatenate(
        [item.reshape(parts, item.shape[0] // parts, item.shape[1]) for item in shards], axis=1
    )


def gather_kernel(
    images, narrow_ref, wide_ref, small_ref, qkv_ref, out_ref, up_ref, down_ref, smalls_ref,
    theirs_ref, mine_ref, mine_wide_ref, local_sem, send_sem, recv_sem, small_send, small_recv,
):
    at = Place(images)
    depth, near = at.depth, at.depth // 2
    peers = [at.partner, at.across_x, at.across_y]
    peers += [at.along_z(k)[0] for k in range(1, depth)]
    others = [(lax.rem(at.img + k, images), at.band) for k in range(1, images)]
    others = peers[:2] + others
    greet(others)
    c = at.c

    first = [
        send(narrow_ref.at[1 - c], theirs_ref, send_sem.at[16], recv_sem.at[16], at.partner)
    ]
    half = wide_ref.shape[0] // 2
    wide = wide_ref.shape[1]
    lanes = pl.ds(pl.multiple_of(c * wide, 128), wide)
    own = pltpu.make_async_copy(
        wide_ref.at[pl.ds(pl.multiple_of(c * half, 8), half), :],
        mine_wide_ref.at[:, lanes],
        local_sem.at[0],
    )
    own.start()
    first.append(
        send(
            wide_ref.at[pl.ds(pl.multiple_of((1 - c) * half, 8), half), :],
            mine_wide_ref.at[:, lanes],
            send_sem.at[17],
            recv_sem.at[17],
            at.partner,
        )
    )
    small_copies = []
    keep = pltpu.make_async_copy(small_ref, smalls_ref.at[at.img], local_sem.at[1])
    keep.start()
    for k in range(1, images):
        small_copies.append(
            send(
                small_ref,
                smalls_ref.at[at.img],
                small_send.at[k - 1],
                small_recv.at[k - 1],
                others[k + 1],
            )
        )
    first[0].wait_recv()
    mine, theirs = narrow_ref[c], theirs_ref[...]
    width = mine.shape[1]
    mine_ref[:, pl.ds(0, width)] = jnp.where(c == 0, mine, theirs)
    mine_ref[:, pl.ds(width, width)] = jnp.where(c == 0, theirs, mine)
    own.wait()
    first[1].wait_recv()

    refs = (qkv_ref, out_ref, up_ref, down_ref)
    views, sources = [], []
    row = 0
    for ref in refs[:3]:
        rows = ref.shape[2] // 2
        sources.append(mine_ref.at[pl.ds(row, rows), :])
        row += rows
    sources.append(mine_wide_ref)

    sends = list(first) + small_copies
    stage = [[None] * 4 for _ in refs]
    locals_ = [keep]

    def rows_of(m):
        rows = refs[m].shape[2] // 2
        return pl.ds(pl.multiple_of(c * rows, 8), rows)

    def lanes_of(m):
        half_lanes = refs[m].shape[3] // 2
        return pl.ds(pl.multiple_of(at.x * half_lanes, 128), half_lanes)

    for m, ref in enumerate(refs):
        piece = ref.at[at.z, at.y, rows_of(m), lanes_of(m)]
        copy = pltpu.make_async_copy(sources[m], piece, local_sem.at[2 + m])
        copy.start()
        stage[m][0] = [copy]
        for k in range(1, depth):
            index = 18 + m * (depth - 1) + k - 1
            stage[m][0].append(
                send(sources[m], piece, send_sem.at[index], recv_sem.at[index], at.along_z(k)[0])
            )

    def second(m):
        stage[m][0][0].wait()
        for copy in stage[m][0][1:]:
            copy.wait_recv()
        region = (pl.ds(0, near), at.y, rows_of(m), lanes_of(m))
        to_x = refs[m].at[region]
        region = (pl.ds(near, depth - near), at.y, rows_of(m), lanes_of(m))
        to_y = refs[m].at[region]
        stage[m][1] = [
            send(to_x, to_x, send_sem.at[4 * m], recv_sem.at[4 * m], at.across_x),
            send(to_y, to_y, send_sem.at[4 * m + 1], recv_sem.at[4 * m + 1], at.across_y),
        ]

    def third(m):
        for copy in stage[m][1]:
            copy.wait_recv()
        to_y = refs[m].at[pl.ds(0, near), at.y, rows_of(m), :]
        to_x = refs[m].at[pl.ds(near, depth - near), :, rows_of(m), lanes_of(m)]
        stage[m][2] = [
            send(to_y, to_y, send_sem.at[4 * m + 2], recv_sem.at[4 * m + 2], at.across_y),
            send(to_x, to_x, send_sem.at[4 * m + 3], recv_sem.at[4 * m + 3], at.across_x),
        ]

    last = 18 + 4 * (depth - 1)

    def fourth(m):
        for copy in stage[m][2]:
            copy.wait_recv()
        part = refs[m].at[:, :, rows_of(m), :]
        stage[m][3] = [
            send(part, part, send_sem.at[last + m], recv_sem.at[last + m], at.partner)
        ]

    second(0)
    second(1)
    third(0)
    second(2)
    third(1)
    fourth(0)
    second(3)
    third(2)
    fourth(1)
    third(3)
    fourth(2)
    fourth(3)
    for m in range(4):
        stage[m][3][0].wait_recv()
        for copy in stage[m][0][1:] + stage[m][1] + stage[m][2] + stage[m][3]:
            copy.wait_send()
    for copy in first:
        copy.wait_send()
    for copy in small_copies:
        copy.wait()
    keep.wait()


def gather(images, narrow, wide, small, widths):
    depth = images // 2
    full = 4 * narrow.shape[2]
    outs = [shape((depth, 2, w, full), BF) for w in widths]
    outs.append(shape((depth, 2, wide.shape[0], 4 * wide.shape[1]), BF))
    outs.append(shape((images,) + small.shape, F))
    count = 18 + 4 * (depth - 1) + 4
    return pl.pallas_call(
        functools.partial(gather_kernel, images),
        name="gather",
        out_shape=tuple(outs),
        in_specs=[VM, VM, VM],
        out_specs=(ANY, ANY, ANY, ANY, VM),
        scratch_shapes=[
            pltpu.VMEM(narrow.shape[1:], BF),
            pltpu.VMEM((narrow.shape[1], 2 * narrow.shape[2]), BF),
            pltpu.VMEM((wide.shape[0] // 2, 2 * wide.shape[1]), BF),
            pltpu.SemaphoreType.DMA((6,)),
            pltpu.SemaphoreType.DMA((count,)),
            pltpu.SemaphoreType.DMA((count,)),
            pltpu.SemaphoreType.DMA((images - 1,)),
            pltpu.SemaphoreType.DMA((images - 1,)),
        ],
        compiler_params=comm_params(0),
    )(narrow, wide, small)


def share_kernel(images, kv_ref, all_ref, local_sem, send_sem, recv_sem):
    at = Place(images)
    greet([at.partner, at.across_x])
    rows = kv_ref.shape[1] // 2
    mine = pltpu.make_async_copy(kv_ref, all_ref.at[at.band], local_sem)
    mine.start()
    copies = []
    for s in range(2):
        lanes = pl.ds(s * rows, rows)
        copies.append(
            send(
                kv_ref.at[:, lanes],
                all_ref.at[at.band, :, lanes],
                send_sem.at[s],
                recv_sem.at[s],
                at.across_x,
            )
        )
    near = send(kv_ref, all_ref.at[at.band], send_sem.at[2], recv_sem.at[2], at.partner)
    passed = []
    for s in range(2):
        copies[s].wait_recv()
        part = all_ref.at[at.across_x[1], :, pl.ds(s * rows, rows)]
        passed.append(send(part, part, send_sem.at[3 + s], recv_sem.at[3 + s], at.partner))
    for copy in passed + [near]:
        copy.wait()
    for copy in copies:
        copy.wait_send()
    mine.wait()


def share(images, bands, kv):
    return pl.pallas_call(
        functools.partial(share_kernel, images),
        name="share",
        out_shape=shape((bands,) + kv.shape, BF),
        in_specs=[VM],
        out_specs=ANY,
        scratch_shapes=[
            pltpu.SemaphoreType.DMA,
            pltpu.SemaphoreType.DMA((5,)),
            pltpu.SemaphoreType.DMA((5,)),
        ],
        compiler_params=comm_params(1),
    )(kv)


def add_rows(total_ref, other_ref, step):
    @pl.loop(0, total_ref.shape[0] // step)
    def _(j):
        rows = pl.ds(pl.multiple_of(j * step, step), step)
        total_ref[rows, :] = (
            total_ref[rows, :].astype(F) + other_ref[rows, :].astype(F)
        ).astype(total_ref.dtype)


def unshare_kernel(images, dkv_ref, sum_ref, near_ref, far_ref, send_sem, recv_sem):
    at = Place(images)
    greet([at.partner, at.across_x])
    mate, far = at.partner[1], at.across_x[1]
    far_mate = at.band + 2 - 4 * at.x + 1 - 2 * at.c
    one = send(dkv_ref.at[far_mate], near_ref.at[0], send_sem.at[0], recv_sem.at[0], at.partner)
    two = send(dkv_ref.at[mate], near_ref.at[1], send_sem.at[1], recv_sem.at[1], at.partner)
    one.wait_recv()
    add_rows(near_ref.at[0], dkv_ref.at[far], 64)
    three = send(near_ref.at[0], far_ref, send_sem.at[2], recv_sem.at[2], at.across_x)
    two.wait_recv()
    add_rows(near_ref.at[1], dkv_ref.at[at.band], 64)
    three.wait_recv()
    sum_ref[...] = near_ref[1]
    add_rows(sum_ref, far_ref, 64)
    for copy in (one, two, three):
        copy.wait_send()


def unshare(images, dkv):
    block = dkv.shape[1:]
    return pl.pallas_call(
        functools.partial(unshare_kernel, images),
        name="unshare",
        out_shape=shape(block, BF),
        in_specs=[VM],
        out_specs=VM,
        scratch_shapes=[
            pltpu.VMEM((2,) + block, BF),
            pltpu.VMEM(block, BF),
            pltpu.SemaphoreType.DMA((3,)),
            pltpu.SemaphoreType.DMA((3,)),
        ],
        compiler_params=comm_params(2),
    )(dkv)


def accumulate(total, other):
    total[...] = (total[...].astype(F) + other[...].astype(F)).astype(total.dtype)


class Reduction:
    def __init__(self, at, make, ref, bufs, target, away):
        one, two_x, two_y, three, four = bufs
        self.at, self.ref, self.one, self.two_x, self.two_y = at, ref, one, two_x, two_y
        self.three, self.four, self.target, self.away = three, four, target, away
        depth, near, c = at.depth, at.depth // 2, at.c
        self.near = near
        rows, half = ref.shape[2] // 2, ref.shape[3] // 2

        def lanes_of(x):
            return pl.ds(pl.multiple_of(x * half, 128), half)

        self.rows = pl.ds(pl.multiple_of(c * rows, 16), rows)
        self.lanes = lanes_of(at.x)
        far_rows = pl.ds(pl.multiple_of((1 - c) * rows, 16), rows)
        far_lanes = lanes_of(1 - at.x)
        upper = depth - near
        self.zero = make(ref.at[:, :, far_rows, :], one, at.partner)
        self.first = [
            make(one.at[pl.ds(0, near), :, :, far_lanes], two_x, at.across_x),
            make(one.at[pl.ds(near, upper), 1 - at.y], two_y, at.across_y),
        ]
        self.second = [
            make(two_x.at[:, 1 - at.y], three.at[pl.ds(0, near)], at.across_y),
            make(two_y.at[:, :, far_lanes], three.at[pl.ds(near, upper)], at.across_x),
        ]
        self.third = [
            make(three.at[z], four.at[k], peer) for k, (peer, z) in enumerate(at.z_peers)
        ]
        self.last = make(away, target.at[c], at.partner)

    def start(self):
        self.zero.start()

    def step_one(self):
        self.zero.wait_recv()

        @pl.loop(0, self.ref.shape[0] * 2)
        def _(j):
            accumulate(
                self.one.at[j // 2, j % 2], self.ref.at[j // 2, j % 2, self.rows, :]
            )

        for copy in self.first:
            copy.start()

    def step_two(self):
        self.first[0].wait_recv()

        @pl.loop(0, 2 * self.near)
        def _(j):
            accumulate(
                self.two_x.at[j // 2, j % 2], self.one.at[j // 2, j % 2, :, self.lanes]
            )

        self.second[0].start()
        self.first[1].wait_recv()

        @pl.loop(0, self.at.depth - self.near)
        def _(j):
            accumulate(self.two_y.at[j], self.one.at[self.near + j, self.at.y])

        self.second[1].start()

    def step_three(self):
        for copy in self.second:
            copy.wait_recv()

        @pl.loop(0, self.near)
        def _(j):
            accumulate(self.three.at[j], self.two_x.at[j, self.at.y])

        @pl.loop(0, self.at.depth - self.near)
        def _(j):
            accumulate(self.three.at[self.near + j], self.two_y.at[j, :, self.lanes])

        for copy in self.third:
            copy.start()

    def step_four(self):
        for copy in self.third:
            copy.wait_recv()
        c = self.at.c
        total = self.three[self.at.z].astype(F)
        for k in range(len(self.third)):
            total = total + self.four[k].astype(F)
        size = total.shape[1] // 2
        low, high = total[:, :size], total[:, size:]
        self.target[c] = jnp.where(c == 0, low, high)
        self.away[...] = jnp.where(c == 0, high, low)
        self.last.start()

    def end(self):
        self.last.wait()
        for copy in [self.zero] + self.first + self.second + self.third:
            copy.wait_send()


def back_kernel(
    images, bands, scalars_ref, q_ref, kv_ref, att_ref, lse_ref, datt_ref, x_ref, h_ref, dmid_ref,
    w_ref, gain_ref, g_out_ref, g_up_ref, g_down_ref, sums_ref,
    gx_ref, p_qkv_ref, p_out_ref, p_up_ref, p_down_ref, total_ref,
    bias_ref, dqkv_ref, dkv_ref, near_ref, far_ref, g_qkv_ref, err_ref,
    small_ref, small_in_ref, small_z_ref, *rest,
):
    at = Place(images)
    depth = at.depth
    send_sem, recv_sem = rest[-2:]
    used = [0]

    def make(src, dst, peer):
        k = used[0]
        used[0] += 1
        return pltpu.make_async_remote_copy(
            src_ref=src,
            dst_ref=dst,
            send_sem=send_sem.at[k],
            recv_sem=recv_sem.at[k],
            device_id=peer,
            device_id_type=MESH,
        )

    width, tokens = x_ref.shape
    rows = tokens // 2
    unroll = 4
    groups = HEADS // unroll
    part = width // groups

    def four_d(ref):
        return ref.reshape(depth, 2, ref.shape[0] // images, ref.shape[1])

    sources = (four_d(g_down_ref), four_d(g_up_ref), four_d(g_out_ref), g_qkv_ref)
    targets = (p_down_ref, p_up_ref, p_out_ref, p_qkv_ref)
    moves = []
    for m in range(4):
        moves.append(
            Reduction(at, make, sources[m], rest[6 * m : 6 * m + 5], targets[m], rest[6 * m + 5])
        )
    down, up, out, qkv = moves
    mate, far = at.partner[1], at.across_x[1]
    far_mate = at.across_x[1] + 1 - 2 * at.c
    one = [make(dkv_ref.at[far_mate, g], near_ref.at[0, g], at.partner) for g in range(groups)]
    two = [make(dkv_ref.at[mate, g], near_ref.at[1, g], at.partner) for g in range(groups)]
    three = [make(near_ref.at[0, g], far_ref.at[g], at.across_x) for g in range(groups)]
    small_steps = [
        make(small_ref.at[k], small_in_ref.at[k], peer)
        for k, peer in enumerate((at.partner, at.across_x, at.across_y))
    ]
    small_last = [
        make(small_z_ref.at[at.z], small_z_ref.at[at.z], peer) for peer, _ in at.z_peers
    ]

    greet([at.partner, at.across_x, at.across_y] + [peer for peer, _ in at.z_peers])
    for move in (down, up, out):
        move.start()
    fill_bias(scalars_ref, bias_ref, rows)

    def share_one(g):
        one[g].start()
        two[g].start()

    def share_two(g):
        one[g].wait_recv()
        add_rows(near_ref.at[0, g], dkv_ref.at[far, g], part)
        three[g].start()

    def share_three(g):
        two[g].wait_recv()
        three[g].wait_recv()
        for half in range(2):
            block = pl.ds(half * part, part)
            to = pl.ds((1 + half) * width + g * part, part)
            dqkv_ref[to, :] = (
                near_ref[1, g, block, :].astype(F)
                + dkv_ref[at.band, g, block, :].astype(F)
                + far_ref[g, block, :].astype(F)
            ).astype(BF)

    events = {}

    def when(j, *actions):
        events.setdefault(j, []).extend(actions)

    when(0, down.step_one)
    when(1, lambda: share_one(0), up.step_one)
    when(2, lambda: share_two(0))
    when(3, lambda: share_one(1), down.step_two, out.step_one)
    when(4, lambda: share_two(1))
    when(5, lambda: share_one(2), down.step_three)
    when(6, lambda: share_two(2), up.step_two)

    @pl.loop(0, 2 * groups)
    def _(j):
        g, s = j // 2, j % 2
        lanes = pl.ds(pl.multiple_of(s * rows, rows), rows)
        for k in range(unroll):

            def put_key(b, values):
                dkv_ref[b, g, pl.ds(k * HEAD_DIM, HEAD_DIM), lanes] = values

            def put_value(b, values):
                dkv_ref[b, g, pl.ds(part + k * HEAD_DIM, HEAD_DIM), lanes] = values

            attend_back_step(
                s * HEADS + g * unroll + k,
                at.x, q_ref, kv_ref, att_ref, lse_ref, datt_ref, bias_ref, dqkv_ref,
                put_key, put_value,
            )
        for when_j, actions in events.items():

            @pl.when(j == when_j)
            def _():
                for action in actions:
                    action()

    share_one(groups - 1)
    block = w_ref.shape[0] // images

    def weight_grad(j):
        piece = dqkv_ref[pl.ds(pl.multiple_of(j * block, 16), block), :]
        g_qkv_ref[j // 2, j % 2] = dg(piece, h_ref[...], 1, 1).astype(BF)

    early = width // block

    @pl.loop(0, early)
    def _(j):
        weight_grad(j)

    share_two(groups - 1)
    out.step_two()
    down.step_four()
    for g in range(groups - 1):
        share_three(g)
    up.step_three()
    share_three(groups - 1)

    @pl.loop(early, images)
    def _(j):
        weight_grad(j)

    qkv.start()
    err_ref[...] = jnp.zeros_like(err_ref)

    @pl.loop(0, images)
    def _(j):
        piece = pl.ds(pl.multiple_of(j * block, 16), block)
        err_ref[...] += dg(w_ref[piece, :], dqkv_ref[piece, :], 0, 0)

    out.step_three()
    qkv.step_one()
    normed, inverse = normalize(x_ref[...].astype(F))
    err = err_ref[...]
    small_ref[0] = sums_ref[...]
    small_ref[0, 0:1] = row_sums(dqkv_ref[pl.ds(0, width), :])[:1]
    small_ref[0, 1:2] = row_sums(dqkv_ref[pl.ds(2 * width, width), :])[:1]
    small_ref[0, 4:5] = row_sums(err * normed)[:1]
    small_ref[0, 5:6] = row_sums(err)[:1]
    small_steps[0].start()
    gx_ref[...] = (dmid_ref[...] + norm_back(err, normed, inverse, gain_ref[...])).astype(BF)
    up.step_four()
    small_steps[0].wait_recv()
    small_ref[1] = small_ref[0] + small_in_ref[0]
    small_steps[1].start()
    qkv.step_two()
    small_steps[1].wait_recv()
    small_ref[2] = small_ref[1] + small_in_ref[1]
    small_steps[2].start()
    out.step_four()
    small_steps[2].wait_recv()
    small_z_ref[at.z] = small_ref[2] + small_in_ref[2]
    for copy in small_last:
        copy.start()
    qkv.step_three()
    for copy in small_last:
        copy.wait_recv()
    total = small_z_ref[0]
    for k in range(1, depth):
        total = total + small_z_ref[k]
    total_ref[...] = total
    qkv.step_four()
    for move in moves:
        move.end()
    for copy in one + two + three + small_steps + small_last:
        copy.wait_send()


def back(images, bands, scalars, q, kv, att, lse, datt, x, h, dmid, w, gain, grads, sums):
    depth = images // 2
    near = depth // 2
    width, tokens = x.shape
    g_out, g_up, g_down = grads
    groups = HEADS // 4
    results, buffers = [], []
    count = 0
    for item in (g_down, g_up, g_out, w):
        block, lanes = item.shape[0] // images // 2, item.shape[1]
        results.append(shape((2, block, lanes // 4), F))
        buffers += [
            pltpu.VMEM((depth, 2, block, lanes), BF),
            pltpu.VMEM((near, 2, block, lanes // 2), BF),
            pltpu.VMEM((depth - near, block, lanes), BF),
            pltpu.VMEM((depth, block, lanes // 2), BF),
            pltpu.VMEM((depth - 1, block, lanes // 2), BF),
            pltpu.VMEM((block, lanes // 4), F),
        ]
        count += 6 + depth - 1
    count += 3 * groups + 3 + depth - 1
    small = (SUM_ROWS, width)
    return pl.pallas_call(
        functools.partial(back_kernel, images, bands),
        name="back",
        out_shape=(shape(x.shape, BF), results[3], results[2], results[1], results[0], shape(small, F)),
        in_specs=[SM] + [VM] * 14,
        out_specs=(VM,) * 6,
        scratch_shapes=[
            pltpu.VMEM((8, tokens // 2), F),
            pltpu.VMEM((3 * width, tokens), BF),
            pltpu.VMEM((bands, groups, 2 * width // groups, tokens), BF),
            pltpu.VMEM((2, groups, 2 * width // groups, tokens), BF),
            pltpu.VMEM((groups, 2 * width // groups, tokens), BF),
            pltpu.VMEM((depth, 2, w.shape[0] // images, width), BF),
            pltpu.VMEM((width, tokens), F),
            pltpu.VMEM((3,) + small, F),
            pltpu.VMEM((3,) + small, F),
            pltpu.VMEM((depth,) + small, F),
        ]
        + buffers
        + [pltpu.SemaphoreType.DMA((count,)), pltpu.SemaphoreType.DMA((count,))],
        compiler_params=comm_params(3),
    )(scalars, q, kv, att, lse, datt, x, h, dmid, w, gain, g_out, g_up, g_down, sums)


def pack_small(parts):
    flat = jnp.concatenate([p.reshape(p.shape[0], -1).astype(F) for p in parts], axis=1)
    size = flat.shape[1]
    lines = -(-size // 1024) * 8
    flat = jnp.pad(flat, ((0, 0), (0, lines * 128 - size)))
    return flat.reshape(flat.shape[0], lines, 128)


def unpack_small(packed, sizes):
    flat = packed.reshape(packed.shape[0], -1)
    pieces, start = [], 0
    for size in sizes:
        pieces.append(flat[:, start : start + size].reshape(-1))
        start += size
    return pieces


def body(
    tokens,
    slot_kind,
    w_qkv,
    w_out,
    w_up,
    w_down,
    bias_qv,
    bias_out,
    bias_up,
    bias_down,
    gain_one,
    shift_one,
    gain_two,
    shift_two,
    cotangent,
):
    rows, slots, width = tokens.shape[1:]
    count = rows * slots
    images, bands = lax.axis_size("img"), lax.axis_size("band")
    band = lax.axis_index("band")
    smalls = (bias_qv, bias_out, bias_up, bias_down, gain_one, shift_one, gain_two, shift_two)
    sizes = [item.shape[0] for item in smalls]
    own = (w_qkv, w_out, w_up)
    widths = [item.shape[1] for item in own]
    direct = images % 4 == 0 and all(w % 16 == 0 for w in widths + [w_down.shape[1]])

    def turn(values):
        return values[0].transpose(2, 1, 0).reshape(width, count)

    def turn_back(values):
        return values.reshape(width, slots, rows).transpose(2, 1, 0)[None]

    x, cot = turn(tokens), turn(cotangent)
    kinds = slot_kind[0].astype(jnp.int32)
    valid = jnp.repeat((kinds > 0).astype(F), rows)[None, :]
    scalars = jnp.concatenate([kinds, (band // 2).astype(jnp.int32)[None]])

    small = pack_small([item[None] for item in smalls])[0]
    if direct:
        narrow = split_rows([item.T for item in own], 2)
        *full, small_all = gather(images, narrow, w_down.T, small, widths)
        full = [item.reshape(-1, item.shape[3]) for item in full]
    else:
        full = [
            lax.all_gather(lax.all_gather(item, "band", axis=0, tiled=True).T, "img", tiled=True)
            for item in (*own, w_down)
        ]
        small_all = lax.all_gather(small, "img")
    full_qkv, full_out, full_up, full_down = full
    columns = [item[:, None] for item in unpack_small(small_all, sizes)]
    c_qv, c_out, c_up, c_down, c_gain_one, c_shift_one, c_gain_two, c_shift_two = columns
    bias = jnp.concatenate([c_qv[:width], jnp.zeros((width, 1), F), c_qv[width:]])

    h, qkv = project(x, full_qkv, c_gain_one, c_shift_one, bias)
    q, kv = qkv[:width], qkv[width:]
    all_kv = share(images, bands, kv)
    att, lse = attend(scalars, q, all_kv)
    out, dmid, datt, g_out, g_up, g_down, sums = middle(
        x, cot, valid, att, full_out, full_up, full_down,
        c_out, c_gain_two, c_shift_two, c_up, c_down,
    )
    if direct:
        gx, *pieces, total = back(
            images, bands, scalars, q, all_kv, att, lse, datt, x, h, dmid,
            full_qkv, c_gain_one, (g_out, g_up, g_down), sums,
        )
        matrices = [item.reshape(-1, item.shape[2]).T for item in pieces]
    else:
        dq, dkv = attend_back(scalars, q, all_kv, att, lse, datt)
        dkv = unshare(images, dkv)
        gx, g_qkv, sums_one = finish(x, h, dq, dkv, full_qkv, c_gain_one, dmid)
        matrices = [
            lax.psum_scatter(
                lax.psum_scatter(item, "img", scatter_dimension=0, tiled=True),
                "band",
                scatter_dimension=1,
                tiled=True,
            )
            .astype(F)
            .T
            for item in (g_qkv, g_out, g_up, g_down)
        ]
        total = lax.psum(sums + sums_one, ("img", "band"))
    own_small = lax.axis_index("img")
    flat = total.reshape(-1)
    starts = [0, 2, UP_ROW, 3, 4, 5, 6, 7]
    small = [
        lax.dynamic_slice(flat, (start * width + own_small * size,), (size,))
        for start, size in zip(starts, sizes)
    ]
    return (turn_back(out), turn_back(gx), *matrices, *small)


def solution(mesh):
    data, weight, vector = P("img", "band", None, None), P("band", "img"), P("img")
    return jax.shard_map(
        body,
        mesh=mesh,
        in_specs=(data, P("img", None)) + (weight,) * 4 + (vector,) * 8 + (data,),
        out_specs=(data, data) + (weight,) * 4 + (vector,) * 8,
        check_vma=False,
    )
```

```python
import functools
import math

import jax
import jax.numpy as jnp
from jax import lax
from jax.experimental import pallas as pl
from jax.experimental.pallas import tpu as pltpu
from jax.sharding import PartitionSpec as P

HEADS = 16
HEAD_DIM = 48
EPSILON = 1e-06
MASKED = -1e30
BF = jnp.bfloat16
F = jnp.float32
MESH = pl.DeviceIdType.MESH
VM = pl.BlockSpec(memory_space=pltpu.VMEM)
SM = pl.BlockSpec(memory_space=pltpu.SMEM)
ANY = pl.BlockSpec(memory_space=pl.ANY)
LIMIT = 67043328
SUM_ROWS, UP_ROW = 16, 8
COLUMNS = 10
BIAS_OUT, BIAS_DOWN, GAIN_ONE, SHIFT_ONE, GAIN_TWO, SHIFT_TWO = (slice(k, k + 1) for k in range(6))
GROUPS_OF_HEADS = 4


def dg(left, right, left_dim, right_dim):
    return lax.dot_general(
        left, right, (((left_dim,), (right_dim,)), ((), ())), preferred_element_type=F
    )


def shape(dims, dtype):
    return jax.ShapeDtypeStruct(tuple(dims), dtype)


def row_sums(values):
    ones = jnp.ones((8, values.shape[1]), BF)
    if values.dtype == BF:
        return dg(ones, values, 1, 1)
    high = values.astype(BF)
    low = (values - high.astype(F)).astype(BF)
    return dg(ones, high, 1, 1) + dg(ones, low, 1, 1)


def normalize(values):
    average = jnp.mean(values, axis=0, keepdims=True)
    centered = values - average
    variance = jnp.mean(centered * centered, axis=0, keepdims=True)
    inverse = lax.rsqrt(variance + EPSILON)
    return centered * inverse, inverse


def norm_back(error, normed, inverse, gain):
    f = gain * error
    mean_f = jnp.mean(f, axis=0, keepdims=True)
    mean_fn = jnp.mean(f * normed, axis=0, keepdims=True)
    return (f - mean_f - normed * mean_fn) * inverse


def project_kernel(x_ref, w_ref, cols_ref, bias_ref, h_ref, qkv_ref):
    width = x_ref.shape[0]
    normed, _ = normalize(x_ref[...].astype(F))
    h_ref[...] = (normed * cols_ref[:, GAIN_ONE] + cols_ref[:, SHIFT_ONE]).astype(BF)
    scale = 1.0 / math.sqrt(HEAD_DIM)
    step = 256

    @pl.loop(0, 3 * width // step)
    def _(j):
        rows = pl.ds(pl.multiple_of(j * step, step), step)
        out = dg(w_ref[rows, :], h_ref[...], 1, 0) + bias_ref[rows, :]
        qkv_ref[rows, :] = (out * jnp.where(j < width // step, scale, 1.0)).astype(BF)


def project(x, w, cols, bias):
    width, tokens = x.shape
    return pl.pallas_call(
        project_kernel,
        name="project",
        out_shape=(shape((width, tokens), BF), shape((3 * width, tokens), BF)),
        in_specs=[VM] * 4,
        out_specs=(VM, VM),
        compiler_params=pltpu.CompilerParams(vmem_limit_bytes=LIMIT),
    )(x, w, cols, bias)


def fill_bias(scalars_ref, bias_ref, rows):
    lane_half = lax.broadcasted_iota(jnp.int32, (1, rows), 1) // (rows // 2)
    for s in range(2):
        small = scalars_ref[s] == 2
        for other in range(2):
            for half in range(2):
                keep = jnp.logical_and(other == 0, lane_half == half)
                masked = jnp.where(small, MASKED, 0.0)
                bias_ref[pl.ds(4 * s + 2 * other + half, 1), :] = jnp.where(
                    keep, jnp.zeros((1, rows), F), jnp.full((1, rows), masked, F)
                )


def add_bias(scores, bias_ref, s, other):
    rows = scores.shape[0]
    at = 4 * s + 2 * other
    return jnp.concatenate(
        [
            scores[: rows // 2] + bias_ref[pl.ds(at, 1), :],
            scores[rows // 2 :] + bias_ref[pl.ds(at + 1, 1), :],
        ],
        axis=0,
    )


def head_slices(i, rows):
    s, h = i // HEADS, i % HEADS
    lanes = pl.ds(pl.multiple_of(s * rows, rows), rows)
    first = pl.ds(pl.multiple_of(h * HEAD_DIM, 16), HEAD_DIM)
    second = pl.ds(pl.multiple_of(HEADS * HEAD_DIM + h * HEAD_DIM, 16), HEAD_DIM)
    return s, lanes, first, second


def attend_step(i, chip_x, q_ref, kv_ref, bias_ref, out_ref, lse_ref):
    bands = kv_ref.shape[0]
    rows = q_ref.shape[1] // 2
    s, lanes, first, second = head_slices(i, rows)
    q = q_ref[first, lanes]
    scores = []
    maximum = None
    for b in range(bands):
        other = jnp.where(chip_x == b // 2, 0, 1)
        keys, _ = kv_rows(kv_ref, b, i % HEADS)
        part = add_bias(dg(keys[:, lanes], q, 0, 0), bias_ref, s, other)
        scores.append(part)
        top = jnp.max(part, axis=0, keepdims=True)
        maximum = top if maximum is None else jnp.maximum(maximum, top)
    total, acc = 0.0, 0.0
    for b in range(bands):
        weight = jnp.exp(scores[b] - maximum)
        total = total + jnp.sum(weight, axis=0, keepdims=True)
        _, values = kv_rows(kv_ref, b, i % HEADS)
        acc = acc + dg(values[:, lanes], weight.astype(BF), 1, 0)
    out_ref[first, lanes] = acc / total
    lse_ref[pl.ds(i, 1), :] = maximum + jnp.log(total)


def attend_kernel(unroll, scalars_ref, q_ref, kv_ref, out_ref, lse_ref, bias_ref):
    fill_bias(scalars_ref, bias_ref, q_ref.shape[1] // 2)

    @pl.loop(0, 2 * HEADS // unroll)
    def _(j):
        for k in range(unroll):
            attend_step(
                j * unroll + k, scalars_ref[2], q_ref, kv_ref, bias_ref, out_ref, lse_ref
            )


def attend(scalars, q, kv):
    width, tokens = q.shape
    return pl.pallas_call(
        functools.partial(attend_kernel, 4),
        name="attend",
        out_shape=(shape((width, tokens), F), shape((2 * HEADS, tokens // 2), F)),
        in_specs=[SM, VM, VM],
        out_specs=(VM, VM),
        scratch_shapes=[pltpu.VMEM((8, tokens // 2), F)],
        compiler_params=pltpu.CompilerParams(vmem_limit_bytes=LIMIT),
    )(scalars, q, kv)


def attend_back_step(
    i, chip_x, q_ref, kv_ref, out_ref, lse_ref, dout_ref, bias_ref, dq_ref, put_key, put_value
):
    bands = kv_ref.shape[0]
    rows = q_ref.shape[1] // 2
    s, lanes, first, second = head_slices(i, rows)
    q = q_ref[first, lanes]
    dout = dout_ref[first, lanes]
    delta = jnp.sum(out_ref[first, lanes] * dout.astype(F), axis=0, keepdims=True)
    lse = lse_ref[pl.ds(i, 1), :]
    dq = 0.0
    for b in range(bands):
        other = jnp.where(chip_x == b // 2, 0, 1)
        k, v = (ref[:, lanes] for ref in kv_rows(kv_ref, b, i % HEADS))
        scores = add_bias(dg(k, q, 0, 0), bias_ref, s, other)
        dweight = dg(v, dout, 0, 0)
        weight = jnp.exp(scores - lse)
        dscores = (weight * (dweight - delta)).astype(BF)
        dq = dq + dg(k, dscores, 1, 0)
        put_key(b, dg(q, dscores, 1, 1).astype(BF))
        put_value(b, dg(dout, weight.astype(BF), 1, 1).astype(BF))
    dq_ref[first, lanes] = (dq * (1.0 / math.sqrt(HEAD_DIM))).astype(BF)


def attend_back_kernel(
    unroll, scalars_ref, q_ref, kv_ref, out_ref, lse_ref, dout_ref, dq_ref, dkv_ref, bias_ref
):
    fill_bias(scalars_ref, bias_ref, q_ref.shape[1] // 2)

    @pl.loop(0, 2 * HEADS // unroll)
    def _(j):
        for k in range(unroll):
            i = j * unroll + k
            _, lanes, first, second = head_slices(i, q_ref.shape[1] // 2)

            def put_key(b, values):
                dkv_ref[b, first, lanes] = values

            def put_value(b, values):
                dkv_ref[b, second, lanes] = values

            attend_back_step(
                i, scalars_ref[2], q_ref, kv_ref, out_ref, lse_ref, dout_ref, bias_ref, dq_ref,
                put_key, put_value,
            )


def attend_back(scalars, q, kv, out, lse, dout):
    return pl.pallas_call(
        functools.partial(attend_back_kernel, 4),
        name="attend_back",
        out_shape=(shape(q.shape, BF), shape((kv.shape[0], 2 * q.shape[0], q.shape[1]), BF)),
        in_specs=[SM] + [VM] * 5,
        out_specs=(VM, VM),
        scratch_shapes=[pltpu.VMEM((8, q.shape[1] // 2), F)],
        compiler_params=pltpu.CompilerParams(vmem_limit_bytes=LIMIT),
    )(scalars, q, kv, out, lse, dout)


def middle_kernel(
    x_ref,
    cot_ref,
    scalars_ref,
    att_ref,
    w_out_ref,
    w_up_ref,
    w_down_ref,
    cols_ref,
    bias_up_ref,
    out_ref,
    dmid_ref,
    datt_ref,
    g_out_ref,
    g_up_ref,
    g_down_ref,
    sums_ref,
    mid_ref,
    norm_ref,
    h_ref,
    dmlp_ref,
    mlp_ref,
    err_ref,
    attb_ref,
    dbranch_ref,
):
    width, tokens = x_ref.shape
    hidden = w_up_ref.shape[0]
    step = 256
    first_slot = lax.broadcasted_iota(jnp.int32, (1, tokens), 1) < tokens // 2
    valid = jnp.where(
        first_slot,
        jnp.where(scalars_ref[0] > 0, 1.0, 0.0),
        jnp.where(scalars_ref[1] > 0, 1.0, 0.0),
    )
    attb_ref[...] = att_ref[...].astype(BF)
    sums_ref[...] = jnp.zeros_like(sums_ref)

    @pl.loop(0, width // step)
    def _(j):
        rows = pl.ds(pl.multiple_of(j * step, step), step)
        mid_ref[rows, :] = (
            dg(w_out_ref[rows, :], attb_ref[...], 1, 0)
            + cols_ref[rows, BIAS_OUT]
            + x_ref[rows, :].astype(F)
        )

    normed, inverse = normalize(mid_ref[...])
    norm_ref[...] = normed
    h_ref[...] = (normed * cols_ref[:, GAIN_TWO] + cols_ref[:, SHIFT_TWO]).astype(BF)
    dmlp_ref[...] = (cot_ref[...].astype(F) * valid).astype(BF)
    mlp_ref[...] = jnp.zeros_like(mlp_ref)
    err_ref[...] = jnp.zeros_like(err_ref)

    @pl.loop(0, hidden // step)
    def _(j):
        rows = pl.ds(pl.multiple_of(j * step, step), step)
        pre = dg(w_up_ref[rows, :], h_ref[...], 1, 0) + bias_up_ref[rows, :]
        phi = 0.5 + 0.5 * lax.erf(pre * math.sqrt(0.5))
        act = (pre * phi).astype(BF)
        slope = phi + pre * jnp.exp(pre * pre * -0.5) * (1.0 / math.sqrt(2.0 * math.pi))
        mlp_ref[...] += dg(w_down_ref[:, rows], act, 1, 0)
        dact = dg(w_down_ref[:, rows], dmlp_ref[...], 0, 0)
        dhid = (slope * dact).astype(BF)
        g_down_ref[:, rows] = dg(dmlp_ref[...], act, 1, 1).astype(BF)
        g_up_ref[rows, :] = dg(dhid, h_ref[...], 1, 1).astype(BF)
        per = width // step
        lanes = pl.ds(pl.multiple_of(j % per * step, step), step)
        sums_ref[pl.ds(UP_ROW + j // per, 1), lanes] = row_sums(dhid)[:1]
        err_ref[...] += dg(w_up_ref[rows, :], dhid, 0, 0)

    out_ref[...] = ((mid_ref[...] + mlp_ref[...] + cols_ref[:, BIAS_DOWN]) * valid).astype(BF)
    err = err_ref[...]
    sums_ref[3:4] = row_sums(dmlp_ref[...])[:1]
    sums_ref[6:7] = row_sums(err * norm_ref[...])[:1]
    sums_ref[7:8] = row_sums(err)[:1]
    dmid = cot_ref[...].astype(F) * valid + norm_back(
        err, norm_ref[...], inverse, cols_ref[:, GAIN_TWO]
    )
    dmid_ref[...] = dmid
    dbranch_ref[...] = dmid.astype(BF)
    sums_ref[2:3] = row_sums(dbranch_ref[...])[:1]
    datt_ref[...] = dg(w_out_ref[...], dbranch_ref[...], 0, 0).astype(BF)

    @pl.loop(0, width // step)
    def _(j):
        rows = pl.ds(pl.multiple_of(j * step, step), step)
        g_out_ref[rows, :] = dg(dbranch_ref[rows, :], attb_ref[...], 1, 1).astype(BF)


def middle(x, cot, scalars, att, w_out, w_up, w_down, cols, bias_up):
    width, tokens = x.shape
    hidden = w_up.shape[0]
    full = (width, tokens)
    return pl.pallas_call(
        middle_kernel,
        name="middle",
        out_shape=(
            shape(full, BF),
            shape(full, F),
            shape(full, BF),
            shape(w_out.shape, BF),
            shape(w_up.shape, BF),
            shape(w_down.shape, BF),
            shape((SUM_ROWS, width), F),
        ),
        in_specs=[VM, VM, SM] + [VM] * 6,
        out_specs=tuple([VM] * 7),
        scratch_shapes=[
            pltpu.VMEM(full, F),
            pltpu.VMEM(full, F),
            pltpu.VMEM(full, BF),
            pltpu.VMEM(full, BF),
            pltpu.VMEM(full, F),
            pltpu.VMEM(full, F),
            pltpu.VMEM(full, BF),
            pltpu.VMEM(full, BF),
        ],
        compiler_params=pltpu.CompilerParams(vmem_limit_bytes=LIMIT),
    )(x, cot, scalars, att, w_out, w_up, w_down, cols, bias_up)


def finish_kernel(
    x_ref, h_ref, dq_ref, dkv_ref, w_ref, cols_ref, dmid_ref, gx_ref, g_ref, sums_ref, err_ref
):
    width, tokens = x_ref.shape
    step = 256
    blocks = width // step
    err_ref[...] = jnp.zeros_like(err_ref)
    for ref, count, base in ((dq_ref, blocks, 0), (dkv_ref, 2 * blocks, blocks)):

        @pl.loop(0, count)
        def _(j):
            rows = pl.ds(pl.multiple_of(j * step, step), step)
            to = pl.ds(pl.multiple_of((j + base) * step, step), step)
            g_ref[to, :] = dg(ref[rows, :], h_ref[...], 1, 1).astype(BF)
            err_ref[...] += dg(w_ref[to, :], ref[rows, :], 0, 0)

    normed, inverse = normalize(x_ref[...].astype(F))
    err = err_ref[...]
    sums_ref[...] = jnp.zeros_like(sums_ref)
    sums_ref[0:1] = row_sums(dq_ref[...])[:1]
    sums_ref[1:2] = row_sums(dkv_ref[pl.ds(width, width), :])[:1]
    sums_ref[4:5] = row_sums(err * normed)[:1]
    sums_ref[5:6] = row_sums(err)[:1]
    gx_ref[...] = (dmid_ref[...] + norm_back(err, normed, inverse, cols_ref[:, GAIN_ONE])).astype(BF)


def finish(x, h, dq, dkv, w, cols, dmid):
    width, tokens = x.shape
    return pl.pallas_call(
        finish_kernel,
        name="finish",
        out_shape=(shape(x.shape, BF), shape(w.shape, BF), shape((SUM_ROWS, width), F)),
        in_specs=[VM] * 7,
        out_specs=(VM, VM, VM),
        scratch_shapes=[pltpu.VMEM(x.shape, F)],
        compiler_params=pltpu.CompilerParams(vmem_limit_bytes=LIMIT),
    )(x, h, dq, dkv, w, cols, dmid)


class Place:
    def __init__(self, images):
        self.images = images
        self.depth = images // 2
        self.img = lax.axis_index("img")
        self.band = lax.axis_index("band")
        self.z, self.y = self.img // 2, self.img % 2
        self.x, self.c = self.band // 2, self.band % 2
        self.partner = (self.img, self.band + 1 - 2 * self.c)
        self.across_x = (self.img, self.band + 2 - 4 * self.x)
        self.across_y = (self.img + 1 - 2 * self.y, self.band)
        self.z_peers = [self.along_z(k) for k in range(1, self.depth)]

    def along_z(self, k):
        z = lax.rem(self.z + k, self.depth)
        return (2 * z + self.y, self.band), z


def greet(peers):
    barrier = pltpu.get_barrier_semaphore()
    for peer in peers:
        pl.semaphore_signal(barrier, inc=1, device_id=peer, device_id_type=MESH)
    pl.semaphore_wait(barrier, len(peers))


def send(src, dst, send_sem, recv_sem, peer):
    copy = pltpu.make_async_remote_copy(
        src_ref=src,
        dst_ref=dst,
        send_sem=send_sem,
        recv_sem=recv_sem,
        device_id=peer,
        device_id_type=MESH,
    )
    copy.start()
    return copy


def comm_params(collective_id):
    return pltpu.CompilerParams(
        collective_id=collective_id, has_side_effects=True, vmem_limit_bytes=LIMIT
    )


def split_rows(shards, parts):
    return jnp.concatenate(
        [item.reshape(parts, item.shape[0] // parts, item.shape[1]) for item in shards], axis=1
    )


class Spread:
    def __init__(self, at, make, order, source, ref, local_sem):
        depth, near, c = at.depth, at.depth // 2, at.c
        rows, half = ref.shape[2] // 2, ref.shape[3] // 2
        rows = pl.ds(pl.multiple_of(c * rows, 16), rows)
        lanes = pl.ds(pl.multiple_of(at.x * half, 128), half)
        low, high = pl.ds(0, near), pl.ds(near, depth - near)

        def same(part, peer):
            return make(part, part, peer)

        piece = ref.at[at.z, at.y, rows, lanes]
        self.keep = pltpu.make_async_copy(source, piece, local_sem)
        if order == "mixed":
            self.stages = [
                [make(source, piece, peer) for peer, _ in at.z_peers],
                [
                    same(ref.at[low, at.y, rows, lanes], at.across_x),
                    same(ref.at[high, at.y, rows, lanes], at.across_y),
                ],
                [
                    same(ref.at[low, at.y, rows, :], at.across_y),
                    same(ref.at[high, :, rows, lanes], at.across_x),
                ],
            ]
        elif order == "zxy":
            self.stages = [
                [make(source, piece, peer) for peer, _ in at.z_peers],
                [same(ref.at[:, at.y, rows, lanes], at.across_x)],
                [same(ref.at[:, at.y, rows, :], at.across_y)],
            ]
        else:
            self.stages = [
                [make(source, piece, at.across_x)],
                [same(ref.at[at.z, at.y, rows, :], at.across_y)],
                [same(ref.at[at.z, :, rows, :], peer) for peer, _ in at.z_peers],
            ]
        self.stages.append([same(ref.at[:, :, rows, :], at.partner)])

    def start(self):
        self.keep.start()
        for copy in self.stages[0]:
            copy.start()

    def step(self, k):
        if k == 1:
            self.keep.wait()
        for copy in self.stages[k - 1]:
            copy.wait_recv()
        for copy in self.stages[k]:
            copy.start()

    def wait(self):
        for copy in self.stages[-1]:
            copy.wait_recv()

    def end(self):
        for stage in self.stages:
            for copy in stage:
                copy.wait_send()


def kv_rows(ref, b, h):
    part = ref.shape[2] // 2
    heads = part // HEAD_DIM
    first = pl.multiple_of(h % heads * HEAD_DIM, 16)
    second = pl.multiple_of(part + h % heads * HEAD_DIM, 16)
    at = ref.at[b, h // heads]
    return at.at[pl.ds(first, HEAD_DIM)], at.at[pl.ds(second, HEAD_DIM)]


def front_kernel(
    images, bands, scalars_ref, narrow_ref, wide_ref, small_ref, x_ref,
    qkv_w_ref, out_w_ref, up_w_ref, down_w_ref, h_ref, q_ref, kv_ref, att_ref, lse_ref,
    cols_ref, up_col_ref,
    theirs_ref, mine_ref, mine_wide_ref, smalls_ref, qv_col_ref, bias_ref,
    local_sem, send_sem, recv_sem,
):
    at = Place(images)
    width, tokens = x_ref.shape
    rows = tokens // 2
    unit = width // images
    groups = kv_ref.shape[1]
    part = width // groups
    c = at.c
    used = [0]

    def make(src, dst, peer):
        k = used[0]
        used[0] += 1
        return pltpu.make_async_remote_copy(
            src_ref=src,
            dst_ref=dst,
            send_sem=send_sem.at[k],
            recv_sem=recv_sem.at[k],
            device_id=peer,
            device_id_type=MESH,
        )

    others = [(lax.rem(at.img + k, images), at.band) for k in range(1, images)]
    half = wide_ref.shape[0] // 2
    wide = wide_ref.shape[1]
    own_lanes = pl.ds(pl.multiple_of(c * wide, 128), wide)
    own_wide = pltpu.make_async_copy(
        wide_ref.at[pl.ds(pl.multiple_of(c * half, 8), half), :],
        mine_wide_ref.at[:, own_lanes],
        local_sem.at[0],
    )
    swap = make(narrow_ref.at[1 - c], theirs_ref, at.partner)
    swap_wide = make(
        wide_ref.at[pl.ds(pl.multiple_of((1 - c) * half, 8), half), :],
        mine_wide_ref.at[:, own_lanes],
        at.partner,
    )
    lines = pl.ds(pl.multiple_of(at.img * 16, 16), 16)
    keep_small = pltpu.make_async_copy(small_ref, smalls_ref.at[lines, :], local_sem.at[1])
    small_copies = [make(small_ref, smalls_ref.at[lines, :], peer) for peer in others]
    refs = (qkv_w_ref, out_w_ref, up_w_ref, down_w_ref)
    sources, row = [], 0
    for ref in refs[:3]:
        count = ref.shape[2] // 2
        sources.append(mine_ref.at[pl.ds(row, count), :])
        row += count
    sources.append(mine_wide_ref)
    orders = ("mixed", "zxy", "zxy", "xyz")
    spreads = [
        Spread(at, make, orders[m], sources[m], refs[m], local_sem.at[2 + m]) for m in range(4)
    ]
    s_qkv, s_out, s_up, s_down = spreads
    mate = kv_ref.at[at.band]
    far = kv_ref.at[at.across_x[1]]
    to_x = [make(mate.at[g], mate.at[g], at.across_x) for g in range(groups)]
    to_mate = [make(mate.at[g], mate.at[g], at.partner) for g in range(groups)]
    passed = [make(far.at[g], far.at[g], at.partner) for g in range(groups)]

    greet([at.partner, at.across_x] + others)
    swap.start()
    own_wide.start()
    swap_wide.start()
    keep_small.start()
    for copy in small_copies:
        copy.start()
    fill_bias(scalars_ref, bias_ref, rows)
    swap.wait_recv()
    mine, theirs = narrow_ref[c], theirs_ref[...]
    lane_count = mine.shape[1]
    mine_ref[:, pl.ds(0, lane_count)] = jnp.where(c == 0, mine, theirs)
    mine_ref[:, pl.ds(lane_count, lane_count)] = jnp.where(c == 0, theirs, mine)
    s_qkv.start()
    own_wide.wait()
    swap_wide.wait_recv()
    s_down.start()
    s_up.start()
    s_out.start()

    keep_small.wait()
    for copy in small_copies:
        copy.wait_recv()
    turned = smalls_ref[...].T
    qv_units, up_units = 2, up_w_ref.shape[2] // unit
    singles = 16 - qv_units - up_units
    for j in range(images):
        block = turned[:unit, 16 * j : 16 * j + 16]
        cols_ref[pl.ds(unit * j, unit), :] = block[:, :singles]
        for u in range(qv_units):
            lane = singles + u
            qv_col_ref[pl.ds(unit * (qv_units * j + u), unit), :] = block[:, lane : lane + 1]
        for u in range(up_units):
            lane = singles + qv_units + u
            up_col_ref[pl.ds(unit * (up_units * j + u), unit), :] = block[:, lane : lane + 1]

    s_down.step(1)
    normed, _ = normalize(x_ref[...].astype(F))
    h_ref[...] = (normed * cols_ref[:, GAIN_ONE] + cols_ref[:, SHIFT_ONE]).astype(BF)
    s_qkv.step(1)
    s_down.step(2)
    s_qkv.step(2)
    s_qkv.step(3)
    s_qkv.wait()

    weights = qkv_w_ref.reshape(3 * width, width)

    def project(row):
        return dg(weights[pl.ds(row, part), :], h_ref[...], 1, 0)

    for g in range(groups):
        kv_ref[at.band, g, pl.ds(0, part), :] = project(width + g * part).astype(BF)
        value = project(2 * width + g * part) + qv_col_ref[pl.ds(width + g * part, part), :]
        kv_ref[at.band, g, pl.ds(part, part), :] = value.astype(BF)
        to_x[g].start()
        to_mate[g].start()
        if g == 0:
            s_up.step(1)
            s_out.step(1)
    scale = 1.0 / math.sqrt(HEAD_DIM)
    for g in range(groups):
        block = pl.ds(g * part, part)
        q_ref[block, :] = ((project(g * part) + qv_col_ref[block, :]) * scale).astype(BF)

    def forward(g):
        to_x[g].wait_recv()
        passed[g].start()

    def arrive(g):
        to_mate[g].wait_recv()
        passed[g].wait_recv()

    events = {}

    def when(j, *actions):
        events.setdefault(j, []).extend(actions)

    for g in range(1, groups):
        when(2 * g - 2, functools.partial(forward, g))
        when(2 * g - 1, functools.partial(arrive, g))
    when(1, functools.partial(s_up.step, 2))
    when(2, functools.partial(s_out.step, 2))
    when(4, functools.partial(s_out.step, 3))
    when(6, functools.partial(s_up.step, 3))
    forward(0)
    arrive(0)
    unroll = HEADS // groups

    @pl.loop(0, 2 * groups)
    def _(j):
        g, s = j // 2, j % 2
        for k in range(unroll):
            attend_step(
                s * HEADS + g * unroll + k, at.x, q_ref, kv_ref, bias_ref, att_ref, lse_ref
            )
        for when_j, actions in events.items():

            @pl.when(j == when_j)
            def _():
                for action in actions:
                    action()

    s_down.step(3)
    for item in spreads[1:]:
        item.wait()
    for item in spreads:
        item.end()
    for copy in [swap, swap_wide] + small_copies + to_x + to_mate + passed:
        copy.wait_send()


def front(images, bands, scalars, narrow, wide, small, x, widths):
    depth = images // 2
    width, tokens = x.shape
    groups = GROUPS_OF_HEADS
    hidden = images * widths[2]
    count = 2 + images - 1 + 2 * (depth + 5) + 2 * (depth + 2) + 3 * groups
    return pl.pallas_call(
        functools.partial(front_kernel, images, bands),
        name="front",
        out_shape=tuple(shape((depth, 2, w, width), BF) for w in widths)
        + (
            shape((depth, 2, wide.shape[0], 4 * wide.shape[1]), BF),
            shape((width, tokens), BF),
            shape((width, tokens), BF),
            shape((bands, groups, 2 * width // groups, tokens), BF),
            shape((width, tokens), F),
            shape((2 * HEADS, tokens // 2), F),
            shape((width, COLUMNS), F),
            shape((hidden, 1), F),
        ),
        in_specs=[SM] + [VM] * 4,
        out_specs=(VM, ANY, ANY, ANY) + (VM,) * 7,
        scratch_shapes=[
            pltpu.VMEM(narrow.shape[1:], BF),
            pltpu.VMEM((narrow.shape[1], 2 * narrow.shape[2]), BF),
            pltpu.VMEM((wide.shape[0] // 2, 2 * wide.shape[1]), BF),
            pltpu.VMEM((16 * images, 128), F),
            pltpu.VMEM((2 * width, 1), F),
            pltpu.VMEM((8, tokens // 2), F),
            pltpu.SemaphoreType.DMA((6,)),
            pltpu.SemaphoreType.DMA((count,)),
            pltpu.SemaphoreType.DMA((count,)),
        ],
        compiler_params=comm_params(0),
    )(scalars, narrow, wide, small, x)


def share_kernel(images, kv_ref, all_ref, local_sem, send_sem, recv_sem):
    at = Place(images)
    greet([at.partner, at.across_x])
    rows = kv_ref.shape[1] // 2
    mine = pltpu.make_async_copy(kv_ref, all_ref.at[at.band], local_sem)
    mine.start()
    copies = []
    for s in range(2):
        lanes = pl.ds(s * rows, rows)
        copies.append(
            send(
                kv_ref.at[:, lanes],
                all_ref.at[at.band, :, lanes],
                send_sem.at[s],
                recv_sem.at[s],
                at.across_x,
            )
        )
    near = send(kv_ref, all_ref.at[at.band], send_sem.at[2], recv_sem.at[2], at.partner)
    passed = []
    for s in range(2):
        copies[s].wait_recv()
        part = all_ref.at[at.across_x[1], :, pl.ds(s * rows, rows)]
        passed.append(send(part, part, send_sem.at[3 + s], recv_sem.at[3 + s], at.partner))
    for copy in passed + [near]:
        copy.wait()
    for copy in copies:
        copy.wait_send()
    mine.wait()


def share(images, bands, kv):
    return pl.pallas_call(
        functools.partial(share_kernel, images),
        name="share",
        out_shape=shape((bands,) + kv.shape, BF),
        in_specs=[VM],
        out_specs=ANY,
        scratch_shapes=[
            pltpu.SemaphoreType.DMA,
            pltpu.SemaphoreType.DMA((5,)),
            pltpu.SemaphoreType.DMA((5,)),
        ],
        compiler_params=comm_params(1),
    )(kv)


def add_rows(total_ref, other_ref, step):
    @pl.loop(0, total_ref.shape[0] // step)
    def _(j):
        rows = pl.ds(pl.multiple_of(j * step, step), step)
        total_ref[rows, :] = (
            total_ref[rows, :].astype(F) + other_ref[rows, :].astype(F)
        ).astype(total_ref.dtype)


def unshare_kernel(images, dkv_ref, sum_ref, near_ref, far_ref, send_sem, recv_sem):
    at = Place(images)
    greet([at.partner, at.across_x])
    mate, far = at.partner[1], at.across_x[1]
    far_mate = at.band + 2 - 4 * at.x + 1 - 2 * at.c
    one = send(dkv_ref.at[far_mate], near_ref.at[0], send_sem.at[0], recv_sem.at[0], at.partner)
    two = send(dkv_ref.at[mate], near_ref.at[1], send_sem.at[1], recv_sem.at[1], at.partner)
    one.wait_recv()
    add_rows(near_ref.at[0], dkv_ref.at[far], 64)
    three = send(near_ref.at[0], far_ref, send_sem.at[2], recv_sem.at[2], at.across_x)
    two.wait_recv()
    add_rows(near_ref.at[1], dkv_ref.at[at.band], 64)
    three.wait_recv()
    sum_ref[...] = near_ref[1]
    add_rows(sum_ref, far_ref, 64)
    for copy in (one, two, three):
        copy.wait_send()


def unshare(images, dkv):
    block = dkv.shape[1:]
    return pl.pallas_call(
        functools.partial(unshare_kernel, images),
        name="unshare",
        out_shape=shape(block, BF),
        in_specs=[VM],
        out_specs=VM,
        scratch_shapes=[
            pltpu.VMEM((2,) + block, BF),
            pltpu.VMEM(block, BF),
            pltpu.SemaphoreType.DMA((3,)),
            pltpu.SemaphoreType.DMA((3,)),
        ],
        compiler_params=comm_params(2),
    )(dkv)


def accumulate(total, other):
    total[...] = (total[...].astype(F) + other[...].astype(F)).astype(total.dtype)


class Reduction:
    def __init__(self, at, make, ref, bufs, target, away):
        one, two_x, two_y, three, four = bufs
        self.at, self.ref, self.one, self.two_x, self.two_y = at, ref, one, two_x, two_y
        self.three, self.four, self.target, self.away = three, four, target, away
        depth, near, c = at.depth, at.depth // 2, at.c
        self.near = near
        rows, half = ref.shape[2] // 2, ref.shape[3] // 2

        def lanes_of(x):
            return pl.ds(pl.multiple_of(x * half, 128), half)

        self.rows = pl.ds(pl.multiple_of(c * rows, 16), rows)
        self.lanes = lanes_of(at.x)
        far_rows = pl.ds(pl.multiple_of((1 - c) * rows, 16), rows)
        far_lanes = lanes_of(1 - at.x)
        upper = depth - near
        self.zero = make(ref.at[:, :, far_rows, :], one, at.partner)
        self.first = [
            make(one.at[pl.ds(0, near), :, :, far_lanes], two_x, at.across_x),
            make(one.at[pl.ds(near, upper), 1 - at.y], two_y, at.across_y),
        ]
        self.second = [
            make(two_x.at[:, 1 - at.y], three.at[pl.ds(0, near)], at.across_y),
            make(two_y.at[:, :, far_lanes], three.at[pl.ds(near, upper)], at.across_x),
        ]
        self.third = [
            make(three.at[z], four.at[k], peer) for k, (peer, z) in enumerate(at.z_peers)
        ]
        self.last = make(away, target.at[c], at.partner)

    def start(self):
        self.zero.start()

    def step_one(self):
        self.zero.wait_recv()

        @pl.loop(0, self.ref.shape[0] * 2)
        def _(j):
            accumulate(
                self.one.at[j // 2, j % 2], self.ref.at[j // 2, j % 2, self.rows, :]
            )

        for copy in self.first:
            copy.start()

    def step_two(self):
        self.first[0].wait_recv()

        @pl.loop(0, 2 * self.near)
        def _(j):
            accumulate(
                self.two_x.at[j // 2, j % 2], self.one.at[j // 2, j % 2, :, self.lanes]
            )

        self.second[0].start()
        self.first[1].wait_recv()

        @pl.loop(0, self.at.depth - self.near)
        def _(j):
            accumulate(self.two_y.at[j], self.one.at[self.near + j, self.at.y])

        self.second[1].start()

    def step_three(self):
        for copy in self.second:
            copy.wait_recv()

        @pl.loop(0, self.near)
        def _(j):
            accumulate(self.three.at[j], self.two_x.at[j, self.at.y])

        @pl.loop(0, self.at.depth - self.near)
        def _(j):
            accumulate(self.three.at[self.near + j], self.two_y.at[j, :, self.lanes])

        for copy in self.third:
            copy.start()

    def step_four(self):
        for copy in self.third:
            copy.wait_recv()
        c = self.at.c
        total = self.three[self.at.z].astype(F)
        for k in range(len(self.third)):
            total = total + self.four[k].astype(F)
        size = total.shape[1] // 2
        low, high = total[:, :size], total[:, size:]
        self.target[c] = jnp.where(c == 0, low, high)
        self.away[...] = jnp.where(c == 0, high, low)
        self.last.start()

    def end(self):
        self.last.wait()
        for copy in [self.zero] + self.first + self.second + self.third:
            copy.wait_send()


def back_kernel(
    images, bands, scalars_ref, q_ref, kv_ref, att_ref, lse_ref, datt_ref, x_ref, h_ref, dmid_ref,
    w_ref, cols_ref, g_out_ref, g_up_ref, g_down_ref, sums_ref,
    gx_ref, p_qkv_ref, p_out_ref, p_up_ref, p_down_ref, total_ref,
    bias_ref, dqkv_ref, dkv_ref, near_ref, far_ref, g_qkv_ref, err_ref,
    small_ref, small_in_ref, small_z_ref, *rest,
):
    at = Place(images)
    depth = at.depth
    send_sem, recv_sem = rest[-2:]
    used = [0]

    def make(src, dst, peer):
        k = used[0]
        used[0] += 1
        return pltpu.make_async_remote_copy(
            src_ref=src,
            dst_ref=dst,
            send_sem=send_sem.at[k],
            recv_sem=recv_sem.at[k],
            device_id=peer,
            device_id_type=MESH,
        )

    width, tokens = x_ref.shape
    rows = tokens // 2
    unroll = 4
    groups = HEADS // unroll
    part = width // groups

    def four_d(ref):
        return ref.reshape(depth, 2, ref.shape[0] // images, ref.shape[1])

    sources = (four_d(g_down_ref), four_d(g_up_ref), four_d(g_out_ref), g_qkv_ref)
    targets = (p_down_ref, p_up_ref, p_out_ref, p_qkv_ref)
    moves = []
    for m in range(4):
        moves.append(
            Reduction(at, make, sources[m], rest[6 * m : 6 * m + 5], targets[m], rest[6 * m + 5])
        )
    down, up, out, qkv = moves
    mate, far = at.partner[1], at.across_x[1]
    far_mate = at.across_x[1] + 1 - 2 * at.c
    one = [make(dkv_ref.at[far_mate, g], near_ref.at[0, g], at.partner) for g in range(groups)]
    two = [make(dkv_ref.at[mate, g], near_ref.at[1, g], at.partner) for g in range(groups)]
    three = [make(near_ref.at[0, g], far_ref.at[g], at.across_x) for g in range(groups)]
    small_steps = [
        make(small_ref.at[k], small_in_ref.at[k], peer)
        for k, peer in enumerate((at.partner, at.across_x, at.across_y))
    ]
    small_last = [
        make(small_z_ref.at[at.z], small_z_ref.at[at.z], peer) for peer, _ in at.z_peers
    ]

    greet([at.partner, at.across_x, at.across_y] + [peer for peer, _ in at.z_peers])
    for move in (down, up, out):
        move.start()
    fill_bias(scalars_ref, bias_ref, rows)

    def share_one(g):
        one[g].start()
        two[g].start()

    def share_two(g):
        one[g].wait_recv()
        add_rows(near_ref.at[0, g], dkv_ref.at[far, g], part)
        three[g].start()

    def share_three(g):
        two[g].wait_recv()
        three[g].wait_recv()
        for half in range(2):
            block = pl.ds(half * part, part)
            to = pl.ds((1 + half) * width + g * part, part)
            dqkv_ref[to, :] = (
                near_ref[1, g, block, :].astype(F)
                + dkv_ref[at.band, g, block, :].astype(F)
                + far_ref[g, block, :].astype(F)
            ).astype(BF)

    events = {}

    def when(j, *actions):
        events.setdefault(j, []).extend(actions)

    when(0, down.step_one)
    when(1, lambda: share_one(0), up.step_one)
    when(2, lambda: share_two(0))
    when(3, lambda: share_one(1), down.step_two, out.step_one)
    when(4, lambda: share_two(1))
    when(5, lambda: share_one(2), down.step_three)
    when(6, lambda: share_two(2), up.step_two)

    @pl.loop(0, 2 * groups)
    def _(j):
        g, s = j // 2, j % 2
        lanes = pl.ds(pl.multiple_of(s * rows, rows), rows)
        for k in range(unroll):

            def put_key(b, values):
                dkv_ref[b, g, pl.ds(k * HEAD_DIM, HEAD_DIM), lanes] = values

            def put_value(b, values):
                dkv_ref[b, g, pl.ds(part + k * HEAD_DIM, HEAD_DIM), lanes] = values

            attend_back_step(
                s * HEADS + g * unroll + k,
                at.x, q_ref, kv_ref, att_ref, lse_ref, datt_ref, bias_ref, dqkv_ref,
                put_key, put_value,
            )
        for when_j, actions in events.items():

            @pl.when(j == when_j)
            def _():
                for action in actions:
                    action()

    share_one(groups - 1)
    block = w_ref.shape[0] // images

    def weight_grad(j):
        piece = dqkv_ref[pl.ds(pl.multiple_of(j * block, 16), block), :]
        g_qkv_ref[j // 2, j % 2] = dg(piece, h_ref[...], 1, 1).astype(BF)

    early = width // block

    @pl.loop(0, early)
    def _(j):
        weight_grad(j)

    share_two(groups - 1)
    out.step_two()
    down.step_four()
    for g in range(groups - 1):
        share_three(g)
    up.step_three()
    share_three(groups - 1)

    @pl.loop(early, images)
    def _(j):
        weight_grad(j)

    qkv.start()
    err_ref[...] = jnp.zeros_like(err_ref)

    @pl.loop(0, images)
    def _(j):
        piece = pl.ds(pl.multiple_of(j * block, 16), block)
        err_ref[...] += dg(w_ref[piece, :], dqkv_ref[piece, :], 0, 0)

    out.step_three()
    qkv.step_one()
    normed, inverse = normalize(x_ref[...].astype(F))
    err = err_ref[...]
    small_ref[0] = sums_ref[...]
    small_ref[0, 0:1] = row_sums(dqkv_ref[pl.ds(0, width), :])[:1]
    small_ref[0, 1:2] = row_sums(dqkv_ref[pl.ds(2 * width, width), :])[:1]
    small_ref[0, 4:5] = row_sums(err * normed)[:1]
    small_ref[0, 5:6] = row_sums(err)[:1]
    small_steps[0].start()
    gx_ref[...] = (dmid_ref[...] + norm_back(err, normed, inverse, cols_ref[:, GAIN_ONE])).astype(BF)
    up.step_four()
    small_steps[0].wait_recv()
    small_ref[1] = small_ref[0] + small_in_ref[0]
    small_steps[1].start()
    qkv.step_two()
    small_steps[1].wait_recv()
    small_ref[2] = small_ref[1] + small_in_ref[1]
    small_steps[2].start()
    out.step_four()
    small_steps[2].wait_recv()
    small_z_ref[at.z] = small_ref[2] + small_in_ref[2]
    for copy in small_last:
        copy.start()
    qkv.step_three()
    for copy in small_last:
        copy.wait_recv()
    total = small_z_ref[0]
    for k in range(1, depth):
        total = total + small_z_ref[k]
    total_ref[...] = total
    qkv.step_four()
    for move in moves:
        move.end()
    for copy in one + two + three + small_steps + small_last:
        copy.wait_send()


def back(images, bands, scalars, q, kv, att, lse, datt, x, h, dmid, w, cols, grads, sums):
    depth = images // 2
    near = depth // 2
    width, tokens = x.shape
    g_out, g_up, g_down = grads
    groups = HEADS // 4
    results, buffers = [], []
    count = 0
    for item in (g_down, g_up, g_out, w):
        block, lanes = item.shape[0] // images // 2, item.shape[1]
        results.append(shape((2, block, lanes // 4), F))
        buffers += [
            pltpu.VMEM((depth, 2, block, lanes), BF),
            pltpu.VMEM((near, 2, block, lanes // 2), BF),
            pltpu.VMEM((depth - near, block, lanes), BF),
            pltpu.VMEM((depth, block, lanes // 2), BF),
            pltpu.VMEM((depth - 1, block, lanes // 2), BF),
            pltpu.VMEM((block, lanes // 4), F),
        ]
        count += 6 + depth - 1
    count += 3 * groups + 3 + depth - 1
    small = (SUM_ROWS, width)
    return pl.pallas_call(
        functools.partial(back_kernel, images, bands),
        name="back",
        out_shape=(shape(x.shape, BF), results[3], results[2], results[1], results[0], shape(small, F)),
        in_specs=[SM] + [VM] * 14,
        out_specs=(VM,) * 6,
        scratch_shapes=[
            pltpu.VMEM((8, tokens // 2), F),
            pltpu.VMEM((3 * width, tokens), BF),
            pltpu.VMEM((bands, groups, 2 * width // groups, tokens), BF),
            pltpu.VMEM((2, groups, 2 * width // groups, tokens), BF),
            pltpu.VMEM((groups, 2 * width // groups, tokens), BF),
            pltpu.VMEM((depth, 2, w.shape[0] // images, width), BF),
            pltpu.VMEM((width, tokens), F),
            pltpu.VMEM((3,) + small, F),
            pltpu.VMEM((3,) + small, F),
            pltpu.VMEM((depth,) + small, F),
        ]
        + buffers
        + [pltpu.SemaphoreType.DMA((count,)), pltpu.SemaphoreType.DMA((count,))],
        compiler_params=comm_params(3),
    )(scalars, q, kv, att, lse, datt, x, h, dmid, w, cols, g_out, g_up, g_down, sums)


def body(
    tokens,
    slot_kind,
    w_qkv,
    w_out,
    w_up,
    w_down,
    bias_qv,
    bias_out,
    bias_up,
    bias_down,
    gain_one,
    shift_one,
    gain_two,
    shift_two,
    cotangent,
):
    rows, slots, width = tokens.shape[1:]
    count = rows * slots
    images, bands = lax.axis_size("img"), lax.axis_size("band")
    band = lax.axis_index("band")
    smalls = (bias_qv, bias_out, bias_up, bias_down, gain_one, shift_one, gain_two, shift_two)
    sizes = [item.shape[0] for item in smalls]
    own = (w_qkv, w_out, w_up)
    widths = [item.shape[1] for item in own]
    direct = images % 4 == 0 and all(w % 32 == 0 for w in widths + [w_down.shape[1]])
    direct = direct and bias_qv.shape[0] == 2 * (width // images) <= 256
    direct = direct and bias_up.shape[0] == 4 * (width // images)

    def turn(values):
        return values[0].transpose(2, 1, 0).reshape(width, count)

    def turn_back(values):
        return values.reshape(width, slots, rows).transpose(2, 1, 0)[None]

    x, cot = turn(tokens), turn(cotangent)
    kinds = slot_kind[0].astype(jnp.int32)
    scalars = jnp.concatenate([kinds, (band // 2).astype(jnp.int32)[None]])
    single = (bias_out, bias_down, gain_one, shift_one, gain_two, shift_two)
    if direct:
        narrow = split_rows([item.T for item in own], 2)
        unit = width // images
        units = [jnp.stack(single), jnp.zeros((4, unit), BF)]
        units += [bias_qv.reshape(2, unit), bias_up.reshape(4, unit)]
        small = jnp.pad(jnp.concatenate(units), ((0, 0), (0, 128 - unit))).astype(F)
        *full, h, q, all_kv, att, lse, cols, c_up = front(
            images, bands, scalars, narrow, w_down.T, small, x, widths
        )
        full_qkv, full_out, full_up, full_down = (item.reshape(-1, item.shape[3]) for item in full)
    else:
        full_qkv, full_out, full_up, full_down = (
            lax.all_gather(lax.all_gather(item, "band", axis=0, tiled=True).T, "img", tiled=True)
            for item in (*own, w_down)
        )
        whole = [lax.all_gather(item, "img", tiled=True).astype(F) for item in single]
        cols = jnp.stack(whole + [whole[0]] * (COLUMNS - len(whole)), axis=1)
        c_qv = lax.all_gather(bias_qv, "img", tiled=True).astype(F)[:, None]
        c_up = lax.all_gather(bias_up, "img", tiled=True).astype(F)[:, None]
        bias = jnp.concatenate([c_qv[:width], jnp.zeros((width, 1), F), c_qv[width:]])
        h, qkv = project(x, full_qkv, cols, bias)
        q = qkv[:width]
        all_kv = share(images, bands, qkv[width:])
        all_kv = all_kv.reshape(bands, 2, GROUPS_OF_HEADS, -1, count).transpose(0, 2, 1, 3, 4)
        all_kv = all_kv.reshape(bands, GROUPS_OF_HEADS, -1, count)
        att, lse = attend(scalars, q, all_kv)
    out, dmid, datt, g_out, g_up, g_down, sums = middle(
        x, cot, scalars, att, full_out, full_up, full_down, cols, c_up
    )
    if direct:
        gx, *pieces, total = back(
            images, bands, scalars, q, all_kv, att, lse, datt, x, h, dmid,
            full_qkv, cols, (g_out, g_up, g_down), sums,
        )
        matrices = [item.reshape(-1, item.shape[2]).T for item in pieces]
    else:
        dq, dkv = attend_back(scalars, q, all_kv, att, lse, datt)
        dkv = unshare(images, dkv)
        gx, g_qkv, sums_one = finish(x, h, dq, dkv, full_qkv, cols, dmid)
        matrices = [
            lax.psum_scatter(
                lax.psum_scatter(item, "img", scatter_dimension=0, tiled=True),
                "band",
                scatter_dimension=1,
                tiled=True,
            )
            .astype(F)
            .T
            for item in (g_qkv, g_out, g_up, g_down)
        ]
        total = lax.psum(sums + sums_one, ("img", "band"))
    own_small = lax.axis_index("img")
    flat = total.reshape(-1)
    starts = [0, 2, UP_ROW, 3, 4, 5, 6, 7]
    small = [
        lax.dynamic_slice(flat, (start * width + own_small * size,), (size,))
        for start, size in zip(starts, sizes)
    ]
    return (turn_back(out), turn_back(gx), *matrices, *small)


def solution(mesh):
    data, weight, vector = P("img", "band", None, None), P("band", "img"), P("img")
    return jax.shard_map(
        body,
        mesh=mesh,
        in_specs=(data, P("img", None)) + (weight,) * 4 + (vector,) * 8 + (data,),
        out_specs=(data, data) + (weight,) * 4 + (vector,) * 8,
        check_vma=False,
    )
```

```python
import functools
import math

import jax
import jax.numpy as jnp
from jax import lax
from jax.experimental import pallas as pl
from jax.experimental.pallas import tpu as pltpu
from jax.sharding import PartitionSpec as P

HEADS = 16
HEAD_DIM = 48
EPSILON = 1e-06
MASKED = -1e30
BF = jnp.bfloat16
F = jnp.float32
MESH = pl.DeviceIdType.MESH
VM = pl.BlockSpec(memory_space=pltpu.VMEM)
SM = pl.BlockSpec(memory_space=pltpu.SMEM)
ANY = pl.BlockSpec(memory_space=pl.ANY)
LIMIT = 67043328
SUM_ROWS, UP_ROW = 16, 8
COLUMNS = 10
BIAS_OUT, BIAS_DOWN, GAIN_ONE, SHIFT_ONE, GAIN_TWO, SHIFT_TWO = (slice(k, k + 1) for k in range(6))
GROUPS_OF_HEADS = 4
FRONT_COPIES, BACK_COPIES = 128, 128


def dg(left, right, left_dim, right_dim):
    return lax.dot_general(
        left, right, (((left_dim,), (right_dim,)), ((), ())), preferred_element_type=F
    )


def shape(dims, dtype):
    return jax.ShapeDtypeStruct(tuple(dims), dtype)


def row_sums(values):
    ones = jnp.ones((8, values.shape[1]), BF)
    if values.dtype == BF:
        return dg(ones, values, 1, 1)
    high = values.astype(BF)
    low = (values - high.astype(F)).astype(BF)
    return dg(ones, high, 1, 1) + dg(ones, low, 1, 1)


def normalize(values):
    average = jnp.mean(values, axis=0, keepdims=True)
    centered = values - average
    variance = jnp.mean(centered * centered, axis=0, keepdims=True)
    inverse = lax.rsqrt(variance + EPSILON)
    return centered * inverse, inverse


def norm_back(error, normed, inverse, gain):
    f = gain * error
    mean_f = jnp.mean(f, axis=0, keepdims=True)
    mean_fn = jnp.mean(f * normed, axis=0, keepdims=True)
    return (f - mean_f - normed * mean_fn) * inverse


def project_kernel(x_ref, w_ref, cols_ref, bias_ref, h_ref, qkv_ref):
    width = x_ref.shape[0]
    normed, _ = normalize(x_ref[...].astype(F))
    h_ref[...] = (normed * cols_ref[:, GAIN_ONE] + cols_ref[:, SHIFT_ONE]).astype(BF)
    scale = 1.0 / math.sqrt(HEAD_DIM)
    step = 256

    @pl.loop(0, 3 * width // step)
    def _(j):
        rows = pl.ds(pl.multiple_of(j * step, step), step)
        out = dg(w_ref[rows, :], h_ref[...], 1, 0) + bias_ref[rows, :]
        qkv_ref[rows, :] = (out * jnp.where(j < width // step, scale, 1.0)).astype(BF)


def project(x, w, cols, bias):
    width, tokens = x.shape
    return pl.pallas_call(
        project_kernel,
        name="project",
        out_shape=(shape((width, tokens), BF), shape((3 * width, tokens), BF)),
        in_specs=[VM] * 4,
        out_specs=(VM, VM),
        compiler_params=pltpu.CompilerParams(vmem_limit_bytes=LIMIT),
    )(x, w, cols, bias)


def fill_bias(scalars_ref, bias_ref, rows):
    lane_half = lax.broadcasted_iota(jnp.int32, (1, rows), 1) // (rows // 2)
    for s in range(2):
        small = scalars_ref[s] == 2
        for other in range(2):
            for half in range(2):
                keep = jnp.logical_and(other == 0, lane_half == half)
                masked = jnp.where(small, MASKED, 0.0)
                bias_ref[pl.ds(4 * s + 2 * other + half, 1), :] = jnp.where(
                    keep, jnp.zeros((1, rows), F), jnp.full((1, rows), masked, F)
                )


def add_bias(scores, bias_ref, s, other):
    rows = scores.shape[0]
    at = 4 * s + 2 * other
    return jnp.concatenate(
        [
            scores[: rows // 2] + bias_ref[pl.ds(at, 1), :],
            scores[rows // 2 :] + bias_ref[pl.ds(at + 1, 1), :],
        ],
        axis=0,
    )


def head_slices(i, rows):
    s, h = i // HEADS, i % HEADS
    lanes = pl.ds(pl.multiple_of(s * rows, rows), rows)
    first = pl.ds(pl.multiple_of(h * HEAD_DIM, 16), HEAD_DIM)
    second = pl.ds(pl.multiple_of(HEADS * HEAD_DIM + h * HEAD_DIM, 16), HEAD_DIM)
    return s, lanes, first, second


def attend_step(i, chip_x, q_ref, kv_ref, bias_ref, out_ref, lse_ref):
    bands = kv_ref.shape[0]
    rows = q_ref.shape[1] // 2
    s, lanes, first, second = head_slices(i, rows)
    q = q_ref[first, lanes]
    scores = []
    maximum = None
    for b in range(bands):
        other = jnp.where(chip_x == b // 2, 0, 1)
        keys, _ = kv_rows(kv_ref, b, i % HEADS)
        part = add_bias(dg(keys[:, lanes], q, 0, 0), bias_ref, s, other)
        scores.append(part)
        top = jnp.max(part, axis=0, keepdims=True)
        maximum = top if maximum is None else jnp.maximum(maximum, top)
    total, acc = 0.0, 0.0
    for b in range(bands):
        weight = jnp.exp(scores[b] - maximum)
        total = total + jnp.sum(weight, axis=0, keepdims=True)
        _, values = kv_rows(kv_ref, b, i % HEADS)
        acc = acc + dg(values[:, lanes], weight.astype(BF), 1, 0)
    out_ref[first, lanes] = acc / total
    lse_ref[pl.ds(i, 1), :] = maximum + jnp.log(total)


def attend_kernel(unroll, scalars_ref, q_ref, kv_ref, out_ref, lse_ref, bias_ref):
    fill_bias(scalars_ref, bias_ref, q_ref.shape[1] // 2)

    @pl.loop(0, 2 * HEADS // unroll)
    def _(j):
        for k in range(unroll):
            attend_step(
                j * unroll + k, scalars_ref[2], q_ref, kv_ref, bias_ref, out_ref, lse_ref
            )


def attend(scalars, q, kv):
    width, tokens = q.shape
    return pl.pallas_call(
        functools.partial(attend_kernel, 4),
        name="attend",
        out_shape=(shape((width, tokens), F), shape((2 * HEADS, tokens // 2), F)),
        in_specs=[SM, VM, VM],
        out_specs=(VM, VM),
        scratch_shapes=[pltpu.VMEM((8, tokens // 2), F)],
        compiler_params=pltpu.CompilerParams(vmem_limit_bytes=LIMIT),
    )(scalars, q, kv)


def attend_back_step(
    i, chip_x, q_ref, kv_ref, delta_ref, lse_ref, dout_ref, bias_ref, dq_ref, put_key, put_value
):
    bands = kv_ref.shape[0]
    rows = q_ref.shape[1] // 2
    s, lanes, first, second = head_slices(i, rows)
    q = q_ref[first, lanes]
    dout = dout_ref[first, lanes]
    delta = delta_ref[pl.ds(i % HEADS, 1), lanes]
    lse = lse_ref[pl.ds(i, 1), :]
    dq = 0.0
    for b in range(bands):
        other = jnp.where(chip_x == b // 2, 0, 1)
        k, v = (ref[:, lanes] for ref in kv_rows(kv_ref, b, i % HEADS))
        scores = add_bias(dg(k, q, 0, 0), bias_ref, s, other)
        dweight = dg(v, dout, 0, 0)
        weight = jnp.exp(scores - lse)
        dscores = (weight * (dweight - delta)).astype(BF)
        dq = dq + dg(k, dscores, 1, 0)
        put_key(b, dg(q, dscores, 1, 1).astype(BF))
        put_value(b, dg(dout, weight.astype(BF), 1, 1).astype(BF))
    dq_ref[first, lanes] = (dq * (1.0 / math.sqrt(HEAD_DIM))).astype(BF)


def attend_back_kernel(
    unroll, scalars_ref, q_ref, kv_ref, delta_ref, lse_ref, dout_ref, dq_ref, dkv_ref, bias_ref
):
    fill_bias(scalars_ref, bias_ref, q_ref.shape[1] // 2)

    @pl.loop(0, 2 * HEADS // unroll)
    def _(j):
        for k in range(unroll):
            i = j * unroll + k
            _, lanes, first, second = head_slices(i, q_ref.shape[1] // 2)

            def put_key(b, values):
                dkv_ref[b, first, lanes] = values

            def put_value(b, values):
                dkv_ref[b, second, lanes] = values

            attend_back_step(
                i, scalars_ref[2], q_ref, kv_ref, delta_ref, lse_ref, dout_ref, bias_ref, dq_ref,
                put_key, put_value,
            )


def attend_back(scalars, q, kv, delta, lse, dout):
    return pl.pallas_call(
        functools.partial(attend_back_kernel, 4),
        name="attend_back",
        out_shape=(shape(q.shape, BF), shape((kv.shape[0], 2 * q.shape[0], q.shape[1]), BF)),
        in_specs=[SM] + [VM] * 5,
        out_specs=(VM, VM),
        scratch_shapes=[pltpu.VMEM((8, q.shape[1] // 2), F)],
        compiler_params=pltpu.CompilerParams(vmem_limit_bytes=LIMIT),
    )(scalars, q, kv, delta, lse, dout)


def middle_kernel(
    x_ref,
    cot_ref,
    scalars_ref,
    att_ref,
    w_out_ref,
    w_up_ref,
    w_down_ref,
    cols_ref,
    bias_up_ref,
    out_ref,
    dmid_ref,
    datt_ref,
    delta_ref,
    g_out_ref,
    g_up_ref,
    g_down_ref,
    sums_ref,
    mid_ref,
    norm_ref,
    h_ref,
    dmlp_ref,
    mlp_ref,
    err_ref,
    attb_ref,
    dbranch_ref,
):
    width, tokens = x_ref.shape
    hidden = w_up_ref.shape[0]
    step = 256
    first_slot = lax.broadcasted_iota(jnp.int32, (1, tokens), 1) < tokens // 2
    valid = jnp.where(
        first_slot,
        jnp.where(scalars_ref[0] > 0, 1.0, 0.0),
        jnp.where(scalars_ref[1] > 0, 1.0, 0.0),
    )
    attb_ref[...] = att_ref[...].astype(BF)
    sums_ref[...] = jnp.zeros_like(sums_ref)

    @pl.loop(0, width // step)
    def _(j):
        rows = pl.ds(pl.multiple_of(j * step, step), step)
        mid_ref[rows, :] = (
            dg(w_out_ref[rows, :], attb_ref[...], 1, 0)
            + cols_ref[rows, BIAS_OUT]
            + x_ref[rows, :].astype(F)
        )

    normed, inverse = normalize(mid_ref[...])
    norm_ref[...] = normed
    h_ref[...] = (normed * cols_ref[:, GAIN_TWO] + cols_ref[:, SHIFT_TWO]).astype(BF)
    dmlp_ref[...] = (cot_ref[...].astype(F) * valid).astype(BF)
    mlp_ref[...] = jnp.zeros_like(mlp_ref)
    err_ref[...] = jnp.zeros_like(err_ref)

    @pl.loop(0, hidden // step)
    def _(j):
        rows = pl.ds(pl.multiple_of(j * step, step), step)
        pre = dg(w_up_ref[rows, :], h_ref[...], 1, 0) + bias_up_ref[rows, :]
        phi = 0.5 + 0.5 * lax.erf(pre * math.sqrt(0.5))
        act = (pre * phi).astype(BF)
        slope = phi + pre * jnp.exp(pre * pre * -0.5) * (1.0 / math.sqrt(2.0 * math.pi))
        mlp_ref[...] += dg(w_down_ref[:, rows], act, 1, 0)
        dact = dg(w_down_ref[:, rows], dmlp_ref[...], 0, 0)
        dhid = (slope * dact).astype(BF)
        g_down_ref[:, rows] = dg(dmlp_ref[...], act, 1, 1).astype(BF)
        g_up_ref[rows, :] = dg(dhid, h_ref[...], 1, 1).astype(BF)
        per = width // step
        lanes = pl.ds(pl.multiple_of(j % per * step, step), step)
        sums_ref[pl.ds(UP_ROW + j // per, 1), lanes] = row_sums(dhid)[:1]
        err_ref[...] += dg(w_up_ref[rows, :], dhid, 0, 0)

    out_ref[...] = ((mid_ref[...] + mlp_ref[...] + cols_ref[:, BIAS_DOWN]) * valid).astype(BF)
    err = err_ref[...]
    sums_ref[3:4] = row_sums(dmlp_ref[...])[:1]
    sums_ref[6:7] = row_sums(err * norm_ref[...])[:1]
    sums_ref[7:8] = row_sums(err)[:1]
    dmid = cot_ref[...].astype(F) * valid + norm_back(
        err, norm_ref[...], inverse, cols_ref[:, GAIN_TWO]
    )
    dmid_ref[...] = dmid
    dbranch_ref[...] = dmid.astype(BF)
    sums_ref[2:3] = row_sums(dbranch_ref[...])[:1]
    datt_ref[...] = dg(w_out_ref[...], dbranch_ref[...], 0, 0).astype(BF)
    inner = att_ref[...] * datt_ref[...].astype(F)
    delta_ref[...] = jnp.sum(inner.reshape(HEADS, width // HEADS, tokens), axis=1)

    @pl.loop(0, width // step)
    def _(j):
        rows = pl.ds(pl.multiple_of(j * step, step), step)
        g_out_ref[rows, :] = dg(dbranch_ref[rows, :], attb_ref[...], 1, 1).astype(BF)


def middle(x, cot, scalars, att, w_out, w_up, w_down, cols, bias_up):
    width, tokens = x.shape
    hidden = w_up.shape[0]
    full = (width, tokens)
    return pl.pallas_call(
        middle_kernel,
        name="middle",
        out_shape=(
            shape(full, BF),
            shape(full, F),
            shape(full, BF),
            shape((HEADS, tokens), F),
            shape(w_out.shape, BF),
            shape(w_up.shape, BF),
            shape(w_down.shape, BF),
            shape((SUM_ROWS, width), F),
        ),
        in_specs=[VM, VM, SM] + [VM] * 6,
        out_specs=tuple([VM] * 8),
        scratch_shapes=[
            pltpu.VMEM(full, F),
            pltpu.VMEM(full, F),
            pltpu.VMEM(full, BF),
            pltpu.VMEM(full, BF),
            pltpu.VMEM(full, F),
            pltpu.VMEM(full, F),
            pltpu.VMEM(full, BF),
            pltpu.VMEM(full, BF),
        ],
        compiler_params=pltpu.CompilerParams(vmem_limit_bytes=LIMIT),
    )(x, cot, scalars, att, w_out, w_up, w_down, cols, bias_up)


def finish_kernel(
    x_ref, h_ref, dq_ref, dkv_ref, w_ref, cols_ref, dmid_ref, gx_ref, g_ref, sums_ref, err_ref
):
    width, tokens = x_ref.shape
    step = 256
    blocks = width // step
    err_ref[...] = jnp.zeros_like(err_ref)
    for ref, count, base in ((dq_ref, blocks, 0), (dkv_ref, 2 * blocks, blocks)):

        @pl.loop(0, count)
        def _(j):
            rows = pl.ds(pl.multiple_of(j * step, step), step)
            to = pl.ds(pl.multiple_of((j + base) * step, step), step)
            g_ref[to, :] = dg(ref[rows, :], h_ref[...], 1, 1).astype(BF)
            err_ref[...] += dg(w_ref[to, :], ref[rows, :], 0, 0)

    normed, inverse = normalize(x_ref[...].astype(F))
    err = err_ref[...]
    sums_ref[...] = jnp.zeros_like(sums_ref)
    sums_ref[0:1] = row_sums(dq_ref[...])[:1]
    sums_ref[1:2] = row_sums(dkv_ref[pl.ds(width, width), :])[:1]
    sums_ref[4:5] = row_sums(err * normed)[:1]
    sums_ref[5:6] = row_sums(err)[:1]
    gx_ref[...] = (dmid_ref[...] + norm_back(err, normed, inverse, cols_ref[:, GAIN_ONE])).astype(BF)


def finish(x, h, dq, dkv, w, cols, dmid):
    width, tokens = x.shape
    return pl.pallas_call(
        finish_kernel,
        name="finish",
        out_shape=(shape(x.shape, BF), shape(w.shape, BF), shape((SUM_ROWS, width), F)),
        in_specs=[VM] * 7,
        out_specs=(VM, VM, VM),
        scratch_shapes=[pltpu.VMEM(x.shape, F)],
        compiler_params=pltpu.CompilerParams(vmem_limit_bytes=LIMIT),
    )(x, h, dq, dkv, w, cols, dmid)


class Place:
    def __init__(self, images):
        self.images = images
        self.depth = images // 2
        self.img = lax.axis_index("img")
        self.band = lax.axis_index("band")
        self.z, self.y = self.img // 2, self.img % 2
        self.x, self.c = self.band // 2, self.band % 2
        self.partner = (self.img, self.band + 1 - 2 * self.c)
        self.across_x = (self.img, self.band + 2 - 4 * self.x)
        self.across_y = (self.img + 1 - 2 * self.y, self.band)
        self.z_peers = [self.along_z(k) for k in range(1, self.depth)]

    def along_z(self, k):
        z = lax.rem(self.z + k, self.depth)
        return (2 * z + self.y, self.band), z


def greet(peers):
    barrier = pltpu.get_barrier_semaphore()
    for peer in peers:
        pl.semaphore_signal(barrier, inc=1, device_id=peer, device_id_type=MESH)
    pl.semaphore_wait(barrier, len(peers))


def send(src, dst, send_sem, recv_sem, peer):
    copy = pltpu.make_async_remote_copy(
        src_ref=src,
        dst_ref=dst,
        send_sem=send_sem,
        recv_sem=recv_sem,
        device_id=peer,
        device_id_type=MESH,
    )
    copy.start()
    return copy


def comm_params(collective_id):
    return pltpu.CompilerParams(
        collective_id=collective_id, has_side_effects=True, vmem_limit_bytes=LIMIT
    )


def split_rows(shards, parts):
    return jnp.concatenate(
        [item.reshape(parts, item.shape[0] // parts, item.shape[1]) for item in shards], axis=1
    )


class Spread:
    def __init__(self, at, make, order, part, parts, source, ref, local_sem):
        depth, near, c = at.depth, at.depth // 2, at.c
        rows, half = ref.shape[2] // 2, ref.shape[3] // 2
        rows = pl.ds(pl.multiple_of(c * rows, 16), rows)
        size = half // parts
        lanes = pl.ds(pl.multiple_of(at.x * half + part * size, 128), size)
        both = [pl.ds(x * half + part * size, size) for x in range(2)]
        if parts == 1:
            both = [slice(None)]
        low, high = pl.ds(0, near), pl.ds(near, depth - near)

        def same(index, peer):
            if len(index) == 4:
                return [make(ref.at[index], ref.at[index], peer)]
            return [make(ref.at[index + (l,)], ref.at[index + (l,)], peer) for l in both]

        piece = ref.at[at.z, at.y, rows, lanes]
        source = source.at[:, pl.ds(part * size, size)]
        self.keep = pltpu.make_async_copy(source, piece, local_sem)
        z_first = [make(source, piece, peer) for peer, _ in at.z_peers]
        if order == "mixed":
            self.stages = [
                z_first,
                same((low, at.y, rows, lanes), at.across_x)
                + same((high, at.y, rows, lanes), at.across_y),
                same((low, at.y, rows), at.across_y)
                + same((high, slice(None), rows, lanes), at.across_x),
            ]
        elif order == "zxy":
            self.stages = [
                z_first,
                same((slice(None), at.y, rows, lanes), at.across_x),
                same((slice(None), at.y, rows), at.across_y),
            ]
        else:
            last = [same((at.z, slice(None), rows), peer) for peer, _ in at.z_peers]
            self.stages = [
                [make(source, piece, at.across_x)],
                same((at.z, at.y, rows), at.across_y),
                sum(last, []),
            ]
        self.stages.append(same((slice(None), slice(None), rows), at.partner))

    def start(self):
        self.keep.start()
        for copy in self.stages[0]:
            copy.start()

    def step(self, k):
        if k == 1:
            self.keep.wait()
        for copy in self.stages[k - 1]:
            copy.wait_recv()
        for copy in self.stages[k]:
            copy.start()

    def wait(self):
        for copy in self.stages[-1]:
            copy.wait_recv()

    def end(self):
        for stage in self.stages:
            for copy in stage:
                copy.wait_send()


def kv_rows(ref, b, h):
    part = ref.shape[2] // 2
    heads = part // HEAD_DIM
    first = pl.multiple_of(h % heads * HEAD_DIM, 16)
    second = pl.multiple_of(part + h % heads * HEAD_DIM, 16)
    at = ref.at[b, h // heads]
    return at.at[pl.ds(first, HEAD_DIM)], at.at[pl.ds(second, HEAD_DIM)]


def front_kernel(
    images, bands, scalars_ref, narrow_ref, wide_ref, small_ref, x_ref,
    qkv_w_ref, out_w_ref, up_w_ref, down_w_ref, h_ref, q_ref, kv_ref, att_ref, lse_ref,
    cols_ref, up_col_ref,
    theirs_ref, mine_ref, mine_wide_ref, smalls_ref, qv_col_ref, bias_ref, x_far_ref,
    local_sem, send_sem, recv_sem,
):
    at = Place(images)
    width, tokens = x_ref.shape
    rows = tokens // 2
    unit = width // images
    groups = kv_ref.shape[1]
    part = width // groups
    c = at.c
    used = [0, 0]

    def make(src, dst, peer):
        k = used[0]
        used[0] += 1
        return pltpu.make_async_remote_copy(
            src_ref=src,
            dst_ref=dst,
            send_sem=send_sem.at[k],
            recv_sem=recv_sem.at[k],
            device_id=peer,
            device_id_type=MESH,
        )

    def local():
        used[1] += 1
        return local_sem.at[used[1] - 1]

    others = [(lax.rem(at.img + k, images), at.band) for k in range(1, images)]
    half = wide_ref.shape[0] // 2
    wide = wide_ref.shape[1]
    own_lanes = pl.ds(pl.multiple_of(c * wide, 128), wide)
    own_wide = pltpu.make_async_copy(
        wide_ref.at[pl.ds(pl.multiple_of(c * half, 8), half), :],
        mine_wide_ref.at[:, own_lanes],
        local(),
    )
    swap = make(narrow_ref.at[1 - c], theirs_ref, at.partner)
    swap_wide = make(
        wide_ref.at[pl.ds(pl.multiple_of((1 - c) * half, 8), half), :],
        mine_wide_ref.at[:, own_lanes],
        at.partner,
    )
    lines = pl.ds(pl.multiple_of(at.img * 16, 16), 16)
    keep_small = pltpu.make_async_copy(small_ref, smalls_ref.at[lines, :], local())
    small_copies = [make(small_ref, smalls_ref.at[lines, :], peer) for peer in others]
    sources, row = [], 0
    for ref in (qkv_w_ref, out_w_ref, up_w_ref):
        count = ref.shape[2] // 2
        sources.append(mine_ref.at[pl.ds(row, count), :])
        row += count
    sources.append(mine_wide_ref)

    def spread(ref, source, orders):
        parts = len(orders)
        return [
            Spread(at, make, orders[k], k, parts, source, ref, local()) for k in range(parts)
        ]

    s_qkv = spread(qkv_w_ref, sources[0], ("mixed",) * 3)
    (s_out,) = spread(out_w_ref, sources[1], ("mixed",))
    s_up = spread(up_w_ref, sources[2], ("mixed", "zxy", "zxy"))
    d_one, d_two = spread(down_w_ref, sources[3], ("xyz", "mixed"))
    x_lanes = [pl.ds(s * rows, rows) for s in range(2)]
    x_moves = [make(x_ref.at[:, l], x_far_ref.at[:, l], at.across_x) for l in x_lanes]
    far = at.across_x[1]
    kv_moves = [
        [
            [
                make(kv_ref.at[b, g, :, x_lanes[s]], kv_ref.at[b, g, :, x_lanes[s]], at.partner)
                for b in (at.band, far)
            ]
            for g in range(groups)
        ]
        for s in range(2)
    ]

    greet([at.partner, at.across_x] + others)
    swap.start()
    x_moves[0].start()
    own_wide.start()
    swap_wide.start()
    keep_small.start()
    for copy in small_copies:
        copy.start()
    fill_bias(scalars_ref, bias_ref, rows)
    swap.wait_recv()
    mine, theirs = narrow_ref[c], theirs_ref[...]
    lane_count = mine.shape[1]
    mine_ref[:, pl.ds(0, lane_count)] = jnp.where(c == 0, mine, theirs)
    mine_ref[:, pl.ds(lane_count, lane_count)] = jnp.where(c == 0, theirs, mine)
    for item in s_qkv:
        item.start()
    own_wide.wait()
    swap_wide.wait_recv()
    d_one.start()
    for item in s_up:
        item.start()
    d_two.start()
    s_out.start()

    keep_small.wait()
    for copy in small_copies:
        copy.wait_recv()
    turned = smalls_ref[...].T
    qv_units, up_units = 2, up_w_ref.shape[2] // unit
    singles = 16 - qv_units - up_units
    for j in range(images):
        block = turned[:unit, 16 * j : 16 * j + 16]
        cols_ref[pl.ds(unit * j, unit), :] = block[:, :singles]
        for u in range(qv_units):
            lane = singles + u
            qv_col_ref[pl.ds(unit * (qv_units * j + u), unit), :] = block[:, lane : lane + 1]
        for u in range(up_units):
            lane = singles + qv_units + u
            up_col_ref[pl.ds(unit * (up_units * j + u), unit), :] = block[:, lane : lane + 1]

    def first_norm(s, ref, side):
        normed, _ = normalize(ref[:, x_lanes[s]].astype(F))
        to = pl.ds(side * tokens + s * rows, rows)
        h_ref[:, to] = (normed * cols_ref[:, GAIN_ONE] + cols_ref[:, SHIFT_ONE]).astype(BF)

    s_qkv[0].step(1)
    s_qkv[1].step(1)
    d_one.step(1)
    s_qkv[0].step(2)
    s_qkv[2].step(1)
    for s in range(2):
        first_norm(s, x_ref, 0)
    s_qkv[1].step(2)
    d_one.step(2)
    s_qkv[0].step(3)
    s_qkv[2].step(2)
    x_moves[1].start()
    x_moves[0].wait_recv()
    first_norm(0, x_far_ref, 1)
    s_qkv[1].step(3)
    s_qkv[2].step(3)
    s_up[0].step(1)
    s_up[1].step(1)
    for item in s_qkv:
        item.wait()

    weights = qkv_w_ref.reshape(3 * width, width)
    scale = 1.0 / math.sqrt(HEAD_DIM)

    def project(s):
        for g in range(groups):
            for k in range(2):
                row = (1 + k) * width + g * part
                to = pl.ds(k * part, part)
                for side, band in enumerate((at.band, far)):
                    lanes = pl.ds(side * tokens + s * rows, rows)
                    out = dg(weights[pl.ds(row, part), :], h_ref[:, lanes], 1, 0)
                    if k == 1:
                        out = out + qv_col_ref[pl.ds(width + g * part, part), :]
                    kv_ref[band, g, to, x_lanes[s]] = out.astype(BF)
            for copy in kv_moves[s][g]:
                copy.start()
        for g in range(groups):
            block = pl.ds(g * part, part)
            out = dg(weights[block, :], h_ref[:, x_lanes[s]], 1, 0) + qv_col_ref[block, :]
            q_ref[block, x_lanes[s]] = (out * scale).astype(BF)

    def second_slot():
        x_moves[1].wait_recv()
        first_norm(1, x_far_ref, 1)
        project(1)

    def arrive(s, g):
        for copy in kv_moves[s][g]:
            copy.wait_recv()

    events = {}

    def when(j, *actions):
        events.setdefault(j, []).extend(actions)

    when(1, functools.partial(s_up[2].step, 1))
    when(2, second_slot)
    for j in range(1, 2 * groups):
        when(j - 1, functools.partial(arrive, j // groups, j % groups))
    when(1, functools.partial(s_up[0].step, 2))
    when(2, functools.partial(d_two.step, 1), functools.partial(s_out.step, 1))
    when(4, functools.partial(s_up[1].step, 2))
    when(5, functools.partial(s_up[2].step, 2))
    when(6, functools.partial(s_up[0].step, 3), functools.partial(s_out.step, 2))
    when(7, functools.partial(d_two.step, 2), functools.partial(s_up[1].step, 3))
    project(0)
    arrive(0, 0)
    unroll = HEADS // groups

    @pl.loop(0, 2 * groups)
    def _(j):
        s, g = j // groups, j % groups
        for k in range(unroll):
            attend_step(
                s * HEADS + g * unroll + k, at.x, q_ref, kv_ref, bias_ref, att_ref, lse_ref
            )
        for when_j, actions in events.items():

            @pl.when(j == when_j)
            def _():
                for action in actions:
                    action()

    s_up[2].step(3)
    s_out.step(3)
    d_two.step(3)
    d_one.step(3)
    for item in s_up + [s_out, d_one, d_two]:
        item.wait()
    for item in s_qkv + s_up + [s_out, d_one, d_two]:
        item.end()
    for copy in [swap, swap_wide] + small_copies + x_moves:
        copy.wait_send()
    for copy in sum(sum(kv_moves, []), []):
        copy.wait_send()


def front(images, bands, scalars, narrow, wide, small, x, widths):
    depth = images // 2
    width, tokens = x.shape
    groups = GROUPS_OF_HEADS
    hidden = images * widths[2]
    return pl.pallas_call(
        functools.partial(front_kernel, images, bands),
        name="front",
        out_shape=tuple(shape((depth, 2, w, width), BF) for w in widths)
        + (
            shape((depth, 2, wide.shape[0], 4 * wide.shape[1]), BF),
            shape((width, 2 * tokens), BF),
            shape((width, tokens), BF),
            shape((bands, groups, 2 * width // groups, tokens), BF),
            shape((width, tokens), F),
            shape((2 * HEADS, tokens // 2), F),
            shape((width, COLUMNS), F),
            shape((hidden, 1), F),
        ),
        in_specs=[SM] + [VM] * 4,
        out_specs=(VM, ANY, ANY, ANY) + (VM,) * 7,
        scratch_shapes=[
            pltpu.VMEM(narrow.shape[1:], BF),
            pltpu.VMEM((narrow.shape[1], 2 * narrow.shape[2]), BF),
            pltpu.VMEM((wide.shape[0] // 2, 2 * wide.shape[1]), BF),
            pltpu.VMEM((16 * images, 128), F),
            pltpu.VMEM((2 * width, 1), F),
            pltpu.VMEM((8, tokens // 2), F),
            pltpu.VMEM((width, tokens), BF),
            pltpu.SemaphoreType.DMA((16,)),
            pltpu.SemaphoreType.DMA((FRONT_COPIES,)),
            pltpu.SemaphoreType.DMA((FRONT_COPIES,)),
        ],
        compiler_params=comm_params(0),
    )(scalars, narrow, wide, small, x)


def share_kernel(images, kv_ref, all_ref, local_sem, send_sem, recv_sem):
    at = Place(images)
    greet([at.partner, at.across_x])
    rows = kv_ref.shape[1] // 2
    mine = pltpu.make_async_copy(kv_ref, all_ref.at[at.band], local_sem)
    mine.start()
    copies = []
    for s in range(2):
        lanes = pl.ds(s * rows, rows)
        copies.append(
            send(
                kv_ref.at[:, lanes],
                all_ref.at[at.band, :, lanes],
                send_sem.at[s],
                recv_sem.at[s],
                at.across_x,
            )
        )
    near = send(kv_ref, all_ref.at[at.band], send_sem.at[2], recv_sem.at[2], at.partner)
    passed = []
    for s in range(2):
        copies[s].wait_recv()
        part = all_ref.at[at.across_x[1], :, pl.ds(s * rows, rows)]
        passed.append(send(part, part, send_sem.at[3 + s], recv_sem.at[3 + s], at.partner))
    for copy in passed + [near]:
        copy.wait()
    for copy in copies:
        copy.wait_send()
    mine.wait()


def share(images, bands, kv):
    return pl.pallas_call(
        functools.partial(share_kernel, images),
        name="share",
        out_shape=shape((bands,) + kv.shape, BF),
        in_specs=[VM],
        out_specs=ANY,
        scratch_shapes=[
            pltpu.SemaphoreType.DMA,
            pltpu.SemaphoreType.DMA((5,)),
            pltpu.SemaphoreType.DMA((5,)),
        ],
        compiler_params=comm_params(1),
    )(kv)


def add_rows(total_ref, other_ref, step):
    @pl.loop(0, total_ref.shape[0] // step)
    def _(j):
        rows = pl.ds(pl.multiple_of(j * step, step), step)
        total_ref[rows, :] = (
            total_ref[rows, :].astype(F) + other_ref[rows, :].astype(F)
        ).astype(total_ref.dtype)


def unshare_kernel(images, dkv_ref, sum_ref, near_ref, far_ref, send_sem, recv_sem):
    at = Place(images)
    greet([at.partner, at.across_x])
    mate, far = at.partner[1], at.across_x[1]
    far_mate = at.band + 2 - 4 * at.x + 1 - 2 * at.c
    one = send(dkv_ref.at[far_mate], near_ref.at[0], send_sem.at[0], recv_sem.at[0], at.partner)
    two = send(dkv_ref.at[mate], near_ref.at[1], send_sem.at[1], recv_sem.at[1], at.partner)
    one.wait_recv()
    add_rows(near_ref.at[0], dkv_ref.at[far], 64)
    three = send(near_ref.at[0], far_ref, send_sem.at[2], recv_sem.at[2], at.across_x)
    two.wait_recv()
    add_rows(near_ref.at[1], dkv_ref.at[at.band], 64)
    three.wait_recv()
    sum_ref[...] = near_ref[1]
    add_rows(sum_ref, far_ref, 64)
    for copy in (one, two, three):
        copy.wait_send()


def unshare(images, dkv):
    block = dkv.shape[1:]
    return pl.pallas_call(
        functools.partial(unshare_kernel, images),
        name="unshare",
        out_shape=shape(block, BF),
        in_specs=[VM],
        out_specs=VM,
        scratch_shapes=[
            pltpu.VMEM((2,) + block, BF),
            pltpu.VMEM(block, BF),
            pltpu.SemaphoreType.DMA((3,)),
            pltpu.SemaphoreType.DMA((3,)),
        ],
        compiler_params=comm_params(2),
    )(dkv)


def accumulate(total, other):
    total[...] = (total[...].astype(F) + other[...].astype(F)).astype(total.dtype)


class Reduction:
    def __init__(self, at, make, order, part, parts, ref, one, bufs, total):
        depth, near, c = at.depth, at.depth // 2, at.c
        rows, half = ref.shape[2] // 2, ref.shape[3] // 2
        size = half // parts
        self.at, self.near, self.ref, self.one, self.order = at, near, ref, one, order
        self.rows = pl.ds(pl.multiple_of(c * rows, 16), rows)

        def lanes_of(x):
            return pl.ds(pl.multiple_of(x * half + part * size, 128), size)

        self.lanes, self.both = lanes_of(at.x), [lanes_of(x) for x in range(2)]
        self.total = total.at[:, pl.ds(part * size, size)]
        far = lanes_of(1 - at.x)
        upper = depth - near
        if order == "mixed":
            two_x, two_y, three, four = bufs
            self.two_x, self.two_y = two_x, two_y
            low, high = pl.ds(0, near), pl.ds(near, upper)
            self.first = [make(one.at[low, :, :, far], two_x, at.across_x)] + [
                make(one.at[high, 1 - at.y, :, self.both[x]], two_y.at[x], at.across_y)
                for x in range(2)
            ]
            self.second = [
                make(two_x.at[:, 1 - at.y], three.at[low], at.across_y),
                make(two_y.at[1 - at.x], three.at[high], at.across_x),
            ]
        else:
            two, three, four = bufs
            self.two = two
            self.first = [
                make(one.at[:, 1 - at.y, :, self.both[x]], two.at[x], at.across_y)
                for x in range(2)
            ]
            self.second = [make(two.at[1 - at.x], three, at.across_x)]
        self.three, self.four = three, four
        self.third = [
            make(three.at[z], four.at[k], peer) for k, (peer, z) in enumerate(at.z_peers)
        ]

    def step_one(self):
        for lanes in self.both:

            @pl.loop(0, 2 * self.at.depth)
            def _(j):
                accumulate(
                    self.one.at[j // 2, j % 2, :, lanes],
                    self.ref.at[j // 2, j % 2, self.rows, lanes],
                )

        for copy in self.first:
            copy.start()

    def step_two(self):
        at = self.at
        if self.order == "mixed":
            self.first[0].wait_recv()

            @pl.loop(0, 2 * self.near)
            def _(j):
                accumulate(
                    self.two_x.at[j // 2, j % 2], self.one.at[j // 2, j % 2, :, self.lanes]
                )

            self.second[0].start()
            for x in range(2):
                self.first[1 + x].wait_recv()

                @pl.loop(0, at.depth - self.near)
                def _(j):
                    accumulate(
                        self.two_y.at[x, j], self.one.at[self.near + j, at.y, :, self.both[x]]
                    )

            self.second[1].start()
        else:
            for x in range(2):
                self.first[x].wait_recv()

                @pl.loop(0, at.depth)
                def _(j):
                    accumulate(self.two.at[x, j], self.one.at[j, at.y, :, self.both[x]])

            self.second[0].start()

    def step_three(self):
        at = self.at
        for copy in self.second:
            copy.wait_recv()
        if self.order == "mixed":

            @pl.loop(0, self.near)
            def _(j):
                accumulate(self.three.at[j], self.two_x.at[j, at.y])

            @pl.loop(0, at.depth - self.near)
            def _(j):
                accumulate(self.three.at[self.near + j], self.two_y.at[at.x, j])

        else:

            @pl.loop(0, at.depth)
            def _(j):
                accumulate(self.three.at[j], self.two.at[at.x, j])

        for copy in self.third:
            copy.start()

    def step_four(self):
        for copy in self.third:
            copy.wait_recv()
        total = self.three[self.at.z].astype(F)
        for k in range(len(self.third)):
            total = total + self.four[k].astype(F)
        self.total[...] = total

    def end(self):
        for copy in self.first + self.second + self.third:
            copy.wait_send()


def reduction_buffers(order, depth, rows, size):
    near = depth // 2
    if order == "mixed":
        first = [(near, 2, rows, size), (2, depth - near, rows, size)]
    else:
        first = [(2, depth, rows, size)]
    return [pltpu.VMEM(s, BF) for s in first + [(depth, rows, size), (depth - 1, rows, size)]]


BACK_ORDERS = (("mixed",) * 2, ("mixed",) * 3, ("mixed",), ("yx",) * 3)


def back_kernel(
    images, bands, scalars_ref, q_ref, kv_ref, delta_ref, lse_ref, datt_ref, x_ref, h_ref, dmid_ref,
    w_ref, cols_ref, g_out_ref, g_up_ref, g_down_ref, sums_ref,
    gx_ref, p_qkv_ref, p_out_ref, p_up_ref, p_down_ref, total_ref,
    bias_ref, dq_ref, dwide_ref, dkv_ref, near_ref, g_qkv_ref, err_ref, err_far_ref, err_in_ref,
    small_ref, small_in_ref, small_z_ref, *rest,
):
    at = Place(images)
    depth = at.depth
    send_sem, recv_sem = rest[-2:]
    rest = list(rest[:-2])
    used = [0]

    def make(src, dst, peer):
        k = used[0]
        used[0] += 1
        return pltpu.make_async_remote_copy(
            src_ref=src,
            dst_ref=dst,
            send_sem=send_sem.at[k],
            recv_sem=recv_sem.at[k],
            device_id=peer,
            device_id_type=MESH,
        )

    width, tokens = x_ref.shape
    rows = tokens // 2
    unroll = 4
    groups = HEADS // unroll
    part = width // groups

    def four_d(ref):
        return ref.reshape(depth, 2, ref.shape[0] // images, ref.shape[1])

    sources = (four_d(g_down_ref), four_d(g_up_ref), four_d(g_out_ref), g_qkv_ref)
    targets = (p_down_ref, p_up_ref, p_out_ref, p_qkv_ref)
    swaps, moves, ends = [], [], []
    for m in range(4):
        one, total, away = rest[:3]
        rest = rest[3:]
        block = sources[m].shape[2] // 2
        far_rows = pl.ds(pl.multiple_of((1 - at.c) * block, 16), block)
        swaps.append(make(sources[m].at[:, :, far_rows, :], one, at.partner))
        orders = BACK_ORDERS[m]
        moves.append([])
        for k, order in enumerate(orders):
            size = 4 if order == "mixed" else 3
            moves[m].append(
                Reduction(
                    at, make, order, k, len(orders), sources[m], one, rest[:size], total
                )
            )
            rest = rest[size:]
        ends.append((total, away, targets[m], make(away, targets[m].at[at.c], at.partner)))
    down, up, out, qkv = moves

    def deliver(m):
        total_ref, away, target, copy = ends[m]
        total = total_ref[...]
        size = total.shape[1] // 2
        low, high = total[:, :size], total[:, size:]
        target[at.c] = jnp.where(at.c == 0, low, high)
        away[...] = jnp.where(at.c == 0, high, low)
        copy.start()

    mate, far = at.partner[1], at.across_x[1]
    far_mate = at.across_x[1] + 1 - 2 * at.c
    one = [make(dkv_ref.at[far_mate, g], near_ref.at[0, g], at.partner) for g in range(groups)]
    two = [make(dkv_ref.at[mate, g], near_ref.at[1, g], at.partner) for g in range(groups)]
    err_moves = [make(err_far_ref.at[s], err_in_ref.at[s], at.across_x) for s in range(2)]
    small_steps = [
        make(small_ref.at[k], small_in_ref.at[k], peer)
        for k, peer in enumerate((at.partner, at.across_x, at.across_y))
    ]
    small_last = [
        make(small_z_ref.at[at.z], small_z_ref.at[at.z], peer) for peer, _ in at.z_peers
    ]

    greet([at.partner, at.across_x, at.across_y] + [peer for peer, _ in at.z_peers])
    for m in range(3):
        swaps[m].start()
    fill_bias(scalars_ref, bias_ref, rows)

    sides = [pl.ds(side * tokens, tokens) for side in range(2)]

    def share_one(g):
        one[g].start()
        two[g].start()

    def share_two(g):
        for copy, side, band in ((one[g], 1, far), (two[g], 0, at.band)):
            copy.wait_recv()
            for half in range(2):
                block = pl.ds(half * part, part)
                to = pl.ds(half * width + g * part, part)
                value = (
                    near_ref[1 - side, g, block, :].astype(F)
                    + dkv_ref[band, g, block, :].astype(F)
                ).astype(BF)
                dwide_ref[to, sides[side]] = value

    events = {}

    def when(j, *actions):
        events.setdefault(j, []).extend(actions)

    when(0, swaps[0].wait_recv, down[0].step_one, down[1].step_one)
    when(1, swaps[1].wait_recv, up[0].step_one, up[1].step_one, lambda: share_one(0))
    when(2, up[2].step_one, down[0].step_two, lambda: share_two(0))
    when(3, swaps[2].wait_recv, out[0].step_one, down[1].step_two, lambda: share_one(1))
    when(4, up[0].step_two, down[0].step_three, lambda: share_two(1))
    when(5, up[1].step_two, down[1].step_three, lambda: share_one(2))
    when(6, up[2].step_two, up[0].step_three, lambda: share_two(2))
    when(7, lambda: share_one(3), out[0].step_two, up[1].step_three)

    @pl.loop(0, 2 * groups)
    def _(j):
        g, s = j // 2, j % 2
        lanes = pl.ds(pl.multiple_of(s * rows, rows), rows)
        for k in range(unroll):

            def put_key(b, values):
                dkv_ref[b, g, pl.ds(k * HEAD_DIM, HEAD_DIM), lanes] = values

            def put_value(b, values):
                dkv_ref[b, g, pl.ds(part + k * HEAD_DIM, HEAD_DIM), lanes] = values

            attend_back_step(
                s * HEADS + g * unroll + k,
                at.x, q_ref, kv_ref, delta_ref, lse_ref, datt_ref, bias_ref, dq_ref,
                put_key, put_value,
            )
        for when_j, actions in events.items():

            @pl.when(j == when_j)
            def _():
                for action in actions:
                    action()

    chunk = width // 2
    g_flat = g_qkv_ref.reshape(3 * width, width)

    @pl.loop(0, 2)
    def _(j):
        block = pl.ds(pl.multiple_of(j * chunk, 128), chunk)
        g_flat[block, :] = dg(dq_ref[block, :], h_ref[:, sides[0]], 1, 1).astype(BF)

    share_two(groups - 1)

    @pl.loop(0, 4)
    def _(j):
        block = pl.ds(pl.multiple_of(j * chunk, 128), chunk)
        to = pl.ds(pl.multiple_of((2 + j) * chunk, 128), chunk)
        g_flat[to, :] = dg(dwide_ref[block, :], h_ref[...], 1, 1).astype(BF)

    swaps[3].start()
    up[2].step_three()
    out[0].step_three()

    def back_through(side):
        err_ref[...] = jnp.zeros_like(err_ref)

        @pl.loop(0, 4)
        def _(j):
            block = pl.ds(pl.multiple_of(j * chunk, 128), chunk)
            source = pl.ds(pl.multiple_of((2 + j) * chunk, 128), chunk)
            err_ref[...] += dg(w_ref[source, :], dwide_ref[block, sides[side]], 0, 0)

    back_through(1)
    swaps[3].wait_recv()
    for item in qkv:
        item.step_one()
    for s in range(2):
        err_far_ref[s] = err_ref[:, pl.ds(s * rows, rows)].astype(BF)
        err_moves[s].start()
    back_through(0)

    @pl.loop(0, 2)
    def _(j):
        block = pl.ds(pl.multiple_of(j * chunk, 128), chunk)
        err_ref[...] += dg(w_ref[block, :], dq_ref[block, :], 0, 0)

    for item in down:
        item.step_four()
    deliver(0)
    qkv[0].step_two()
    up[0].step_four()
    up[1].step_four()
    qkv[1].step_two()
    up[2].step_four()
    deliver(1)
    qkv[0].step_three()
    qkv[2].step_two()
    out[0].step_four()
    deliver(2)
    qkv[1].step_three()
    small_ref[0] = sums_ref[...]
    small_ref[0, 0:1] = row_sums(dq_ref[...])[:1]
    small_ref[0, 1:2] = row_sums(dwide_ref[pl.ds(width, width), :])[:1]
    gain_row, shift_row = 0.0, 0.0
    for s in range(2):
        err_moves[s].wait_recv()
        lanes = slice(s * rows, (s + 1) * rows)
        err = err_ref[:, lanes] + err_in_ref[s].astype(F)
        normed, inverse = normalize(x_ref[:, lanes].astype(F))
        gain_row = gain_row + row_sums(err * normed)[:1]
        shift_row = shift_row + row_sums(err)[:1]
        gx_ref[:, lanes] = (
            dmid_ref[:, lanes] + norm_back(err, normed, inverse, cols_ref[:, GAIN_ONE])
        ).astype(BF)
    small_ref[0, 4:5] = gain_row
    small_ref[0, 5:6] = shift_row
    small_steps[0].start()
    qkv[2].step_three()
    small_steps[0].wait_recv()
    small_ref[1] = small_ref[0] + small_in_ref[0]
    small_steps[1].start()
    qkv[0].step_four()
    small_steps[1].wait_recv()
    small_ref[2] = small_ref[1] + small_in_ref[1]
    small_steps[2].start()
    qkv[1].step_four()
    small_steps[2].wait_recv()
    small_z_ref[at.z] = small_ref[2] + small_in_ref[2]
    for copy in small_last:
        copy.start()
    qkv[2].step_four()
    deliver(3)
    for copy in small_last:
        copy.wait_recv()
    total = small_z_ref[0]
    for k in range(1, depth):
        total = total + small_z_ref[k]
    total_ref[...] = total
    for m in range(4):
        ends[m][3].wait()
        swaps[m].wait_send()
        for item in moves[m]:
            item.end()
    for copy in one + two + err_moves + small_steps + small_last:
        copy.wait_send()


def back(images, bands, scalars, q, kv, delta, lse, datt, x, h, dmid, w, cols, grads, sums):
    depth = images // 2
    width, tokens = x.shape
    g_out, g_up, g_down = grads
    groups = HEADS // 4
    results, buffers = [], []
    for m, item in enumerate((g_down, g_up, g_out, w)):
        block, lanes = item.shape[0] // images // 2, item.shape[1]
        results.append(shape((2, block, lanes // 4), F))
        buffers += [
            pltpu.VMEM((depth, 2, block, lanes), BF),
            pltpu.VMEM((block, lanes // 2), F),
            pltpu.VMEM((block, lanes // 4), F),
        ]
        orders = BACK_ORDERS[m]
        for order in orders:
            buffers += reduction_buffers(order, depth, block, lanes // 2 // len(orders))
    small = (SUM_ROWS, width)
    return pl.pallas_call(
        functools.partial(back_kernel, images, bands),
        name="back",
        out_shape=(shape(x.shape, BF), results[3], results[2], results[1], results[0], shape(small, F)),
        in_specs=[SM] + [VM] * 14,
        out_specs=(VM,) * 6,
        scratch_shapes=[
            pltpu.VMEM((8, tokens // 2), F),
            pltpu.VMEM((width, tokens), BF),
            pltpu.VMEM((2 * width, 2 * tokens), BF),
            pltpu.VMEM((bands, groups, 2 * width // groups, tokens), BF),
            pltpu.VMEM((2, groups, 2 * width // groups, tokens), BF),
            pltpu.VMEM((depth, 2, w.shape[0] // images, width), BF),
            pltpu.VMEM((width, tokens), F),
            pltpu.VMEM((2, width, tokens // 2), BF),
            pltpu.VMEM((2, width, tokens // 2), BF),
            pltpu.VMEM((3,) + small, F),
            pltpu.VMEM((3,) + small, F),
            pltpu.VMEM((depth,) + small, F),
        ]
        + buffers
        + [pltpu.SemaphoreType.DMA((BACK_COPIES,)), pltpu.SemaphoreType.DMA((BACK_COPIES,))],
        compiler_params=comm_params(3),
    )(scalars, q, kv, delta, lse, datt, x, h, dmid, w, cols, g_out, g_up, g_down, sums)


def body(
    tokens,
    slot_kind,
    w_qkv,
    w_out,
    w_up,
    w_down,
    bias_qv,
    bias_out,
    bias_up,
    bias_down,
    gain_one,
    shift_one,
    gain_two,
    shift_two,
    cotangent,
):
    rows, slots, width = tokens.shape[1:]
    count = rows * slots
    images, bands = lax.axis_size("img"), lax.axis_size("band")
    band = lax.axis_index("band")
    smalls = (bias_qv, bias_out, bias_up, bias_down, gain_one, shift_one, gain_two, shift_two)
    sizes = [item.shape[0] for item in smalls]
    own = (w_qkv, w_out, w_up)
    widths = [item.shape[1] for item in own]
    direct = images % 4 == 0 and all(w % 32 == 0 for w in widths + [w_down.shape[1]])
    direct = direct and bias_qv.shape[0] == 2 * (width // images) <= 256
    direct = direct and bias_up.shape[0] == 4 * (width // images)

    def turn(values):
        return values[0].transpose(2, 1, 0).reshape(width, count)

    def turn_back(values):
        return values.reshape(width, slots, rows).transpose(2, 1, 0)[None]

    x, cot = turn(tokens), turn(cotangent)
    kinds = slot_kind[0].astype(jnp.int32)
    scalars = jnp.concatenate([kinds, (band // 2).astype(jnp.int32)[None]])
    single = (bias_out, bias_down, gain_one, shift_one, gain_two, shift_two)
    if direct:
        narrow = split_rows([item.T for item in own], 2)
        unit = width // images
        units = [jnp.stack(single), jnp.zeros((4, unit), BF)]
        units += [bias_qv.reshape(2, unit), bias_up.reshape(4, unit)]
        small = jnp.pad(jnp.concatenate(units), ((0, 0), (0, 128 - unit))).astype(F)
        *full, h, q, all_kv, att, lse, cols, c_up = front(
            images, bands, scalars, narrow, w_down.T, small, x, widths
        )
        full_qkv, full_out, full_up, full_down = (item.reshape(-1, item.shape[3]) for item in full)
    else:
        full_qkv, full_out, full_up, full_down = (
            lax.all_gather(lax.all_gather(item, "band", axis=0, tiled=True).T, "img", tiled=True)
            for item in (*own, w_down)
        )
        whole = [lax.all_gather(item, "img", tiled=True).astype(F) for item in single]
        cols = jnp.stack(whole + [whole[0]] * (COLUMNS - len(whole)), axis=1)
        c_qv = lax.all_gather(bias_qv, "img", tiled=True).astype(F)[:, None]
        c_up = lax.all_gather(bias_up, "img", tiled=True).astype(F)[:, None]
        bias = jnp.concatenate([c_qv[:width], jnp.zeros((width, 1), F), c_qv[width:]])
        h, qkv = project(x, full_qkv, cols, bias)
        q = qkv[:width]
        all_kv = share(images, bands, qkv[width:])
        all_kv = all_kv.reshape(bands, 2, GROUPS_OF_HEADS, -1, count).transpose(0, 2, 1, 3, 4)
        all_kv = all_kv.reshape(bands, GROUPS_OF_HEADS, -1, count)
        att, lse = attend(scalars, q, all_kv)
    out, dmid, datt, delta, g_out, g_up, g_down, sums = middle(
        x, cot, scalars, att, full_out, full_up, full_down, cols, c_up
    )
    if direct:
        gx, *pieces, total = back(
            images, bands, scalars, q, all_kv, delta, lse, datt, x, h, dmid,
            full_qkv, cols, (g_out, g_up, g_down), sums,
        )
        matrices = [item.reshape(-1, item.shape[2]).T for item in pieces]
    else:
        dq, dkv = attend_back(scalars, q, all_kv, delta, lse, datt)
        dkv = unshare(images, dkv)
        gx, g_qkv, sums_one = finish(x, h, dq, dkv, full_qkv, cols, dmid)
        matrices = [
            lax.psum_scatter(
                lax.psum_scatter(item, "img", scatter_dimension=0, tiled=True),
                "band",
                scatter_dimension=1,
                tiled=True,
            )
            .astype(F)
            .T
            for item in (g_qkv, g_out, g_up, g_down)
        ]
        total = lax.psum(sums + sums_one, ("img", "band"))
    own_small = lax.axis_index("img")
    flat = total.reshape(-1)
    starts = [0, 2, UP_ROW, 3, 4, 5, 6, 7]
    small = [
        lax.dynamic_slice(flat, (start * width + own_small * size,), (size,))
        for start, size in zip(starts, sizes)
    ]
    return (turn_back(out), turn_back(gx), *matrices, *small)


def solution(mesh):
    data, weight, vector = P("img", "band", None, None), P("band", "img"), P("img")
    return jax.shard_map(
        body,
        mesh=mesh,
        in_specs=(data, P("img", None)) + (weight,) * 4 + (vector,) * 8 + (data,),
        out_specs=(data, data) + (weight,) * 4 + (vector,) * 8,
        check_vma=False,
    )
```

```python
import functools
import math

import jax
import jax.numpy as jnp
from jax import lax
from jax.experimental import pallas as pl
from jax.experimental.pallas import tpu as pltpu
from jax.sharding import PartitionSpec as P

HEADS = 16
HEAD_DIM = 48
EPSILON = 1e-06
MASKED = -1e30
BF = jnp.bfloat16
F = jnp.float32
MESH = pl.DeviceIdType.MESH
VM = pl.BlockSpec(memory_space=pltpu.VMEM)
SM = pl.BlockSpec(memory_space=pltpu.SMEM)
ANY = pl.BlockSpec(memory_space=pl.ANY)
LIMIT = 67043328
SUM_ROWS, UP_ROW = 16, 8
COLUMNS = 10
BIAS_OUT, BIAS_DOWN, GAIN_ONE, SHIFT_ONE, GAIN_TWO, SHIFT_TWO = (slice(k, k + 1) for k in range(6))
GROUPS_OF_HEADS = 4
FRONT_COPIES, BACK_COPIES = 128, 128


def dg(left, right, left_dim, right_dim):
    return lax.dot_general(
        left, right, (((left_dim,), (right_dim,)), ((), ())), preferred_element_type=F
    )


def shape(dims, dtype):
    return jax.ShapeDtypeStruct(tuple(dims), dtype)


def row_sums(values):
    ones = jnp.ones((8, values.shape[1]), BF)
    if values.dtype == BF:
        return dg(ones, values, 1, 1)
    high = values.astype(BF)
    low = (values - high.astype(F)).astype(BF)
    return dg(ones, high, 1, 1) + dg(ones, low, 1, 1)


def normalize(values):
    average = jnp.mean(values, axis=0, keepdims=True)
    centered = values - average
    variance = jnp.mean(centered * centered, axis=0, keepdims=True)
    inverse = lax.rsqrt(variance + EPSILON)
    return centered * inverse, inverse


def norm_back(error, normed, inverse, gain):
    f = gain * error
    mean_f = jnp.mean(f, axis=0, keepdims=True)
    mean_fn = jnp.mean(f * normed, axis=0, keepdims=True)
    return (f - mean_f - normed * mean_fn) * inverse


def project_kernel(x_ref, w_ref, cols_ref, bias_ref, h_ref, qkv_ref):
    width = x_ref.shape[0]
    normed, _ = normalize(x_ref[...].astype(F))
    h_ref[...] = (normed * cols_ref[:, GAIN_ONE] + cols_ref[:, SHIFT_ONE]).astype(BF)
    scale = 1.0 / math.sqrt(HEAD_DIM)
    step = 256

    @pl.loop(0, 3 * width // step)
    def _(j):
        rows = pl.ds(pl.multiple_of(j * step, step), step)
        out = dg(w_ref[rows, :], h_ref[...], 1, 0) + bias_ref[rows, :]
        qkv_ref[rows, :] = (out * jnp.where(j < width // step, scale, 1.0)).astype(BF)


def project(x, w, cols, bias):
    width, tokens = x.shape
    return pl.pallas_call(
        project_kernel,
        name="project",
        out_shape=(shape((width, tokens), BF), shape((3 * width, tokens), BF)),
        in_specs=[VM] * 4,
        out_specs=(VM, VM),
        compiler_params=pltpu.CompilerParams(vmem_limit_bytes=LIMIT),
    )(x, w, cols, bias)


def fill_bias(scalars_ref, bias_ref, rows):
    lane_half = lax.broadcasted_iota(jnp.int32, (1, rows), 1) // (rows // 2)
    for s in range(2):
        small = scalars_ref[s] == 2
        for other in range(2):
            for half in range(2):
                keep = jnp.logical_and(other == 0, lane_half == half)
                masked = jnp.where(small, MASKED, 0.0)
                bias_ref[pl.ds(4 * s + 2 * other + half, 1), :] = jnp.where(
                    keep, jnp.zeros((1, rows), F), jnp.full((1, rows), masked, F)
                )


def add_bias(scores, bias_ref, s, other):
    rows = scores.shape[0]
    at = 4 * s + 2 * other
    return jnp.concatenate(
        [
            scores[: rows // 2] + bias_ref[pl.ds(at, 1), :],
            scores[rows // 2 :] + bias_ref[pl.ds(at + 1, 1), :],
        ],
        axis=0,
    )


def head_slices(i, rows):
    s, h = i // HEADS, i % HEADS
    lanes = pl.ds(pl.multiple_of(s * rows, rows), rows)
    first = pl.ds(pl.multiple_of(h * HEAD_DIM, 16), HEAD_DIM)
    second = pl.ds(pl.multiple_of(HEADS * HEAD_DIM + h * HEAD_DIM, 16), HEAD_DIM)
    return s, lanes, first, second


def attend_step(i, chip_x, q_ref, kv_ref, bias_ref, out_ref, lse_ref):
    bands = kv_ref.shape[0]
    rows = q_ref.shape[1] // 2
    s, lanes, first, second = head_slices(i, rows)
    q = q_ref[first, lanes]
    scores = []
    maximum = None
    for b in range(bands):
        other = jnp.where(chip_x == b // 2, 0, 1)
        keys, _ = kv_rows(kv_ref, b, i % HEADS)
        part = add_bias(dg(keys[:, lanes], q, 0, 0), bias_ref, s, other)
        scores.append(part)
        top = jnp.max(part, axis=0, keepdims=True)
        maximum = top if maximum is None else jnp.maximum(maximum, top)
    total, acc = 0.0, 0.0
    for b in range(bands):
        weight = jnp.exp(scores[b] - maximum)
        total = total + jnp.sum(weight, axis=0, keepdims=True)
        _, values = kv_rows(kv_ref, b, i % HEADS)
        acc = acc + dg(values[:, lanes], weight.astype(BF), 1, 0)
    out_ref[first, lanes] = acc / total
    lse_ref[pl.ds(i, 1), :] = maximum + jnp.log(total)


def attend_kernel(unroll, scalars_ref, q_ref, kv_ref, out_ref, lse_ref, bias_ref):
    fill_bias(scalars_ref, bias_ref, q_ref.shape[1] // 2)

    @pl.loop(0, 2 * HEADS // unroll)
    def _(j):
        for k in range(unroll):
            attend_step(
                j * unroll + k, scalars_ref[2], q_ref, kv_ref, bias_ref, out_ref, lse_ref
            )


def attend(scalars, q, kv):
    width, tokens = q.shape
    return pl.pallas_call(
        functools.partial(attend_kernel, 4),
        name="attend",
        out_shape=(shape((width, tokens), F), shape((2 * HEADS, tokens // 2), F)),
        in_specs=[SM, VM, VM],
        out_specs=(VM, VM),
        scratch_shapes=[pltpu.VMEM((8, tokens // 2), F)],
        compiler_params=pltpu.CompilerParams(vmem_limit_bytes=LIMIT),
    )(scalars, q, kv)


def attend_back_step(
    i, chip_x, q_ref, kv_ref, delta_ref, lse_ref, dout_ref, bias_ref, dq_ref, put_key, put_value
):
    bands = kv_ref.shape[0]
    rows = q_ref.shape[1] // 2
    s, lanes, first, second = head_slices(i, rows)
    q = q_ref[first, lanes]
    dout = dout_ref[first, lanes]
    delta = delta_ref[pl.ds(i % HEADS, 1), lanes]
    lse = lse_ref[pl.ds(i, 1), :]
    dq = 0.0
    for b in range(bands):
        other = jnp.where(chip_x == b // 2, 0, 1)
        k, v = (ref[:, lanes] for ref in kv_rows(kv_ref, b, i % HEADS))
        scores = add_bias(dg(k, q, 0, 0), bias_ref, s, other)
        dweight = dg(v, dout, 0, 0)
        weight = jnp.exp(scores - lse)
        dscores = (weight * (dweight - delta)).astype(BF)
        dq = dq + dg(k, dscores, 1, 0)
        put_key(b, dg(q, dscores, 1, 1).astype(BF))
        put_value(b, dg(dout, weight.astype(BF), 1, 1).astype(BF))
    dq_ref[first, lanes] = (dq * (1.0 / math.sqrt(HEAD_DIM))).astype(BF)


def attend_back_kernel(
    unroll, scalars_ref, q_ref, kv_ref, delta_ref, lse_ref, dout_ref, dq_ref, dkv_ref, bias_ref
):
    fill_bias(scalars_ref, bias_ref, q_ref.shape[1] // 2)

    @pl.loop(0, 2 * HEADS // unroll)
    def _(j):
        for k in range(unroll):
            i = j * unroll + k
            _, lanes, first, second = head_slices(i, q_ref.shape[1] // 2)

            def put_key(b, values):
                dkv_ref[b, first, lanes] = values

            def put_value(b, values):
                dkv_ref[b, second, lanes] = values

            attend_back_step(
                i, scalars_ref[2], q_ref, kv_ref, delta_ref, lse_ref, dout_ref, bias_ref, dq_ref,
                put_key, put_value,
            )


def attend_back(scalars, q, kv, delta, lse, dout):
    return pl.pallas_call(
        functools.partial(attend_back_kernel, 4),
        name="attend_back",
        out_shape=(shape(q.shape, BF), shape((kv.shape[0], 2 * q.shape[0], q.shape[1]), BF)),
        in_specs=[SM] + [VM] * 5,
        out_specs=(VM, VM),
        scratch_shapes=[pltpu.VMEM((8, q.shape[1] // 2), F)],
        compiler_params=pltpu.CompilerParams(vmem_limit_bytes=LIMIT),
    )(scalars, q, kv, delta, lse, dout)


def middle_kernel(
    x_ref, cot_ref, scalars_ref, att_ref, w_out_in, w_up_in, w_down_in, cols_ref, bias_up_ref,
    out_ref, dmid_ref, datt_ref, delta_ref, g_out_ref, g_up_out, g_down_out, sums_ref,
    w_out_ref, w_up_ref, w_down_ref, g_up_ref, g_down_ref,
    mid_ref, norm_ref, h_ref, dmlp_ref, mlp_ref, err_ref, attb_ref, dbranch_ref,
    in_sem, up_sem, down_sem,
):
    width, tokens = x_ref.shape
    hidden = w_up_ref.shape[0]
    step = 256
    loads = [
        pltpu.make_async_copy(source, target, in_sem.at[k])
        for k, (source, target) in enumerate(
            ((w_out_in, w_out_ref), (w_up_in, w_up_ref), (w_down_in, w_down_ref))
        )
    ]
    for copy in loads:
        copy.start()
    first_slot = lax.broadcasted_iota(jnp.int32, (1, tokens), 1) < tokens // 2
    valid = jnp.where(
        first_slot,
        jnp.where(scalars_ref[0] > 0, 1.0, 0.0),
        jnp.where(scalars_ref[1] > 0, 1.0, 0.0),
    )
    attb_ref[...] = att_ref[...].astype(BF)
    dmlp_ref[...] = (cot_ref[...].astype(F) * valid).astype(BF)
    sums_ref[...] = jnp.zeros_like(sums_ref)
    mlp_ref[...] = jnp.zeros_like(mlp_ref)
    err_ref[...] = jnp.zeros_like(err_ref)
    loads[0].wait()

    @pl.loop(0, width // step)
    def _(j):
        rows = pl.ds(pl.multiple_of(j * step, step), step)
        mid_ref[rows, :] = (
            dg(w_out_ref[rows, :], attb_ref[...], 1, 0)
            + cols_ref[rows, BIAS_OUT]
            + x_ref[rows, :].astype(F)
        )

    normed, inverse = normalize(mid_ref[...])
    norm_ref[...] = normed
    h_ref[...] = (normed * cols_ref[:, GAIN_TWO] + cols_ref[:, SHIFT_TWO]).astype(BF)
    loads[1].wait()
    loads[2].wait()

    def stores(j):
        rows = pl.ds(pl.multiple_of(j * step, step), step)
        return (
            pltpu.make_async_copy(g_up_ref.at[rows, :], g_up_out.at[rows, :], up_sem.at[j]),
            pltpu.make_async_copy(g_down_ref.at[:, rows], g_down_out.at[:, rows], down_sem.at[j]),
        )

    @pl.loop(0, hidden // step)
    def _(j):
        rows = pl.ds(pl.multiple_of(j * step, step), step)
        pre = dg(w_up_ref[rows, :], h_ref[...], 1, 0) + bias_up_ref[rows, :]
        phi = 0.5 + 0.5 * lax.erf(pre * math.sqrt(0.5))
        act = (pre * phi).astype(BF)
        slope = phi + pre * jnp.exp(pre * pre * -0.5) * (1.0 / math.sqrt(2.0 * math.pi))
        mlp_ref[...] += dg(w_down_ref[:, rows], act, 1, 0)
        dact = dg(w_down_ref[:, rows], dmlp_ref[...], 0, 0)
        dhid = (slope * dact).astype(BF)
        g_down_ref[:, rows] = dg(dmlp_ref[...], act, 1, 1).astype(BF)
        g_up_ref[rows, :] = dg(dhid, h_ref[...], 1, 1).astype(BF)
        per = width // step
        lanes = pl.ds(pl.multiple_of(j % per * step, step), step)
        sums_ref[pl.ds(UP_ROW + j // per, 1), lanes] = row_sums(dhid)[:1]
        err_ref[...] += dg(w_up_ref[rows, :], dhid, 0, 0)
        for copy in stores(j):
            copy.start()

    out_ref[...] = ((mid_ref[...] + mlp_ref[...] + cols_ref[:, BIAS_DOWN]) * valid).astype(BF)
    err = err_ref[...]
    sums_ref[3:4] = row_sums(dmlp_ref[...])[:1]
    sums_ref[6:7] = row_sums(err * norm_ref[...])[:1]
    sums_ref[7:8] = row_sums(err)[:1]
    dmid = cot_ref[...].astype(F) * valid + norm_back(
        err, norm_ref[...], inverse, cols_ref[:, GAIN_TWO]
    )
    dmid_ref[...] = dmid
    dbranch_ref[...] = dmid.astype(BF)
    sums_ref[2:3] = row_sums(dbranch_ref[...])[:1]
    datt_ref[...] = dg(w_out_ref[...], dbranch_ref[...], 0, 0).astype(BF)
    inner = att_ref[...] * datt_ref[...].astype(F)
    delta_ref[...] = jnp.sum(inner.reshape(HEADS, width // HEADS, tokens), axis=1)

    @pl.loop(0, width // step)
    def _(j):
        rows = pl.ds(pl.multiple_of(j * step, step), step)
        g_out_ref[rows, :] = dg(dbranch_ref[rows, :], attb_ref[...], 1, 1).astype(BF)

    @pl.loop(0, hidden // step)
    def _(j):
        for copy in stores(j):
            copy.wait()


def middle(x, cot, scalars, att, w_out, w_up, w_down, cols, bias_up):
    width, tokens = x.shape
    hidden = w_up.shape[0]
    full = (width, tokens)
    weights = [w_out.shape, w_up.shape, w_down.shape]
    return pl.pallas_call(
        middle_kernel,
        name="middle",
        out_shape=(
            shape(full, BF),
            shape(full, F),
            shape(full, BF),
            shape((HEADS, tokens), F),
            shape(w_out.shape, BF),
            shape(w_up.shape, BF),
            shape(w_down.shape, BF),
            shape((SUM_ROWS, width), F),
        ),
        in_specs=[VM, VM, SM, VM] + [ANY] * 3 + [VM] * 2,
        out_specs=(VM,) * 5 + (ANY, ANY, VM),
        scratch_shapes=[pltpu.VMEM(s, BF) for s in weights + weights[1:]]
        + [
            pltpu.VMEM(full, F),
            pltpu.VMEM(full, F),
            pltpu.VMEM(full, BF),
            pltpu.VMEM(full, BF),
            pltpu.VMEM(full, F),
            pltpu.VMEM(full, F),
            pltpu.VMEM(full, BF),
            pltpu.VMEM(full, BF),
            pltpu.SemaphoreType.DMA((3,)),
            pltpu.SemaphoreType.DMA((hidden // 256,)),
            pltpu.SemaphoreType.DMA((hidden // 256,)),
        ],
        compiler_params=pltpu.CompilerParams(vmem_limit_bytes=LIMIT),
    )(x, cot, scalars, att, w_out, w_up, w_down, cols, bias_up)


def finish_kernel(
    x_ref, h_ref, dq_ref, dkv_ref, w_ref, cols_ref, dmid_ref, gx_ref, g_ref, sums_ref, err_ref
):
    width, tokens = x_ref.shape
    step = 256
    blocks = width // step
    err_ref[...] = jnp.zeros_like(err_ref)
    for ref, count, base in ((dq_ref, blocks, 0), (dkv_ref, 2 * blocks, blocks)):

        @pl.loop(0, count)
        def _(j):
            rows = pl.ds(pl.multiple_of(j * step, step), step)
            to = pl.ds(pl.multiple_of((j + base) * step, step), step)
            g_ref[to, :] = dg(ref[rows, :], h_ref[...], 1, 1).astype(BF)
            err_ref[...] += dg(w_ref[to, :], ref[rows, :], 0, 0)

    normed, inverse = normalize(x_ref[...].astype(F))
    err = err_ref[...]
    sums_ref[...] = jnp.zeros_like(sums_ref)
    sums_ref[0:1] = row_sums(dq_ref[...])[:1]
    sums_ref[1:2] = row_sums(dkv_ref[pl.ds(width, width), :])[:1]
    sums_ref[4:5] = row_sums(err * normed)[:1]
    sums_ref[5:6] = row_sums(err)[:1]
    gx_ref[...] = (dmid_ref[...] + norm_back(err, normed, inverse, cols_ref[:, GAIN_ONE])).astype(BF)


def finish(x, h, dq, dkv, w, cols, dmid):
    width, tokens = x.shape
    return pl.pallas_call(
        finish_kernel,
        name="finish",
        out_shape=(shape(x.shape, BF), shape(w.shape, BF), shape((SUM_ROWS, width), F)),
        in_specs=[VM] * 7,
        out_specs=(VM, VM, VM),
        scratch_shapes=[pltpu.VMEM(x.shape, F)],
        compiler_params=pltpu.CompilerParams(vmem_limit_bytes=LIMIT),
    )(x, h, dq, dkv, w, cols, dmid)


class Place:
    def __init__(self, images):
        self.images = images
        self.depth = images // 2
        self.img = lax.axis_index("img")
        self.band = lax.axis_index("band")
        self.z, self.y = self.img // 2, self.img % 2
        self.x, self.c = self.band // 2, self.band % 2
        self.partner = (self.img, self.band + 1 - 2 * self.c)
        self.across_x = (self.img, self.band + 2 - 4 * self.x)
        self.across_y = (self.img + 1 - 2 * self.y, self.band)
        self.z_peers = [self.along_z(k) for k in range(1, self.depth)]

    def along_z(self, k):
        z = lax.rem(self.z + k, self.depth)
        return (2 * z + self.y, self.band), z


def greet(peers):
    barrier = pltpu.get_barrier_semaphore()
    for peer in peers:
        pl.semaphore_signal(barrier, inc=1, device_id=peer, device_id_type=MESH)
    pl.semaphore_wait(barrier, len(peers))


def send(src, dst, send_sem, recv_sem, peer):
    copy = pltpu.make_async_remote_copy(
        src_ref=src,
        dst_ref=dst,
        send_sem=send_sem,
        recv_sem=recv_sem,
        device_id=peer,
        device_id_type=MESH,
    )
    copy.start()
    return copy


def comm_params(collective_id):
    return pltpu.CompilerParams(
        collective_id=collective_id, has_side_effects=True, vmem_limit_bytes=LIMIT
    )


def split_rows(shards, parts):
    return jnp.concatenate(
        [item.reshape(parts, item.shape[0] // parts, item.shape[1]) for item in shards], axis=1
    )


class Spread:
    def __init__(self, at, make, order, part, parts, source, ref, local_sem):
        depth, near, c = at.depth, at.depth // 2, at.c
        rows, half = ref.shape[2] // 2, ref.shape[3] // 2
        rows = pl.ds(pl.multiple_of(c * rows, 16), rows)
        size = half // parts
        lanes = pl.ds(pl.multiple_of(at.x * half + part * size, 128), size)
        both = [pl.ds(x * half + part * size, size) for x in range(2)]
        if parts == 1:
            both = [slice(None)]
        low, high = pl.ds(0, near), pl.ds(near, depth - near)

        def same(index, peer):
            if len(index) == 4:
                return [make(ref.at[index], ref.at[index], peer)]
            return [make(ref.at[index + (l,)], ref.at[index + (l,)], peer) for l in both]

        piece = ref.at[at.z, at.y, rows, lanes]
        source = source.at[:, pl.ds(part * size, size)]
        self.keep = pltpu.make_async_copy(source, piece, local_sem)
        z_first = []
        if order != "xyz":
            z_first = [make(source, piece, peer) for peer, _ in at.z_peers]
        if order == "mixed":
            self.stages = [
                z_first,
                same((low, at.y, rows, lanes), at.across_x)
                + same((high, at.y, rows, lanes), at.across_y),
                same((low, at.y, rows), at.across_y)
                + same((high, slice(None), rows, lanes), at.across_x),
            ]
        elif order == "zxy":
            self.stages = [
                z_first,
                same((slice(None), at.y, rows, lanes), at.across_x),
                same((slice(None), at.y, rows), at.across_y),
            ]
        else:
            last = [same((at.z, slice(None), rows), peer) for peer, _ in at.z_peers]
            self.stages = [
                [make(source, piece, at.across_x)],
                same((at.z, at.y, rows), at.across_y),
                sum(last, []),
            ]
        self.stages.append(same((slice(None), slice(None), rows), at.partner))

    def start(self):
        self.keep.start()
        for copy in self.stages[0]:
            copy.start()

    def step(self, k):
        if k == 1:
            self.keep.wait()
        for copy in self.stages[k - 1]:
            copy.wait_recv()
        for copy in self.stages[k]:
            copy.start()

    def wait(self):
        for copy in self.stages[-1]:
            copy.wait_recv()

    def end(self):
        for stage in self.stages:
            for copy in stage:
                copy.wait_send()


def kv_rows(ref, b, h):
    part = ref.shape[2] // 2
    heads = part // HEAD_DIM
    first = pl.multiple_of(h % heads * HEAD_DIM, 16)
    second = pl.multiple_of(part + h % heads * HEAD_DIM, 16)
    at = ref.at[b, h // heads]
    return at.at[pl.ds(first, HEAD_DIM)], at.at[pl.ds(second, HEAD_DIM)]


def front_kernel(
    images, bands, scalars_ref, narrow_ref, wide_ref, small_ref, x_ref,
    qkv_w_out, out_w_ref, up_w_ref, down_w_ref, h_out, kv_out, x_far_out,
    q_ref, att_ref, lse_ref, cols_ref, up_col_ref,
    qkv_w_ref, h_ref, kv_ref,
    theirs_ref, mine_ref, mine_wide_ref, smalls_ref, qv_col_ref, bias_ref, x_far_ref,
    local_sem, send_sem, recv_sem,
):
    at = Place(images)
    width, tokens = x_ref.shape
    rows = tokens // 2
    unit = width // images
    groups = kv_ref.shape[1]
    part = width // groups
    c = at.c
    used = [0, 0]

    def make(src, dst, peer):
        k = used[0]
        used[0] += 1
        return pltpu.make_async_remote_copy(
            src_ref=src,
            dst_ref=dst,
            send_sem=send_sem.at[k],
            recv_sem=recv_sem.at[k],
            device_id=peer,
            device_id_type=MESH,
        )

    def local():
        used[1] += 1
        return local_sem.at[used[1] - 1]

    others = [(lax.rem(at.img + k, images), at.band) for k in range(1, images)]
    half = wide_ref.shape[0] // 2
    wide = wide_ref.shape[1]
    own_lanes = pl.ds(pl.multiple_of(c * wide, 128), wide)
    own_wide = pltpu.make_async_copy(
        wide_ref.at[pl.ds(pl.multiple_of(c * half, 8), half), :],
        mine_wide_ref.at[:, own_lanes],
        local(),
    )
    swap = make(narrow_ref.at[1 - c], theirs_ref, at.partner)
    swap_wide = make(
        wide_ref.at[pl.ds(pl.multiple_of((1 - c) * half, 8), half), :],
        mine_wide_ref.at[:, own_lanes],
        at.partner,
    )
    lines = pl.ds(pl.multiple_of(at.img * 16, 16), 16)
    keep_small = pltpu.make_async_copy(small_ref, smalls_ref.at[lines, :], local())
    small_copies = [make(small_ref, smalls_ref.at[lines, :], peer) for peer in others]
    sources, row = [], 0
    for ref in (qkv_w_ref, out_w_ref, up_w_ref):
        count = ref.shape[2] // 2
        sources.append(mine_ref.at[pl.ds(row, count), :])
        row += count
    sources.append(mine_wide_ref)

    def spread(ref, source, orders):
        parts = len(orders)
        return [
            Spread(at, make, orders[k], k, parts, source, ref, local()) for k in range(parts)
        ]

    s_qkv = spread(qkv_w_ref, sources[0], ("mixed",) * 3)
    (s_out,) = spread(out_w_ref, sources[1], ("mixed",))
    s_up = spread(up_w_ref, sources[2], ("mixed", "zxy", "zxy"))
    d_one, d_two = spread(down_w_ref, sources[3], ("xyz", "mixed"))
    save_w = pltpu.make_async_copy(qkv_w_ref, qkv_w_out, local())
    save_h = pltpu.make_async_copy(h_ref, h_out, local())
    save_x = pltpu.make_async_copy(x_far_ref, x_far_out, local())
    save_kv = [
        pltpu.make_async_copy(kv_ref.at[:, g], kv_out.at[:, g], local()) for g in range(groups)
    ]
    x_lanes = [pl.ds(s * rows, rows) for s in range(2)]
    x_moves = [make(x_ref.at[:, l], x_far_ref.at[:, l], at.across_x) for l in x_lanes]
    far = at.across_x[1]
    kv_moves = [
        [
            [
                make(kv_ref.at[b, g, :, x_lanes[s]], kv_ref.at[b, g, :, x_lanes[s]], at.partner)
                for b in (at.band, far)
            ]
            for g in range(groups)
        ]
        for s in range(2)
    ]

    greet([at.partner, at.across_x] + others)
    swap.start()
    x_moves[0].start()
    own_wide.start()
    swap_wide.start()
    keep_small.start()
    for copy in small_copies:
        copy.start()
    fill_bias(scalars_ref, bias_ref, rows)
    swap.wait_recv()
    mine, theirs = narrow_ref[c], theirs_ref[...]
    lane_count = mine.shape[1]
    mine_ref[:, pl.ds(0, lane_count)] = jnp.where(c == 0, mine, theirs)
    mine_ref[:, pl.ds(lane_count, lane_count)] = jnp.where(c == 0, theirs, mine)
    for item in s_qkv:
        item.start()
    own_wide.wait()
    swap_wide.wait_recv()
    d_one.start()
    for item in s_up:
        item.start()
    d_two.start()
    s_out.start()

    keep_small.wait()
    for copy in small_copies:
        copy.wait_recv()
    turned = smalls_ref[...].T
    qv_units, up_units = 2, up_w_ref.shape[2] // unit
    singles = 16 - qv_units - up_units
    for j in range(images):
        block = turned[:unit, 16 * j : 16 * j + 16]
        cols_ref[pl.ds(unit * j, unit), :] = block[:, :singles]
        for u in range(qv_units):
            lane = singles + u
            qv_col_ref[pl.ds(unit * (qv_units * j + u), unit), :] = block[:, lane : lane + 1]
        for u in range(up_units):
            lane = singles + qv_units + u
            up_col_ref[pl.ds(unit * (up_units * j + u), unit), :] = block[:, lane : lane + 1]

    def first_norm(s, ref, side):
        normed, _ = normalize(ref[:, x_lanes[s]].astype(F))
        to = pl.ds(side * tokens + s * rows, rows)
        h_ref[:, to] = (normed * cols_ref[:, GAIN_ONE] + cols_ref[:, SHIFT_ONE]).astype(BF)

    s_qkv[0].step(1)
    s_qkv[1].step(1)
    d_one.step(1)
    s_qkv[0].step(2)
    s_qkv[2].step(1)
    for s in range(2):
        first_norm(s, x_ref, 0)
    s_qkv[1].step(2)
    d_one.step(2)
    s_qkv[0].step(3)
    s_qkv[2].step(2)
    x_moves[1].start()
    x_moves[0].wait_recv()
    first_norm(0, x_far_ref, 1)
    s_qkv[1].step(3)
    s_qkv[2].step(3)
    s_up[0].step(1)
    s_up[1].step(1)
    for item in s_qkv:
        item.wait()
    save_w.start()

    weights = qkv_w_ref.reshape(3 * width, width)
    scale = 1.0 / math.sqrt(HEAD_DIM)

    def project(s):
        for g in range(groups):
            for k in range(2):
                row = (1 + k) * width + g * part
                to = pl.ds(k * part, part)
                for side, band in enumerate((at.band, far)):
                    lanes = pl.ds(side * tokens + s * rows, rows)
                    out = dg(weights[pl.ds(row, part), :], h_ref[:, lanes], 1, 0)
                    if k == 1:
                        out = out + qv_col_ref[pl.ds(width + g * part, part), :]
                    kv_ref[band, g, to, x_lanes[s]] = out.astype(BF)
            for copy in kv_moves[s][g]:
                copy.start()
        for g in range(groups):
            block = pl.ds(g * part, part)
            out = dg(weights[block, :], h_ref[:, x_lanes[s]], 1, 0) + qv_col_ref[block, :]
            q_ref[block, x_lanes[s]] = (out * scale).astype(BF)

    def second_slot():
        x_moves[1].wait_recv()
        first_norm(1, x_far_ref, 1)
        project(1)
        save_h.start()
        save_x.start()

    def arrive(s, g):
        for copy in kv_moves[s][g]:
            copy.wait_recv()
        if s == 1:
            save_kv[g].start()

    events = {}

    def when(j, *actions):
        events.setdefault(j, []).extend(actions)

    when(1, functools.partial(s_up[2].step, 1))
    when(2, second_slot)
    for j in range(1, 2 * groups):
        when(j - 1, functools.partial(arrive, j // groups, j % groups))
    when(1, functools.partial(s_up[0].step, 2))
    when(2, functools.partial(d_two.step, 1), functools.partial(s_out.step, 1))
    when(4, functools.partial(s_up[1].step, 2))
    when(5, functools.partial(s_up[2].step, 2))
    when(6, functools.partial(s_up[0].step, 3), functools.partial(s_out.step, 2))
    when(7, functools.partial(d_two.step, 2), functools.partial(s_up[1].step, 3))
    project(0)
    arrive(0, 0)
    unroll = HEADS // groups

    @pl.loop(0, 2 * groups)
    def _(j):
        s, g = j // groups, j % groups
        for k in range(unroll):
            attend_step(
                s * HEADS + g * unroll + k, at.x, q_ref, kv_ref, bias_ref, att_ref, lse_ref
            )
        for when_j, actions in events.items():

            @pl.when(j == when_j)
            def _():
                for action in actions:
                    action()

    s_up[2].step(3)
    s_out.step(3)
    d_two.step(3)
    d_one.step(3)
    for item in s_up + [s_out, d_one, d_two]:
        item.wait()
    for item in s_qkv + s_up + [s_out, d_one, d_two]:
        item.end()
    for copy in [save_w, save_h, save_x] + save_kv:
        copy.wait()
    for copy in [swap, swap_wide] + small_copies + x_moves:
        copy.wait_send()
    for copy in sum(sum(kv_moves, []), []):
        copy.wait_send()


def front(images, bands, scalars, narrow, wide, small, x, widths):
    depth = images // 2
    width, tokens = x.shape
    groups = GROUPS_OF_HEADS
    hidden = images * widths[2]
    return pl.pallas_call(
        functools.partial(front_kernel, images, bands),
        name="front",
        out_shape=tuple(shape((depth, 2, w, width), BF) for w in widths)
        + (
            shape((depth, 2, wide.shape[0], 4 * wide.shape[1]), BF),
            shape((width, 2 * tokens), BF),
            shape((bands, groups, 2 * width // groups, tokens), BF),
            shape((width, tokens), BF),
            shape((width, tokens), BF),
            shape((width, tokens), F),
            shape((2 * HEADS, tokens // 2), F),
            shape((width, COLUMNS), F),
            shape((hidden, 1), F),
        ),
        in_specs=[SM] + [VM] * 4,
        out_specs=(ANY,) * 7 + (VM,) * 5,
        scratch_shapes=[
            pltpu.VMEM((depth, 2, widths[0], width), BF),
            pltpu.VMEM((width, 2 * tokens), BF),
            pltpu.VMEM((bands, groups, 2 * width // groups, tokens), BF),
            pltpu.VMEM(narrow.shape[1:], BF),
            pltpu.VMEM((narrow.shape[1], 2 * narrow.shape[2]), BF),
            pltpu.VMEM((wide.shape[0] // 2, 2 * wide.shape[1]), BF),
            pltpu.VMEM((16 * images, 128), F),
            pltpu.VMEM((2 * width, 1), F),
            pltpu.VMEM((8, tokens // 2), F),
            pltpu.VMEM((width, tokens), BF),
            pltpu.SemaphoreType.DMA((24,)),
            pltpu.SemaphoreType.DMA((FRONT_COPIES,)),
            pltpu.SemaphoreType.DMA((FRONT_COPIES,)),
        ],
        compiler_params=comm_params(0),
    )(scalars, narrow, wide, small, x)


def share_kernel(images, kv_ref, all_ref, local_sem, send_sem, recv_sem):
    at = Place(images)
    greet([at.partner, at.across_x])
    rows = kv_ref.shape[1] // 2
    mine = pltpu.make_async_copy(kv_ref, all_ref.at[at.band], local_sem)
    mine.start()
    copies = []
    for s in range(2):
        lanes = pl.ds(s * rows, rows)
        copies.append(
            send(
                kv_ref.at[:, lanes],
                all_ref.at[at.band, :, lanes],
                send_sem.at[s],
                recv_sem.at[s],
                at.across_x,
            )
        )
    near = send(kv_ref, all_ref.at[at.band], send_sem.at[2], recv_sem.at[2], at.partner)
    passed = []
    for s in range(2):
        copies[s].wait_recv()
        part = all_ref.at[at.across_x[1], :, pl.ds(s * rows, rows)]
        passed.append(send(part, part, send_sem.at[3 + s], recv_sem.at[3 + s], at.partner))
    for copy in passed + [near]:
        copy.wait()
    for copy in copies:
        copy.wait_send()
    mine.wait()


def share(images, bands, kv):
    return pl.pallas_call(
        functools.partial(share_kernel, images),
        name="share",
        out_shape=shape((bands,) + kv.shape, BF),
        in_specs=[VM],
        out_specs=ANY,
        scratch_shapes=[
            pltpu.SemaphoreType.DMA,
            pltpu.SemaphoreType.DMA((5,)),
            pltpu.SemaphoreType.DMA((5,)),
        ],
        compiler_params=comm_params(1),
    )(kv)


def add_rows(total_ref, other_ref, step):
    @pl.loop(0, total_ref.shape[0] // step)
    def _(j):
        rows = pl.ds(pl.multiple_of(j * step, step), step)
        total_ref[rows, :] = (
            total_ref[rows, :].astype(F) + other_ref[rows, :].astype(F)
        ).astype(total_ref.dtype)


def unshare_kernel(images, dkv_ref, sum_ref, near_ref, far_ref, send_sem, recv_sem):
    at = Place(images)
    greet([at.partner, at.across_x])
    mate, far = at.partner[1], at.across_x[1]
    far_mate = at.band + 2 - 4 * at.x + 1 - 2 * at.c
    one = send(dkv_ref.at[far_mate], near_ref.at[0], send_sem.at[0], recv_sem.at[0], at.partner)
    two = send(dkv_ref.at[mate], near_ref.at[1], send_sem.at[1], recv_sem.at[1], at.partner)
    one.wait_recv()
    add_rows(near_ref.at[0], dkv_ref.at[far], 64)
    three = send(near_ref.at[0], far_ref, send_sem.at[2], recv_sem.at[2], at.across_x)
    two.wait_recv()
    add_rows(near_ref.at[1], dkv_ref.at[at.band], 64)
    three.wait_recv()
    sum_ref[...] = near_ref[1]
    add_rows(sum_ref, far_ref, 64)
    for copy in (one, two, three):
        copy.wait_send()


def unshare(images, dkv):
    block = dkv.shape[1:]
    return pl.pallas_call(
        functools.partial(unshare_kernel, images),
        name="unshare",
        out_shape=shape(block, BF),
        in_specs=[VM],
        out_specs=VM,
        scratch_shapes=[
            pltpu.VMEM((2,) + block, BF),
            pltpu.VMEM(block, BF),
            pltpu.SemaphoreType.DMA((3,)),
            pltpu.SemaphoreType.DMA((3,)),
        ],
        compiler_params=comm_params(2),
    )(dkv)


def accumulate(total, other):
    total[...] = total[...] + other[...]


class Reduction:
    def __init__(self, at, make, order, start, size, ref, one, other, bufs, total):
        depth, near = at.depth, at.depth // 2
        half = ref.shape[3] // 2
        self.at, self.near, self.one, self.other, self.order = at, near, one, other, order

        def lanes_of(x):
            return pl.ds(pl.multiple_of(x * half + start, 128), size)

        self.lanes, self.both = lanes_of(at.x), [lanes_of(x) for x in range(2)]
        self.total = total.at[:, pl.ds(start, size)]
        far = lanes_of(1 - at.x)
        upper = depth - near
        if order == "mixed":
            two_x, two_y, three, four = bufs
            self.two_x, self.two_y = two_x, two_y
            low, high = pl.ds(0, near), pl.ds(near, upper)
            self.first = [make(one.at[low, :, :, far], two_x, at.across_x)] + [
                make(one.at[high, 1 - at.y, :, self.both[x]], two_y.at[x], at.across_y)
                for x in range(2)
            ]
            self.second = [
                make(two_x.at[:, 1 - at.y], three.at[low], at.across_y),
                make(two_y.at[1 - at.x], three.at[high], at.across_x),
            ]
        else:
            two, three, four = bufs
            self.two = two
            self.first = [
                make(one.at[:, 1 - at.y, :, self.both[x]], two.at[x], at.across_y)
                for x in range(2)
            ]
            self.second = [make(two.at[1 - at.x], three, at.across_x)]
        self.three, self.four = three, four
        self.third = [
            make(three.at[z], four.at[k], peer) for k, (peer, z) in enumerate(at.z_peers)
        ]

    def step_one(self):
        for lanes in self.both:

            @pl.loop(0, 2 * self.at.depth)
            def _(j):
                accumulate(
                    self.one.at[j // 2, j % 2, :, lanes],
                    self.other.at[j // 2, j % 2, :, lanes],
                )

        for copy in self.first:
            copy.start()

    def step_two(self):
        at = self.at
        if self.order == "mixed":
            self.first[0].wait_recv()

            @pl.loop(0, 2 * self.near)
            def _(j):
                accumulate(
                    self.two_x.at[j // 2, j % 2], self.one.at[j // 2, j % 2, :, self.lanes]
                )

            self.second[0].start()
            for x in range(2):
                self.first[1 + x].wait_recv()

                @pl.loop(0, at.depth - self.near)
                def _(j):
                    accumulate(
                        self.two_y.at[x, j], self.one.at[self.near + j, at.y, :, self.both[x]]
                    )

            self.second[1].start()
        else:
            for x in range(2):
                self.first[x].wait_recv()

                @pl.loop(0, at.depth)
                def _(j):
                    accumulate(self.two.at[x, j], self.one.at[j, at.y, :, self.both[x]])

            self.second[0].start()

    def step_three(self):
        at = self.at
        for copy in self.second:
            copy.wait_recv()
        if self.order == "mixed":

            @pl.loop(0, self.near)
            def _(j):
                accumulate(self.three.at[j], self.two_x.at[j, at.y])

            @pl.loop(0, at.depth - self.near)
            def _(j):
                accumulate(self.three.at[self.near + j], self.two_y.at[at.x, j])

        else:

            @pl.loop(0, at.depth)
            def _(j):
                accumulate(self.three.at[j], self.two.at[at.x, j])

        for copy in self.third:
            copy.start()

    def step_four(self):
        for copy in self.third:
            copy.wait_recv()
        total = self.three[self.at.z].astype(F)
        for k in range(len(self.third)):
            total = total + self.four[k].astype(F)
        self.total[...] = total

    def end(self):
        for copy in self.first + self.second + self.third:
            copy.wait_send()


def reduction_buffers(order, depth, rows, size):
    near = depth // 2
    if order == "mixed":
        first = [(near, 2, rows, size), (2, depth - near, rows, size)]
    else:
        first = [(2, depth, rows, size)]
    return [pltpu.VMEM(s, BF) for s in first + [(depth, rows, size), (depth - 1, rows, size)]]


BACK_ORDERS = (
    (("mixed", 1), ("mixed", 1)),
    (("mixed", 1), ("mixed", 1), ("mixed", 1)),
    (("mixed", 1),),
    (("mixed", 2), ("yx", 1)),
)


def lane_parts(orders, half):
    unit = half // sum(share for _, share in orders)
    parts, start = [], 0
    for order, share in orders:
        parts.append((order, start, share * unit))
        start += share * unit
    return parts


def back_kernel(
    images, bands, scalars_ref, q_ref, delta_ref, lse_ref, datt_ref, cols_ref, sums_ref,
    kv_in, x_in, x_far_in, h_in, dmid_in, w_in, g_out_ref, g_up_ref, g_down_ref,
    gx_ref, p_qkv_ref, p_out_ref, p_up_ref, p_down_ref, total_ref,
    kv_ref, x_ref, x_far_ref, h_ref, dmid_ref, w_ref,
    bias_ref, dq_ref, dwide_ref, dkv_ref, near_ref, g_qkv_ref, err_ref, err_far_ref, err_in_ref,
    small_ref, small_in_ref, small_z_ref, *rest,
):
    at = Place(images)
    depth = at.depth
    local_sem, send_sem, recv_sem = rest[-3:]
    rest = list(rest[:-3])
    used = [0, 0]

    def make(src, dst, peer):
        k = used[0]
        used[0] += 1
        return pltpu.make_async_remote_copy(
            src_ref=src,
            dst_ref=dst,
            send_sem=send_sem.at[k],
            recv_sem=recv_sem.at[k],
            device_id=peer,
            device_id_type=MESH,
        )

    def load(src, dst):
        used[1] += 1
        return pltpu.make_async_copy(src, dst, local_sem.at[used[1] - 1])

    width, tokens = x_ref.shape
    rows = tokens // 2
    unroll = 4
    groups = HEADS // unroll
    part = width // groups

    def four_d(ref):
        return ref.reshape(depth, 2, ref.shape[0] // images, ref.shape[1])

    sources = (four_d(g_down_ref), four_d(g_up_ref), four_d(g_out_ref), g_qkv_ref)
    targets = (p_down_ref, p_up_ref, p_out_ref, p_qkv_ref)
    swaps, owns, moves, ends = [], [], [], []
    for m in range(4):
        one, total, away = rest[:3]
        rest = rest[3:]
        block, lanes = sources[m].shape[2] // 2, sources[m].shape[3]
        near_rows = pl.ds(pl.multiple_of(at.c * block, 16), block)
        far_rows = pl.ds(pl.multiple_of((1 - at.c) * block, 16), block)
        parts = lane_parts(BACK_ORDERS[m], lanes // 2)
        if m < 3:
            other = rest.pop(0)
            owns.append(load(sources[m].at[:, :, near_rows, :], one))
            swaps.append([make(sources[m].at[:, :, far_rows, :], other, at.partner)])
        else:
            other = sources[m].at[:, :, near_rows, :]
            for _, start, size in parts:
                both = [pl.ds(x * (lanes // 2) + start, size) for x in range(2)]
                swaps.append(
                    [
                        make(sources[m].at[:, :, far_rows, l], one.at[:, :, :, l], at.partner)
                        for l in both
                    ]
                )
        moves.append([])
        for order, start, size in parts:
            count = 4 if order == "mixed" else 3
            moves[m].append(
                Reduction(
                    at, make, order, start, size, sources[m], one, other, rest[:count], total
                )
            )
            rest = rest[count:]
        ends.append((total, away, targets[m], make(away, targets[m].at[at.c], at.partner)))
    down, up, out, qkv = moves

    def deliver(m):
        total_ref, away, target, copy = ends[m]
        total = total_ref[...]
        size = total.shape[1] // 2
        low, high = total[:, :size], total[:, size:]
        target[at.c] = jnp.where(at.c == 0, low, high)
        away[...] = jnp.where(at.c == 0, high, low)
        copy.start()

    mate, far = at.partner[1], at.across_x[1]
    far_mate = at.across_x[1] + 1 - 2 * at.c
    one = [make(dkv_ref.at[far_mate, g], near_ref.at[0, g], at.partner) for g in range(groups)]
    two = [make(dkv_ref.at[mate, g], near_ref.at[1, g], at.partner) for g in range(groups)]
    err_moves = [make(err_far_ref.at[s], err_in_ref.at[s], at.across_x) for s in range(2)]
    small_steps = [
        make(small_ref.at[k], small_in_ref.at[k], peer)
        for k, peer in enumerate((at.partner, at.across_x, at.across_y))
    ]
    small_last = [
        make(small_z_ref.at[at.z], small_z_ref.at[at.z], peer) for peer, _ in at.z_peers
    ]

    kv_loads = [load(kv_in.at[:, g], kv_ref.at[:, g]) for g in range(groups)]
    late_loads = [
        load(h_in, h_ref),
        load(w_in, w_ref),
        load(x_in, x_ref),
        load(x_far_in, x_far_ref),
        load(dmid_in, dmid_ref),
    ]
    kv_loads[0].start()
    owns[0].start()
    greet([at.partner, at.across_x, at.across_y] + [peer for peer, _ in at.z_peers])
    for m in range(3):
        swaps[m][0].start()
    for copy in owns[1:] + kv_loads[1:] + late_loads:
        copy.start()
    fill_bias(scalars_ref, bias_ref, rows)

    sides = [pl.ds(side * tokens, tokens) for side in range(2)]

    def share_one(g):
        one[g].start()
        two[g].start()

    def share_two(g):
        for copy, side, band in ((one[g], 1, far), (two[g], 0, at.band)):
            copy.wait_recv()
            for half in range(2):
                block = pl.ds(half * part, part)
                to = pl.ds(half * width + g * part, part)
                value = (
                    near_ref[1 - side, g, block, :].astype(F)
                    + dkv_ref[band, g, block, :].astype(F)
                ).astype(BF)
                dwide_ref[to, sides[side]] = value

    events = {}

    def when(j, *actions):
        events.setdefault(j, []).extend(actions)

    def received(m):
        owns[m].wait()
        swaps[m][0].wait_recv()

    for g in range(1, groups):
        when(2 * g - 1, kv_loads[g].wait)
    when(0, down[1].step_one)
    when(0, lambda: received(1), up[0].step_one)
    when(1, up[1].step_one, lambda: share_one(0))
    when(2, up[2].step_one, down[0].step_two, lambda: share_two(0))
    when(3, lambda: received(2), out[0].step_one, down[1].step_two, lambda: share_one(1))
    when(4, up[0].step_two, down[0].step_three, lambda: share_two(1))
    when(5, up[1].step_two, down[1].step_three, lambda: share_one(2))
    when(6, up[2].step_two, up[0].step_three, lambda: share_two(2))
    when(7, lambda: share_one(3), out[0].step_two, up[1].step_three)
    received(0)
    down[0].step_one()
    kv_loads[0].wait()

    @pl.loop(0, 2 * groups)
    def _(j):
        g, s = j // 2, j % 2
        lanes = pl.ds(pl.multiple_of(s * rows, rows), rows)
        for k in range(unroll):

            def put_key(b, values):
                dkv_ref[b, g, pl.ds(k * HEAD_DIM, HEAD_DIM), lanes] = values

            def put_value(b, values):
                dkv_ref[b, g, pl.ds(part + k * HEAD_DIM, HEAD_DIM), lanes] = values

            attend_back_step(
                s * HEADS + g * unroll + k,
                at.x, q_ref, kv_ref, delta_ref, lse_ref, datt_ref, bias_ref, dq_ref,
                put_key, put_value,
            )
        for when_j, actions in events.items():

            @pl.when(j == when_j)
            def _():
                for action in actions:
                    action()

    chunk = width // 2
    g_flat = g_qkv_ref.reshape(3 * width, width)
    parts = lane_parts(BACK_ORDERS[3], width // 2)

    def weight_grad(part, source_ref, first, count, tokens_at):
        _, start, size = parts[part]
        lanes = [pl.ds(x * (width // 2) + start, size) for x in range(2)]

        @pl.loop(0, count)
        def _(j):
            block = pl.ds(pl.multiple_of(j * chunk, 128), chunk)
            to = pl.ds(pl.multiple_of((first + j) * chunk, 128), chunk)
            both = jnp.concatenate([h_ref[l, tokens_at] for l in lanes], axis=0)
            result = dg(source_ref[block, :], both, 1, 1).astype(BF)
            g_flat[to, lanes[0]] = result[:, :size]
            g_flat[to, lanes[1]] = result[:, size:]

    def back_through(side):
        err_ref[...] = jnp.zeros_like(err_ref)

        @pl.loop(0, 4)
        def _(j):
            block = pl.ds(pl.multiple_of(j * chunk, 128), chunk)
            source = pl.ds(pl.multiple_of((2 + j) * chunk, 128), chunk)
            err_ref[...] += dg(w_ref[source, :], dwide_ref[block, sides[side]], 0, 0)

    def start_swap(part):
        for copy in swaps[3 + part]:
            copy.start()

    def first_sum(part):
        for copy in swaps[3 + part]:
            copy.wait_recv()
        qkv[part].step_one()

    for copy in late_loads:
        copy.wait()
    for p in range(2):
        weight_grad(p, dq_ref, 0, 2, sides[0])
    share_two(groups - 1)
    weight_grad(0, dwide_ref, 2, 4, slice(None))
    start_swap(0)
    back_through(1)
    err_far = err_ref[...]
    for s in range(2):
        err_far_ref[s] = err_far[:, s * rows : (s + 1) * rows].astype(BF)
    first_sum(0)
    err_moves[0].start()
    weight_grad(1, dwide_ref, 2, 4, slice(None))
    start_swap(1)
    normed_far, _ = normalize(x_far_ref[...].astype(F))
    gain_row = row_sums(err_ref[...] * normed_far)[:1]
    shift_row = row_sums(err_ref[...])[:1]
    first_sum(1)
    up[2].step_three()
    out[0].step_three()
    back_through(0)

    @pl.loop(0, 2)
    def _(j):
        block = pl.ds(pl.multiple_of(j * chunk, 128), chunk)
        err_ref[...] += dg(w_ref[block, :], dq_ref[block, :], 0, 0)

    small_ref[0] = sums_ref[...]
    small_ref[0, 0:1] = row_sums(dq_ref[...])[:1]
    small_ref[0, 1:2] = row_sums(dwide_ref[pl.ds(width, width), :])[:1]
    normed, _ = normalize(x_ref[...].astype(F))
    small_ref[0, 4:5] = gain_row + row_sums(err_ref[...] * normed)[:1]
    small_ref[0, 5:6] = shift_row + row_sums(err_ref[...])[:1]
    small_steps[0].start()
    qkv[0].step_two()
    err_moves[1].start()
    for item in down:
        item.step_four()
    deliver(0)
    small_steps[0].wait_recv()
    small_ref[1] = small_ref[0] + small_in_ref[0]
    small_steps[1].start()
    qkv[1].step_two()
    qkv[0].step_three()
    small_steps[1].wait_recv()
    small_ref[2] = small_ref[1] + small_in_ref[1]
    small_steps[2].start()
    for item in up:
        item.step_four()
    deliver(1)
    small_steps[2].wait_recv()
    small_z_ref[at.z] = small_ref[2] + small_in_ref[2]
    for copy in small_last:
        copy.start()
    out[0].step_four()
    deliver(2)
    qkv[1].step_three()

    def finish_slot(s):
        err_moves[s].wait_recv()
        lanes = slice(s * rows, (s + 1) * rows)
        err = err_ref[:, lanes] + err_in_ref[s].astype(F)
        normed, inverse = normalize(x_ref[:, lanes].astype(F))
        gx_ref[:, lanes] = (
            dmid_ref[:, lanes] + norm_back(err, normed, inverse, cols_ref[:, GAIN_ONE])
        ).astype(BF)

    finish_slot(0)
    qkv[0].step_four()
    for copy in small_last:
        copy.wait_recv()
    total = small_z_ref[0]
    for k in range(1, depth):
        total = total + small_z_ref[k]
    total_ref[...] = total
    qkv[1].step_four()
    deliver(3)
    finish_slot(1)
    for m in range(4):
        ends[m][3].wait()
        for item in moves[m]:
            item.end()
    for copy in sum(swaps, []) + one + two + err_moves + small_steps + small_last:
        copy.wait_send()


def back(
    images, bands, scalars, q, kv, delta, lse, datt, x, x_far, h, dmid, w, cols, grads, sums
):
    depth = images // 2
    width, tokens = x.shape
    g_out, g_up, g_down = grads
    groups = HEADS // 4
    results, buffers = [], []
    for m, item in enumerate((g_down, g_up, g_out, w)):
        block, lanes = item.shape[0] // images // 2, item.shape[1]
        results.append(shape((2, block, lanes // 4), F))
        buffers += [
            pltpu.VMEM((depth, 2, block, lanes), BF),
            pltpu.VMEM((block, lanes // 2), F),
            pltpu.VMEM((block, lanes // 4), F),
        ]
        if m < 3:
            buffers.append(pltpu.VMEM((depth, 2, block, lanes), BF))
        for order, _, size in lane_parts(BACK_ORDERS[m], lanes // 2):
            buffers += reduction_buffers(order, depth, block, size)
    small = (SUM_ROWS, width)
    return pl.pallas_call(
        functools.partial(back_kernel, images, bands),
        name="back",
        out_shape=(shape(x.shape, BF), results[3], results[2], results[1], results[0], shape(small, F)),
        in_specs=[SM] + [VM] * 6 + [ANY] * 9,
        out_specs=(VM,) * 6,
        scratch_shapes=[
            pltpu.VMEM(kv.shape, BF),
            pltpu.VMEM((width, tokens), BF),
            pltpu.VMEM((width, tokens), BF),
            pltpu.VMEM((width, 2 * tokens), BF),
            pltpu.VMEM((width, tokens), F),
            pltpu.VMEM(w.shape, BF),
            pltpu.VMEM((8, tokens // 2), F),
            pltpu.VMEM((width, tokens), BF),
            pltpu.VMEM((2 * width, 2 * tokens), BF),
            pltpu.VMEM((bands, groups, 2 * width // groups, tokens), BF),
            pltpu.VMEM((2, groups, 2 * width // groups, tokens), BF),
            pltpu.VMEM((depth, 2, w.shape[0] // images, width), BF),
            pltpu.VMEM((width, tokens), F),
            pltpu.VMEM((2, width, tokens // 2), BF),
            pltpu.VMEM((2, width, tokens // 2), BF),
            pltpu.VMEM((3,) + small, F),
            pltpu.VMEM((3,) + small, F),
            pltpu.VMEM((depth,) + small, F),
        ]
        + buffers
        + [
            pltpu.SemaphoreType.DMA((16,)),
            pltpu.SemaphoreType.DMA((BACK_COPIES,)),
            pltpu.SemaphoreType.DMA((BACK_COPIES,)),
        ],
        compiler_params=comm_params(3),
    )(
        scalars, q, delta, lse, datt, cols, sums, kv, x, x_far, h, dmid, w, g_out, g_up, g_down
    )


def body(
    tokens,
    slot_kind,
    w_qkv,
    w_out,
    w_up,
    w_down,
    bias_qv,
    bias_out,
    bias_up,
    bias_down,
    gain_one,
    shift_one,
    gain_two,
    shift_two,
    cotangent,
):
    rows, slots, width = tokens.shape[1:]
    count = rows * slots
    images, bands = lax.axis_size("img"), lax.axis_size("band")
    band = lax.axis_index("band")
    smalls = (bias_qv, bias_out, bias_up, bias_down, gain_one, shift_one, gain_two, shift_two)
    sizes = [item.shape[0] for item in smalls]
    own = (w_qkv, w_out, w_up)
    widths = [item.shape[1] for item in own]
    direct = images % 4 == 0 and all(w % 32 == 0 for w in widths + [w_down.shape[1]])
    direct = direct and bias_qv.shape[0] == 2 * (width // images) <= 256
    direct = direct and bias_up.shape[0] == 4 * (width // images)

    def turn(values):
        return values[0].transpose(2, 1, 0).reshape(width, count)

    def turn_back(values):
        return values.reshape(width, slots, rows).transpose(2, 1, 0)[None]

    x, cot = turn(tokens), turn(cotangent)
    kinds = slot_kind[0].astype(jnp.int32)
    scalars = jnp.concatenate([kinds, (band // 2).astype(jnp.int32)[None]])
    single = (bias_out, bias_down, gain_one, shift_one, gain_two, shift_two)
    if direct:
        narrow = split_rows([item.T for item in own], 2)
        unit = width // images
        units = [jnp.stack(single), jnp.zeros((4, unit), BF)]
        units += [bias_qv.reshape(2, unit), bias_up.reshape(4, unit)]
        small = jnp.pad(jnp.concatenate(units), ((0, 0), (0, 128 - unit))).astype(F)
        *full, h, all_kv, x_far, q, att, lse, cols, c_up = front(
            images, bands, scalars, narrow, w_down.T, small, x, widths
        )
        full_qkv, full_out, full_up, full_down = (item.reshape(-1, item.shape[3]) for item in full)
    else:
        full_qkv, full_out, full_up, full_down = (
            lax.all_gather(lax.all_gather(item, "band", axis=0, tiled=True).T, "img", tiled=True)
            for item in (*own, w_down)
        )
        whole = [lax.all_gather(item, "img", tiled=True).astype(F) for item in single]
        cols = jnp.stack(whole + [whole[0]] * (COLUMNS - len(whole)), axis=1)
        c_qv = lax.all_gather(bias_qv, "img", tiled=True).astype(F)[:, None]
        c_up = lax.all_gather(bias_up, "img", tiled=True).astype(F)[:, None]
        bias = jnp.concatenate([c_qv[:width], jnp.zeros((width, 1), F), c_qv[width:]])
        h, qkv = project(x, full_qkv, cols, bias)
        q = qkv[:width]
        all_kv = share(images, bands, qkv[width:])
        all_kv = all_kv.reshape(bands, 2, GROUPS_OF_HEADS, -1, count).transpose(0, 2, 1, 3, 4)
        all_kv = all_kv.reshape(bands, GROUPS_OF_HEADS, -1, count)
        att, lse = attend(scalars, q, all_kv)
    out, dmid, datt, delta, g_out, g_up, g_down, sums = middle(
        x, cot, scalars, att, full_out, full_up, full_down, cols, c_up
    )
    if direct:
        gx, *pieces, total = back(
            images, bands, scalars, q, all_kv, delta, lse, datt, x, x_far, h, dmid,
            full_qkv, cols, (g_out, g_up, g_down), sums,
        )
        matrices = [item.reshape(-1, item.shape[2]).T for item in pieces]
    else:
        dq, dkv = attend_back(scalars, q, all_kv, delta, lse, datt)
        dkv = unshare(images, dkv)
        gx, g_qkv, sums_one = finish(x, h, dq, dkv, full_qkv, cols, dmid)
        matrices = [
            lax.psum_scatter(
                lax.psum_scatter(item, "img", scatter_dimension=0, tiled=True),
                "band",
                scatter_dimension=1,
                tiled=True,
            )
            .astype(F)
            .T
            for item in (g_qkv, g_out, g_up, g_down)
        ]
        total = lax.psum(sums + sums_one, ("img", "band"))
    own_small = lax.axis_index("img")
    flat = total.reshape(-1)
    starts = [0, 2, UP_ROW, 3, 4, 5, 6, 7]
    small = [
        lax.dynamic_slice(flat, (start * width + own_small * size,), (size,))
        for start, size in zip(starts, sizes)
    ]
    return (turn_back(out), turn_back(gx), *matrices, *small)


def solution(mesh):
    data, weight, vector = P("img", "band", None, None), P("band", "img"), P("img")
    return jax.shard_map(
        body,
        mesh=mesh,
        in_specs=(data, P("img", None)) + (weight,) * 4 + (vector,) * 8 + (data,),
        out_specs=(data, data) + (weight,) * 4 + (vector,) * 8,
        check_vma=False,
    )
```

```python
import functools
import math

import jax
import jax.numpy as jnp
from jax import lax
from jax.experimental import pallas as pl
from jax.experimental.pallas import tpu as pltpu
from jax.sharding import PartitionSpec as P

HEADS = 16
HEAD_DIM = 48
EPSILON = 1e-06
MASKED = -1e30
BF = jnp.bfloat16
F = jnp.float32
MESH = pl.DeviceIdType.MESH
VM = pl.BlockSpec(memory_space=pltpu.VMEM)
SM = pl.BlockSpec(memory_space=pltpu.SMEM)
ANY = pl.BlockSpec(memory_space=pl.ANY)
LIMIT = 67043328
SUM_ROWS, UP_ROW = 16, 8
COLUMNS = 10
BIAS_OUT, BIAS_DOWN, GAIN_ONE, SHIFT_ONE, GAIN_TWO, SHIFT_TWO = (slice(k, k + 1) for k in range(6))
GROUPS_OF_HEADS = 4
FRONT_COPIES, BACK_COPIES = 128, 128


def dg(left, right, left_dim, right_dim):
    return lax.dot_general(
        left, right, (((left_dim,), (right_dim,)), ((), ())), preferred_element_type=F
    )


def shape(dims, dtype):
    return jax.ShapeDtypeStruct(tuple(dims), dtype)


def row_sums(values):
    ones = jnp.ones((8, values.shape[1]), BF)
    if values.dtype == BF:
        return dg(ones, values, 1, 1)
    high = values.astype(BF)
    low = (values - high.astype(F)).astype(BF)
    return dg(ones, high, 1, 1) + dg(ones, low, 1, 1)


def normalize(values):
    average = jnp.mean(values, axis=0, keepdims=True)
    centered = values - average
    variance = jnp.mean(centered * centered, axis=0, keepdims=True)
    inverse = lax.rsqrt(variance + EPSILON)
    return centered * inverse, inverse


def norm_back(error, normed, inverse, gain):
    f = gain * error
    mean_f = jnp.mean(f, axis=0, keepdims=True)
    mean_fn = jnp.mean(f * normed, axis=0, keepdims=True)
    return (f - mean_f - normed * mean_fn) * inverse


def project_kernel(x_ref, w_ref, cols_ref, bias_ref, h_ref, qkv_ref):
    width = x_ref.shape[0]
    normed, _ = normalize(x_ref[...].astype(F))
    h_ref[...] = (normed * cols_ref[:, GAIN_ONE] + cols_ref[:, SHIFT_ONE]).astype(BF)
    scale = 1.0 / math.sqrt(HEAD_DIM)
    step = 256

    @pl.loop(0, 3 * width // step)
    def _(j):
        rows = pl.ds(pl.multiple_of(j * step, step), step)
        out = dg(w_ref[rows, :], h_ref[...], 1, 0) + bias_ref[rows, :]
        qkv_ref[rows, :] = (out * jnp.where(j < width // step, scale, 1.0)).astype(BF)


def project(x, w, cols, bias):
    width, tokens = x.shape
    return pl.pallas_call(
        project_kernel,
        name="project",
        out_shape=(shape((width, tokens), BF), shape((3 * width, tokens), BF)),
        in_specs=[VM] * 4,
        out_specs=(VM, VM),
        compiler_params=pltpu.CompilerParams(vmem_limit_bytes=LIMIT),
    )(x, w, cols, bias)


def fill_bias(scalars_ref, bias_ref, rows):
    lane_half = lax.broadcasted_iota(jnp.int32, (1, rows), 1) // (rows // 2)
    for s in range(2):
        small = scalars_ref[s] == 2
        for other in range(2):
            for half in range(2):
                keep = jnp.logical_and(other == 0, lane_half == half)
                masked = jnp.where(small, MASKED, 0.0)
                bias_ref[pl.ds(4 * s + 2 * other + half, 1), :] = jnp.where(
                    keep, jnp.zeros((1, rows), F), jnp.full((1, rows), masked, F)
                )


def add_bias(scores, bias_ref, s, other):
    rows = scores.shape[0]
    at = 4 * s + 2 * other
    return jnp.concatenate(
        [
            scores[: rows // 2] + bias_ref[pl.ds(at, 1), :],
            scores[rows // 2 :] + bias_ref[pl.ds(at + 1, 1), :],
        ],
        axis=0,
    )


def head_slices(i, rows):
    s, h = i // HEADS, i % HEADS
    lanes = pl.ds(pl.multiple_of(s * rows, rows), rows)
    first = pl.ds(pl.multiple_of(h * HEAD_DIM, 16), HEAD_DIM)
    second = pl.ds(pl.multiple_of(HEADS * HEAD_DIM + h * HEAD_DIM, 16), HEAD_DIM)
    return s, lanes, first, second


def attend_step(i, chip_x, q_ref, kv_ref, bias_ref, out_ref, lse_ref):
    bands = kv_ref.shape[0]
    rows = q_ref.shape[1] // 2
    s, lanes, first, second = head_slices(i, rows)
    q = q_ref[first, lanes]
    scores = []
    maximum = None
    for b in range(bands):
        other = jnp.where(chip_x == b // 2, 0, 1)
        keys, _ = kv_rows(kv_ref, b, i % HEADS)
        part = add_bias(dg(keys[:, lanes], q, 0, 0), bias_ref, s, other)
        scores.append(part)
        top = jnp.max(part, axis=0, keepdims=True)
        maximum = top if maximum is None else jnp.maximum(maximum, top)
    total, acc = 0.0, 0.0
    for b in range(bands):
        weight = jnp.exp(scores[b] - maximum)
        total = total + jnp.sum(weight, axis=0, keepdims=True)
        _, values = kv_rows(kv_ref, b, i % HEADS)
        acc = acc + dg(values[:, lanes], weight.astype(BF), 1, 0)
    out_ref[first, lanes] = acc / total
    lse_ref[pl.ds(i, 1), :] = maximum + jnp.log(total)


def attend_kernel(unroll, scalars_ref, q_ref, kv_ref, out_ref, lse_ref, bias_ref):
    fill_bias(scalars_ref, bias_ref, q_ref.shape[1] // 2)

    @pl.loop(0, 2 * HEADS // unroll)
    def _(j):
        for k in range(unroll):
            attend_step(
                j * unroll + k, scalars_ref[2], q_ref, kv_ref, bias_ref, out_ref, lse_ref
            )


def attend(scalars, q, kv):
    width, tokens = q.shape
    return pl.pallas_call(
        functools.partial(attend_kernel, 4),
        name="attend",
        out_shape=(shape((width, tokens), F), shape((2 * HEADS, tokens // 2), F)),
        in_specs=[SM, VM, VM],
        out_specs=(VM, VM),
        scratch_shapes=[pltpu.VMEM((8, tokens // 2), F)],
        compiler_params=pltpu.CompilerParams(vmem_limit_bytes=LIMIT),
    )(scalars, q, kv)


def attend_back_step(
    i, chip_x, q_ref, kv_ref, delta_ref, lse_ref, dout_ref, bias_ref, dq_ref, put_key, put_value
):
    bands = kv_ref.shape[0]
    rows = q_ref.shape[1] // 2
    s, lanes, first, second = head_slices(i, rows)
    q = q_ref[first, lanes]
    dout = dout_ref[first, lanes]
    delta = delta_ref[pl.ds(i % HEADS, 1), lanes]
    lse = lse_ref[pl.ds(i, 1), :]
    dq = 0.0
    for b in range(bands):
        other = jnp.where(chip_x == b // 2, 0, 1)
        k, v = (ref[:, lanes] for ref in kv_rows(kv_ref, b, i % HEADS))
        scores = add_bias(dg(k, q, 0, 0), bias_ref, s, other)
        dweight = dg(v, dout, 0, 0)
        weight = jnp.exp(scores - lse)
        dscores = (weight * (dweight - delta)).astype(BF)
        dq = dq + dg(k, dscores, 1, 0)
        put_key(b, dg(q, dscores, 1, 1).astype(BF))
        put_value(b, dg(dout, weight.astype(BF), 1, 1).astype(BF))
    dq_ref[first, lanes] = (dq * (1.0 / math.sqrt(HEAD_DIM))).astype(BF)


def attend_back_kernel(
    unroll, scalars_ref, q_ref, kv_ref, delta_ref, lse_ref, dout_ref, dq_ref, dkv_ref, bias_ref
):
    fill_bias(scalars_ref, bias_ref, q_ref.shape[1] // 2)

    @pl.loop(0, 2 * HEADS // unroll)
    def _(j):
        for k in range(unroll):
            i = j * unroll + k
            _, lanes, first, second = head_slices(i, q_ref.shape[1] // 2)

            def put_key(b, values):
                dkv_ref[b, first, lanes] = values

            def put_value(b, values):
                dkv_ref[b, second, lanes] = values

            attend_back_step(
                i, scalars_ref[2], q_ref, kv_ref, delta_ref, lse_ref, dout_ref, bias_ref, dq_ref,
                put_key, put_value,
            )


def attend_back(scalars, q, kv, delta, lse, dout):
    return pl.pallas_call(
        functools.partial(attend_back_kernel, 4),
        name="attend_back",
        out_shape=(shape(q.shape, BF), shape((kv.shape[0], 2 * q.shape[0], q.shape[1]), BF)),
        in_specs=[SM] + [VM] * 5,
        out_specs=(VM, VM),
        scratch_shapes=[pltpu.VMEM((8, q.shape[1] // 2), F)],
        compiler_params=pltpu.CompilerParams(vmem_limit_bytes=LIMIT),
    )(scalars, q, kv, delta, lse, dout)


def middle_body(
    x_ref, cot_ref, scalars_ref, att_ref, w_out_ref, w_up_ref, w_down_ref, cols_ref, bias_up_ref,
    out_ref, dmid_ref, datt_ref, delta_ref, g_out_ref, g_up_out, g_down_out, sums_ref,
    g_up_ref, g_down_ref,
    mid_ref, norm_ref, h_ref, dmlp_ref, mlp_ref, err_ref, attb_ref, dbranch_ref,
    up_sem, down_sem, wait_out, wait_up, passes,
):
    width, tokens = x_ref.shape
    hidden = w_up_ref.shape[0]
    step = 256
    first_slot = lax.broadcasted_iota(jnp.int32, (1, tokens), 1) < tokens // 2
    valid = jnp.where(
        first_slot,
        jnp.where(scalars_ref[0] > 0, 1.0, 0.0),
        jnp.where(scalars_ref[1] > 0, 1.0, 0.0),
    )
    attb_ref[...] = att_ref[...].astype(BF)
    dmlp_ref[...] = (cot_ref[...].astype(F) * valid).astype(BF)
    sums_ref[...] = jnp.zeros_like(sums_ref)
    mlp_ref[...] = jnp.zeros_like(mlp_ref)
    err_ref[...] = jnp.zeros_like(err_ref)
    wait_out()

    @pl.loop(0, width // step)
    def _(j):
        rows = pl.ds(pl.multiple_of(j * step, step), step)
        mid_ref[rows, :] = (
            dg(w_out_ref[rows, :], attb_ref[...], 1, 0)
            + cols_ref[rows, BIAS_OUT]
            + x_ref[rows, :].astype(F)
        )

    normed, inverse = normalize(mid_ref[...])
    norm_ref[...] = normed
    h_ref[...] = (normed * cols_ref[:, GAIN_TWO] + cols_ref[:, SHIFT_TWO]).astype(BF)
    wait_up()

    def stores(j):
        rows = pl.ds(pl.multiple_of(j * step, step), step)
        return (
            pltpu.make_async_copy(g_up_ref.at[rows, :], g_up_out.at[rows, :], up_sem.at[j]),
            pltpu.make_async_copy(g_down_ref.at[:, rows], g_down_out.at[:, rows], down_sem.at[j]),
        )

    def block(j):
        rows = pl.ds(pl.multiple_of(j * step, step), step)
        pre = dg(w_up_ref[rows, :], h_ref[...], 1, 0) + bias_up_ref[rows, :]
        phi = 0.5 + 0.5 * lax.erf(pre * math.sqrt(0.5))
        act = (pre * phi).astype(BF)
        slope = phi + pre * jnp.exp(pre * pre * -0.5) * (1.0 / math.sqrt(2.0 * math.pi))
        mlp_ref[...] += dg(w_down_ref[:, rows], act, 1, 0)
        dact = dg(w_down_ref[:, rows], dmlp_ref[...], 0, 0)
        dhid = (slope * dact).astype(BF)
        g_down_ref[:, rows] = dg(dmlp_ref[...], act, 1, 1).astype(BF)
        g_up_ref[rows, :] = dg(dhid, h_ref[...], 1, 1).astype(BF)
        per = width // step
        lanes = pl.ds(pl.multiple_of(j % per * step, step), step)
        sums_ref[pl.ds(UP_ROW + j // per, 1), lanes] = row_sums(dhid)[:1]
        err_ref[...] += dg(w_up_ref[rows, :], dhid, 0, 0)
        for copy in stores(j):
            copy.start()

    for wait, count, place in passes:
        wait()

        @pl.loop(0, count)
        def _(t):
            block(place(t))

    out_ref[...] = ((mid_ref[...] + mlp_ref[...] + cols_ref[:, BIAS_DOWN]) * valid).astype(BF)
    err = err_ref[...]
    sums_ref[3:4] = row_sums(dmlp_ref[...])[:1]
    sums_ref[6:7] = row_sums(err * norm_ref[...])[:1]
    sums_ref[7:8] = row_sums(err)[:1]
    dmid = cot_ref[...].astype(F) * valid + norm_back(
        err, norm_ref[...], inverse, cols_ref[:, GAIN_TWO]
    )
    dmid_ref[...] = dmid
    dbranch_ref[...] = dmid.astype(BF)
    sums_ref[2:3] = row_sums(dbranch_ref[...])[:1]
    datt_ref[...] = dg(w_out_ref[...], dbranch_ref[...], 0, 0).astype(BF)
    inner = att_ref[...] * datt_ref[...].astype(F)
    delta_ref[...] = jnp.sum(inner.reshape(HEADS, width // HEADS, tokens), axis=1)

    @pl.loop(0, width // step)
    def _(j):
        rows = pl.ds(pl.multiple_of(j * step, step), step)
        g_out_ref[rows, :] = dg(dbranch_ref[rows, :], attb_ref[...], 1, 1).astype(BF)

    @pl.loop(0, hidden // step)
    def _(j):
        for copy in stores(j):
            copy.wait()


def middle_kernel(*refs):
    x_ref, cot_ref, scalars_ref, att_ref, w_out_in, w_up_in, w_down_in = refs[:7]
    outputs = refs[7:17]
    w_out_ref, w_up_ref, w_down_ref = refs[17:20]
    scratch, in_sem = refs[20:30], refs[30]
    loads = [
        pltpu.make_async_copy(source, target, in_sem.at[k])
        for k, (source, target) in enumerate(
            ((w_out_in, w_out_ref), (w_up_in, w_up_ref), (w_down_in, w_down_ref))
        )
    ]
    for copy in loads:
        copy.start()
    middle_body(
        x_ref, cot_ref, scalars_ref, att_ref, w_out_ref, w_up_ref, w_down_ref, *outputs, *scratch,
        *refs[31:], loads[0].wait, loads[1].wait,
        [(loads[2].wait, w_up_ref.shape[0] // 256, lambda t: t)],
    )


def middle(x, cot, scalars, att, w_out, w_up, w_down, cols, bias_up):
    width, tokens = x.shape
    hidden = w_up.shape[0]
    full = (width, tokens)
    weights = [w_out.shape, w_up.shape, w_down.shape]
    return pl.pallas_call(
        middle_kernel,
        name="middle",
        out_shape=(
            shape(full, BF),
            shape(full, F),
            shape(full, BF),
            shape((HEADS, tokens), F),
            shape(w_out.shape, BF),
            shape(w_up.shape, BF),
            shape(w_down.shape, BF),
            shape((SUM_ROWS, width), F),
        ),
        in_specs=[VM, VM, SM, VM] + [ANY] * 3 + [VM] * 2,
        out_specs=(VM,) * 5 + (ANY, ANY, VM),
        scratch_shapes=[pltpu.VMEM(s, BF) for s in weights + weights[1:]]
        + [
            pltpu.VMEM(full, F),
            pltpu.VMEM(full, F),
            pltpu.VMEM(full, BF),
            pltpu.VMEM(full, BF),
            pltpu.VMEM(full, F),
            pltpu.VMEM(full, F),
            pltpu.VMEM(full, BF),
            pltpu.VMEM(full, BF),
            pltpu.SemaphoreType.DMA((3,)),
            pltpu.SemaphoreType.DMA((hidden // 256,)),
            pltpu.SemaphoreType.DMA((hidden // 256,)),
        ],
        compiler_params=pltpu.CompilerParams(vmem_limit_bytes=LIMIT),
    )(x, cot, scalars, att, w_out, w_up, w_down, cols, bias_up)


def finish_kernel(
    x_ref, h_ref, dq_ref, dkv_ref, w_ref, cols_ref, dmid_ref, gx_ref, g_ref, sums_ref, err_ref
):
    width, tokens = x_ref.shape
    step = 256
    blocks = width // step
    err_ref[...] = jnp.zeros_like(err_ref)
    for ref, count, base in ((dq_ref, blocks, 0), (dkv_ref, 2 * blocks, blocks)):

        @pl.loop(0, count)
        def _(j):
            rows = pl.ds(pl.multiple_of(j * step, step), step)
            to = pl.ds(pl.multiple_of((j + base) * step, step), step)
            g_ref[to, :] = dg(ref[rows, :], h_ref[...], 1, 1).astype(BF)
            err_ref[...] += dg(w_ref[to, :], ref[rows, :], 0, 0)

    normed, inverse = normalize(x_ref[...].astype(F))
    err = err_ref[...]
    sums_ref[...] = jnp.zeros_like(sums_ref)
    sums_ref[0:1] = row_sums(dq_ref[...])[:1]
    sums_ref[1:2] = row_sums(dkv_ref[pl.ds(width, width), :])[:1]
    sums_ref[4:5] = row_sums(err * normed)[:1]
    sums_ref[5:6] = row_sums(err)[:1]
    gx_ref[...] = (dmid_ref[...] + norm_back(err, normed, inverse, cols_ref[:, GAIN_ONE])).astype(BF)


def finish(x, h, dq, dkv, w, cols, dmid):
    width, tokens = x.shape
    return pl.pallas_call(
        finish_kernel,
        name="finish",
        out_shape=(shape(x.shape, BF), shape(w.shape, BF), shape((SUM_ROWS, width), F)),
        in_specs=[VM] * 7,
        out_specs=(VM, VM, VM),
        scratch_shapes=[pltpu.VMEM(x.shape, F)],
        compiler_params=pltpu.CompilerParams(vmem_limit_bytes=LIMIT),
    )(x, h, dq, dkv, w, cols, dmid)


class Place:
    def __init__(self, images):
        self.images = images
        self.depth = images // 2
        self.img = lax.axis_index("img")
        self.band = lax.axis_index("band")
        self.z, self.y = self.img // 2, self.img % 2
        self.x, self.c = self.band // 2, self.band % 2
        self.partner = (self.img, self.band + 1 - 2 * self.c)
        self.across_x = (self.img, self.band + 2 - 4 * self.x)
        self.across_y = (self.img + 1 - 2 * self.y, self.band)
        self.z_peers = [self.along_z(k) for k in range(1, self.depth)]

    def along_z(self, k):
        z = lax.rem(self.z + k, self.depth)
        return (2 * z + self.y, self.band), z


def greet(peers):
    barrier = pltpu.get_barrier_semaphore()
    for peer in peers:
        pl.semaphore_signal(barrier, inc=1, device_id=peer, device_id_type=MESH)
    pl.semaphore_wait(barrier, len(peers))


def send(src, dst, send_sem, recv_sem, peer):
    copy = pltpu.make_async_remote_copy(
        src_ref=src,
        dst_ref=dst,
        send_sem=send_sem,
        recv_sem=recv_sem,
        device_id=peer,
        device_id_type=MESH,
    )
    copy.start()
    return copy


def comm_params(collective_id):
    return pltpu.CompilerParams(
        collective_id=collective_id, has_side_effects=True, vmem_limit_bytes=LIMIT
    )


def split_rows(shards, parts):
    return jnp.concatenate(
        [item.reshape(parts, item.shape[0] // parts, item.shape[1]) for item in shards], axis=1
    )


class Spread:
    def __init__(self, at, make, order, part, parts, source, ref, local_sem):
        depth, near, c = at.depth, at.depth // 2, at.c
        rows, half = ref.shape[2] // 2, ref.shape[3] // 2
        rows = pl.ds(pl.multiple_of(c * rows, 16), rows)
        size = half // parts
        lanes = pl.ds(pl.multiple_of(at.x * half + part * size, 128), size)
        both = [pl.ds(x * half + part * size, size) for x in range(2)]
        if parts == 1:
            both = [slice(None)]
        low, high = pl.ds(0, near), pl.ds(near, depth - near)

        def same(index, peer):
            if len(index) == 4:
                return [make(ref.at[index], ref.at[index], peer)]
            return [make(ref.at[index + (l,)], ref.at[index + (l,)], peer) for l in both]

        piece = ref.at[at.z, at.y, rows, lanes]
        source = source.at[:, pl.ds(part * size, size)]
        self.keep = pltpu.make_async_copy(source, piece, local_sem)
        z_first = []
        if order != "xyz":
            z_first = [make(source, piece, peer) for peer, _ in at.z_peers]
        if order == "mixed":
            self.stages = [
                z_first,
                same((low, at.y, rows, lanes), at.across_x)
                + same((high, at.y, rows, lanes), at.across_y),
                same((low, at.y, rows), at.across_y)
                + same((high, slice(None), rows, lanes), at.across_x),
            ]
        elif order == "zxy":
            self.stages = [
                z_first,
                same((slice(None), at.y, rows, lanes), at.across_x),
                same((slice(None), at.y, rows), at.across_y),
            ]
        else:
            last = [same((at.z, slice(None), rows), peer) for peer, _ in at.z_peers]
            self.stages = [
                [make(source, piece, at.across_x)],
                same((at.z, at.y, rows), at.across_y),
                sum(last, []),
            ]
        self.stages.append(same((slice(None), slice(None), rows), at.partner))

    def start(self):
        self.keep.start()
        for copy in self.stages[0]:
            copy.start()

    def step(self, k):
        if k == 1:
            self.keep.wait()
        for copy in self.stages[k - 1]:
            copy.wait_recv()
        for copy in self.stages[k]:
            copy.start()

    def wait(self):
        for copy in self.stages[-1]:
            copy.wait_recv()

    def end(self):
        for stage in self.stages:
            for copy in stage:
                copy.wait_send()


def kv_rows(ref, b, h):
    part = ref.shape[2] // 2
    heads = part // HEAD_DIM
    first = pl.multiple_of(h % heads * HEAD_DIM, 16)
    second = pl.multiple_of(part + h % heads * HEAD_DIM, 16)
    at = ref.at[b, h // heads]
    return at.at[pl.ds(first, HEAD_DIM)], at.at[pl.ds(second, HEAD_DIM)]


def front_kernel(
    images, bands, scalars_ref, narrow_ref, wide_ref, small_ref, x_ref, cot_ref,
    qkv_w_out, h_out, kv_out, x_far_out, q_ref, lse_ref, cols_ref, *rest,
):
    results, rest = rest[:8], rest[8:]
    qkv_w_ref, out_w_ref, up_w_ref, down_w_ref, h_ref, kv_ref, att_ref, up_col_ref = rest[:8]
    theirs_ref, mine_ref, mine_wide_ref, smalls_ref, qv_col_ref, bias_ref, x_far_ref = rest[8:15]
    local_sem, send_sem, recv_sem = rest[15:18]
    middle_scratch = rest[18:]
    at = Place(images)
    width, tokens = x_ref.shape
    rows = tokens // 2
    unit = width // images
    groups = kv_ref.shape[1]
    part = width // groups
    c = at.c
    used = [0, 0]

    def make(src, dst, peer):
        k = used[0]
        used[0] += 1
        return pltpu.make_async_remote_copy(
            src_ref=src,
            dst_ref=dst,
            send_sem=send_sem.at[k],
            recv_sem=recv_sem.at[k],
            device_id=peer,
            device_id_type=MESH,
        )

    def local():
        used[1] += 1
        return local_sem.at[used[1] - 1]

    others = [(lax.rem(at.img + k, images), at.band) for k in range(1, images)]
    half = wide_ref.shape[0] // 2
    wide = wide_ref.shape[1]
    own_lanes = pl.ds(pl.multiple_of(c * wide, 128), wide)
    own_wide = pltpu.make_async_copy(
        wide_ref.at[pl.ds(pl.multiple_of(c * half, 8), half), :],
        mine_wide_ref.at[:, own_lanes],
        local(),
    )
    swap = make(narrow_ref.at[1 - c], theirs_ref, at.partner)
    swap_wide = make(
        wide_ref.at[pl.ds(pl.multiple_of((1 - c) * half, 8), half), :],
        mine_wide_ref.at[:, own_lanes],
        at.partner,
    )
    lines = pl.ds(pl.multiple_of(at.img * 16, 16), 16)
    keep_small = pltpu.make_async_copy(small_ref, smalls_ref.at[lines, :], local())
    small_copies = [make(small_ref, smalls_ref.at[lines, :], peer) for peer in others]
    sources, row = [], 0
    for ref in (qkv_w_ref, out_w_ref, up_w_ref):
        count = ref.shape[2] // 2
        sources.append(mine_ref.at[pl.ds(row, count), :])
        row += count
    sources.append(mine_wide_ref)

    def spread(ref, source, orders):
        parts = len(orders)
        return [
            Spread(at, make, orders[k], k, parts, source, ref, local()) for k in range(parts)
        ]

    s_qkv = spread(qkv_w_ref, sources[0], ("mixed",) * 3)
    (s_out,) = spread(out_w_ref, sources[1], ("mixed",))
    s_up = spread(up_w_ref, sources[2], ("mixed", "zxy", "zxy"))
    d_one, d_two = spread(down_w_ref, sources[3], ("xyz", "mixed"))
    save_w = pltpu.make_async_copy(qkv_w_ref, qkv_w_out, local())
    save_h = pltpu.make_async_copy(h_ref, h_out, local())
    save_x = pltpu.make_async_copy(x_far_ref, x_far_out, local())
    save_kv = [
        pltpu.make_async_copy(kv_ref.at[:, g], kv_out.at[:, g], local()) for g in range(groups)
    ]
    x_lanes = [pl.ds(s * rows, rows) for s in range(2)]
    x_moves = [make(x_ref.at[:, l], x_far_ref.at[:, l], at.across_x) for l in x_lanes]
    far = at.across_x[1]
    kv_moves = [
        [
            [
                make(kv_ref.at[b, g, :, x_lanes[s]], kv_ref.at[b, g, :, x_lanes[s]], at.partner)
                for b in (at.band, far)
            ]
            for g in range(groups)
        ]
        for s in range(2)
    ]

    greet([at.partner, at.across_x] + others)
    swap.start()
    x_moves[0].start()
    own_wide.start()
    swap_wide.start()
    keep_small.start()
    for copy in small_copies:
        copy.start()
    fill_bias(scalars_ref, bias_ref, rows)
    swap.wait_recv()
    mine, theirs = narrow_ref[c], theirs_ref[...]
    lane_count = mine.shape[1]
    mine_ref[:, pl.ds(0, lane_count)] = jnp.where(c == 0, mine, theirs)
    mine_ref[:, pl.ds(lane_count, lane_count)] = jnp.where(c == 0, theirs, mine)
    for item in s_qkv:
        item.start()
    own_wide.wait()
    swap_wide.wait_recv()
    d_one.start()
    for item in s_up:
        item.start()
    d_two.start()
    s_out.start()

    keep_small.wait()
    for copy in small_copies:
        copy.wait_recv()
    turned = smalls_ref[...].T
    qv_units, up_units = 2, up_w_ref.shape[2] // unit
    singles = 16 - qv_units - up_units
    for j in range(images):
        block = turned[:unit, 16 * j : 16 * j + 16]
        cols_ref[pl.ds(unit * j, unit), :] = block[:, :singles]
        for u in range(qv_units):
            lane = singles + u
            qv_col_ref[pl.ds(unit * (qv_units * j + u), unit), :] = block[:, lane : lane + 1]
        for u in range(up_units):
            lane = singles + qv_units + u
            up_col_ref[pl.ds(unit * (up_units * j + u), unit), :] = block[:, lane : lane + 1]

    def first_norm(s, ref, side):
        normed, _ = normalize(ref[:, x_lanes[s]].astype(F))
        to = pl.ds(side * tokens + s * rows, rows)
        h_ref[:, to] = (normed * cols_ref[:, GAIN_ONE] + cols_ref[:, SHIFT_ONE]).astype(BF)

    s_qkv[0].step(1)
    s_qkv[1].step(1)
    d_one.step(1)
    s_qkv[0].step(2)
    s_qkv[2].step(1)
    for s in range(2):
        first_norm(s, x_ref, 0)
    s_qkv[1].step(2)
    d_one.step(2)
    s_qkv[0].step(3)
    s_qkv[2].step(2)
    x_moves[1].start()
    x_moves[0].wait_recv()
    first_norm(0, x_far_ref, 1)
    s_qkv[1].step(3)
    s_qkv[2].step(3)
    s_up[0].step(1)
    s_up[1].step(1)
    for item in s_qkv:
        item.wait()
    save_w.start()

    weights = qkv_w_ref.reshape(3 * width, width)
    scale = 1.0 / math.sqrt(HEAD_DIM)

    def project(s):
        for g in range(groups):
            for k in range(2):
                row = (1 + k) * width + g * part
                to = pl.ds(k * part, part)
                for side, band in enumerate((at.band, far)):
                    lanes = pl.ds(side * tokens + s * rows, rows)
                    out = dg(weights[pl.ds(row, part), :], h_ref[:, lanes], 1, 0)
                    if k == 1:
                        out = out + qv_col_ref[pl.ds(width + g * part, part), :]
                    kv_ref[band, g, to, x_lanes[s]] = out.astype(BF)
            for copy in kv_moves[s][g]:
                copy.start()
        for g in range(groups):
            block = pl.ds(g * part, part)
            out = dg(weights[block, :], h_ref[:, x_lanes[s]], 1, 0) + qv_col_ref[block, :]
            q_ref[block, x_lanes[s]] = (out * scale).astype(BF)

    def second_slot():
        x_moves[1].wait_recv()
        first_norm(1, x_far_ref, 1)
        project(1)
        save_h.start()
        save_x.start()

    def arrive(s, g):
        for copy in kv_moves[s][g]:
            copy.wait_recv()
        if s == 1:
            save_kv[g].start()

    events = {}

    def when(j, *actions):
        events.setdefault(j, []).extend(actions)

    when(1, functools.partial(s_up[2].step, 1))
    when(2, second_slot)
    for j in range(1, 2 * groups):
        when(j - 1, functools.partial(arrive, j // groups, j % groups))
    when(1, functools.partial(s_up[0].step, 2))
    when(2, functools.partial(d_two.step, 1), functools.partial(s_out.step, 1))
    when(4, functools.partial(s_up[1].step, 2))
    when(5, functools.partial(s_up[2].step, 2))
    when(6, functools.partial(s_up[0].step, 3), functools.partial(s_out.step, 2))
    when(7, functools.partial(d_two.step, 2), functools.partial(s_up[1].step, 3))
    project(0)
    arrive(0, 0)
    unroll = HEADS // groups

    @pl.loop(0, 2 * groups)
    def _(j):
        s, g = j // groups, j % groups
        for k in range(unroll):
            attend_step(
                s * HEADS + g * unroll + k, at.x, q_ref, kv_ref, bias_ref, att_ref, lse_ref
            )
        for when_j, actions in events.items():

            @pl.when(j == when_j)
            def _():
                for action in actions:
                    action()

    hidden = up_w_ref.shape[0] * 2 * up_w_ref.shape[2]
    blocks = hidden // 256
    quarter = blocks // 4

    def wait_out():
        s_out.step(3)
        s_up[2].step(3)
        s_out.wait()

    def wait_up():
        d_two.step(3)
        for item in s_up:
            item.wait()

    def wait_one():
        d_one.step(3)
        d_one.wait()

    def flat(ref):
        return ref.reshape(ref.shape[0] * 2 * ref.shape[2], ref.shape[3])

    middle_body(
        x_ref, cot_ref, scalars_ref, att_ref, flat(out_w_ref), flat(up_w_ref), flat(down_w_ref),
        cols_ref, up_col_ref, *results, *middle_scratch, wait_out, wait_up,
        [
            (d_two.wait, 2 * quarter, lambda t: t + t // quarter * quarter + quarter),
            (wait_one, 2 * quarter, lambda t: t + t // quarter * quarter),
        ],
    )
    for item in s_qkv + s_up + [s_out, d_one, d_two]:
        item.end()
    for copy in [save_w, save_h, save_x] + save_kv:
        copy.wait()
    for copy in [swap, swap_wide] + small_copies + x_moves:
        copy.wait_send()
    for copy in sum(sum(kv_moves, []), []):
        copy.wait_send()


def front(images, bands, scalars, narrow, wide, small, x, cot, widths):
    depth = images // 2
    width, tokens = x.shape
    groups = GROUPS_OF_HEADS
    hidden = images * widths[2]
    full = (width, tokens)
    kv = (bands, groups, 2 * width // groups, tokens)
    weights = [(depth, 2, w, width) for w in widths]
    weights.append((depth, 2, wide.shape[0], 4 * wide.shape[1]))
    return pl.pallas_call(
        functools.partial(front_kernel, images, bands),
        name="front",
        out_shape=(
            shape(weights[0], BF),
            shape((width, 2 * tokens), BF),
            shape(kv, BF),
            shape(full, BF),
            shape(full, BF),
            shape((2 * HEADS, tokens // 2), F),
            shape((width, COLUMNS), F),
            shape(full, BF),
            shape(full, F),
            shape(full, BF),
            shape((HEADS, tokens), F),
            shape((width, width), BF),
            shape((hidden, width), BF),
            shape((width, hidden), BF),
            shape((SUM_ROWS, width), F),
        ),
        in_specs=[SM] + [VM] * 5,
        out_specs=(ANY,) * 4 + (VM,) * 8 + (ANY, ANY, VM),
        scratch_shapes=[pltpu.VMEM(s, BF) for s in weights]
        + [
            pltpu.VMEM((width, 2 * tokens), BF),
            pltpu.VMEM(kv, BF),
            pltpu.VMEM(full, F),
            pltpu.VMEM((hidden, 1), F),
            pltpu.VMEM(narrow.shape[1:], BF),
            pltpu.VMEM((narrow.shape[1], 2 * narrow.shape[2]), BF),
            pltpu.VMEM((wide.shape[0] // 2, 2 * wide.shape[1]), BF),
            pltpu.VMEM((16 * images, 128), F),
            pltpu.VMEM((2 * width, 1), F),
            pltpu.VMEM((8, tokens // 2), F),
            pltpu.VMEM(full, BF),
            pltpu.SemaphoreType.DMA((24,)),
            pltpu.SemaphoreType.DMA((FRONT_COPIES,)),
            pltpu.SemaphoreType.DMA((FRONT_COPIES,)),
            pltpu.VMEM((hidden, width), BF),
            pltpu.VMEM((width, hidden), BF),
            pltpu.VMEM(full, F),
            pltpu.VMEM(full, F),
            pltpu.VMEM(full, BF),
            pltpu.VMEM(full, BF),
            pltpu.VMEM(full, F),
            pltpu.VMEM(full, F),
            pltpu.VMEM(full, BF),
            pltpu.VMEM(full, BF),
            pltpu.SemaphoreType.DMA((hidden // 256,)),
            pltpu.SemaphoreType.DMA((hidden // 256,)),
        ],
        compiler_params=comm_params(0),
    )(scalars, narrow, wide, small, x, cot)


def share_kernel(images, kv_ref, all_ref, local_sem, send_sem, recv_sem):
    at = Place(images)
    greet([at.partner, at.across_x])
    rows = kv_ref.shape[1] // 2
    mine = pltpu.make_async_copy(kv_ref, all_ref.at[at.band], local_sem)
    mine.start()
    copies = []
    for s in range(2):
        lanes = pl.ds(s * rows, rows)
        copies.append(
            send(
                kv_ref.at[:, lanes],
                all_ref.at[at.band, :, lanes],
                send_sem.at[s],
                recv_sem.at[s],
                at.across_x,
            )
        )
    near = send(kv_ref, all_ref.at[at.band], send_sem.at[2], recv_sem.at[2], at.partner)
    passed = []
    for s in range(2):
        copies[s].wait_recv()
        part = all_ref.at[at.across_x[1], :, pl.ds(s * rows, rows)]
        passed.append(send(part, part, send_sem.at[3 + s], recv_sem.at[3 + s], at.partner))
    for copy in passed + [near]:
        copy.wait()
    for copy in copies:
        copy.wait_send()
    mine.wait()


def share(images, bands, kv):
    return pl.pallas_call(
        functools.partial(share_kernel, images),
        name="share",
        out_shape=shape((bands,) + kv.shape, BF),
        in_specs=[VM],
        out_specs=ANY,
        scratch_shapes=[
            pltpu.SemaphoreType.DMA,
            pltpu.SemaphoreType.DMA((5,)),
            pltpu.SemaphoreType.DMA((5,)),
        ],
        compiler_params=comm_params(1),
    )(kv)


def add_rows(total_ref, other_ref, step):
    @pl.loop(0, total_ref.shape[0] // step)
    def _(j):
        rows = pl.ds(pl.multiple_of(j * step, step), step)
        total_ref[rows, :] = (
            total_ref[rows, :].astype(F) + other_ref[rows, :].astype(F)
        ).astype(total_ref.dtype)


def unshare_kernel(images, dkv_ref, sum_ref, near_ref, far_ref, send_sem, recv_sem):
    at = Place(images)
    greet([at.partner, at.across_x])
    mate, far = at.partner[1], at.across_x[1]
    far_mate = at.band + 2 - 4 * at.x + 1 - 2 * at.c
    one = send(dkv_ref.at[far_mate], near_ref.at[0], send_sem.at[0], recv_sem.at[0], at.partner)
    two = send(dkv_ref.at[mate], near_ref.at[1], send_sem.at[1], recv_sem.at[1], at.partner)
    one.wait_recv()
    add_rows(near_ref.at[0], dkv_ref.at[far], 64)
    three = send(near_ref.at[0], far_ref, send_sem.at[2], recv_sem.at[2], at.across_x)
    two.wait_recv()
    add_rows(near_ref.at[1], dkv_ref.at[at.band], 64)
    three.wait_recv()
    sum_ref[...] = near_ref[1]
    add_rows(sum_ref, far_ref, 64)
    for copy in (one, two, three):
        copy.wait_send()


def unshare(images, dkv):
    block = dkv.shape[1:]
    return pl.pallas_call(
        functools.partial(unshare_kernel, images),
        name="unshare",
        out_shape=shape(block, BF),
        in_specs=[VM],
        out_specs=VM,
        scratch_shapes=[
            pltpu.VMEM((2,) + block, BF),
            pltpu.VMEM(block, BF),
            pltpu.SemaphoreType.DMA((3,)),
            pltpu.SemaphoreType.DMA((3,)),
        ],
        compiler_params=comm_params(2),
    )(dkv)


def accumulate(total, other):
    total[...] = total[...] + other[...]


class Reduction:
    def __init__(self, at, make, order, start, size, ref, one, other, bufs, total):
        depth, near = at.depth, at.depth // 2
        half = ref.shape[3] // 2
        self.at, self.near, self.one, self.other, self.order = at, near, one, other, order

        def lanes_of(x):
            return pl.ds(pl.multiple_of(x * half + start, 128), size)

        self.lanes, self.both = lanes_of(at.x), [lanes_of(x) for x in range(2)]
        self.total = total.at[:, pl.ds(start, size)]
        far = lanes_of(1 - at.x)
        upper = depth - near
        if order == "mixed":
            two_x, two_y, three, four = bufs
            self.two_x, self.two_y = two_x, two_y
            low, high = pl.ds(0, near), pl.ds(near, upper)
            self.first = [make(one.at[low, :, :, far], two_x, at.across_x)] + [
                make(one.at[high, 1 - at.y, :, self.both[x]], two_y.at[x], at.across_y)
                for x in range(2)
            ]
            self.second = [
                make(two_x.at[:, 1 - at.y], three.at[low], at.across_y),
                make(two_y.at[1 - at.x], three.at[high], at.across_x),
            ]
        else:
            two, three, four = bufs
            self.two = two
            self.first = [
                make(one.at[:, 1 - at.y, :, self.both[x]], two.at[x], at.across_y)
                for x in range(2)
            ]
            self.second = [make(two.at[1 - at.x], three, at.across_x)]
        self.three, self.four = three, four
        self.third = [
            make(three.at[z], four.at[k], peer) for k, (peer, z) in enumerate(at.z_peers)
        ]

    def step_one(self):
        for lanes in self.both:

            @pl.loop(0, 2 * self.at.depth)
            def _(j):
                accumulate(
                    self.one.at[j // 2, j % 2, :, lanes],
                    self.other.at[j // 2, j % 2, :, lanes],
                )

        for copy in self.first:
            copy.start()

    def step_two(self):
        at = self.at
        if self.order == "mixed":
            self.first[0].wait_recv()

            @pl.loop(0, 2 * self.near)
            def _(j):
                accumulate(
                    self.two_x.at[j // 2, j % 2], self.one.at[j // 2, j % 2, :, self.lanes]
                )

            self.second[0].start()
            for x in range(2):
                self.first[1 + x].wait_recv()

                @pl.loop(0, at.depth - self.near)
                def _(j):
                    accumulate(
                        self.two_y.at[x, j], self.one.at[self.near + j, at.y, :, self.both[x]]
                    )

            self.second[1].start()
        else:
            for x in range(2):
                self.first[x].wait_recv()

                @pl.loop(0, at.depth)
                def _(j):
                    accumulate(self.two.at[x, j], self.one.at[j, at.y, :, self.both[x]])

            self.second[0].start()

    def step_three(self):
        at = self.at
        for copy in self.second:
            copy.wait_recv()
        if self.order == "mixed":

            @pl.loop(0, self.near)
            def _(j):
                accumulate(self.three.at[j], self.two_x.at[j, at.y])

            @pl.loop(0, at.depth - self.near)
            def _(j):
                accumulate(self.three.at[self.near + j], self.two_y.at[at.x, j])

        else:

            @pl.loop(0, at.depth)
            def _(j):
                accumulate(self.three.at[j], self.two.at[at.x, j])

        for copy in self.third:
            copy.start()

    def step_four(self):
        for copy in self.third:
            copy.wait_recv()
        total = self.three[self.at.z].astype(F)
        for k in range(len(self.third)):
            total = total + self.four[k].astype(F)
        self.total[...] = total

    def end(self):
        for copy in self.first + self.second + self.third:
            copy.wait_send()


def reduction_buffers(order, depth, rows, size):
    near = depth // 2
    if order == "mixed":
        first = [(near, 2, rows, size), (2, depth - near, rows, size)]
    else:
        first = [(2, depth, rows, size)]
    return [pltpu.VMEM(s, BF) for s in first + [(depth, rows, size), (depth - 1, rows, size)]]


BACK_ORDERS = (
    (("mixed", 1), ("mixed", 1)),
    (("mixed", 1), ("mixed", 1), ("mixed", 1)),
    (("mixed", 1),),
    (("mixed", 2), ("yx", 1)),
)


def lane_parts(orders, half):
    unit = half // sum(share for _, share in orders)
    parts, start = [], 0
    for order, share in orders:
        parts.append((order, start, share * unit))
        start += share * unit
    return parts


def back_kernel(
    images, bands, scalars_ref, q_ref, delta_ref, lse_ref, datt_ref, cols_ref, sums_ref,
    kv_in, x_in, x_far_in, h_in, dmid_in, w_in, g_out_ref, g_up_ref, g_down_ref,
    gx_ref, p_qkv_ref, p_out_ref, p_up_ref, p_down_ref, total_ref,
    kv_ref, x_ref, x_far_ref, h_ref, dmid_ref, w_ref,
    bias_ref, dq_ref, dwide_ref, dkv_ref, near_ref, g_qkv_ref, err_ref, err_far_ref, err_in_ref,
    small_ref, small_in_ref, small_z_ref, *rest,
):
    at = Place(images)
    depth = at.depth
    local_sem, send_sem, recv_sem = rest[-3:]
    rest = list(rest[:-3])
    used = [0, 0]

    def make(src, dst, peer):
        k = used[0]
        used[0] += 1
        return pltpu.make_async_remote_copy(
            src_ref=src,
            dst_ref=dst,
            send_sem=send_sem.at[k],
            recv_sem=recv_sem.at[k],
            device_id=peer,
            device_id_type=MESH,
        )

    def load(src, dst):
        used[1] += 1
        return pltpu.make_async_copy(src, dst, local_sem.at[used[1] - 1])

    width, tokens = x_ref.shape
    rows = tokens // 2
    unroll = 4
    groups = HEADS // unroll
    part = width // groups

    def four_d(ref):
        return ref.reshape(depth, 2, ref.shape[0] // images, ref.shape[1])

    sources = (four_d(g_down_ref), four_d(g_up_ref), four_d(g_out_ref), g_qkv_ref)
    targets = (p_down_ref, p_up_ref, p_out_ref, p_qkv_ref)
    swaps, owns, moves, ends = [], [], [], []
    for m in range(4):
        one, total, away = rest[:3]
        rest = rest[3:]
        block, lanes = sources[m].shape[2] // 2, sources[m].shape[3]
        near_rows = pl.ds(pl.multiple_of(at.c * block, 16), block)
        far_rows = pl.ds(pl.multiple_of((1 - at.c) * block, 16), block)
        parts = lane_parts(BACK_ORDERS[m], lanes // 2)
        if m < 3:
            other = rest.pop(0)
            owns.append(load(sources[m].at[:, :, near_rows, :], one))
            swaps.append([make(sources[m].at[:, :, far_rows, :], other, at.partner)])
        else:
            other = sources[m].at[:, :, near_rows, :]
            for _, start, size in parts:
                both = [pl.ds(x * (lanes // 2) + start, size) for x in range(2)]
                swaps.append(
                    [
                        make(sources[m].at[:, :, far_rows, l], one.at[:, :, :, l], at.partner)
                        for l in both
                    ]
                )
        moves.append([])
        for order, start, size in parts:
            count = 4 if order == "mixed" else 3
            moves[m].append(
                Reduction(
                    at, make, order, start, size, sources[m], one, other, rest[:count], total
                )
            )
            rest = rest[count:]
        ends.append((total, away, targets[m], make(away, targets[m].at[at.c], at.partner)))
    down, up, out, qkv = moves

    def deliver(m):
        total_ref, away, target, copy = ends[m]
        total = total_ref[...]
        size = total.shape[1] // 2
        low, high = total[:, :size], total[:, size:]
        target[at.c] = jnp.where(at.c == 0, low, high)
        away[...] = jnp.where(at.c == 0, high, low)
        copy.start()

    mate, far = at.partner[1], at.across_x[1]
    far_mate = at.across_x[1] + 1 - 2 * at.c
    one = [make(dkv_ref.at[far_mate, g], near_ref.at[0, g], at.partner) for g in range(groups)]
    two = [make(dkv_ref.at[mate, g], near_ref.at[1, g], at.partner) for g in range(groups)]
    err_moves = [make(err_far_ref.at[s], err_in_ref.at[s], at.across_x) for s in range(2)]
    small_steps = [
        make(small_ref.at[k], small_in_ref.at[k], peer)
        for k, peer in enumerate((at.partner, at.across_x, at.across_y))
    ]
    small_last = [
        make(small_z_ref.at[at.z], small_z_ref.at[at.z], peer) for peer, _ in at.z_peers
    ]

    kv_loads = [load(kv_in.at[:, g], kv_ref.at[:, g]) for g in range(groups)]
    late_loads = [
        load(h_in, h_ref),
        load(w_in, w_ref),
        load(x_in, x_ref),
        load(x_far_in, x_far_ref),
        load(dmid_in, dmid_ref),
    ]
    kv_loads[0].start()
    owns[0].start()
    greet([at.partner, at.across_x, at.across_y] + [peer for peer, _ in at.z_peers])
    for m in range(3):
        swaps[m][0].start()
    for copy in owns[1:] + kv_loads[1:] + late_loads:
        copy.start()
    fill_bias(scalars_ref, bias_ref, rows)

    sides = [pl.ds(side * tokens, tokens) for side in range(2)]

    def share_one(g):
        one[g].start()
        two[g].start()

    def share_two(g):
        for copy, side, band in ((one[g], 1, far), (two[g], 0, at.band)):
            copy.wait_recv()
            for half in range(2):
                block = pl.ds(half * part, part)
                to = pl.ds(half * width + g * part, part)
                value = (
                    near_ref[1 - side, g, block, :].astype(F)
                    + dkv_ref[band, g, block, :].astype(F)
                ).astype(BF)
                dwide_ref[to, sides[side]] = value

    events = {}

    def when(j, *actions):
        events.setdefault(j, []).extend(actions)

    def received(m):
        owns[m].wait()
        swaps[m][0].wait_recv()

    for g in range(1, groups):
        when(2 * g - 1, kv_loads[g].wait)
    when(0, down[1].step_one)
    when(0, lambda: received(1), up[0].step_one)
    when(1, up[1].step_one, lambda: share_one(0))
    when(2, up[2].step_one, down[0].step_two, lambda: share_two(0))
    when(3, lambda: received(2), out[0].step_one, down[1].step_two, lambda: share_one(1))
    when(4, up[0].step_two, down[0].step_three, lambda: share_two(1))
    when(5, up[1].step_two, down[1].step_three, lambda: share_one(2))
    when(6, up[2].step_two, up[0].step_three, lambda: share_two(2))
    when(7, lambda: share_one(3), out[0].step_two, up[1].step_three)
    received(0)
    down[0].step_one()
    kv_loads[0].wait()

    @pl.loop(0, 2 * groups)
    def _(j):
        g, s = j // 2, j % 2
        lanes = pl.ds(pl.multiple_of(s * rows, rows), rows)
        for k in range(unroll):

            def put_key(b, values):
                dkv_ref[b, g, pl.ds(k * HEAD_DIM, HEAD_DIM), lanes] = values

            def put_value(b, values):
                dkv_ref[b, g, pl.ds(part + k * HEAD_DIM, HEAD_DIM), lanes] = values

            attend_back_step(
                s * HEADS + g * unroll + k,
                at.x, q_ref, kv_ref, delta_ref, lse_ref, datt_ref, bias_ref, dq_ref,
                put_key, put_value,
            )
        for when_j, actions in events.items():

            @pl.when(j == when_j)
            def _():
                for action in actions:
                    action()

    chunk = width // 2
    g_flat = g_qkv_ref.reshape(3 * width, width)
    parts = lane_parts(BACK_ORDERS[3], width // 2)

    def weight_grad(part, source_ref, first, count, tokens_at):
        _, start, size = parts[part]
        lanes = [pl.ds(x * (width // 2) + start, size) for x in range(2)]

        @pl.loop(0, count)
        def _(j):
            block = pl.ds(pl.multiple_of(j * chunk, 128), chunk)
            to = pl.ds(pl.multiple_of((first + j) * chunk, 128), chunk)
            both = jnp.concatenate([h_ref[l, tokens_at] for l in lanes], axis=0)
            result = dg(source_ref[block, :], both, 1, 1).astype(BF)
            g_flat[to, lanes[0]] = result[:, :size]
            g_flat[to, lanes[1]] = result[:, size:]

    def back_through(side):
        err_ref[...] = jnp.zeros_like(err_ref)

        @pl.loop(0, 4)
        def _(j):
            block = pl.ds(pl.multiple_of(j * chunk, 128), chunk)
            source = pl.ds(pl.multiple_of((2 + j) * chunk, 128), chunk)
            err_ref[...] += dg(w_ref[source, :], dwide_ref[block, sides[side]], 0, 0)

    def start_swap(part):
        for copy in swaps[3 + part]:
            copy.start()

    def first_sum(part):
        for copy in swaps[3 + part]:
            copy.wait_recv()
        qkv[part].step_one()

    for copy in late_loads:
        copy.wait()
    for p in range(2):
        weight_grad(p, dq_ref, 0, 2, sides[0])
    share_two(groups - 1)
    weight_grad(0, dwide_ref, 2, 4, slice(None))
    start_swap(0)
    back_through(1)
    err_far = err_ref[...]
    for s in range(2):
        err_far_ref[s] = err_far[:, s * rows : (s + 1) * rows].astype(BF)
    first_sum(0)
    err_moves[0].start()
    weight_grad(1, dwide_ref, 2, 4, slice(None))
    start_swap(1)
    normed_far, _ = normalize(x_far_ref[...].astype(F))
    gain_row = row_sums(err_ref[...] * normed_far)[:1]
    shift_row = row_sums(err_ref[...])[:1]
    first_sum(1)
    up[2].step_three()
    out[0].step_three()
    back_through(0)

    @pl.loop(0, 2)
    def _(j):
        block = pl.ds(pl.multiple_of(j * chunk, 128), chunk)
        err_ref[...] += dg(w_ref[block, :], dq_ref[block, :], 0, 0)

    small_ref[0] = sums_ref[...]
    small_ref[0, 0:1] = row_sums(dq_ref[...])[:1]
    small_ref[0, 1:2] = row_sums(dwide_ref[pl.ds(width, width), :])[:1]
    normed, _ = normalize(x_ref[...].astype(F))
    small_ref[0, 4:5] = gain_row + row_sums(err_ref[...] * normed)[:1]
    small_ref[0, 5:6] = shift_row + row_sums(err_ref[...])[:1]
    small_steps[0].start()
    qkv[0].step_two()
    err_moves[1].start()
    for item in down:
        item.step_four()
    deliver(0)
    small_steps[0].wait_recv()
    small_ref[1] = small_ref[0] + small_in_ref[0]
    small_steps[1].start()
    qkv[1].step_two()
    qkv[0].step_three()
    small_steps[1].wait_recv()
    small_ref[2] = small_ref[1] + small_in_ref[1]
    small_steps[2].start()
    for item in up:
        item.step_four()
    deliver(1)
    small_steps[2].wait_recv()
    small_z_ref[at.z] = small_ref[2] + small_in_ref[2]
    for copy in small_last:
        copy.start()
    out[0].step_four()
    deliver(2)
    qkv[1].step_three()

    def finish_slot(s):
        err_moves[s].wait_recv()
        lanes = slice(s * rows, (s + 1) * rows)
        err = err_ref[:, lanes] + err_in_ref[s].astype(F)
        normed, inverse = normalize(x_ref[:, lanes].astype(F))
        gx_ref[:, lanes] = (
            dmid_ref[:, lanes] + norm_back(err, normed, inverse, cols_ref[:, GAIN_ONE])
        ).astype(BF)

    finish_slot(0)
    qkv[0].step_four()
    for copy in small_last:
        copy.wait_recv()
    total = small_z_ref[0]
    for k in range(1, depth):
        total = total + small_z_ref[k]
    total_ref[...] = total
    qkv[1].step_four()
    deliver(3)
    finish_slot(1)
    for m in range(4):
        ends[m][3].wait()
        for item in moves[m]:
            item.end()
    for copy in sum(swaps, []) + one + two + err_moves + small_steps + small_last:
        copy.wait_send()


def back(
    images, bands, scalars, q, kv, delta, lse, datt, x, x_far, h, dmid, w, cols, grads, sums
):
    depth = images // 2
    width, tokens = x.shape
    g_out, g_up, g_down = grads
    groups = HEADS // 4
    results, buffers = [], []
    for m, item in enumerate((g_down, g_up, g_out, w)):
        block, lanes = item.shape[0] // images // 2, item.shape[1]
        results.append(shape((2, block, lanes // 4), F))
        buffers += [
            pltpu.VMEM((depth, 2, block, lanes), BF),
            pltpu.VMEM((block, lanes // 2), F),
            pltpu.VMEM((block, lanes // 4), F),
        ]
        if m < 3:
            buffers.append(pltpu.VMEM((depth, 2, block, lanes), BF))
        for order, _, size in lane_parts(BACK_ORDERS[m], lanes // 2):
            buffers += reduction_buffers(order, depth, block, size)
    small = (SUM_ROWS, width)
    return pl.pallas_call(
        functools.partial(back_kernel, images, bands),
        name="back",
        out_shape=(shape(x.shape, BF), results[3], results[2], results[1], results[0], shape(small, F)),
        in_specs=[SM] + [VM] * 6 + [ANY] * 9,
        out_specs=(VM,) * 6,
        scratch_shapes=[
            pltpu.VMEM(kv.shape, BF),
            pltpu.VMEM((width, tokens), BF),
            pltpu.VMEM((width, tokens), BF),
            pltpu.VMEM((width, 2 * tokens), BF),
            pltpu.VMEM((width, tokens), F),
            pltpu.VMEM(w.shape, BF),
            pltpu.VMEM((8, tokens // 2), F),
            pltpu.VMEM((width, tokens), BF),
            pltpu.VMEM((2 * width, 2 * tokens), BF),
            pltpu.VMEM((bands, groups, 2 * width // groups, tokens), BF),
            pltpu.VMEM((2, groups, 2 * width // groups, tokens), BF),
            pltpu.VMEM((depth, 2, w.shape[0] // images, width), BF),
            pltpu.VMEM((width, tokens), F),
            pltpu.VMEM((2, width, tokens // 2), BF),
            pltpu.VMEM((2, width, tokens // 2), BF),
            pltpu.VMEM((3,) + small, F),
            pltpu.VMEM((3,) + small, F),
            pltpu.VMEM((depth,) + small, F),
        ]
        + buffers
        + [
            pltpu.SemaphoreType.DMA((16,)),
            pltpu.SemaphoreType.DMA((BACK_COPIES,)),
            pltpu.SemaphoreType.DMA((BACK_COPIES,)),
        ],
        compiler_params=comm_params(3),
    )(
        scalars, q, delta, lse, datt, cols, sums, kv, x, x_far, h, dmid, w, g_out, g_up, g_down
    )


def body(
    tokens,
    slot_kind,
    w_qkv,
    w_out,
    w_up,
    w_down,
    bias_qv,
    bias_out,
    bias_up,
    bias_down,
    gain_one,
    shift_one,
    gain_two,
    shift_two,
    cotangent,
):
    rows, slots, width = tokens.shape[1:]
    count = rows * slots
    images, bands = lax.axis_size("img"), lax.axis_size("band")
    band = lax.axis_index("band")
    smalls = (bias_qv, bias_out, bias_up, bias_down, gain_one, shift_one, gain_two, shift_two)
    sizes = [item.shape[0] for item in smalls]
    own = (w_qkv, w_out, w_up)
    widths = [item.shape[1] for item in own]
    direct = images % 4 == 0 and all(w % 32 == 0 for w in widths + [w_down.shape[1]])
    direct = direct and bias_qv.shape[0] == 2 * (width // images) <= 256
    direct = direct and bias_up.shape[0] == 4 * (width // images)

    def turn(values):
        return values[0].transpose(2, 1, 0).reshape(width, count)

    def turn_back(values):
        return values.reshape(width, slots, rows).transpose(2, 1, 0)[None]

    x, cot = turn(tokens), turn(cotangent)
    kinds = slot_kind[0].astype(jnp.int32)
    scalars = jnp.concatenate([kinds, (band // 2).astype(jnp.int32)[None]])
    single = (bias_out, bias_down, gain_one, shift_one, gain_two, shift_two)
    if direct:
        narrow = split_rows([item.T for item in own], 2)
        unit = width // images
        units = [jnp.stack(single), jnp.zeros((4, unit), BF)]
        units += [bias_qv.reshape(2, unit), bias_up.reshape(4, unit)]
        small = jnp.pad(jnp.concatenate(units), ((0, 0), (0, 128 - unit))).astype(F)
        full_qkv, h, all_kv, x_far, q, lse, cols, *rest = front(
            images, bands, scalars, narrow, w_down.T, small, x, cot, widths
        )
        full_qkv = full_qkv.reshape(-1, width)
    else:
        full_qkv, full_out, full_up, full_down = (
            lax.all_gather(lax.all_gather(item, "band", axis=0, tiled=True).T, "img", tiled=True)
            for item in (*own, w_down)
        )
        whole = [lax.all_gather(item, "img", tiled=True).astype(F) for item in single]
        cols = jnp.stack(whole + [whole[0]] * (COLUMNS - len(whole)), axis=1)
        c_qv = lax.all_gather(bias_qv, "img", tiled=True).astype(F)[:, None]
        c_up = lax.all_gather(bias_up, "img", tiled=True).astype(F)[:, None]
        bias = jnp.concatenate([c_qv[:width], jnp.zeros((width, 1), F), c_qv[width:]])
        h, qkv = project(x, full_qkv, cols, bias)
        q = qkv[:width]
        all_kv = share(images, bands, qkv[width:])
        all_kv = all_kv.reshape(bands, 2, GROUPS_OF_HEADS, -1, count).transpose(0, 2, 1, 3, 4)
        all_kv = all_kv.reshape(bands, GROUPS_OF_HEADS, -1, count)
        att, lse = attend(scalars, q, all_kv)
        rest = middle(x, cot, scalars, att, full_out, full_up, full_down, cols, c_up)
    out, dmid, datt, delta, g_out, g_up, g_down, sums = rest
    if direct:
        gx, *pieces, total = back(
            images, bands, scalars, q, all_kv, delta, lse, datt, x, x_far, h, dmid,
            full_qkv, cols, (g_out, g_up, g_down), sums,
        )
        matrices = [item.reshape(-1, item.shape[2]).T for item in pieces]
    else:
        dq, dkv = attend_back(scalars, q, all_kv, delta, lse, datt)
        dkv = unshare(images, dkv)
        gx, g_qkv, sums_one = finish(x, h, dq, dkv, full_qkv, cols, dmid)
        matrices = [
            lax.psum_scatter(
                lax.psum_scatter(item, "img", scatter_dimension=0, tiled=True),
                "band",
                scatter_dimension=1,
                tiled=True,
            )
            .astype(F)
            .T
            for item in (g_qkv, g_out, g_up, g_down)
        ]
        total = lax.psum(sums + sums_one, ("img", "band"))
    own_small = lax.axis_index("img")
    flat = total.reshape(-1)
    starts = [0, 2, UP_ROW, 3, 4, 5, 6, 7]
    small = [
        lax.dynamic_slice(flat, (start * width + own_small * size,), (size,))
        for start, size in zip(starts, sizes)
    ]
    return (turn_back(out), turn_back(gx), *matrices, *small)


def solution(mesh):
    data, weight, vector = P("img", "band", None, None), P("band", "img"), P("img")
    return jax.shard_map(
        body,
        mesh=mesh,
        in_specs=(data, P("img", None)) + (weight,) * 4 + (vector,) * 8 + (data,),
        out_specs=(data, data) + (weight,) * 4 + (vector,) * 8,
        check_vma=False,
    )
```

```python
import functools
import math

import jax
import jax.numpy as jnp
from jax import lax
from jax.experimental import pallas as pl
from jax.experimental.pallas import tpu as pltpu
from jax.sharding import PartitionSpec as P

HEADS = 16
HEAD_DIM = 48
EPSILON = 1e-06
MASKED = -1e30
BF = jnp.bfloat16
F = jnp.float32
MESH = pl.DeviceIdType.MESH
VM = pl.BlockSpec(memory_space=pltpu.VMEM)
SM = pl.BlockSpec(memory_space=pltpu.SMEM)
ANY = pl.BlockSpec(memory_space=pl.ANY)
LIMIT = 67043328
SUM_ROWS, UP_ROW = 16, 8
COLUMNS = 10
BIAS_OUT, BIAS_DOWN, GAIN_ONE, SHIFT_ONE, GAIN_TWO, SHIFT_TWO = (slice(k, k + 1) for k in range(6))
GROUPS_OF_HEADS = 4
FRONT_COPIES, BACK_COPIES = 128, 128


def dg(left, right, left_dim, right_dim):
    return lax.dot_general(
        left, right, (((left_dim,), (right_dim,)), ((), ())), preferred_element_type=F
    )


def shape(dims, dtype):
    return jax.ShapeDtypeStruct(tuple(dims), dtype)


def row_sums(values):
    ones = jnp.ones((8, values.shape[1]), BF)
    if values.dtype == BF:
        return dg(ones, values, 1, 1)
    high = values.astype(BF)
    low = (values - high.astype(F)).astype(BF)
    return dg(ones, high, 1, 1) + dg(ones, low, 1, 1)


def normalize(values):
    average = jnp.mean(values, axis=0, keepdims=True)
    centered = values - average
    variance = jnp.mean(centered * centered, axis=0, keepdims=True)
    inverse = lax.rsqrt(variance + EPSILON)
    return centered * inverse, inverse


def norm_back(error, normed, inverse, gain):
    f = gain * error
    mean_f = jnp.mean(f, axis=0, keepdims=True)
    mean_fn = jnp.mean(f * normed, axis=0, keepdims=True)
    return (f - mean_f - normed * mean_fn) * inverse


def project_kernel(x_ref, w_ref, cols_ref, bias_ref, h_ref, qkv_ref):
    width = x_ref.shape[0]
    normed, _ = normalize(x_ref[...].astype(F))
    h_ref[...] = (normed * cols_ref[:, GAIN_ONE] + cols_ref[:, SHIFT_ONE]).astype(BF)
    scale = 1.0 / math.sqrt(HEAD_DIM)
    step = 256

    @pl.loop(0, 3 * width // step)
    def _(j):
        rows = pl.ds(pl.multiple_of(j * step, step), step)
        out = dg(w_ref[rows, :], h_ref[...], 1, 0) + bias_ref[rows, :]
        qkv_ref[rows, :] = (out * jnp.where(j < width // step, scale, 1.0)).astype(BF)


def project(x, w, cols, bias):
    width, tokens = x.shape
    return pl.pallas_call(
        project_kernel,
        name="project",
        out_shape=(shape((width, tokens), BF), shape((3 * width, tokens), BF)),
        in_specs=[VM] * 4,
        out_specs=(VM, VM),
        compiler_params=pltpu.CompilerParams(vmem_limit_bytes=LIMIT),
    )(x, w, cols, bias)


def fill_bias(scalars_ref, bias_ref, rows):
    lane_half = lax.broadcasted_iota(jnp.int32, (1, rows), 1) // (rows // 2)
    for s in range(2):
        small = scalars_ref[0, s] == 2
        for other in range(2):
            for half in range(2):
                keep = jnp.logical_and(other == 0, lane_half == half)
                masked = jnp.where(small, MASKED, 0.0)
                bias_ref[pl.ds(4 * s + 2 * other + half, 1), :] = jnp.where(
                    keep, jnp.zeros((1, rows), F), jnp.full((1, rows), masked, F)
                )


def add_bias(scores, bias_ref, s, other):
    rows = scores.shape[0]
    at = 4 * s + 2 * other
    return jnp.concatenate(
        [
            scores[: rows // 2] + bias_ref[pl.ds(at, 1), :],
            scores[rows // 2 :] + bias_ref[pl.ds(at + 1, 1), :],
        ],
        axis=0,
    )


def head_slices(i, rows):
    s, h = i // HEADS, i % HEADS
    lanes = pl.ds(pl.multiple_of(s * rows, rows), rows)
    first = pl.ds(pl.multiple_of(h * HEAD_DIM, 16), HEAD_DIM)
    second = pl.ds(pl.multiple_of(HEADS * HEAD_DIM + h * HEAD_DIM, 16), HEAD_DIM)
    return s, lanes, first, second


def attend_step(i, chip_x, q_ref, kv_ref, bias_ref, out_ref, lse_ref):
    bands = kv_ref.shape[0]
    rows = q_ref.shape[1] // 2
    s, lanes, first, second = head_slices(i, rows)
    q = q_ref[first, lanes]
    scores = []
    maximum = None
    for b in range(bands):
        other = jnp.where(chip_x == b // 2, 0, 1)
        keys, _ = kv_rows(kv_ref, b, i % HEADS)
        part = add_bias(dg(keys[:, lanes], q, 0, 0), bias_ref, s, other)
        scores.append(part)
        top = jnp.max(part, axis=0, keepdims=True)
        maximum = top if maximum is None else jnp.maximum(maximum, top)
    total, acc = 0.0, 0.0
    for b in range(bands):
        weight = jnp.exp(scores[b] - maximum)
        total = total + jnp.sum(weight, axis=0, keepdims=True)
        _, values = kv_rows(kv_ref, b, i % HEADS)
        acc = acc + dg(values[:, lanes], weight.astype(BF), 1, 0)
    out_ref[first, lanes] = acc / total
    lse_ref[pl.ds(i, 1), :] = maximum + jnp.log(total)


def attend_kernel(unroll, scalars_ref, q_ref, kv_ref, out_ref, lse_ref, bias_ref):
    fill_bias(scalars_ref, bias_ref, q_ref.shape[1] // 2)

    @pl.loop(0, 2 * HEADS // unroll)
    def _(j):
        for k in range(unroll):
            attend_step(
                j * unroll + k, scalars_ref[0, 2], q_ref, kv_ref, bias_ref, out_ref, lse_ref
            )


def attend(scalars, q, kv):
    width, tokens = q.shape
    return pl.pallas_call(
        functools.partial(attend_kernel, 4),
        name="attend",
        out_shape=(shape((width, tokens), F), shape((2 * HEADS, tokens // 2), F)),
        in_specs=[SM, VM, VM],
        out_specs=(VM, VM),
        scratch_shapes=[pltpu.VMEM((8, tokens // 2), F)],
        compiler_params=pltpu.CompilerParams(vmem_limit_bytes=LIMIT),
    )(scalars, q, kv)


def attend_back_step(
    i, chip_x, q_ref, kv_ref, delta_ref, lse_ref, dout_ref, bias_ref, dq_ref, put_key, put_value
):
    bands = kv_ref.shape[0]
    rows = q_ref.shape[1] // 2
    s, lanes, first, second = head_slices(i, rows)
    q = q_ref[first, lanes]
    dout = dout_ref[first, lanes]
    delta = delta_ref[pl.ds(i % HEADS, 1), lanes]
    lse = lse_ref[pl.ds(i, 1), :]
    dq = 0.0
    for b in range(bands):
        other = jnp.where(chip_x == b // 2, 0, 1)
        k, v = (ref[:, lanes] for ref in kv_rows(kv_ref, b, i % HEADS))
        scores = add_bias(dg(k, q, 0, 0), bias_ref, s, other)
        dweight = dg(v, dout, 0, 0)
        weight = jnp.exp(scores - lse)
        dscores = (weight * (dweight - delta)).astype(BF)
        dq = dq + dg(k, dscores, 1, 0)
        put_key(b, dg(q, dscores, 1, 1).astype(BF))
        put_value(b, dg(dout, weight.astype(BF), 1, 1).astype(BF))
    dq_ref[first, lanes] = (dq * (1.0 / math.sqrt(HEAD_DIM))).astype(BF)


def attend_back_kernel(
    unroll, scalars_ref, q_ref, kv_ref, delta_ref, lse_ref, dout_ref, dq_ref, dkv_ref, bias_ref
):
    fill_bias(scalars_ref, bias_ref, q_ref.shape[1] // 2)

    @pl.loop(0, 2 * HEADS // unroll)
    def _(j):
        for k in range(unroll):
            i = j * unroll + k
            _, lanes, first, second = head_slices(i, q_ref.shape[1] // 2)

            def put_key(b, values):
                dkv_ref[b, first, lanes] = values

            def put_value(b, values):
                dkv_ref[b, second, lanes] = values

            attend_back_step(
                i, scalars_ref[0, 2], q_ref, kv_ref, delta_ref, lse_ref, dout_ref, bias_ref, dq_ref,
                put_key, put_value,
            )


def attend_back(scalars, q, kv, delta, lse, dout):
    return pl.pallas_call(
        functools.partial(attend_back_kernel, 4),
        name="attend_back",
        out_shape=(shape(q.shape, BF), shape((kv.shape[0], 2 * q.shape[0], q.shape[1]), BF)),
        in_specs=[SM] + [VM] * 5,
        out_specs=(VM, VM),
        scratch_shapes=[pltpu.VMEM((8, q.shape[1] // 2), F)],
        compiler_params=pltpu.CompilerParams(vmem_limit_bytes=LIMIT),
    )(scalars, q, kv, delta, lse, dout)


def middle_body(
    x_ref, cot_ref, scalars_ref, att_ref, w_out_ref, w_up_ref, w_down_ref, cols_ref, bias_up_ref,
    out_ref, dmid_ref, datt_ref, delta_ref, g_out_ref, g_up_out, g_down_out, sums_ref,
    g_up_ref, g_down_ref,
    mid_ref, norm_ref, h_ref, dmlp_ref, mlp_ref, err_ref, attb_ref, dbranch_ref,
    up_sem, down_sem, wait_out, wait_up, passes,
):
    width, tokens = x_ref.shape
    hidden = w_up_ref.shape[0]
    step = 256
    first_slot = lax.broadcasted_iota(jnp.int32, (1, tokens), 1) < tokens // 2
    valid = jnp.where(
        first_slot,
        jnp.where(scalars_ref[0, 0] > 0, 1.0, 0.0),
        jnp.where(scalars_ref[0, 1] > 0, 1.0, 0.0),
    )
    attb_ref[...] = att_ref[...].astype(BF)
    dmlp_ref[...] = (cot_ref[...].astype(F) * valid).astype(BF)
    sums_ref[...] = jnp.zeros_like(sums_ref)
    mlp_ref[...] = jnp.zeros_like(mlp_ref)
    err_ref[...] = jnp.zeros_like(err_ref)
    wait_out()

    @pl.loop(0, width // step)
    def _(j):
        rows = pl.ds(pl.multiple_of(j * step, step), step)
        mid_ref[rows, :] = (
            dg(w_out_ref[rows, :], attb_ref[...], 1, 0)
            + cols_ref[rows, BIAS_OUT]
            + x_ref[rows, :].astype(F)
        )

    normed, inverse = normalize(mid_ref[...])
    norm_ref[...] = normed
    h_ref[...] = (normed * cols_ref[:, GAIN_TWO] + cols_ref[:, SHIFT_TWO]).astype(BF)
    wait_up()

    def stores(j):
        rows = pl.ds(pl.multiple_of(j * step, step), step)
        return (
            pltpu.make_async_copy(g_up_ref.at[rows, :], g_up_out.at[rows, :], up_sem.at[j]),
            pltpu.make_async_copy(g_down_ref.at[:, rows], g_down_out.at[:, rows], down_sem.at[j]),
        )

    def block(j):
        rows = pl.ds(pl.multiple_of(j * step, step), step)
        pre = dg(w_up_ref[rows, :], h_ref[...], 1, 0) + bias_up_ref[rows, :]
        phi = 0.5 + 0.5 * lax.erf(pre * math.sqrt(0.5))
        act = (pre * phi).astype(BF)
        slope = phi + pre * jnp.exp(pre * pre * -0.5) * (1.0 / math.sqrt(2.0 * math.pi))
        mlp_ref[...] += dg(w_down_ref[:, rows], act, 1, 0)
        dact = dg(w_down_ref[:, rows], dmlp_ref[...], 0, 0)
        dhid = (slope * dact).astype(BF)
        g_down_ref[:, rows] = dg(dmlp_ref[...], act, 1, 1).astype(BF)
        g_up_ref[rows, :] = dg(dhid, h_ref[...], 1, 1).astype(BF)
        per = width // step
        lanes = pl.ds(pl.multiple_of(j % per * step, step), step)
        sums_ref[pl.ds(UP_ROW + j // per, 1), lanes] = row_sums(dhid)[:1]
        err_ref[...] += dg(w_up_ref[rows, :], dhid, 0, 0)
        for copy in stores(j):
            copy.start()

    for wait, count, place in passes:
        wait()

        @pl.loop(0, count)
        def _(t):
            block(place(t))

    out = (mid_ref[...] + mlp_ref[...] + cols_ref[:, BIAS_DOWN]) * valid
    out_ref[...] = out.T.astype(BF)
    err = err_ref[...]
    sums_ref[3:4] = row_sums(dmlp_ref[...])[:1]
    sums_ref[6:7] = row_sums(err * norm_ref[...])[:1]
    sums_ref[7:8] = row_sums(err)[:1]
    dmid = cot_ref[...].astype(F) * valid + norm_back(
        err, norm_ref[...], inverse, cols_ref[:, GAIN_TWO]
    )
    dmid_ref[...] = dmid
    dbranch_ref[...] = dmid.astype(BF)
    sums_ref[2:3] = row_sums(dbranch_ref[...])[:1]
    datt_ref[...] = dg(w_out_ref[...], dbranch_ref[...], 0, 0).astype(BF)
    inner = att_ref[...] * datt_ref[...].astype(F)
    delta_ref[...] = jnp.sum(inner.reshape(HEADS, width // HEADS, tokens), axis=1)

    @pl.loop(0, width // step)
    def _(j):
        rows = pl.ds(pl.multiple_of(j * step, step), step)
        g_out_ref[rows, :] = dg(dbranch_ref[rows, :], attb_ref[...], 1, 1).astype(BF)

    @pl.loop(0, hidden // step)
    def _(j):
        for copy in stores(j):
            copy.wait()


def middle_kernel(*refs):
    x_ref, cot_ref, scalars_ref, att_ref, w_out_in, w_up_in, w_down_in = refs[:7]
    outputs = refs[7:17]
    w_out_ref, w_up_ref, w_down_ref = refs[17:20]
    scratch, in_sem = refs[20:30], refs[30]
    loads = [
        pltpu.make_async_copy(source, target, in_sem.at[k])
        for k, (source, target) in enumerate(
            ((w_out_in, w_out_ref), (w_up_in, w_up_ref), (w_down_in, w_down_ref))
        )
    ]
    for copy in loads:
        copy.start()
    middle_body(
        x_ref, cot_ref, scalars_ref, att_ref, w_out_ref, w_up_ref, w_down_ref, *outputs, *scratch,
        *refs[31:], loads[0].wait, loads[1].wait,
        [(loads[2].wait, w_up_ref.shape[0] // 256, lambda t: t)],
    )


def middle(x, cot, scalars, att, w_out, w_up, w_down, cols, bias_up):
    width, tokens = x.shape
    hidden = w_up.shape[0]
    full = (width, tokens)
    weights = [w_out.shape, w_up.shape, w_down.shape]
    return pl.pallas_call(
        middle_kernel,
        name="middle",
        out_shape=(
            shape((tokens, width), BF),
            shape(full, F),
            shape(full, BF),
            shape((HEADS, tokens), F),
            shape(w_out.shape, BF),
            shape(w_up.shape, BF),
            shape(w_down.shape, BF),
            shape((SUM_ROWS, width), F),
        ),
        in_specs=[VM, VM, SM, VM] + [ANY] * 3 + [VM] * 2,
        out_specs=(VM,) * 5 + (ANY, ANY, VM),
        scratch_shapes=[pltpu.VMEM(s, BF) for s in weights + weights[1:]]
        + [
            pltpu.VMEM(full, F),
            pltpu.VMEM(full, F),
            pltpu.VMEM(full, BF),
            pltpu.VMEM(full, BF),
            pltpu.VMEM(full, F),
            pltpu.VMEM(full, F),
            pltpu.VMEM(full, BF),
            pltpu.VMEM(full, BF),
            pltpu.SemaphoreType.DMA((3,)),
            pltpu.SemaphoreType.DMA((hidden // 256,)),
            pltpu.SemaphoreType.DMA((hidden // 256,)),
        ],
        compiler_params=pltpu.CompilerParams(vmem_limit_bytes=LIMIT),
    )(x, cot, scalars, att, w_out, w_up, w_down, cols, bias_up)


def finish_kernel(
    x_ref, h_ref, dq_ref, dkv_ref, w_ref, cols_ref, dmid_ref, gx_ref, g_ref, sums_ref, err_ref
):
    width, tokens = x_ref.shape
    step = 256
    blocks = width // step
    err_ref[...] = jnp.zeros_like(err_ref)
    for ref, count, base in ((dq_ref, blocks, 0), (dkv_ref, 2 * blocks, blocks)):

        @pl.loop(0, count)
        def _(j):
            rows = pl.ds(pl.multiple_of(j * step, step), step)
            to = pl.ds(pl.multiple_of((j + base) * step, step), step)
            g_ref[to, :] = dg(ref[rows, :], h_ref[...], 1, 1).astype(BF)
            err_ref[...] += dg(w_ref[to, :], ref[rows, :], 0, 0)

    normed, inverse = normalize(x_ref[...].astype(F))
    err = err_ref[...]
    sums_ref[...] = jnp.zeros_like(sums_ref)
    sums_ref[0:1] = row_sums(dq_ref[...])[:1]
    sums_ref[1:2] = row_sums(dkv_ref[pl.ds(width, width), :])[:1]
    sums_ref[4:5] = row_sums(err * normed)[:1]
    sums_ref[5:6] = row_sums(err)[:1]
    grad = dmid_ref[...] + norm_back(err, normed, inverse, cols_ref[:, GAIN_ONE])
    gx_ref[...] = grad.T.astype(BF)


def finish(x, h, dq, dkv, w, cols, dmid):
    width, tokens = x.shape
    return pl.pallas_call(
        finish_kernel,
        name="finish",
        out_shape=(shape((tokens, width), BF), shape(w.shape, BF), shape((SUM_ROWS, width), F)),
        in_specs=[VM] * 7,
        out_specs=(VM, VM, VM),
        scratch_shapes=[pltpu.VMEM(x.shape, F)],
        compiler_params=pltpu.CompilerParams(vmem_limit_bytes=LIMIT),
    )(x, h, dq, dkv, w, cols, dmid)


class Place:
    def __init__(self, images):
        self.images = images
        self.depth = images // 2
        self.img = lax.axis_index("img")
        self.band = lax.axis_index("band")
        self.z, self.y = self.img // 2, self.img % 2
        self.x, self.c = self.band // 2, self.band % 2
        self.partner = (self.img, self.band + 1 - 2 * self.c)
        self.across_x = (self.img, self.band + 2 - 4 * self.x)
        self.across_y = (self.img + 1 - 2 * self.y, self.band)
        self.z_peers = [self.along_z(k) for k in range(1, self.depth)]

    def along_z(self, k):
        z = lax.rem(self.z + k, self.depth)
        return (2 * z + self.y, self.band), z


def greet(peers):
    barrier = pltpu.get_barrier_semaphore()
    for peer in peers:
        pl.semaphore_signal(barrier, inc=1, device_id=peer, device_id_type=MESH)
    pl.semaphore_wait(barrier, len(peers))


def send(src, dst, send_sem, recv_sem, peer):
    copy = pltpu.make_async_remote_copy(
        src_ref=src,
        dst_ref=dst,
        send_sem=send_sem,
        recv_sem=recv_sem,
        device_id=peer,
        device_id_type=MESH,
    )
    copy.start()
    return copy


def comm_params(collective_id):
    return pltpu.CompilerParams(
        collective_id=collective_id, has_side_effects=True, vmem_limit_bytes=LIMIT
    )


class Spread:
    def __init__(self, at, make, order, part, parts, source, ref, local_sem):
        depth, near, c = at.depth, at.depth // 2, at.c
        rows, half = ref.shape[2] // 2, ref.shape[3] // 2
        rows = pl.ds(pl.multiple_of(c * rows, 16), rows)
        size = half // parts
        lanes = pl.ds(pl.multiple_of(at.x * half + part * size, 128), size)
        both = [pl.ds(x * half + part * size, size) for x in range(2)]
        if parts == 1:
            both = [slice(None)]
        low, high = pl.ds(0, near), pl.ds(near, depth - near)

        def same(index, peer):
            if len(index) == 4:
                return [make(ref.at[index], ref.at[index], peer)]
            return [make(ref.at[index + (l,)], ref.at[index + (l,)], peer) for l in both]

        piece = ref.at[at.z, at.y, rows, lanes]
        source = source.at[:, pl.ds(part * size, size)]
        self.keep = pltpu.make_async_copy(source, piece, local_sem)
        z_first = []
        if order != "xyz":
            z_first = [make(source, piece, peer) for peer, _ in at.z_peers]
        if order == "mixed":
            self.stages = [
                z_first,
                same((low, at.y, rows, lanes), at.across_x)
                + same((high, at.y, rows, lanes), at.across_y),
                same((low, at.y, rows), at.across_y)
                + same((high, slice(None), rows, lanes), at.across_x),
            ]
        elif order == "zxy":
            self.stages = [
                z_first,
                same((slice(None), at.y, rows, lanes), at.across_x),
                same((slice(None), at.y, rows), at.across_y),
            ]
        else:
            last = [same((at.z, slice(None), rows), peer) for peer, _ in at.z_peers]
            self.stages = [
                [make(source, piece, at.across_x)],
                same((at.z, at.y, rows), at.across_y),
                sum(last, []),
            ]
        self.stages.append(same((slice(None), slice(None), rows), at.partner))

    def start(self):
        self.keep.start()
        for copy in self.stages[0]:
            copy.start()

    def step(self, k):
        if k == 1:
            self.keep.wait()
        for copy in self.stages[k - 1]:
            copy.wait_recv()
        for copy in self.stages[k]:
            copy.start()

    def wait(self):
        for copy in self.stages[-1]:
            copy.wait_recv()

    def end(self):
        for stage in self.stages:
            for copy in stage:
                copy.wait_send()


def kv_rows(ref, b, h):
    part = ref.shape[2] // 2
    heads = part // HEAD_DIM
    first = pl.multiple_of(h % heads * HEAD_DIM, 16)
    second = pl.multiple_of(part + h % heads * HEAD_DIM, 16)
    at = ref.at[b, h // heads]
    return at.at[pl.ds(first, HEAD_DIM)], at.at[pl.ds(second, HEAD_DIM)]


def front_kernel(
    images, bands, scalars_ref, shard_qkv_ref, shard_out_ref, shard_up_ref, shard_down_ref,
    small_ref, tokens_ref, cot_tokens_ref,
    qkv_w_out, h_out, kv_out, x_out, x_far_out, q_ref, lse_ref, cols_ref, *rest,
):
    results, rest = rest[:8], rest[8:]
    narrow_ref, wide_ref, x_ref, cot_ref, far_tokens_ref = rest[:5]
    rest = rest[5:]
    qkv_w_ref, out_w_ref, up_w_ref, down_w_ref, h_ref, kv_ref, att_ref, up_col_ref = rest[:8]
    theirs_ref, mine_ref, mine_wide_ref, smalls_ref, qv_col_ref, bias_ref, x_far_ref = rest[8:15]
    local_sem, send_sem, recv_sem = rest[15:18]
    middle_scratch = rest[18:]
    at = Place(images)
    width, tokens = x_ref.shape
    rows = tokens // 2
    unit = width // images
    groups = kv_ref.shape[1]
    part = width // groups
    c = at.c
    used = [0, 0]

    def make(src, dst, peer):
        k = used[0]
        used[0] += 1
        return pltpu.make_async_remote_copy(
            src_ref=src,
            dst_ref=dst,
            send_sem=send_sem.at[k],
            recv_sem=recv_sem.at[k],
            device_id=peer,
            device_id_type=MESH,
        )

    def local():
        used[1] += 1
        return local_sem.at[used[1] - 1]

    others = [(lax.rem(at.img + k, images), at.band) for k in range(1, images)]
    half = wide_ref.shape[0] // 2
    wide = wide_ref.shape[1]
    own_lanes = pl.ds(pl.multiple_of(c * wide, 128), wide)
    own_wide = pltpu.make_async_copy(
        wide_ref.at[pl.ds(pl.multiple_of(c * half, 8), half), :],
        mine_wide_ref.at[:, own_lanes],
        local(),
    )
    swap = make(narrow_ref.at[1 - c], theirs_ref, at.partner)
    swap_wide = make(
        wide_ref.at[pl.ds(pl.multiple_of((1 - c) * half, 8), half), :],
        mine_wide_ref.at[:, own_lanes],
        at.partner,
    )
    lines = pl.ds(pl.multiple_of(at.img * 16, 16), 16)
    keep_small = pltpu.make_async_copy(small_ref, smalls_ref.at[lines, :], local())
    small_copies = [make(small_ref, smalls_ref.at[lines, :], peer) for peer in others]
    sources, row = [], 0
    for ref in (qkv_w_ref, out_w_ref, up_w_ref):
        count = ref.shape[2] // 2
        sources.append(mine_ref.at[pl.ds(row, count), :])
        row += count
    sources.append(mine_wide_ref)

    def spread(ref, source, orders):
        parts = len(orders)
        return [
            Spread(at, make, orders[k], k, parts, source, ref, local()) for k in range(parts)
        ]

    s_qkv = spread(qkv_w_ref, sources[0], ("mixed",) * 3)
    (s_out,) = spread(out_w_ref, sources[1], ("mixed",))
    s_up = spread(up_w_ref, sources[2], ("mixed", "mixed", "zxy"))
    d_one, d_two = spread(down_w_ref, sources[3], ("xyz", "mixed"))
    save_w = pltpu.make_async_copy(qkv_w_ref, qkv_w_out, local())
    save_h = pltpu.make_async_copy(h_ref, h_out, local())
    save_x = pltpu.make_async_copy(x_ref, x_out, local())
    save_far = pltpu.make_async_copy(x_far_ref, x_far_out, local())
    save_kv = [
        pltpu.make_async_copy(kv_ref.at[:, g], kv_out.at[:, g], local()) for g in range(groups)
    ]
    x_lanes = [pl.ds(s * rows, rows) for s in range(2)]
    x_moves = [make(tokens_ref.at[l], far_tokens_ref.at[l], at.across_x) for l in x_lanes]
    far = at.across_x[1]
    kv_moves = [
        [
            [
                make(kv_ref.at[b, g, :, x_lanes[s]], kv_ref.at[b, g, :, x_lanes[s]], at.partner)
                for b in (at.band, far)
            ]
            for g in range(groups)
        ]
        for s in range(2)
    ]

    row = 0
    for ref in (shard_qkv_ref, shard_out_ref, shard_up_ref):
        turned = ref[...].astype(F).T.astype(BF)
        count = turned.shape[0] // 2
        for core in range(2):
            narrow_ref[core, pl.ds(row, count), :] = turned[core * count : (core + 1) * count]
        row += count
    wide_ref[...] = shard_down_ref[...].astype(F).T.astype(BF)
    greet([at.partner, at.across_x] + others)
    x_moves[0].start()
    swap.start()
    own_wide.start()
    swap_wide.start()
    keep_small.start()
    for copy in small_copies:
        copy.start()
    fill_bias(scalars_ref, bias_ref, rows)
    swap.wait_recv()
    mine, theirs = narrow_ref[c], theirs_ref[...]
    lane_count = mine.shape[1]
    mine_ref[:, pl.ds(0, lane_count)] = jnp.where(c == 0, mine, theirs)
    mine_ref[:, pl.ds(lane_count, lane_count)] = jnp.where(c == 0, theirs, mine)
    for item in s_qkv:
        item.start()
    own_wide.wait()
    swap_wide.wait_recv()
    d_one.start()
    s_out.start()
    for item in s_up:
        item.start()
    d_two.start()

    for s in range(2):
        x_ref[:, x_lanes[s]] = tokens_ref[x_lanes[s], :].astype(F).T.astype(BF)
        cot_ref[:, x_lanes[s]] = cot_tokens_ref[x_lanes[s], :].astype(F).T.astype(BF)
    save_x.start()

    keep_small.wait()
    for copy in small_copies:
        copy.wait_recv()
    turned = smalls_ref[...].T
    qv_units, up_units = 2, up_w_ref.shape[2] // unit
    singles = 16 - qv_units - up_units
    for j in range(images):
        block = turned[:unit, 16 * j : 16 * j + 16]
        cols_ref[pl.ds(unit * j, unit), :] = block[:, :singles]
        for u in range(qv_units):
            lane = singles + u
            qv_col_ref[pl.ds(unit * (qv_units * j + u), unit), :] = block[:, lane : lane + 1]
        for u in range(up_units):
            lane = singles + qv_units + u
            up_col_ref[pl.ds(unit * (up_units * j + u), unit), :] = block[:, lane : lane + 1]

    def far_tokens(s):
        x_moves[s].wait_recv()
        x_far_ref[:, x_lanes[s]] = far_tokens_ref[x_lanes[s], :].astype(F).T.astype(BF)

    def first_norm(s, ref, side):
        normed, _ = normalize(ref[:, x_lanes[s]].astype(F))
        to = pl.ds(side * tokens + s * rows, rows)
        h_ref[:, to] = (normed * cols_ref[:, GAIN_ONE] + cols_ref[:, SHIFT_ONE]).astype(BF)

    s_qkv[0].step(1)
    s_qkv[1].step(1)
    d_one.step(1)
    s_qkv[0].step(2)
    s_qkv[2].step(1)
    for s in range(2):
        first_norm(s, x_ref, 0)
    s_qkv[1].step(2)
    d_one.step(2)
    s_qkv[0].step(3)
    s_qkv[2].step(2)
    x_moves[1].start()
    s_out.step(1)
    far_tokens(0)
    first_norm(0, x_far_ref, 1)
    s_qkv[1].step(3)
    s_up[0].step(1)
    s_up[1].step(1)
    s_qkv[2].step(3)
    s_up[2].step(1)
    d_two.step(1)
    for item in s_qkv:
        item.wait()
    save_w.start()

    weights = qkv_w_ref.reshape(3 * width, width)
    scale = 1.0 / math.sqrt(HEAD_DIM)

    def project(s):
        for g in range(groups):
            for k in range(2):
                row = (1 + k) * width + g * part
                to = pl.ds(k * part, part)
                for side, band in enumerate((at.band, far)):
                    lanes = pl.ds(side * tokens + s * rows, rows)
                    out = dg(weights[pl.ds(row, part), :], h_ref[:, lanes], 1, 0)
                    if k == 1:
                        out = out + qv_col_ref[pl.ds(width + g * part, part), :]
                    kv_ref[band, g, to, x_lanes[s]] = out.astype(BF)
            for copy in kv_moves[s][g]:
                copy.start()
        for g in range(groups):
            block = pl.ds(g * part, part)
            out = dg(weights[block, :], h_ref[:, x_lanes[s]], 1, 0) + qv_col_ref[block, :]
            q_ref[block, x_lanes[s]] = (out * scale).astype(BF)

    def second_slot():
        far_tokens(1)
        first_norm(1, x_far_ref, 1)
        project(1)
        save_h.start()
        save_far.start()

    def arrive(s, g):
        for copy in kv_moves[s][g]:
            copy.wait_recv()
        if s == 1:
            save_kv[g].start()

    events = {}

    def when(j, *actions):
        events.setdefault(j, []).extend(actions)

    when(2, second_slot)
    for j in range(1, 2 * groups):
        when(j - 1, functools.partial(arrive, j // groups, j % groups))
    when(0, functools.partial(s_out.step, 2))
    when(1, functools.partial(s_up[0].step, 2))
    when(3, functools.partial(s_up[1].step, 2), functools.partial(s_out.step, 3))
    when(4, functools.partial(s_up[2].step, 2))
    when(5, functools.partial(d_two.step, 2))
    when(6, functools.partial(s_up[0].step, 3))
    when(7, functools.partial(s_up[1].step, 3))
    project(0)
    arrive(0, 0)
    unroll = HEADS // groups

    @pl.loop(0, 2 * groups)
    def _(j):
        s, g = j // groups, j % groups
        for k in range(unroll):
            attend_step(
                s * HEADS + g * unroll + k, at.x, q_ref, kv_ref, bias_ref, att_ref, lse_ref
            )
        for when_j, actions in events.items():

            @pl.when(j == when_j)
            def _():
                for action in actions:
                    action()

    hidden = up_w_ref.shape[0] * 2 * up_w_ref.shape[2]
    blocks = hidden // 256
    quarter = blocks // 4

    def wait_out():
        s_up[2].step(3)
        s_out.wait()

    def wait_up():
        d_two.step(3)
        for item in s_up:
            item.wait()

    def wait_one():
        d_one.step(3)
        d_one.wait()

    def flat(ref):
        return ref.reshape(ref.shape[0] * 2 * ref.shape[2], ref.shape[3])

    middle_body(
        x_ref, cot_ref, scalars_ref, att_ref, flat(out_w_ref), flat(up_w_ref), flat(down_w_ref),
        cols_ref, up_col_ref, *results, *middle_scratch, wait_out, wait_up,
        [
            (d_two.wait, 2 * quarter, lambda t: t + t // quarter * quarter + quarter),
            (wait_one, 2 * quarter, lambda t: t + t // quarter * quarter),
        ],
    )
    for item in s_qkv + s_up + [s_out, d_one, d_two]:
        item.end()
    for copy in [save_w, save_h, save_x, save_far] + save_kv:
        copy.wait()
    for copy in [swap, swap_wide] + small_copies + x_moves:
        copy.wait_send()
    for copy in sum(sum(kv_moves, []), []):
        copy.wait_send()


def front(images, bands, scalars, shards, small, tokens_by_slot, cot_by_slot):
    depth = images // 2
    tokens, width = tokens_by_slot.shape
    groups = GROUPS_OF_HEADS
    widths = [item.shape[1] for item in shards[:3]]
    hidden = images * widths[2]
    full = (width, tokens)
    part = shards[0].shape[0]
    narrow = (2, sum(widths) // 2, part)
    wide = (shards[3].shape[1], shards[3].shape[0])
    kv = (bands, groups, 2 * width // groups, tokens)
    weights = [(depth, 2, w, width) for w in widths]
    weights.append((depth, 2, wide[0], 4 * wide[1]))
    return pl.pallas_call(
        functools.partial(front_kernel, images, bands),
        name="front",
        out_shape=(
            shape(weights[0], BF),
            shape((width, 2 * tokens), BF),
            shape(kv, BF),
            shape(full, BF),
            shape(full, BF),
            shape(full, BF),
            shape((2 * HEADS, tokens // 2), F),
            shape((width, COLUMNS), F),
            shape((tokens, width), BF),
            shape(full, F),
            shape(full, BF),
            shape((HEADS, tokens), F),
            shape((width, width), BF),
            shape((hidden, width), BF),
            shape((width, hidden), BF),
            shape((SUM_ROWS, width), F),
        ),
        in_specs=[SM] + [VM] * 7,
        out_specs=(ANY,) * 5 + (VM,) * 8 + (ANY, ANY, VM),
        scratch_shapes=[pltpu.VMEM(s, BF) for s in (narrow, wide, full, full, (tokens, width))]
        + [pltpu.VMEM(s, BF) for s in weights]
        + [
            pltpu.VMEM((width, 2 * tokens), BF),
            pltpu.VMEM(kv, BF),
            pltpu.VMEM(full, F),
            pltpu.VMEM((hidden, 1), F),
            pltpu.VMEM(narrow[1:], BF),
            pltpu.VMEM((narrow[1], 2 * narrow[2]), BF),
            pltpu.VMEM((wide[0] // 2, 2 * wide[1]), BF),
            pltpu.VMEM((16 * images, 128), F),
            pltpu.VMEM((2 * width, 1), F),
            pltpu.VMEM((8, tokens // 2), F),
            pltpu.VMEM(full, BF),
            pltpu.SemaphoreType.DMA((24,)),
            pltpu.SemaphoreType.DMA((FRONT_COPIES,)),
            pltpu.SemaphoreType.DMA((FRONT_COPIES,)),
            pltpu.VMEM((hidden, width), BF),
            pltpu.VMEM((width, hidden), BF),
            pltpu.VMEM(full, F),
            pltpu.VMEM(full, F),
            pltpu.VMEM(full, BF),
            pltpu.VMEM(full, BF),
            pltpu.VMEM(full, F),
            pltpu.VMEM(full, F),
            pltpu.VMEM(full, BF),
            pltpu.VMEM(full, BF),
            pltpu.SemaphoreType.DMA((hidden // 256,)),
            pltpu.SemaphoreType.DMA((hidden // 256,)),
        ],
        compiler_params=comm_params(0),
    )(scalars, *shards, small, tokens_by_slot, cot_by_slot)


def share_kernel(images, kv_ref, all_ref, local_sem, send_sem, recv_sem):
    at = Place(images)
    greet([at.partner, at.across_x])
    rows = kv_ref.shape[1] // 2
    mine = pltpu.make_async_copy(kv_ref, all_ref.at[at.band], local_sem)
    mine.start()
    copies = []
    for s in range(2):
        lanes = pl.ds(s * rows, rows)
        copies.append(
            send(
                kv_ref.at[:, lanes],
                all_ref.at[at.band, :, lanes],
                send_sem.at[s],
                recv_sem.at[s],
                at.across_x,
            )
        )
    near = send(kv_ref, all_ref.at[at.band], send_sem.at[2], recv_sem.at[2], at.partner)
    passed = []
    for s in range(2):
        copies[s].wait_recv()
        part = all_ref.at[at.across_x[1], :, pl.ds(s * rows, rows)]
        passed.append(send(part, part, send_sem.at[3 + s], recv_sem.at[3 + s], at.partner))
    for copy in passed + [near]:
        copy.wait()
    for copy in copies:
        copy.wait_send()
    mine.wait()


def share(images, bands, kv):
    return pl.pallas_call(
        functools.partial(share_kernel, images),
        name="share",
        out_shape=shape((bands,) + kv.shape, BF),
        in_specs=[VM],
        out_specs=ANY,
        scratch_shapes=[
            pltpu.SemaphoreType.DMA,
            pltpu.SemaphoreType.DMA((5,)),
            pltpu.SemaphoreType.DMA((5,)),
        ],
        compiler_params=comm_params(1),
    )(kv)


def add_rows(total_ref, other_ref, step):
    @pl.loop(0, total_ref.shape[0] // step)
    def _(j):
        rows = pl.ds(pl.multiple_of(j * step, step), step)
        total_ref[rows, :] = (
            total_ref[rows, :].astype(F) + other_ref[rows, :].astype(F)
        ).astype(total_ref.dtype)


def unshare_kernel(images, dkv_ref, sum_ref, near_ref, far_ref, send_sem, recv_sem):
    at = Place(images)
    greet([at.partner, at.across_x])
    mate, far = at.partner[1], at.across_x[1]
    far_mate = at.band + 2 - 4 * at.x + 1 - 2 * at.c
    one = send(dkv_ref.at[far_mate], near_ref.at[0], send_sem.at[0], recv_sem.at[0], at.partner)
    two = send(dkv_ref.at[mate], near_ref.at[1], send_sem.at[1], recv_sem.at[1], at.partner)
    one.wait_recv()
    add_rows(near_ref.at[0], dkv_ref.at[far], 64)
    three = send(near_ref.at[0], far_ref, send_sem.at[2], recv_sem.at[2], at.across_x)
    two.wait_recv()
    add_rows(near_ref.at[1], dkv_ref.at[at.band], 64)
    three.wait_recv()
    sum_ref[...] = near_ref[1]
    add_rows(sum_ref, far_ref, 64)
    for copy in (one, two, three):
        copy.wait_send()


def unshare(images, dkv):
    block = dkv.shape[1:]
    return pl.pallas_call(
        functools.partial(unshare_kernel, images),
        name="unshare",
        out_shape=shape(block, BF),
        in_specs=[VM],
        out_specs=VM,
        scratch_shapes=[
            pltpu.VMEM((2,) + block, BF),
            pltpu.VMEM(block, BF),
            pltpu.SemaphoreType.DMA((3,)),
            pltpu.SemaphoreType.DMA((3,)),
        ],
        compiler_params=comm_params(2),
    )(dkv)


def accumulate(total, other):
    total[...] = total[...] + other[...]


class Reduction:
    def __init__(self, at, make, order, start, size, ref, one, other, bufs, total):
        depth, near = at.depth, at.depth // 2
        half = ref.shape[3] // 2
        self.at, self.near, self.one, self.other, self.order = at, near, one, other, order

        def lanes_of(x):
            return pl.ds(pl.multiple_of(x * half + start, 128), size)

        self.lanes, self.both = lanes_of(at.x), [lanes_of(x) for x in range(2)]
        self.total = total.at[:, pl.ds(start, size)]
        far = lanes_of(1 - at.x)
        upper = depth - near
        if order == "mixed":
            two_x, two_y, three, four = bufs
            self.two_x, self.two_y = two_x, two_y
            low, high = pl.ds(0, near), pl.ds(near, upper)
            self.first = [make(one.at[low, :, :, far], two_x, at.across_x)] + [
                make(one.at[high, 1 - at.y, :, self.both[x]], two_y.at[x], at.across_y)
                for x in range(2)
            ]
            self.second = [
                make(two_x.at[:, 1 - at.y], three.at[low], at.across_y),
                make(two_y.at[1 - at.x], three.at[high], at.across_x),
            ]
        else:
            two, three, four = bufs
            self.two = two
            self.first = [
                make(one.at[:, 1 - at.y, :, self.both[x]], two.at[x], at.across_y)
                for x in range(2)
            ]
            self.second = [make(two.at[1 - at.x], three, at.across_x)]
        self.three, self.four = three, four
        self.third = [
            make(three.at[z], four.at[k], peer) for k, (peer, z) in enumerate(at.z_peers)
        ]

    def step_one(self):
        for lanes in self.both:

            @pl.loop(0, 2 * self.at.depth)
            def _(j):
                accumulate(
                    self.one.at[j // 2, j % 2, :, lanes],
                    self.other.at[j // 2, j % 2, :, lanes],
                )

        for copy in self.first:
            copy.start()

    def step_two(self):
        at = self.at
        if self.order == "mixed":
            self.first[0].wait_recv()

            @pl.loop(0, 2 * self.near)
            def _(j):
                accumulate(
                    self.two_x.at[j // 2, j % 2], self.one.at[j // 2, j % 2, :, self.lanes]
                )

            self.second[0].start()
            for x in range(2):
                self.first[1 + x].wait_recv()

                @pl.loop(0, at.depth - self.near)
                def _(j):
                    accumulate(
                        self.two_y.at[x, j], self.one.at[self.near + j, at.y, :, self.both[x]]
                    )

            self.second[1].start()
        else:
            for x in range(2):
                self.first[x].wait_recv()

                @pl.loop(0, at.depth)
                def _(j):
                    accumulate(self.two.at[x, j], self.one.at[j, at.y, :, self.both[x]])

            self.second[0].start()

    def step_three(self):
        at = self.at
        for copy in self.second:
            copy.wait_recv()
        if self.order == "mixed":

            @pl.loop(0, self.near)
            def _(j):
                accumulate(self.three.at[j], self.two_x.at[j, at.y])

            @pl.loop(0, at.depth - self.near)
            def _(j):
                accumulate(self.three.at[self.near + j], self.two_y.at[at.x, j])

        else:

            @pl.loop(0, at.depth)
            def _(j):
                accumulate(self.three.at[j], self.two.at[at.x, j])

        for copy in self.third:
            copy.start()

    def step_four(self):
        for copy in self.third:
            copy.wait_recv()
        total = self.three[self.at.z].astype(F)
        for k in range(len(self.third)):
            total = total + self.four[k].astype(F)
        self.total[...] = total

    def end(self):
        for copy in self.first + self.second + self.third:
            copy.wait_send()


def reduction_buffers(order, depth, rows, size):
    near = depth // 2
    if order == "mixed":
        first = [(near, 2, rows, size), (2, depth - near, rows, size)]
    else:
        first = [(2, depth, rows, size)]
    return [pltpu.VMEM(s, BF) for s in first + [(depth, rows, size), (depth - 1, rows, size)]]


BACK_ORDERS = (
    (("mixed", 1), ("mixed", 1)),
    (("mixed", 1), ("mixed", 1), ("mixed", 1)),
    (("mixed", 1),),
    (("mixed", 2), ("yx", 1)),
)


def lane_parts(orders, half):
    unit = half // sum(share for _, share in orders)
    parts, start = [], 0
    for order, share in orders:
        parts.append((order, start, share * unit))
        start += share * unit
    return parts


def back_kernel(
    images, bands, scalars_ref, q_ref, delta_ref, lse_ref, datt_ref, cols_ref, sums_ref,
    kv_in, x_in, x_far_in, h_in, dmid_in, w_in, g_out_ref, g_up_ref, g_down_ref,
    gx_ref, p_qkv_ref, p_out_ref, p_up_ref, p_down_ref, total_ref,
    kv_ref, x_ref, x_far_ref, h_ref, dmid_ref, w_ref,
    bias_ref, dq_ref, dwide_ref, dkv_ref, near_ref, g_qkv_ref, err_ref, err_far_ref, err_in_ref,
    small_ref, small_in_ref, small_z_ref, *rest,
):
    at = Place(images)
    depth = at.depth
    local_sem, send_sem, recv_sem = rest[-3:]
    rest = list(rest[:-3])
    used = [0, 0]

    def make(src, dst, peer):
        k = used[0]
        used[0] += 1
        return pltpu.make_async_remote_copy(
            src_ref=src,
            dst_ref=dst,
            send_sem=send_sem.at[k],
            recv_sem=recv_sem.at[k],
            device_id=peer,
            device_id_type=MESH,
        )

    def load(src, dst):
        used[1] += 1
        return pltpu.make_async_copy(src, dst, local_sem.at[used[1] - 1])

    width, tokens = x_ref.shape
    rows = tokens // 2
    unroll = 4
    groups = HEADS // unroll
    part = width // groups

    def four_d(ref):
        return ref.reshape(depth, 2, ref.shape[0] // images, ref.shape[1])

    sources = (four_d(g_down_ref), four_d(g_up_ref), four_d(g_out_ref), g_qkv_ref)
    targets = (p_down_ref, p_up_ref, p_out_ref, p_qkv_ref)
    swaps, owns, moves, ends = [], [], [], []
    for m in range(4):
        one, total, away = rest[:3]
        rest = rest[3:]
        block, lanes = sources[m].shape[2] // 2, sources[m].shape[3]
        near_rows = pl.ds(pl.multiple_of(at.c * block, 16), block)
        far_rows = pl.ds(pl.multiple_of((1 - at.c) * block, 16), block)
        parts = lane_parts(BACK_ORDERS[m], lanes // 2)
        if m < 3:
            other = rest.pop(0)
            owns.append(load(sources[m].at[:, :, near_rows, :], one))
            swaps.append([make(sources[m].at[:, :, far_rows, :], other, at.partner)])
        else:
            other = sources[m].at[:, :, near_rows, :]
            for _, start, size in parts:
                both = [pl.ds(x * (lanes // 2) + start, size) for x in range(2)]
                swaps.append(
                    [
                        make(sources[m].at[:, :, far_rows, l], one.at[:, :, :, l], at.partner)
                        for l in both
                    ]
                )
        moves.append([])
        for order, start, size in parts:
            count = 4 if order == "mixed" else 3
            moves[m].append(
                Reduction(
                    at, make, order, start, size, sources[m], one, other, rest[:count], total
                )
            )
            rest = rest[count:]
        ends.append((total, away, targets[m], make(away, targets[m].at[at.c], at.partner)))
    down, up, out, qkv = moves

    def deliver(m):
        total_ref, away, target, copy = ends[m]
        total = total_ref[...]
        size = total.shape[1] // 2
        low, high = total[:, :size], total[:, size:]
        target[at.c] = jnp.where(at.c == 0, low, high)
        away[...] = jnp.where(at.c == 0, high, low)
        copy.start()

    mate, far = at.partner[1], at.across_x[1]
    far_mate = at.across_x[1] + 1 - 2 * at.c
    one = [make(dkv_ref.at[far_mate, g], near_ref.at[0, g], at.partner) for g in range(groups)]
    two = [make(dkv_ref.at[mate, g], near_ref.at[1, g], at.partner) for g in range(groups)]
    err_moves = [make(err_far_ref.at[s], err_in_ref.at[s], at.across_x) for s in range(2)]
    small_steps = [
        make(small_ref.at[k], small_in_ref.at[k], peer)
        for k, peer in enumerate((at.partner, at.across_x, at.across_y))
    ]
    small_last = [
        make(small_z_ref.at[at.z], small_z_ref.at[at.z], peer) for peer, _ in at.z_peers
    ]

    kv_loads = [load(kv_in.at[:, g], kv_ref.at[:, g]) for g in range(groups)]
    late_loads = [
        load(h_in, h_ref),
        load(w_in, w_ref),
        load(x_in, x_ref),
        load(x_far_in, x_far_ref),
        load(dmid_in, dmid_ref),
    ]
    kv_loads[0].start()
    owns[0].start()
    greet([at.partner, at.across_x, at.across_y] + [peer for peer, _ in at.z_peers])
    for m in range(3):
        swaps[m][0].start()
    for copy in owns[1:] + kv_loads[1:] + late_loads:
        copy.start()
    fill_bias(scalars_ref, bias_ref, rows)

    sides = [pl.ds(side * tokens, tokens) for side in range(2)]

    def share_one(g):
        one[g].start()
        two[g].start()

    def share_two(g):
        for copy, side, band in ((one[g], 1, far), (two[g], 0, at.band)):
            copy.wait_recv()
            for half in range(2):
                block = pl.ds(half * part, part)
                to = pl.ds(half * width + g * part, part)
                value = (
                    near_ref[1 - side, g, block, :].astype(F)
                    + dkv_ref[band, g, block, :].astype(F)
                ).astype(BF)
                dwide_ref[to, sides[side]] = value

    events = {}

    def when(j, *actions):
        events.setdefault(j, []).extend(actions)

    def received(m):
        owns[m].wait()
        swaps[m][0].wait_recv()

    for g in range(1, groups):
        when(2 * g - 1, kv_loads[g].wait)
    when(0, down[1].step_one)
    when(0, lambda: received(1), up[0].step_one)
    when(1, up[1].step_one, lambda: share_one(0))
    when(2, up[2].step_one, down[0].step_two, lambda: share_two(0))
    when(3, lambda: received(2), out[0].step_one, down[1].step_two, lambda: share_one(1))
    when(4, up[0].step_two, down[0].step_three, lambda: share_two(1))
    when(5, up[1].step_two, down[1].step_three, lambda: share_one(2))
    when(6, up[2].step_two, up[0].step_three, lambda: share_two(2))
    when(7, lambda: share_one(3), out[0].step_two, up[1].step_three)
    received(0)
    down[0].step_one()
    kv_loads[0].wait()

    @pl.loop(0, 2 * groups)
    def _(j):
        g, s = j // 2, j % 2
        lanes = pl.ds(pl.multiple_of(s * rows, rows), rows)
        for k in range(unroll):

            def put_key(b, values):
                dkv_ref[b, g, pl.ds(k * HEAD_DIM, HEAD_DIM), lanes] = values

            def put_value(b, values):
                dkv_ref[b, g, pl.ds(part + k * HEAD_DIM, HEAD_DIM), lanes] = values

            attend_back_step(
                s * HEADS + g * unroll + k,
                at.x, q_ref, kv_ref, delta_ref, lse_ref, datt_ref, bias_ref, dq_ref,
                put_key, put_value,
            )
        for when_j, actions in events.items():

            @pl.when(j == when_j)
            def _():
                for action in actions:
                    action()

    chunk = width // 2
    g_flat = g_qkv_ref.reshape(3 * width, width)
    parts = lane_parts(BACK_ORDERS[3], width // 2)

    def weight_grad(part, source_ref, first, count, tokens_at):
        _, start, size = parts[part]
        lanes = [pl.ds(x * (width // 2) + start, size) for x in range(2)]

        @pl.loop(0, count)
        def _(j):
            block = pl.ds(pl.multiple_of(j * chunk, 128), chunk)
            to = pl.ds(pl.multiple_of((first + j) * chunk, 128), chunk)
            both = jnp.concatenate([h_ref[l, tokens_at] for l in lanes], axis=0)
            result = dg(source_ref[block, :], both, 1, 1).astype(BF)
            g_flat[to, lanes[0]] = result[:, :size]
            g_flat[to, lanes[1]] = result[:, size:]

    def back_through(side):
        err_ref[...] = jnp.zeros_like(err_ref)

        @pl.loop(0, 4)
        def _(j):
            block = pl.ds(pl.multiple_of(j * chunk, 128), chunk)
            source = pl.ds(pl.multiple_of((2 + j) * chunk, 128), chunk)
            err_ref[...] += dg(w_ref[source, :], dwide_ref[block, sides[side]], 0, 0)

    def start_swap(part):
        for copy in swaps[3 + part]:
            copy.start()

    def first_sum(part):
        for copy in swaps[3 + part]:
            copy.wait_recv()
        qkv[part].step_one()

    for copy in late_loads:
        copy.wait()
    for p in range(2):
        weight_grad(p, dq_ref, 0, 2, sides[0])
    share_two(groups - 1)
    weight_grad(0, dwide_ref, 2, 4, slice(None))
    start_swap(0)
    back_through(1)
    err_far = err_ref[...]
    for s in range(2):
        err_far_ref[s] = err_far[:, s * rows : (s + 1) * rows].astype(BF)
    first_sum(0)
    err_moves[0].start()
    weight_grad(1, dwide_ref, 2, 4, slice(None))
    start_swap(1)
    normed_far, _ = normalize(x_far_ref[...].astype(F))
    gain_row = row_sums(err_ref[...] * normed_far)[:1]
    shift_row = row_sums(err_ref[...])[:1]
    first_sum(1)
    up[2].step_three()
    out[0].step_three()
    back_through(0)

    @pl.loop(0, 2)
    def _(j):
        block = pl.ds(pl.multiple_of(j * chunk, 128), chunk)
        err_ref[...] += dg(w_ref[block, :], dq_ref[block, :], 0, 0)

    small_ref[0] = sums_ref[...]
    small_ref[0, 0:1] = row_sums(dq_ref[...])[:1]
    small_ref[0, 1:2] = row_sums(dwide_ref[pl.ds(width, width), :])[:1]
    normed, _ = normalize(x_ref[...].astype(F))
    small_ref[0, 4:5] = gain_row + row_sums(err_ref[...] * normed)[:1]
    small_ref[0, 5:6] = shift_row + row_sums(err_ref[...])[:1]
    small_steps[0].start()
    qkv[0].step_two()
    for item in down:
        item.step_four()
    deliver(0)
    small_steps[0].wait_recv()
    small_ref[1] = small_ref[0] + small_in_ref[0]
    small_steps[1].start()
    qkv[1].step_two()
    err_moves[1].start()
    qkv[0].step_three()
    small_steps[1].wait_recv()
    small_ref[2] = small_ref[1] + small_in_ref[1]
    small_steps[2].start()
    for item in up:
        item.step_four()
    deliver(1)
    small_steps[2].wait_recv()
    small_z_ref[at.z] = small_ref[2] + small_in_ref[2]
    for copy in small_last:
        copy.start()
    out[0].step_four()
    deliver(2)
    qkv[1].step_three()

    def finish_slot(s):
        err_moves[s].wait_recv()
        lanes = slice(s * rows, (s + 1) * rows)
        err = err_ref[:, lanes] + err_in_ref[s].astype(F)
        normed, inverse = normalize(x_ref[:, lanes].astype(F))
        grad = dmid_ref[:, lanes] + norm_back(err, normed, inverse, cols_ref[:, GAIN_ONE])
        gx_ref[lanes, :] = grad.T.astype(BF)

    finish_slot(0)
    qkv[0].step_four()
    for copy in small_last:
        copy.wait_recv()
    total = small_z_ref[0]
    for k in range(1, depth):
        total = total + small_z_ref[k]
    total_ref[...] = total
    qkv[1].step_four()
    deliver(3)
    finish_slot(1)
    for m in range(4):
        ends[m][3].wait()
        for item in moves[m]:
            item.end()
    for copy in sum(swaps, []) + one + two + err_moves + small_steps + small_last:
        copy.wait_send()


def back(
    images, bands, scalars, q, kv, delta, lse, datt, x, x_far, h, dmid, w, cols, grads, sums
):
    depth = images // 2
    width, tokens = x.shape
    g_out, g_up, g_down = grads
    groups = HEADS // 4
    results, buffers = [], []
    for m, item in enumerate((g_down, g_up, g_out, w)):
        block, lanes = item.shape[0] // images // 2, item.shape[1]
        results.append(shape((2, block, lanes // 4), F))
        buffers += [
            pltpu.VMEM((depth, 2, block, lanes), BF),
            pltpu.VMEM((block, lanes // 2), F),
            pltpu.VMEM((block, lanes // 4), F),
        ]
        if m < 3:
            buffers.append(pltpu.VMEM((depth, 2, block, lanes), BF))
        for order, _, size in lane_parts(BACK_ORDERS[m], lanes // 2):
            buffers += reduction_buffers(order, depth, block, size)
    small = (SUM_ROWS, width)
    return pl.pallas_call(
        functools.partial(back_kernel, images, bands),
        name="back",
        out_shape=(shape((tokens, width), BF), results[3], results[2], results[1], results[0], shape(small, F)),
        in_specs=[SM] + [VM] * 6 + [ANY] * 9,
        out_specs=(VM,) * 6,
        scratch_shapes=[
            pltpu.VMEM(kv.shape, BF),
            pltpu.VMEM((width, tokens), BF),
            pltpu.VMEM((width, tokens), BF),
            pltpu.VMEM((width, 2 * tokens), BF),
            pltpu.VMEM((width, tokens), F),
            pltpu.VMEM(w.shape, BF),
            pltpu.VMEM((8, tokens // 2), F),
            pltpu.VMEM((width, tokens), BF),
            pltpu.VMEM((2 * width, 2 * tokens), BF),
            pltpu.VMEM((bands, groups, 2 * width // groups, tokens), BF),
            pltpu.VMEM((2, groups, 2 * width // groups, tokens), BF),
            pltpu.VMEM((depth, 2, w.shape[0] // images, width), BF),
            pltpu.VMEM((width, tokens), F),
            pltpu.VMEM((2, width, tokens // 2), BF),
            pltpu.VMEM((2, width, tokens // 2), BF),
            pltpu.VMEM((3,) + small, F),
            pltpu.VMEM((3,) + small, F),
            pltpu.VMEM((depth,) + small, F),
        ]
        + buffers
        + [
            pltpu.SemaphoreType.DMA((16,)),
            pltpu.SemaphoreType.DMA((BACK_COPIES,)),
            pltpu.SemaphoreType.DMA((BACK_COPIES,)),
        ],
        compiler_params=comm_params(3),
    )(
        scalars, q, delta, lse, datt, cols, sums, kv, x, x_far, h, dmid, w, g_out, g_up, g_down
    )


def body(
    tokens,
    slot_kind,
    w_qkv,
    w_out,
    w_up,
    w_down,
    bias_qv,
    bias_out,
    bias_up,
    bias_down,
    gain_one,
    shift_one,
    gain_two,
    shift_two,
    cotangent,
):
    rows, slots, width = tokens.shape[1:]
    count = rows * slots
    images, bands = lax.axis_size("img"), lax.axis_size("band")
    band = lax.axis_index("band")
    smalls = (bias_qv, bias_out, bias_up, bias_down, gain_one, shift_one, gain_two, shift_two)
    sizes = [item.shape[0] for item in smalls]
    own = (w_qkv, w_out, w_up)
    widths = [item.shape[1] for item in own]
    direct = images % 4 == 0 and all(w % 32 == 0 for w in widths + [w_down.shape[1]])
    direct = direct and bias_qv.shape[0] == 2 * (width // images) <= 256
    direct = direct and bias_up.shape[0] == 4 * (width // images)

    def by_slot(values):
        return values[0].transpose(1, 0, 2).reshape(count, width)

    def turn(values):
        return by_slot(values).T

    def turn_back(values):
        return values.reshape(slots, rows, width).transpose(1, 0, 2)[None]

    scalars = slot_kind
    single = (bias_out, bias_down, gain_one, shift_one, gain_two, shift_two)
    if direct:
        unit = width // images
        pieces = list(single) + [jnp.zeros((unit,), BF)] * 4
        for item in (bias_qv, bias_up):
            pieces += [item[k : k + unit] for k in range(0, item.shape[0], unit)]
        small = jnp.stack([jnp.pad(item, (0, 128 - unit)) for item in pieces]).astype(F)
        full_qkv, h, all_kv, x, x_far, q, lse, cols, *rest = front(
            images, bands, scalars, (*own, w_down), small, by_slot(tokens), by_slot(cotangent)
        )
        full_qkv = full_qkv.reshape(-1, width)
    else:
        scalars = jnp.concatenate([slot_kind, jnp.full((1, 1), band // 2, jnp.int32)], axis=1)
        x, cot = turn(tokens), turn(cotangent)
        full_qkv, full_out, full_up, full_down = (
            lax.all_gather(lax.all_gather(item, "band", axis=0, tiled=True).T, "img", tiled=True)
            for item in (*own, w_down)
        )
        whole = [lax.all_gather(item, "img", tiled=True).astype(F) for item in single]
        cols = jnp.stack(whole + [whole[0]] * (COLUMNS - len(whole)), axis=1)
        c_qv = lax.all_gather(bias_qv, "img", tiled=True).astype(F)[:, None]
        c_up = lax.all_gather(bias_up, "img", tiled=True).astype(F)[:, None]
        bias = jnp.concatenate([c_qv[:width], jnp.zeros((width, 1), F), c_qv[width:]])
        h, qkv = project(x, full_qkv, cols, bias)
        q = qkv[:width]
        all_kv = share(images, bands, qkv[width:])
        all_kv = all_kv.reshape(bands, 2, GROUPS_OF_HEADS, -1, count).transpose(0, 2, 1, 3, 4)
        all_kv = all_kv.reshape(bands, GROUPS_OF_HEADS, -1, count)
        att, lse = attend(scalars, q, all_kv)
        rest = middle(x, cot, scalars, att, full_out, full_up, full_down, cols, c_up)
    out, dmid, datt, delta, g_out, g_up, g_down, sums = rest
    if direct:
        gx, *pieces, total = back(
            images, bands, scalars, q, all_kv, delta, lse, datt, x, x_far, h, dmid,
            full_qkv, cols, (g_out, g_up, g_down), sums,
        )
        matrices = [item.reshape(-1, item.shape[2]).T for item in pieces]
    else:
        dq, dkv = attend_back(scalars, q, all_kv, delta, lse, datt)
        dkv = unshare(images, dkv)
        gx, g_qkv, sums_one = finish(x, h, dq, dkv, full_qkv, cols, dmid)
        matrices = [
            lax.psum_scatter(
                lax.psum_scatter(item, "img", scatter_dimension=0, tiled=True),
                "band",
                scatter_dimension=1,
                tiled=True,
            )
            .astype(F)
            .T
            for item in (g_qkv, g_out, g_up, g_down)
        ]
        total = lax.psum(sums + sums_one, ("img", "band"))
    own_small = lax.axis_index("img")
    flat = total.reshape(-1)
    starts = [0, 2, UP_ROW, 3, 4, 5, 6, 7]
    small = [
        lax.dynamic_slice(flat, (start * width + own_small * size,), (size,))
        for start, size in zip(starts, sizes)
    ]
    return (turn_back(out), turn_back(gx), *matrices, *small)


def solution(mesh):
    data, weight, vector = P("img", "band", None, None), P("band", "img"), P("img")
    return jax.shard_map(
        body,
        mesh=mesh,
        in_specs=(data, P("img", None)) + (weight,) * 4 + (vector,) * 8 + (data,),
        out_specs=(data, data) + (weight,) * 4 + (vector,) * 8,
        check_vma=False,
    )
```

```python
import functools
import math

import jax
import jax.numpy as jnp
from jax import lax
from jax.experimental import pallas as pl
from jax.experimental.pallas import tpu as pltpu
from jax.sharding import PartitionSpec as P

HEADS = 16
HEAD_DIM = 48
EPSILON = 1e-06
MASKED = -1e30
BF = jnp.bfloat16
F = jnp.float32
MESH = pl.DeviceIdType.MESH
VM = pl.BlockSpec(memory_space=pltpu.VMEM)
SM = pl.BlockSpec(memory_space=pltpu.SMEM)
ANY = pl.BlockSpec(memory_space=pl.ANY)
LIMIT = 67043328
SUM_ROWS, UP_ROW = 16, 8
COLUMNS = 10
BIAS_OUT, BIAS_DOWN, GAIN_ONE, SHIFT_ONE, GAIN_TWO, SHIFT_TWO = (slice(k, k + 1) for k in range(6))
GROUPS_OF_HEADS = 4
FRONT_COPIES, BACK_COPIES = 128, 128


def dg(left, right, left_dim, right_dim):
    return lax.dot_general(
        left, right, (((left_dim,), (right_dim,)), ((), ())), preferred_element_type=F
    )


def shape(dims, dtype):
    return jax.ShapeDtypeStruct(tuple(dims), dtype)


def row_sums(values):
    ones = jnp.ones((8, values.shape[1]), BF)
    if values.dtype == BF:
        return dg(ones, values, 1, 1)
    high = values.astype(BF)
    low = (values - high.astype(F)).astype(BF)
    return dg(ones, high, 1, 1) + dg(ones, low, 1, 1)


def normalize(values):
    average = jnp.mean(values, axis=0, keepdims=True)
    centered = values - average
    variance = jnp.mean(centered * centered, axis=0, keepdims=True)
    inverse = lax.rsqrt(variance + EPSILON)
    return centered * inverse, inverse


def norm_back(error, normed, inverse, gain):
    f = gain * error
    mean_f = jnp.mean(f, axis=0, keepdims=True)
    mean_fn = jnp.mean(f * normed, axis=0, keepdims=True)
    return (f - mean_f - normed * mean_fn) * inverse


def project_kernel(x_ref, w_ref, cols_ref, bias_ref, h_ref, qkv_ref):
    width = x_ref.shape[0]
    normed, _ = normalize(x_ref[...].astype(F))
    h_ref[...] = (normed * cols_ref[:, GAIN_ONE] + cols_ref[:, SHIFT_ONE]).astype(BF)
    scale = 1.0 / math.sqrt(HEAD_DIM)
    step = 256

    @pl.loop(0, 3 * width // step)
    def _(j):
        rows = pl.ds(pl.multiple_of(j * step, step), step)
        out = dg(w_ref[rows, :], h_ref[...], 1, 0) + bias_ref[rows, :]
        qkv_ref[rows, :] = (out * jnp.where(j < width // step, scale, 1.0)).astype(BF)


def project(x, w, cols, bias):
    width, tokens = x.shape
    return pl.pallas_call(
        project_kernel,
        name="project",
        out_shape=(shape((width, tokens), BF), shape((3 * width, tokens), BF)),
        in_specs=[VM] * 4,
        out_specs=(VM, VM),
        compiler_params=pltpu.CompilerParams(vmem_limit_bytes=LIMIT),
    )(x, w, cols, bias)


def fill_bias(scalars_ref, bias_ref, rows):
    lane_half = lax.broadcasted_iota(jnp.int32, (1, rows), 1) // (rows // 2)
    for s in range(2):
        small = scalars_ref[0, s] == 2
        for other in range(2):
            for half in range(2):
                keep = jnp.logical_and(other == 0, lane_half == half)
                masked = jnp.where(small, MASKED, 0.0)
                bias_ref[pl.ds(4 * s + 2 * other + half, 1), :] = jnp.where(
                    keep, jnp.zeros((1, rows), F), jnp.full((1, rows), masked, F)
                )


def add_bias(scores, bias_ref, s, other):
    rows = scores.shape[0]
    at = 4 * s + 2 * other
    return jnp.concatenate(
        [
            scores[: rows // 2] + bias_ref[pl.ds(at, 1), :],
            scores[rows // 2 :] + bias_ref[pl.ds(at + 1, 1), :],
        ],
        axis=0,
    )


def head_slices(i, rows):
    s, h = i // HEADS, i % HEADS
    lanes = pl.ds(pl.multiple_of(s * rows, rows), rows)
    first = pl.ds(pl.multiple_of(h * HEAD_DIM, 16), HEAD_DIM)
    second = pl.ds(pl.multiple_of(HEADS * HEAD_DIM + h * HEAD_DIM, 16), HEAD_DIM)
    return s, lanes, first, second


def attend_step(i, chip_x, q_ref, kv_ref, bias_ref, out_ref, lse_ref):
    bands = kv_ref.shape[0]
    rows = q_ref.shape[1] // 2
    s, lanes, first, second = head_slices(i, rows)
    q = q_ref[first, lanes]
    scores = []
    maximum = None
    for b in range(bands):
        other = jnp.where(chip_x == b // 2, 0, 1)
        keys, _ = kv_rows(kv_ref, b, i % HEADS)
        part = add_bias(dg(keys[:, lanes], q, 0, 0), bias_ref, s, other)
        scores.append(part)
        top = jnp.max(part, axis=0, keepdims=True)
        maximum = top if maximum is None else jnp.maximum(maximum, top)
    total, acc = 0.0, 0.0
    for b in range(bands):
        weight = jnp.exp(scores[b] - maximum)
        total = total + jnp.sum(weight, axis=0, keepdims=True)
        _, values = kv_rows(kv_ref, b, i % HEADS)
        acc = acc + dg(values[:, lanes], weight.astype(BF), 1, 0)
    out_ref[first, lanes] = acc / total
    lse_ref[pl.ds(i, 1), :] = maximum + jnp.log(total)


def attend_kernel(unroll, scalars_ref, q_ref, kv_ref, out_ref, lse_ref, bias_ref):
    fill_bias(scalars_ref, bias_ref, q_ref.shape[1] // 2)

    @pl.loop(0, 2 * HEADS // unroll)
    def _(j):
        for k in range(unroll):
            attend_step(
                j * unroll + k, scalars_ref[0, 2], q_ref, kv_ref, bias_ref, out_ref, lse_ref
            )


def attend(scalars, q, kv):
    width, tokens = q.shape
    return pl.pallas_call(
        functools.partial(attend_kernel, 4),
        name="attend",
        out_shape=(shape((width, tokens), F), shape((2 * HEADS, tokens // 2), F)),
        in_specs=[SM, VM, VM],
        out_specs=(VM, VM),
        scratch_shapes=[pltpu.VMEM((8, tokens // 2), F)],
        compiler_params=pltpu.CompilerParams(vmem_limit_bytes=LIMIT),
    )(scalars, q, kv)


def attend_back_step(
    i, chip_x, q_ref, kv_ref, delta_ref, lse_ref, dout_ref, bias_ref, dq_ref, put_key, put_value
):
    bands = kv_ref.shape[0]
    rows = q_ref.shape[1] // 2
    s, lanes, first, second = head_slices(i, rows)
    q = q_ref[first, lanes]
    dout = dout_ref[first, lanes]
    delta = delta_ref[pl.ds(i % HEADS, 1), lanes]
    lse = lse_ref[pl.ds(i, 1), :]
    dq = 0.0
    for b in range(bands):
        other = jnp.where(chip_x == b // 2, 0, 1)
        k, v = (ref[:, lanes] for ref in kv_rows(kv_ref, b, i % HEADS))
        scores = add_bias(dg(k, q, 0, 0), bias_ref, s, other)
        dweight = dg(v, dout, 0, 0)
        weight = jnp.exp(scores - lse)
        dscores = (weight * (dweight - delta)).astype(BF)
        dq = dq + dg(k, dscores, 1, 0)
        put_key(b, dg(q, dscores, 1, 1).astype(BF))
        put_value(b, dg(dout, weight.astype(BF), 1, 1).astype(BF))
    dq_ref[first, lanes] = (dq * (1.0 / math.sqrt(HEAD_DIM))).astype(BF)


def attend_back_kernel(
    unroll, scalars_ref, q_ref, kv_ref, delta_ref, lse_ref, dout_ref, dq_ref, dkv_ref, bias_ref
):
    fill_bias(scalars_ref, bias_ref, q_ref.shape[1] // 2)

    @pl.loop(0, 2 * HEADS // unroll)
    def _(j):
        for k in range(unroll):
            i = j * unroll + k
            _, lanes, first, second = head_slices(i, q_ref.shape[1] // 2)

            def put_key(b, values):
                dkv_ref[b, first, lanes] = values

            def put_value(b, values):
                dkv_ref[b, second, lanes] = values

            attend_back_step(
                i, scalars_ref[0, 2], q_ref, kv_ref, delta_ref, lse_ref, dout_ref, bias_ref, dq_ref,
                put_key, put_value,
            )


def attend_back(scalars, q, kv, delta, lse, dout):
    return pl.pallas_call(
        functools.partial(attend_back_kernel, 4),
        name="attend_back",
        out_shape=(shape(q.shape, BF), shape((kv.shape[0], 2 * q.shape[0], q.shape[1]), BF)),
        in_specs=[SM] + [VM] * 5,
        out_specs=(VM, VM),
        scratch_shapes=[pltpu.VMEM((8, q.shape[1] // 2), F)],
        compiler_params=pltpu.CompilerParams(vmem_limit_bytes=LIMIT),
    )(scalars, q, kv, delta, lse, dout)


def middle_body(
    x_ref, cot_ref, scalars_ref, att_ref, w_out_ref, w_up_ref, w_down_ref, cols_ref, bias_up_ref,
    out_ref, dmid_ref, datt_ref, delta_ref, g_out_ref, g_up_out, g_down_out, sums_ref,
    g_up_ref, g_down_ref,
    mid_ref, norm_ref, h_ref, dmlp_ref, mlp_ref, err_ref, attb_ref, dbranch_ref,
    up_sem, down_sem, wait_out, wait_up, passes,
):
    width, tokens = x_ref.shape
    hidden = w_up_ref.shape[0]
    step = 256
    first_slot = lax.broadcasted_iota(jnp.int32, (1, tokens), 1) < tokens // 2
    valid = jnp.where(
        first_slot,
        jnp.where(scalars_ref[0, 0] > 0, 1.0, 0.0),
        jnp.where(scalars_ref[0, 1] > 0, 1.0, 0.0),
    )
    attb_ref[...] = att_ref[...].astype(BF)
    dmlp_ref[...] = (cot_ref[...].astype(F) * valid).astype(BF)
    sums_ref[...] = jnp.zeros_like(sums_ref)
    mlp_ref[...] = jnp.zeros_like(mlp_ref)
    err_ref[...] = jnp.zeros_like(err_ref)
    wait_out()

    @pl.loop(0, width // step)
    def _(j):
        rows = pl.ds(pl.multiple_of(j * step, step), step)
        mid_ref[rows, :] = (
            dg(w_out_ref[rows, :], attb_ref[...], 1, 0)
            + cols_ref[rows, BIAS_OUT]
            + x_ref[rows, :].astype(F)
        )

    normed, inverse = normalize(mid_ref[...])
    norm_ref[...] = normed
    h_ref[...] = (normed * cols_ref[:, GAIN_TWO] + cols_ref[:, SHIFT_TWO]).astype(BF)
    wait_up()

    def stores(j):
        rows = pl.ds(pl.multiple_of(j * step, step), step)
        return (
            pltpu.make_async_copy(g_up_ref.at[rows, :], g_up_out.at[rows, :], up_sem.at[j]),
            pltpu.make_async_copy(g_down_ref.at[:, rows], g_down_out.at[:, rows], down_sem.at[j]),
        )

    def block(j):
        rows = pl.ds(pl.multiple_of(j * step, step), step)
        pre = dg(w_up_ref[rows, :], h_ref[...], 1, 0) + bias_up_ref[rows, :]
        phi = 0.5 + 0.5 * lax.erf(pre * math.sqrt(0.5))
        act = (pre * phi).astype(BF)
        slope = phi + pre * jnp.exp(pre * pre * -0.5) * (1.0 / math.sqrt(2.0 * math.pi))
        mlp_ref[...] += dg(w_down_ref[:, rows], act, 1, 0)
        dact = dg(w_down_ref[:, rows], dmlp_ref[...], 0, 0)
        dhid = (slope * dact).astype(BF)
        g_down_ref[:, rows] = dg(dmlp_ref[...], act, 1, 1).astype(BF)
        g_up_ref[rows, :] = dg(dhid, h_ref[...], 1, 1).astype(BF)
        per = width // step
        lanes = pl.ds(pl.multiple_of(j % per * step, step), step)
        sums_ref[pl.ds(UP_ROW + j // per, 1), lanes] = row_sums(dhid)[:1]
        err_ref[...] += dg(w_up_ref[rows, :], dhid, 0, 0)
        for copy in stores(j):
            copy.start()

    for wait, count, place in passes:
        wait()

        @pl.loop(0, count)
        def _(t):
            block(place(t))

    out = (mid_ref[...] + mlp_ref[...] + cols_ref[:, BIAS_DOWN]) * valid
    out_ref[...] = out.T.astype(BF)
    err = err_ref[...]
    sums_ref[3:4] = row_sums(dmlp_ref[...])[:1]
    sums_ref[6:7] = row_sums(err * norm_ref[...])[:1]
    sums_ref[7:8] = row_sums(err)[:1]
    dmid = cot_ref[...].astype(F) * valid + norm_back(
        err, norm_ref[...], inverse, cols_ref[:, GAIN_TWO]
    )
    dmid_ref[...] = dmid
    dbranch_ref[...] = dmid.astype(BF)
    sums_ref[2:3] = row_sums(dbranch_ref[...])[:1]
    datt_ref[...] = dg(w_out_ref[...], dbranch_ref[...], 0, 0).astype(BF)
    inner = att_ref[...] * datt_ref[...].astype(F)
    delta_ref[...] = jnp.sum(inner.reshape(HEADS, width // HEADS, tokens), axis=1)

    @pl.loop(0, width // step)
    def _(j):
        rows = pl.ds(pl.multiple_of(j * step, step), step)
        g_out_ref[rows, :] = dg(dbranch_ref[rows, :], attb_ref[...], 1, 1).astype(BF)

    @pl.loop(0, hidden // step)
    def _(j):
        for copy in stores(j):
            copy.wait()


def middle_kernel(*refs):
    x_ref, cot_ref, scalars_ref, att_ref, w_out_in, w_up_in, w_down_in = refs[:7]
    outputs = refs[7:17]
    w_out_ref, w_up_ref, w_down_ref = refs[17:20]
    scratch, in_sem = refs[20:30], refs[30]
    loads = [
        pltpu.make_async_copy(source, target, in_sem.at[k])
        for k, (source, target) in enumerate(
            ((w_out_in, w_out_ref), (w_up_in, w_up_ref), (w_down_in, w_down_ref))
        )
    ]
    for copy in loads:
        copy.start()
    middle_body(
        x_ref, cot_ref, scalars_ref, att_ref, w_out_ref, w_up_ref, w_down_ref, *outputs, *scratch,
        *refs[31:], loads[0].wait, loads[1].wait,
        [(loads[2].wait, w_up_ref.shape[0] // 256, lambda t: t)],
    )


def middle(x, cot, scalars, att, w_out, w_up, w_down, cols, bias_up):
    width, tokens = x.shape
    hidden = w_up.shape[0]
    full = (width, tokens)
    weights = [w_out.shape, w_up.shape, w_down.shape]
    return pl.pallas_call(
        middle_kernel,
        name="middle",
        out_shape=(
            shape((tokens, width), BF),
            shape(full, F),
            shape(full, BF),
            shape((HEADS, tokens), F),
            shape(w_out.shape, BF),
            shape(w_up.shape, BF),
            shape(w_down.shape, BF),
            shape((SUM_ROWS, width), F),
        ),
        in_specs=[VM, VM, SM, VM] + [ANY] * 3 + [VM] * 2,
        out_specs=(VM,) * 5 + (ANY, ANY, VM),
        scratch_shapes=[pltpu.VMEM(s, BF) for s in weights + weights[1:]]
        + [
            pltpu.VMEM(full, F),
            pltpu.VMEM(full, F),
            pltpu.VMEM(full, BF),
            pltpu.VMEM(full, BF),
            pltpu.VMEM(full, F),
            pltpu.VMEM(full, F),
            pltpu.VMEM(full, BF),
            pltpu.VMEM(full, BF),
            pltpu.SemaphoreType.DMA((3,)),
            pltpu.SemaphoreType.DMA((hidden // 256,)),
            pltpu.SemaphoreType.DMA((hidden // 256,)),
        ],
        compiler_params=pltpu.CompilerParams(vmem_limit_bytes=LIMIT),
    )(x, cot, scalars, att, w_out, w_up, w_down, cols, bias_up)


def finish_kernel(
    x_ref, h_ref, dq_ref, dkv_ref, w_ref, cols_ref, dmid_ref, gx_ref, g_ref, sums_ref, err_ref
):
    width, tokens = x_ref.shape
    step = 256
    blocks = width // step
    err_ref[...] = jnp.zeros_like(err_ref)
    for ref, count, base in ((dq_ref, blocks, 0), (dkv_ref, 2 * blocks, blocks)):

        @pl.loop(0, count)
        def _(j):
            rows = pl.ds(pl.multiple_of(j * step, step), step)
            to = pl.ds(pl.multiple_of((j + base) * step, step), step)
            g_ref[to, :] = dg(ref[rows, :], h_ref[...], 1, 1).astype(BF)
            err_ref[...] += dg(w_ref[to, :], ref[rows, :], 0, 0)

    normed, inverse = normalize(x_ref[...].astype(F))
    err = err_ref[...]
    sums_ref[...] = jnp.zeros_like(sums_ref)
    sums_ref[0:1] = row_sums(dq_ref[...])[:1]
    sums_ref[1:2] = row_sums(dkv_ref[pl.ds(width, width), :])[:1]
    sums_ref[4:5] = row_sums(err * normed)[:1]
    sums_ref[5:6] = row_sums(err)[:1]
    grad = dmid_ref[...] + norm_back(err, normed, inverse, cols_ref[:, GAIN_ONE])
    gx_ref[...] = grad.T.astype(BF)


def finish(x, h, dq, dkv, w, cols, dmid):
    width, tokens = x.shape
    return pl.pallas_call(
        finish_kernel,
        name="finish",
        out_shape=(shape((tokens, width), BF), shape(w.shape, BF), shape((SUM_ROWS, width), F)),
        in_specs=[VM] * 7,
        out_specs=(VM, VM, VM),
        scratch_shapes=[pltpu.VMEM(x.shape, F)],
        compiler_params=pltpu.CompilerParams(vmem_limit_bytes=LIMIT),
    )(x, h, dq, dkv, w, cols, dmid)


class Place:
    def __init__(self, images):
        self.images = images
        self.depth = images // 2
        self.img = lax.axis_index("img")
        self.band = lax.axis_index("band")
        self.z, self.y = self.img // 2, self.img % 2
        self.x, self.c = self.band // 2, self.band % 2
        self.partner = (self.img, self.band + 1 - 2 * self.c)
        self.across_x = (self.img, self.band + 2 - 4 * self.x)
        self.across_y = (self.img + 1 - 2 * self.y, self.band)
        self.z_peers = [self.along_z(k) for k in range(1, self.depth)]

    def along_z(self, k):
        z = lax.rem(self.z + k, self.depth)
        return (2 * z + self.y, self.band), z


def greet(peers):
    barrier = pltpu.get_barrier_semaphore()
    for peer in peers:
        pl.semaphore_signal(barrier, inc=1, device_id=peer, device_id_type=MESH)
    pl.semaphore_wait(barrier, len(peers))


def send(src, dst, send_sem, recv_sem, peer):
    copy = pltpu.make_async_remote_copy(
        src_ref=src,
        dst_ref=dst,
        send_sem=send_sem,
        recv_sem=recv_sem,
        device_id=peer,
        device_id_type=MESH,
    )
    copy.start()
    return copy


def comm_params(collective_id):
    return pltpu.CompilerParams(
        collective_id=collective_id, has_side_effects=True, vmem_limit_bytes=LIMIT
    )


class Spread:
    def __init__(self, at, make, order, part, parts, source, ref, local_sem):
        depth, near, c = at.depth, at.depth // 2, at.c
        rows, half = ref.shape[2] // 2, ref.shape[3] // 2
        rows = pl.ds(pl.multiple_of(c * rows, 16), rows)
        size = half // parts
        lanes = pl.ds(pl.multiple_of(at.x * half + part * size, 128), size)
        both = [pl.ds(x * half + part * size, size) for x in range(2)]
        if parts == 1:
            both = [slice(None)]
        low, high = pl.ds(0, near), pl.ds(near, depth - near)

        def same(index, peer):
            if len(index) == 4:
                return [make(ref.at[index], ref.at[index], peer)]
            return [make(ref.at[index + (l,)], ref.at[index + (l,)], peer) for l in both]

        piece = ref.at[at.z, at.y, rows, lanes]
        source = source.at[:, pl.ds(part * size, size)]
        self.keep = pltpu.make_async_copy(source, piece, local_sem)
        z_first = []
        if order != "xyz":
            z_first = [make(source, piece, peer) for peer, _ in at.z_peers]
        if order == "mixed":
            self.stages = [
                z_first,
                same((low, at.y, rows, lanes), at.across_x)
                + same((high, at.y, rows, lanes), at.across_y),
                same((low, at.y, rows), at.across_y)
                + same((high, slice(None), rows, lanes), at.across_x),
            ]
        elif order == "zxy":
            self.stages = [
                z_first,
                same((slice(None), at.y, rows, lanes), at.across_x),
                same((slice(None), at.y, rows), at.across_y),
            ]
        else:
            last = [same((at.z, slice(None), rows), peer) for peer, _ in at.z_peers]
            self.stages = [
                [make(source, piece, at.across_x)],
                same((at.z, at.y, rows), at.across_y),
                sum(last, []),
            ]
        self.stages.append(same((slice(None), slice(None), rows), at.partner))

    def start(self):
        self.keep.start()
        for copy in self.stages[0]:
            copy.start()

    def step(self, k):
        if k == 1:
            self.keep.wait()
        for copy in self.stages[k - 1]:
            copy.wait_recv()
        for copy in self.stages[k]:
            copy.start()

    def wait(self):
        for copy in self.stages[-1]:
            copy.wait_recv()

    def end(self):
        for stage in self.stages:
            for copy in stage:
                copy.wait_send()


def kv_rows(ref, b, h):
    part = ref.shape[2] // 2
    heads = part // HEAD_DIM
    first = pl.multiple_of(h % heads * HEAD_DIM, 16)
    second = pl.multiple_of(part + h % heads * HEAD_DIM, 16)
    at = ref.at[b, h // heads]
    return at.at[pl.ds(first, HEAD_DIM)], at.at[pl.ds(second, HEAD_DIM)]


def front_kernel(
    images, bands, scalars_ref, shard_qkv_ref, shard_out_ref, shard_up_ref, shard_down_ref,
    small_ref, tokens_ref, cot_tokens_ref,
    qkv_w_out, h_out, kv_out, x_out, x_far_out, q_ref, lse_ref, cols_ref, *rest,
):
    results, rest = rest[:8], rest[8:]
    narrow_ref, wide_ref, x_ref, cot_ref, far_tokens_ref = rest[:5]
    rest = rest[5:]
    qkv_w_ref, out_w_ref, up_w_ref, down_w_ref, h_ref, kv_ref, att_ref, up_col_ref = rest[:8]
    theirs_ref, mine_ref, mine_wide_ref, smalls_ref, qv_col_ref, bias_ref, x_far_ref = rest[8:15]
    local_sem, send_sem, recv_sem = rest[15:18]
    middle_scratch = rest[18:]
    at = Place(images)
    width, tokens = x_ref.shape
    rows = tokens // 2
    unit = width // images
    groups = kv_ref.shape[1]
    part = width // groups
    c = at.c
    used = [0, 0]

    def make(src, dst, peer):
        k = used[0]
        used[0] += 1
        return pltpu.make_async_remote_copy(
            src_ref=src,
            dst_ref=dst,
            send_sem=send_sem.at[k],
            recv_sem=recv_sem.at[k],
            device_id=peer,
            device_id_type=MESH,
        )

    def local():
        used[1] += 1
        return local_sem.at[used[1] - 1]

    others = [(lax.rem(at.img + k, images), at.band) for k in range(1, images)]
    half = wide_ref.shape[0] // 2
    wide = wide_ref.shape[1]
    own_lanes = pl.ds(pl.multiple_of(c * wide, 128), wide)
    own_wide = pltpu.make_async_copy(
        wide_ref.at[pl.ds(pl.multiple_of(c * half, 8), half), :],
        mine_wide_ref.at[:, own_lanes],
        local(),
    )
    swap = make(narrow_ref.at[1 - c], theirs_ref, at.partner)
    swap_wide = make(
        wide_ref.at[pl.ds(pl.multiple_of((1 - c) * half, 8), half), :],
        mine_wide_ref.at[:, own_lanes],
        at.partner,
    )
    lines = pl.ds(pl.multiple_of(at.img * 16, 16), 16)
    keep_small = pltpu.make_async_copy(small_ref, smalls_ref.at[lines, :], local())
    small_copies = [make(small_ref, smalls_ref.at[lines, :], peer) for peer in others]
    sources, row = [], 0
    for ref in (qkv_w_ref, out_w_ref, up_w_ref):
        count = ref.shape[2] // 2
        sources.append(mine_ref.at[pl.ds(row, count), :])
        row += count
    sources.append(mine_wide_ref)

    def spread(ref, source, orders):
        parts = len(orders)
        return [
            Spread(at, make, orders[k], k, parts, source, ref, local()) for k in range(parts)
        ]

    s_qkv = spread(qkv_w_ref, sources[0], ("mixed",) * 3)
    (s_out,) = spread(out_w_ref, sources[1], ("mixed",))
    s_up = spread(up_w_ref, sources[2], ("mixed", "mixed", "mixed"))
    d_one, d_two = spread(down_w_ref, sources[3], ("mixed", "mixed"))
    save_w = pltpu.make_async_copy(qkv_w_ref, qkv_w_out, local())
    save_h = pltpu.make_async_copy(h_ref, h_out, local())
    save_x = pltpu.make_async_copy(x_ref, x_out, local())
    save_far = pltpu.make_async_copy(x_far_ref, x_far_out, local())
    save_kv = [
        pltpu.make_async_copy(kv_ref.at[:, g], kv_out.at[:, g], local()) for g in range(groups)
    ]
    x_lanes = [pl.ds(s * rows, rows) for s in range(2)]
    x_moves = [make(tokens_ref.at[l], far_tokens_ref.at[l], at.across_x) for l in x_lanes]
    far = at.across_x[1]
    kv_moves = [
        [
            [
                make(kv_ref.at[b, g, :, x_lanes[s]], kv_ref.at[b, g, :, x_lanes[s]], at.partner)
                for b in (at.band, far)
            ]
            for g in range(groups)
        ]
        for s in range(2)
    ]

    row = 0
    for ref in (shard_qkv_ref, shard_out_ref, shard_up_ref):
        turned = ref[...].astype(F).T.astype(BF)
        count = turned.shape[0] // 2
        for core in range(2):
            narrow_ref[core, pl.ds(row, count), :] = turned[core * count : (core + 1) * count]
        row += count
    wide_ref[...] = shard_down_ref[...].astype(F).T.astype(BF)
    greet([at.partner, at.across_x] + others)
    x_moves[0].start()
    x_moves[1].start()
    swap.start()
    own_wide.start()
    swap_wide.start()
    keep_small.start()
    for copy in small_copies:
        copy.start()
    fill_bias(scalars_ref, bias_ref, rows)
    swap.wait_recv()
    mine, theirs = narrow_ref[c], theirs_ref[...]
    lane_count = mine.shape[1]
    mine_ref[:, pl.ds(0, lane_count)] = jnp.where(c == 0, mine, theirs)
    mine_ref[:, pl.ds(lane_count, lane_count)] = jnp.where(c == 0, theirs, mine)
    for item in s_qkv:
        item.start()
    own_wide.wait()
    swap_wide.wait_recv()
    s_out.start()
    for item in s_up:
        item.start()
    d_two.start()
    d_one.start()

    for s in range(2):
        x_ref[:, x_lanes[s]] = tokens_ref[x_lanes[s], :].astype(F).T.astype(BF)
        cot_ref[:, x_lanes[s]] = cot_tokens_ref[x_lanes[s], :].astype(F).T.astype(BF)
    save_x.start()

    keep_small.wait()
    for copy in small_copies:
        copy.wait_recv()
    turned = smalls_ref[...].T
    qv_units, up_units = 2, up_w_ref.shape[2] // unit
    singles = 16 - qv_units - up_units
    for j in range(images):
        block = turned[:unit, 16 * j : 16 * j + 16]
        cols_ref[pl.ds(unit * j, unit), :] = block[:, :singles]
        for u in range(qv_units):
            lane = singles + u
            qv_col_ref[pl.ds(unit * (qv_units * j + u), unit), :] = block[:, lane : lane + 1]
        for u in range(up_units):
            lane = singles + qv_units + u
            up_col_ref[pl.ds(unit * (up_units * j + u), unit), :] = block[:, lane : lane + 1]

    def far_tokens(s):
        x_moves[s].wait_recv()
        x_far_ref[:, x_lanes[s]] = far_tokens_ref[x_lanes[s], :].astype(F).T.astype(BF)

    def first_norm(s, ref, side):
        normed, _ = normalize(ref[:, x_lanes[s]].astype(F))
        to = pl.ds(side * tokens + s * rows, rows)
        h_ref[:, to] = (normed * cols_ref[:, GAIN_ONE] + cols_ref[:, SHIFT_ONE]).astype(BF)

    s_qkv[0].step(1)
    s_qkv[1].step(1)
    s_qkv[0].step(2)
    s_qkv[2].step(1)
    for s in range(2):
        first_norm(s, x_ref, 0)
    s_qkv[1].step(2)
    s_qkv[0].step(3)
    s_qkv[2].step(2)
    s_out.step(1)
    far_tokens(0)
    first_norm(0, x_far_ref, 1)
    s_qkv[1].step(3)
    s_up[0].step(1)
    s_up[1].step(1)
    s_qkv[2].step(3)
    s_up[2].step(1)
    d_two.step(1)
    for item in s_qkv:
        item.wait()
    d_one.step(1)
    save_w.start()

    weights = qkv_w_ref.reshape(3 * width, width)
    scale = 1.0 / math.sqrt(HEAD_DIM)

    def project(s):
        for g in range(groups):
            for k in range(2):
                row = (1 + k) * width + g * part
                to = pl.ds(k * part, part)
                for side, band in enumerate((at.band, far)):
                    lanes = pl.ds(side * tokens + s * rows, rows)
                    out = dg(weights[pl.ds(row, part), :], h_ref[:, lanes], 1, 0)
                    if k == 1:
                        out = out + qv_col_ref[pl.ds(width + g * part, part), :]
                    kv_ref[band, g, to, x_lanes[s]] = out.astype(BF)
            for copy in kv_moves[s][g]:
                copy.start()
        for g in range(groups):
            block = pl.ds(g * part, part)
            out = dg(weights[block, :], h_ref[:, x_lanes[s]], 1, 0) + qv_col_ref[block, :]
            q_ref[block, x_lanes[s]] = (out * scale).astype(BF)

    def second_slot():
        far_tokens(1)
        first_norm(1, x_far_ref, 1)
        project(1)
        save_h.start()
        save_far.start()

    def arrive(s, g):
        for copy in kv_moves[s][g]:
            copy.wait_recv()
        if s == 1:
            save_kv[g].start()

    events = {}

    def when(j, *actions):
        events.setdefault(j, []).extend(actions)

    when(2, second_slot)
    for j in range(1, 2 * groups):
        when(j - 1, functools.partial(arrive, j // groups, j % groups))
    when(0, functools.partial(s_out.step, 2))
    when(1, functools.partial(s_up[0].step, 2))
    when(2, functools.partial(s_up[1].step, 2))
    when(3, functools.partial(s_up[2].step, 2), functools.partial(s_out.step, 3))
    when(4, functools.partial(d_two.step, 2))
    when(5, functools.partial(d_one.step, 2))
    when(6, functools.partial(s_up[0].step, 3))
    when(7, functools.partial(s_up[1].step, 3))
    project(0)
    arrive(0, 0)
    unroll = HEADS // groups

    @pl.loop(0, 2 * groups)
    def _(j):
        s, g = j // groups, j % groups
        for k in range(unroll):
            attend_step(
                s * HEADS + g * unroll + k, at.x, q_ref, kv_ref, bias_ref, att_ref, lse_ref
            )
        for when_j, actions in events.items():

            @pl.when(j == when_j)
            def _():
                for action in actions:
                    action()

    hidden = up_w_ref.shape[0] * 2 * up_w_ref.shape[2]
    blocks = hidden // 256
    quarter = blocks // 4

    def wait_out():
        s_up[2].step(3)
        s_out.wait()

    def wait_up():
        d_two.step(3)
        for item in s_up:
            item.wait()

    def wait_one():
        d_one.step(3)
        d_one.wait()

    def flat(ref):
        return ref.reshape(ref.shape[0] * 2 * ref.shape[2], ref.shape[3])

    middle_body(
        x_ref, cot_ref, scalars_ref, att_ref, flat(out_w_ref), flat(up_w_ref), flat(down_w_ref),
        cols_ref, up_col_ref, *results, *middle_scratch, wait_out, wait_up,
        [
            (d_two.wait, 2 * quarter, lambda t: t + t // quarter * quarter + quarter),
            (wait_one, 2 * quarter, lambda t: t + t // quarter * quarter),
        ],
    )
    for item in s_qkv + s_up + [s_out, d_one, d_two]:
        item.end()
    for copy in [save_w, save_h, save_x, save_far] + save_kv:
        copy.wait()
    for copy in [swap, swap_wide] + small_copies + x_moves:
        copy.wait_send()
    for copy in sum(sum(kv_moves, []), []):
        copy.wait_send()


def front(images, bands, scalars, shards, small, tokens_by_slot, cot_by_slot):
    depth = images // 2
    tokens, width = tokens_by_slot.shape
    groups = GROUPS_OF_HEADS
    widths = [item.shape[1] for item in shards[:3]]
    hidden = images * widths[2]
    full = (width, tokens)
    part = shards[0].shape[0]
    narrow = (2, sum(widths) // 2, part)
    wide = (shards[3].shape[1], shards[3].shape[0])
    kv = (bands, groups, 2 * width // groups, tokens)
    weights = [(depth, 2, w, width) for w in widths]
    weights.append((depth, 2, wide[0], 4 * wide[1]))
    return pl.pallas_call(
        functools.partial(front_kernel, images, bands),
        name="front",
        out_shape=(
            shape(weights[0], BF),
            shape((width, 2 * tokens), BF),
            shape(kv, BF),
            shape(full, BF),
            shape(full, BF),
            shape(full, BF),
            shape((2 * HEADS, tokens // 2), F),
            shape((width, COLUMNS), F),
            shape((tokens, width), BF),
            shape(full, F),
            shape(full, BF),
            shape((HEADS, tokens), F),
            shape((width, width), BF),
            shape((hidden, width), BF),
            shape((width, hidden), BF),
            shape((SUM_ROWS, width), F),
        ),
        in_specs=[SM] + [VM] * 7,
        out_specs=(ANY,) * 5 + (VM,) * 8 + (ANY, ANY, VM),
        scratch_shapes=[pltpu.VMEM(s, BF) for s in (narrow, wide, full, full, (tokens, width))]
        + [pltpu.VMEM(s, BF) for s in weights]
        + [
            pltpu.VMEM((width, 2 * tokens), BF),
            pltpu.VMEM(kv, BF),
            pltpu.VMEM(full, F),
            pltpu.VMEM((hidden, 1), F),
            pltpu.VMEM(narrow[1:], BF),
            pltpu.VMEM((narrow[1], 2 * narrow[2]), BF),
            pltpu.VMEM((wide[0] // 2, 2 * wide[1]), BF),
            pltpu.VMEM((16 * images, 128), F),
            pltpu.VMEM((2 * width, 1), F),
            pltpu.VMEM((8, tokens // 2), F),
            pltpu.VMEM(full, BF),
            pltpu.SemaphoreType.DMA((24,)),
            pltpu.SemaphoreType.DMA((FRONT_COPIES,)),
            pltpu.SemaphoreType.DMA((FRONT_COPIES,)),
            pltpu.VMEM((hidden, width), BF),
            pltpu.VMEM((width, hidden), BF),
            pltpu.VMEM(full, F),
            pltpu.VMEM(full, F),
            pltpu.VMEM(full, BF),
            pltpu.VMEM(full, BF),
            pltpu.VMEM(full, F),
            pltpu.VMEM(full, F),
            pltpu.VMEM(full, BF),
            pltpu.VMEM(full, BF),
            pltpu.SemaphoreType.DMA((hidden // 256,)),
            pltpu.SemaphoreType.DMA((hidden // 256,)),
        ],
        compiler_params=comm_params(0),
    )(scalars, *shards, small, tokens_by_slot, cot_by_slot)


def share_kernel(images, kv_ref, all_ref, local_sem, send_sem, recv_sem):
    at = Place(images)
    greet([at.partner, at.across_x])
    rows = kv_ref.shape[1] // 2
    mine = pltpu.make_async_copy(kv_ref, all_ref.at[at.band], local_sem)
    mine.start()
    copies = []
    for s in range(2):
        lanes = pl.ds(s * rows, rows)
        copies.append(
            send(
                kv_ref.at[:, lanes],
                all_ref.at[at.band, :, lanes],
                send_sem.at[s],
                recv_sem.at[s],
                at.across_x,
            )
        )
    near = send(kv_ref, all_ref.at[at.band], send_sem.at[2], recv_sem.at[2], at.partner)
    passed = []
    for s in range(2):
        copies[s].wait_recv()
        part = all_ref.at[at.across_x[1], :, pl.ds(s * rows, rows)]
        passed.append(send(part, part, send_sem.at[3 + s], recv_sem.at[3 + s], at.partner))
    for copy in passed + [near]:
        copy.wait()
    for copy in copies:
        copy.wait_send()
    mine.wait()


def share(images, bands, kv):
    return pl.pallas_call(
        functools.partial(share_kernel, images),
        name="share",
        out_shape=shape((bands,) + kv.shape, BF),
        in_specs=[VM],
        out_specs=ANY,
        scratch_shapes=[
            pltpu.SemaphoreType.DMA,
            pltpu.SemaphoreType.DMA((5,)),
            pltpu.SemaphoreType.DMA((5,)),
        ],
        compiler_params=comm_params(1),
    )(kv)


def add_rows(total_ref, other_ref, step):
    @pl.loop(0, total_ref.shape[0] // step)
    def _(j):
        rows = pl.ds(pl.multiple_of(j * step, step), step)
        total_ref[rows, :] = (
            total_ref[rows, :].astype(F) + other_ref[rows, :].astype(F)
        ).astype(total_ref.dtype)


def unshare_kernel(images, dkv_ref, sum_ref, near_ref, far_ref, send_sem, recv_sem):
    at = Place(images)
    greet([at.partner, at.across_x])
    mate, far = at.partner[1], at.across_x[1]
    far_mate = at.band + 2 - 4 * at.x + 1 - 2 * at.c
    one = send(dkv_ref.at[far_mate], near_ref.at[0], send_sem.at[0], recv_sem.at[0], at.partner)
    two = send(dkv_ref.at[mate], near_ref.at[1], send_sem.at[1], recv_sem.at[1], at.partner)
    one.wait_recv()
    add_rows(near_ref.at[0], dkv_ref.at[far], 64)
    three = send(near_ref.at[0], far_ref, send_sem.at[2], recv_sem.at[2], at.across_x)
    two.wait_recv()
    add_rows(near_ref.at[1], dkv_ref.at[at.band], 64)
    three.wait_recv()
    sum_ref[...] = near_ref[1]
    add_rows(sum_ref, far_ref, 64)
    for copy in (one, two, three):
        copy.wait_send()


def unshare(images, dkv):
    block = dkv.shape[1:]
    return pl.pallas_call(
        functools.partial(unshare_kernel, images),
        name="unshare",
        out_shape=shape(block, BF),
        in_specs=[VM],
        out_specs=VM,
        scratch_shapes=[
            pltpu.VMEM((2,) + block, BF),
            pltpu.VMEM(block, BF),
            pltpu.SemaphoreType.DMA((3,)),
            pltpu.SemaphoreType.DMA((3,)),
        ],
        compiler_params=comm_params(2),
    )(dkv)


def accumulate(total, other):
    total[...] = total[...] + other[...]


class Reduction:
    def __init__(self, at, make, order, start, size, ref, one, other, bufs, total):
        depth, near = at.depth, at.depth // 2
        half = ref.shape[3] // 2
        self.at, self.near, self.one, self.other, self.order = at, near, one, other, order

        def lanes_of(x):
            return pl.ds(pl.multiple_of(x * half + start, 128), size)

        self.lanes, self.both = lanes_of(at.x), [lanes_of(x) for x in range(2)]
        self.total = total.at[:, pl.ds(start, size)]
        far = lanes_of(1 - at.x)
        upper = depth - near
        if order == "mixed":
            two_x, two_y, three, four = bufs
            self.two_x, self.two_y = two_x, two_y
            low, high = pl.ds(0, near), pl.ds(near, upper)
            self.first = [make(one.at[low, :, :, far], two_x, at.across_x)] + [
                make(one.at[high, 1 - at.y, :, self.both[x]], two_y.at[x], at.across_y)
                for x in range(2)
            ]
            self.second = [
                make(two_x.at[:, 1 - at.y], three.at[low], at.across_y),
                make(two_y.at[1 - at.x], three.at[high], at.across_x),
            ]
        else:
            two, three, four = bufs
            self.two = two
            self.first = [
                make(one.at[:, 1 - at.y, :, self.both[x]], two.at[x], at.across_y)
                for x in range(2)
            ]
            self.second = [make(two.at[1 - at.x], three, at.across_x)]
        self.three, self.four = three, four
        self.third = [
            make(three.at[z], four.at[k], peer) for k, (peer, z) in enumerate(at.z_peers)
        ]

    def step_one(self):
        for lanes in self.both:

            @pl.loop(0, 2 * self.at.depth)
            def _(j):
                accumulate(
                    self.one.at[j // 2, j % 2, :, lanes],
                    self.other.at[j // 2, j % 2, :, lanes],
                )

        for copy in self.first:
            copy.start()

    def step_two(self):
        at = self.at
        if self.order == "mixed":
            self.first[0].wait_recv()

            @pl.loop(0, 2 * self.near)
            def _(j):
                accumulate(
                    self.two_x.at[j // 2, j % 2], self.one.at[j // 2, j % 2, :, self.lanes]
                )

            self.second[0].start()
            for x in range(2):
                self.first[1 + x].wait_recv()

                @pl.loop(0, at.depth - self.near)
                def _(j):
                    accumulate(
                        self.two_y.at[x, j], self.one.at[self.near + j, at.y, :, self.both[x]]
                    )

            self.second[1].start()
        else:
            for x in range(2):
                self.first[x].wait_recv()

                @pl.loop(0, at.depth)
                def _(j):
                    accumulate(self.two.at[x, j], self.one.at[j, at.y, :, self.both[x]])

            self.second[0].start()

    def step_three(self):
        at = self.at
        for copy in self.second:
            copy.wait_recv()
        if self.order == "mixed":

            @pl.loop(0, self.near)
            def _(j):
                accumulate(self.three.at[j], self.two_x.at[j, at.y])

            @pl.loop(0, at.depth - self.near)
            def _(j):
                accumulate(self.three.at[self.near + j], self.two_y.at[at.x, j])

        else:

            @pl.loop(0, at.depth)
            def _(j):
                accumulate(self.three.at[j], self.two.at[at.x, j])

        for copy in self.third:
            copy.start()

    def step_four(self):
        for copy in self.third:
            copy.wait_recv()
        total = self.three[self.at.z].astype(F)
        for k in range(len(self.third)):
            total = total + self.four[k].astype(F)
        self.total[...] = total

    def end(self):
        for copy in self.first + self.second + self.third:
            copy.wait_send()


def reduction_buffers(order, depth, rows, size):
    near = depth // 2
    if order == "mixed":
        first = [(near, 2, rows, size), (2, depth - near, rows, size)]
    else:
        first = [(2, depth, rows, size)]
    return [pltpu.VMEM(s, BF) for s in first + [(depth, rows, size), (depth - 1, rows, size)]]


BACK_ORDERS = (
    (("mixed", 1), ("mixed", 1)),
    (("mixed", 1), ("mixed", 1), ("mixed", 1)),
    (("mixed", 1),),
    (("mixed", 2), ("yx", 1)),
)


def lane_parts(orders, half):
    unit = half // sum(share for _, share in orders)
    parts, start = [], 0
    for order, share in orders:
        parts.append((order, start, share * unit))
        start += share * unit
    return parts


def back_kernel(
    images, bands, scalars_ref, q_ref, delta_ref, lse_ref, datt_ref, cols_ref, sums_ref,
    kv_in, x_in, x_far_in, h_in, dmid_in, w_in, g_out_ref, g_up_ref, g_down_ref,
    gx_ref, o_qkv_ref, o_out_ref, o_up_ref, o_down_ref, total_ref,
    p_down_ref, p_up_ref, p_out_ref, p_qkv_ref,
    kv_ref, x_ref, x_far_ref, h_ref, dmid_ref, w_ref,
    bias_ref, dq_ref, dwide_ref, dkv_ref, near_ref, g_qkv_ref, err_ref, err_far_ref, err_in_ref,
    small_ref, small_in_ref, small_z_ref, *rest,
):
    at = Place(images)
    depth = at.depth
    local_sem, send_sem, recv_sem = rest[-3:]
    rest = list(rest[:-3])
    used = [0, 0]

    def make(src, dst, peer):
        k = used[0]
        used[0] += 1
        return pltpu.make_async_remote_copy(
            src_ref=src,
            dst_ref=dst,
            send_sem=send_sem.at[k],
            recv_sem=recv_sem.at[k],
            device_id=peer,
            device_id_type=MESH,
        )

    def load(src, dst):
        used[1] += 1
        return pltpu.make_async_copy(src, dst, local_sem.at[used[1] - 1])

    width, tokens = x_ref.shape
    rows = tokens // 2
    unroll = 4
    groups = HEADS // unroll
    part = width // groups

    def four_d(ref):
        return ref.reshape(depth, 2, ref.shape[0] // images, ref.shape[1])

    sources = (four_d(g_down_ref), four_d(g_up_ref), four_d(g_out_ref), g_qkv_ref)
    targets = (p_down_ref, p_up_ref, p_out_ref, p_qkv_ref)
    swaps, owns, moves, ends = [], [], [], []
    for m in range(4):
        one, total, away = rest[:3]
        rest = rest[3:]
        block, lanes = sources[m].shape[2] // 2, sources[m].shape[3]
        near_rows = pl.ds(pl.multiple_of(at.c * block, 16), block)
        far_rows = pl.ds(pl.multiple_of((1 - at.c) * block, 16), block)
        parts = lane_parts(BACK_ORDERS[m], lanes // 2)
        if m < 3:
            other = rest.pop(0)
            owns.append(load(sources[m].at[:, :, near_rows, :], one))
            swaps.append([make(sources[m].at[:, :, far_rows, :], other, at.partner)])
        else:
            other = sources[m].at[:, :, near_rows, :]
            for _, start, size in parts:
                both = [pl.ds(x * (lanes // 2) + start, size) for x in range(2)]
                swaps.append(
                    [
                        make(sources[m].at[:, :, far_rows, l], one.at[:, :, :, l], at.partner)
                        for l in both
                    ]
                )
        moves.append([])
        for order, start, size in parts:
            count = 4 if order == "mixed" else 3
            moves[m].append(
                Reduction(
                    at, make, order, start, size, sources[m], one, other, rest[:count], total
                )
            )
            rest = rest[count:]
        ends.append((total, away, targets[m], make(away, targets[m].at[at.c], at.partner)))
    down, up, out, qkv = moves

    def deliver(m):
        total_ref, away, target, copy = ends[m]
        total = total_ref[...]
        size = total.shape[1] // 2
        low, high = total[:, :size], total[:, size:]
        target[at.c] = jnp.where(at.c == 0, low, high)
        away[...] = jnp.where(at.c == 0, high, low)
        copy.start()

    mate, far = at.partner[1], at.across_x[1]
    far_mate = at.across_x[1] + 1 - 2 * at.c
    one = [make(dkv_ref.at[far_mate, g], near_ref.at[0, g], at.partner) for g in range(groups)]
    two = [make(dkv_ref.at[mate, g], near_ref.at[1, g], at.partner) for g in range(groups)]
    err_moves = [make(err_far_ref.at[s], err_in_ref.at[s], at.across_x) for s in range(2)]
    small_steps = [
        make(small_ref.at[k], small_in_ref.at[k], peer)
        for k, peer in enumerate((at.partner, at.across_x, at.across_y))
    ]
    small_last = [
        make(small_z_ref.at[at.z], small_z_ref.at[at.z], peer) for peer, _ in at.z_peers
    ]

    kv_loads = [load(kv_in.at[:, g], kv_ref.at[:, g]) for g in range(groups)]
    late_loads = [
        load(h_in, h_ref),
        load(w_in, w_ref),
        load(x_in, x_ref),
        load(x_far_in, x_far_ref),
        load(dmid_in, dmid_ref),
    ]
    kv_loads[0].start()
    owns[0].start()
    greet([at.partner, at.across_x, at.across_y] + [peer for peer, _ in at.z_peers])
    for m in range(3):
        swaps[m][0].start()
    for copy in owns[1:] + kv_loads[1:] + late_loads:
        copy.start()
    fill_bias(scalars_ref, bias_ref, rows)

    sides = [pl.ds(side * tokens, tokens) for side in range(2)]

    def share_one(g):
        one[g].start()
        two[g].start()

    def share_two(g):
        for copy, side, band in ((one[g], 1, far), (two[g], 0, at.band)):
            copy.wait_recv()
            for half in range(2):
                block = pl.ds(half * part, part)
                to = pl.ds(half * width + g * part, part)
                value = (
                    near_ref[1 - side, g, block, :].astype(F)
                    + dkv_ref[band, g, block, :].astype(F)
                ).astype(BF)
                dwide_ref[to, sides[side]] = value

    events = {}

    def when(j, *actions):
        events.setdefault(j, []).extend(actions)

    def received(m):
        owns[m].wait()
        swaps[m][0].wait_recv()

    for g in range(1, groups):
        when(2 * g - 1, kv_loads[g].wait)
    when(0, down[1].step_one)
    when(0, lambda: received(1), up[0].step_one)
    when(1, up[1].step_one, lambda: share_one(0))
    when(2, up[2].step_one, down[0].step_two, lambda: share_two(0))
    when(3, lambda: received(2), out[0].step_one, down[1].step_two, lambda: share_one(1))
    when(4, up[0].step_two, down[0].step_three, lambda: share_two(1))
    when(5, up[1].step_two, down[1].step_three, lambda: share_one(2))
    when(6, up[2].step_two, up[0].step_three, lambda: share_two(2))
    when(7, lambda: share_one(3), out[0].step_two, up[1].step_three)
    received(0)
    down[0].step_one()
    kv_loads[0].wait()

    @pl.loop(0, 2 * groups)
    def _(j):
        g, s = j // 2, j % 2
        lanes = pl.ds(pl.multiple_of(s * rows, rows), rows)
        for k in range(unroll):

            def put_key(b, values):
                dkv_ref[b, g, pl.ds(k * HEAD_DIM, HEAD_DIM), lanes] = values

            def put_value(b, values):
                dkv_ref[b, g, pl.ds(part + k * HEAD_DIM, HEAD_DIM), lanes] = values

            attend_back_step(
                s * HEADS + g * unroll + k,
                at.x, q_ref, kv_ref, delta_ref, lse_ref, datt_ref, bias_ref, dq_ref,
                put_key, put_value,
            )
        for when_j, actions in events.items():

            @pl.when(j == when_j)
            def _():
                for action in actions:
                    action()

    chunk = width // 2
    g_flat = g_qkv_ref.reshape(3 * width, width)
    parts = lane_parts(BACK_ORDERS[3], width // 2)

    def weight_grad(part, source_ref, first, count, tokens_at):
        _, start, size = parts[part]
        lanes = [pl.ds(x * (width // 2) + start, size) for x in range(2)]

        @pl.loop(0, count)
        def _(j):
            block = pl.ds(pl.multiple_of(j * chunk, 128), chunk)
            to = pl.ds(pl.multiple_of((first + j) * chunk, 128), chunk)
            both = jnp.concatenate([h_ref[l, tokens_at] for l in lanes], axis=0)
            result = dg(source_ref[block, :], both, 1, 1).astype(BF)
            g_flat[to, lanes[0]] = result[:, :size]
            g_flat[to, lanes[1]] = result[:, size:]

    def back_through(side):
        err_ref[...] = jnp.zeros_like(err_ref)

        @pl.loop(0, 4)
        def _(j):
            block = pl.ds(pl.multiple_of(j * chunk, 128), chunk)
            source = pl.ds(pl.multiple_of((2 + j) * chunk, 128), chunk)
            err_ref[...] += dg(w_ref[source, :], dwide_ref[block, sides[side]], 0, 0)

    def start_swap(part):
        for copy in swaps[3 + part]:
            copy.start()

    def first_sum(part):
        for copy in swaps[3 + part]:
            copy.wait_recv()
        qkv[part].step_one()

    for copy in late_loads:
        copy.wait()
    for p in range(2):
        weight_grad(p, dq_ref, 0, 2, sides[0])
    share_two(groups - 1)
    weight_grad(0, dwide_ref, 2, 4, slice(None))
    start_swap(0)
    back_through(1)
    err_far = err_ref[...]
    for s in range(2):
        err_far_ref[s] = err_far[:, s * rows : (s + 1) * rows].astype(BF)
    first_sum(0)
    err_moves[0].start()
    weight_grad(1, dwide_ref, 2, 4, slice(None))
    start_swap(1)
    normed_far, _ = normalize(x_far_ref[...].astype(F))
    gain_row = row_sums(err_ref[...] * normed_far)[:1]
    shift_row = row_sums(err_ref[...])[:1]
    first_sum(1)
    up[2].step_three()
    out[0].step_three()
    back_through(0)

    @pl.loop(0, 2)
    def _(j):
        block = pl.ds(pl.multiple_of(j * chunk, 128), chunk)
        err_ref[...] += dg(w_ref[block, :], dq_ref[block, :], 0, 0)

    small_ref[0] = sums_ref[...]
    small_ref[0, 0:1] = row_sums(dq_ref[...])[:1]
    small_ref[0, 1:2] = row_sums(dwide_ref[pl.ds(width, width), :])[:1]
    normed, _ = normalize(x_ref[...].astype(F))
    small_ref[0, 4:5] = gain_row + row_sums(err_ref[...] * normed)[:1]
    small_ref[0, 5:6] = shift_row + row_sums(err_ref[...])[:1]
    small_steps[0].start()
    qkv[0].step_two()
    for item in down:
        item.step_four()
    deliver(0)
    small_steps[0].wait_recv()
    small_ref[1] = small_ref[0] + small_in_ref[0]
    small_steps[1].start()
    qkv[1].step_two()
    err_moves[1].start()
    qkv[0].step_three()
    small_steps[1].wait_recv()
    small_ref[2] = small_ref[1] + small_in_ref[1]
    small_steps[2].start()
    for item in up:
        item.step_four()
    deliver(1)
    small_steps[2].wait_recv()
    small_z_ref[at.z] = small_ref[2] + small_in_ref[2]
    for copy in small_last:
        copy.start()
    out[0].step_four()
    deliver(2)
    qkv[1].step_three()

    def finish_slot(s):
        err_moves[s].wait_recv()
        lanes = slice(s * rows, (s + 1) * rows)
        err = err_ref[:, lanes] + err_in_ref[s].astype(F)
        normed, inverse = normalize(x_ref[:, lanes].astype(F))
        grad = dmid_ref[:, lanes] + norm_back(err, normed, inverse, cols_ref[:, GAIN_ONE])
        gx_ref[lanes, :] = grad.T.astype(BF)

    finish_slot(0)
    qkv[0].step_four()
    for copy in small_last:
        copy.wait_recv()
    total = small_z_ref[0]
    for k in range(1, depth):
        total = total + small_z_ref[k]
    total_ref[...] = total
    qkv[1].step_four()
    deliver(3)
    finish_slot(1)
    for m, ref in enumerate((o_down_ref, o_up_ref, o_out_ref, o_qkv_ref)):
        ends[m][3].wait()
        ref[...] = jnp.concatenate([targets[m][k] for k in range(2)], axis=0).T
        for item in moves[m]:
            item.end()
    for copy in sum(swaps, []) + one + two + err_moves + small_steps + small_last:
        copy.wait_send()


def back(
    images, bands, scalars, q, kv, delta, lse, datt, x, x_far, h, dmid, w, cols, grads, sums
):
    depth = images // 2
    width, tokens = x.shape
    g_out, g_up, g_down = grads
    groups = HEADS // 4
    results, placed, buffers = [], [], []
    for m, item in enumerate((g_down, g_up, g_out, w)):
        block, lanes = item.shape[0] // images // 2, item.shape[1]
        results.append(shape((lanes // 4, 2 * block), F))
        placed.append(pltpu.VMEM((2, block, lanes // 4), F))
        buffers += [
            pltpu.VMEM((depth, 2, block, lanes), BF),
            pltpu.VMEM((block, lanes // 2), F),
            pltpu.VMEM((block, lanes // 4), F),
        ]
        if m < 3:
            buffers.append(pltpu.VMEM((depth, 2, block, lanes), BF))
        for order, _, size in lane_parts(BACK_ORDERS[m], lanes // 2):
            buffers += reduction_buffers(order, depth, block, size)
    small = (SUM_ROWS, width)
    return pl.pallas_call(
        functools.partial(back_kernel, images, bands),
        name="back",
        out_shape=(shape((tokens, width), BF), results[3], results[2], results[1], results[0], shape(small, F)),
        in_specs=[SM] + [VM] * 6 + [ANY] * 9,
        out_specs=(VM,) * 6,
        scratch_shapes=placed
        + [
            pltpu.VMEM(kv.shape, BF),
            pltpu.VMEM((width, tokens), BF),
            pltpu.VMEM((width, tokens), BF),
            pltpu.VMEM((width, 2 * tokens), BF),
            pltpu.VMEM((width, tokens), F),
            pltpu.VMEM(w.shape, BF),
            pltpu.VMEM((8, tokens // 2), F),
            pltpu.VMEM((width, tokens), BF),
            pltpu.VMEM((2 * width, 2 * tokens), BF),
            pltpu.VMEM((bands, groups, 2 * width // groups, tokens), BF),
            pltpu.VMEM((2, groups, 2 * width // groups, tokens), BF),
            pltpu.VMEM((depth, 2, w.shape[0] // images, width), BF),
            pltpu.VMEM((width, tokens), F),
            pltpu.VMEM((2, width, tokens // 2), BF),
            pltpu.VMEM((2, width, tokens // 2), BF),
            pltpu.VMEM((3,) + small, F),
            pltpu.VMEM((3,) + small, F),
            pltpu.VMEM((depth,) + small, F),
        ]
        + buffers
        + [
            pltpu.SemaphoreType.DMA((16,)),
            pltpu.SemaphoreType.DMA((BACK_COPIES,)),
            pltpu.SemaphoreType.DMA((BACK_COPIES,)),
        ],
        compiler_params=comm_params(3),
    )(
        scalars, q, delta, lse, datt, cols, sums, kv, x, x_far, h, dmid, w, g_out, g_up, g_down
    )


def body(
    tokens,
    slot_kind,
    w_qkv,
    w_out,
    w_up,
    w_down,
    bias_qv,
    bias_out,
    bias_up,
    bias_down,
    gain_one,
    shift_one,
    gain_two,
    shift_two,
    cotangent,
):
    rows, slots, width = tokens.shape[1:]
    count = rows * slots
    images, bands = lax.axis_size("img"), lax.axis_size("band")
    band = lax.axis_index("band")
    smalls = (bias_qv, bias_out, bias_up, bias_down, gain_one, shift_one, gain_two, shift_two)
    sizes = [item.shape[0] for item in smalls]
    own = (w_qkv, w_out, w_up)
    widths = [item.shape[1] for item in own]
    direct = images % 4 == 0 and all(w % 32 == 0 for w in widths + [w_down.shape[1]])
    direct = direct and bias_qv.shape[0] == 2 * (width // images) <= 256
    direct = direct and bias_up.shape[0] == 4 * (width // images)

    def by_slot(values):
        return values[0].transpose(1, 0, 2).reshape(count, width)

    def turn(values):
        return by_slot(values).T

    def turn_back(values):
        return values.reshape(slots, rows, width).transpose(1, 0, 2)[None]

    scalars = slot_kind
    single = (bias_out, bias_down, gain_one, shift_one, gain_two, shift_two)
    if direct:
        unit = width // images
        gap = jnp.zeros((128 - unit,), BF)
        pieces = []
        for item in single:
            pieces += [item, gap]
        pieces.append(jnp.zeros((4 * 128,), BF))
        for item in (bias_qv, bias_up):
            for k in range(0, item.shape[0], unit):
                pieces += [item[k : k + unit], gap]
        small = jnp.concatenate(pieces).astype(F).reshape(16, 128)
        full_qkv, h, all_kv, x, x_far, q, lse, cols, *rest = front(
            images, bands, scalars, (*own, w_down), small, by_slot(tokens), by_slot(cotangent)
        )
        full_qkv = full_qkv.reshape(-1, width)
    else:
        scalars = jnp.concatenate([slot_kind, jnp.full((1, 1), band // 2, jnp.int32)], axis=1)
        x, cot = turn(tokens), turn(cotangent)
        full_qkv, full_out, full_up, full_down = (
            lax.all_gather(lax.all_gather(item, "band", axis=0, tiled=True).T, "img", tiled=True)
            for item in (*own, w_down)
        )
        whole = [lax.all_gather(item, "img", tiled=True).astype(F) for item in single]
        cols = jnp.stack(whole + [whole[0]] * (COLUMNS - len(whole)), axis=1)
        c_qv = lax.all_gather(bias_qv, "img", tiled=True).astype(F)[:, None]
        c_up = lax.all_gather(bias_up, "img", tiled=True).astype(F)[:, None]
        bias = jnp.concatenate([c_qv[:width], jnp.zeros((width, 1), F), c_qv[width:]])
        h, qkv = project(x, full_qkv, cols, bias)
        q = qkv[:width]
        all_kv = share(images, bands, qkv[width:])
        all_kv = all_kv.reshape(bands, 2, GROUPS_OF_HEADS, -1, count).transpose(0, 2, 1, 3, 4)
        all_kv = all_kv.reshape(bands, GROUPS_OF_HEADS, -1, count)
        att, lse = attend(scalars, q, all_kv)
        rest = middle(x, cot, scalars, att, full_out, full_up, full_down, cols, c_up)
    out, dmid, datt, delta, g_out, g_up, g_down, sums = rest
    if direct:
        gx, *matrices, total = back(
            images, bands, scalars, q, all_kv, delta, lse, datt, x, x_far, h, dmid,
            full_qkv, cols, (g_out, g_up, g_down), sums,
        )
    else:
        dq, dkv = attend_back(scalars, q, all_kv, delta, lse, datt)
        dkv = unshare(images, dkv)
        gx, g_qkv, sums_one = finish(x, h, dq, dkv, full_qkv, cols, dmid)
        matrices = [
            lax.psum_scatter(
                lax.psum_scatter(item, "img", scatter_dimension=0, tiled=True),
                "band",
                scatter_dimension=1,
                tiled=True,
            )
            .astype(F)
            .T
            for item in (g_qkv, g_out, g_up, g_down)
        ]
        total = lax.psum(sums + sums_one, ("img", "band"))
    own_small = lax.axis_index("img")
    flat = total.reshape(-1)
    starts = [0, 2, UP_ROW, 3, 4, 5, 6, 7]
    small = [
        lax.dynamic_slice(flat, (start * width + own_small * size,), (size,))
        for start, size in zip(starts, sizes)
    ]
    return (turn_back(out), turn_back(gx), *matrices, *small)


def solution(mesh):
    data, weight, vector = P("img", "band", None, None), P("band", "img"), P("img")
    return jax.shard_map(
        body,
        mesh=mesh,
        in_specs=(data, P("img", None)) + (weight,) * 4 + (vector,) * 8 + (data,),
        out_specs=(data, data) + (weight,) * 4 + (vector,) * 8,
        check_vma=False,
    )
```

```python
import functools
import math

import jax
import jax.numpy as jnp
from jax import lax
from jax.experimental import pallas as pl
from jax.experimental.pallas import tpu as pltpu
from jax.sharding import PartitionSpec as P

HEADS = 16
HEAD_DIM = 48
EPSILON = 1e-06
MASKED = -1e30
BF = jnp.bfloat16
F = jnp.float32
MESH = pl.DeviceIdType.MESH
VM = pl.BlockSpec(memory_space=pltpu.VMEM)
SM = pl.BlockSpec(memory_space=pltpu.SMEM)
ANY = pl.BlockSpec(memory_space=pl.ANY)
LIMIT = 67043328
SUM_ROWS, UP_ROW = 16, 8
COLUMNS = 10
BIAS_OUT, BIAS_DOWN, GAIN_ONE, SHIFT_ONE, GAIN_TWO, SHIFT_TWO = (slice(k, k + 1) for k in range(6))
GROUPS_OF_HEADS = 4
FRONT_COPIES, BACK_COPIES = 128, 128


def dg(left, right, left_dim, right_dim):
    return lax.dot_general(
        left, right, (((left_dim,), (right_dim,)), ((), ())), preferred_element_type=F
    )


def shape(dims, dtype):
    return jax.ShapeDtypeStruct(tuple(dims), dtype)


def row_sums(values):
    ones = jnp.ones((8, values.shape[1]), BF)
    if values.dtype == BF:
        return dg(ones, values, 1, 1)
    high = values.astype(BF)
    low = (values - high.astype(F)).astype(BF)
    return dg(ones, high, 1, 1) + dg(ones, low, 1, 1)


def normalize(values):
    average = jnp.mean(values, axis=0, keepdims=True)
    centered = values - average
    variance = jnp.mean(centered * centered, axis=0, keepdims=True)
    inverse = lax.rsqrt(variance + EPSILON)
    return centered * inverse, inverse


def norm_back(error, normed, inverse, gain):
    f = gain * error
    mean_f = jnp.mean(f, axis=0, keepdims=True)
    mean_fn = jnp.mean(f * normed, axis=0, keepdims=True)
    return (f - mean_f - normed * mean_fn) * inverse


def project_kernel(x_ref, w_ref, cols_ref, bias_ref, h_ref, qkv_ref):
    width = x_ref.shape[0]
    normed, _ = normalize(x_ref[...].astype(F))
    h_ref[...] = (normed * cols_ref[:, GAIN_ONE] + cols_ref[:, SHIFT_ONE]).astype(BF)
    scale = 1.0 / math.sqrt(HEAD_DIM)
    step = 256

    @pl.loop(0, 3 * width // step)
    def _(j):
        rows = pl.ds(pl.multiple_of(j * step, step), step)
        out = dg(w_ref[rows, :], h_ref[...], 1, 0) + bias_ref[rows, :]
        qkv_ref[rows, :] = (out * jnp.where(j < width // step, scale, 1.0)).astype(BF)


def project(x, w, cols, bias):
    width, tokens = x.shape
    return pl.pallas_call(
        project_kernel,
        name="project",
        out_shape=(shape((width, tokens), BF), shape((3 * width, tokens), BF)),
        in_specs=[VM] * 4,
        out_specs=(VM, VM),
        compiler_params=pltpu.CompilerParams(vmem_limit_bytes=LIMIT),
    )(x, w, cols, bias)


def fill_bias(scalars_ref, bias_ref, rows):
    lane_half = lax.broadcasted_iota(jnp.int32, (1, rows), 1) // (rows // 2)
    for s in range(2):
        small = scalars_ref[0, s] == 2
        for other in range(2):
            for half in range(2):
                keep = jnp.logical_and(other == 0, lane_half == half)
                masked = jnp.where(small, MASKED, 0.0)
                bias_ref[pl.ds(4 * s + 2 * other + half, 1), :] = jnp.where(
                    keep, jnp.zeros((1, rows), F), jnp.full((1, rows), masked, F)
                )


def add_bias(scores, bias_ref, s, other):
    rows = scores.shape[0]
    at = 4 * s + 2 * other
    return jnp.concatenate(
        [
            scores[: rows // 2] + bias_ref[pl.ds(at, 1), :],
            scores[rows // 2 :] + bias_ref[pl.ds(at + 1, 1), :],
        ],
        axis=0,
    )


def head_slices(i, rows):
    s, h = i // HEADS, i % HEADS
    lanes = pl.ds(pl.multiple_of(s * rows, rows), rows)
    first = pl.ds(pl.multiple_of(h * HEAD_DIM, 16), HEAD_DIM)
    second = pl.ds(pl.multiple_of(HEADS * HEAD_DIM + h * HEAD_DIM, 16), HEAD_DIM)
    return s, lanes, first, second


def attend_step(i, chip_x, q_ref, kv_ref, bias_ref, out_ref, lse_ref):
    bands = kv_ref.shape[0]
    rows = q_ref.shape[1] // 2
    s, lanes, first, second = head_slices(i, rows)
    q = q_ref[first, lanes]
    scores = []
    maximum = None
    for b in range(bands):
        other = jnp.where(chip_x == b // 2, 0, 1)
        keys, _ = kv_rows(kv_ref, b, i % HEADS)
        part = add_bias(dg(keys[:, lanes], q, 0, 0), bias_ref, s, other)
        scores.append(part)
        top = jnp.max(part, axis=0, keepdims=True)
        maximum = top if maximum is None else jnp.maximum(maximum, top)
    total, acc = 0.0, 0.0
    for b in range(bands):
        weight = jnp.exp(scores[b] - maximum)
        total = total + jnp.sum(weight, axis=0, keepdims=True)
        _, values = kv_rows(kv_ref, b, i % HEADS)
        acc = acc + dg(values[:, lanes], weight.astype(BF), 1, 0)
    out_ref[first, lanes] = acc / total
    lse_ref[pl.ds(i, 1), :] = maximum + jnp.log(total)


def attend_kernel(unroll, scalars_ref, q_ref, kv_ref, out_ref, lse_ref, bias_ref):
    fill_bias(scalars_ref, bias_ref, q_ref.shape[1] // 2)

    @pl.loop(0, 2 * HEADS // unroll)
    def _(j):
        for k in range(unroll):
            attend_step(
                j * unroll + k, scalars_ref[0, 2], q_ref, kv_ref, bias_ref, out_ref, lse_ref
            )


def attend(scalars, q, kv):
    width, tokens = q.shape
    return pl.pallas_call(
        functools.partial(attend_kernel, 4),
        name="attend",
        out_shape=(shape((width, tokens), F), shape((2 * HEADS, tokens // 2), F)),
        in_specs=[SM, VM, VM],
        out_specs=(VM, VM),
        scratch_shapes=[pltpu.VMEM((8, tokens // 2), F)],
        compiler_params=pltpu.CompilerParams(vmem_limit_bytes=LIMIT),
    )(scalars, q, kv)


def attend_back_step(
    i, chip_x, q_ref, kv_ref, delta_ref, lse_ref, dout_ref, bias_ref, dq_ref, put_key, put_value
):
    bands = kv_ref.shape[0]
    rows = q_ref.shape[1] // 2
    s, lanes, first, second = head_slices(i, rows)
    q = q_ref[first, lanes]
    dout = dout_ref[first, lanes]
    delta = delta_ref[pl.ds(i % HEADS, 1), lanes]
    lse = lse_ref[pl.ds(i, 1), :]
    dq = 0.0
    for b in range(bands):
        other = jnp.where(chip_x == b // 2, 0, 1)
        k, v = (ref[:, lanes] for ref in kv_rows(kv_ref, b, i % HEADS))
        scores = add_bias(dg(k, q, 0, 0), bias_ref, s, other)
        dweight = dg(v, dout, 0, 0)
        weight = jnp.exp(scores - lse)
        dscores = (weight * (dweight - delta)).astype(BF)
        dq = dq + dg(k, dscores, 1, 0)
        put_key(b, dg(q, dscores, 1, 1).astype(BF))
        put_value(b, dg(dout, weight.astype(BF), 1, 1).astype(BF))
    dq_ref[first, lanes] = (dq * (1.0 / math.sqrt(HEAD_DIM))).astype(BF)


def attend_back_kernel(
    unroll, scalars_ref, q_ref, kv_ref, delta_ref, lse_ref, dout_ref, dq_ref, dkv_ref, bias_ref
):
    fill_bias(scalars_ref, bias_ref, q_ref.shape[1] // 2)

    @pl.loop(0, 2 * HEADS // unroll)
    def _(j):
        for k in range(unroll):
            i = j * unroll + k
            _, lanes, first, second = head_slices(i, q_ref.shape[1] // 2)

            def put_key(b, values):
                dkv_ref[b, first, lanes] = values

            def put_value(b, values):
                dkv_ref[b, second, lanes] = values

            attend_back_step(
                i, scalars_ref[0, 2], q_ref, kv_ref, delta_ref, lse_ref, dout_ref, bias_ref, dq_ref,
                put_key, put_value,
            )


def attend_back(scalars, q, kv, delta, lse, dout):
    return pl.pallas_call(
        functools.partial(attend_back_kernel, 4),
        name="attend_back",
        out_shape=(shape(q.shape, BF), shape((kv.shape[0], 2 * q.shape[0], q.shape[1]), BF)),
        in_specs=[SM] + [VM] * 5,
        out_specs=(VM, VM),
        scratch_shapes=[pltpu.VMEM((8, q.shape[1] // 2), F)],
        compiler_params=pltpu.CompilerParams(vmem_limit_bytes=LIMIT),
    )(scalars, q, kv, delta, lse, dout)


def middle_body(
    x_ref, cot_ref, scalars_ref, att_ref, w_out_ref, w_up_ref, w_down_ref, cols_ref, bias_up_ref,
    out_ref, dmid_ref, datt_ref, delta_ref, g_out_ref, g_up_out, g_down_out, sums_ref,
    g_up_ref, g_down_ref,
    mid_ref, norm_ref, h_ref, dmlp_ref, mlp_ref, err_ref, attb_ref, dbranch_ref,
    up_sem, down_sem, wait_out, wait_up, passes,
):
    width, tokens = x_ref.shape
    hidden = w_up_ref.shape[0]
    step = 256
    first_slot = lax.broadcasted_iota(jnp.int32, (1, tokens), 1) < tokens // 2
    valid = jnp.where(
        first_slot,
        jnp.where(scalars_ref[0, 0] > 0, 1.0, 0.0),
        jnp.where(scalars_ref[0, 1] > 0, 1.0, 0.0),
    )
    attb_ref[...] = att_ref[...].astype(BF)
    dmlp_ref[...] = (cot_ref[...].astype(F) * valid).astype(BF)
    sums_ref[...] = jnp.zeros_like(sums_ref)
    mlp_ref[...] = jnp.zeros_like(mlp_ref)
    err_ref[...] = jnp.zeros_like(err_ref)
    wait_out()

    @pl.loop(0, width // step)
    def _(j):
        rows = pl.ds(pl.multiple_of(j * step, step), step)
        mid_ref[rows, :] = (
            dg(w_out_ref[rows, :], attb_ref[...], 1, 0)
            + cols_ref[rows, BIAS_OUT]
            + x_ref[rows, :].astype(F)
        )

    normed, inverse = normalize(mid_ref[...])
    norm_ref[...] = normed
    h_ref[...] = (normed * cols_ref[:, GAIN_TWO] + cols_ref[:, SHIFT_TWO]).astype(BF)
    wait_up()

    def stores(j):
        rows = pl.ds(pl.multiple_of(j * step, step), step)
        return (
            pltpu.make_async_copy(g_up_ref.at[rows, :], g_up_out.at[rows, :], up_sem.at[j]),
            pltpu.make_async_copy(g_down_ref.at[:, rows], g_down_out.at[:, rows], down_sem.at[j]),
        )

    def block(j):
        rows = pl.ds(pl.multiple_of(j * step, step), step)
        pre = dg(w_up_ref[rows, :], h_ref[...], 1, 0) + bias_up_ref[rows, :]
        phi = 0.5 + 0.5 * lax.erf(pre * math.sqrt(0.5))
        act = (pre * phi).astype(BF)
        slope = phi + pre * jnp.exp(pre * pre * -0.5) * (1.0 / math.sqrt(2.0 * math.pi))
        mlp_ref[...] += dg(w_down_ref[:, rows], act, 1, 0)
        dact = dg(w_down_ref[:, rows], dmlp_ref[...], 0, 0)
        dhid = (slope * dact).astype(BF)
        g_down_ref[:, rows] = dg(dmlp_ref[...], act, 1, 1).astype(BF)
        g_up_ref[rows, :] = dg(dhid, h_ref[...], 1, 1).astype(BF)
        per = width // step
        lanes = pl.ds(pl.multiple_of(j % per * step, step), step)
        sums_ref[pl.ds(UP_ROW + j // per, 1), lanes] = row_sums(dhid)[:1]
        err_ref[...] += dg(w_up_ref[rows, :], dhid, 0, 0)
        for copy in stores(j):
            copy.start()

    for wait, count, place in passes:
        wait()

        @pl.loop(0, count)
        def _(t):
            block(place(t))

    out = (mid_ref[...] + mlp_ref[...] + cols_ref[:, BIAS_DOWN]) * valid
    out_ref[...] = out.T.astype(BF)
    err = err_ref[...]
    sums_ref[3:4] = row_sums(dmlp_ref[...])[:1]
    sums_ref[6:7] = row_sums(err * norm_ref[...])[:1]
    sums_ref[7:8] = row_sums(err)[:1]
    dmid = cot_ref[...].astype(F) * valid + norm_back(
        err, norm_ref[...], inverse, cols_ref[:, GAIN_TWO]
    )
    dmid_ref[...] = dmid
    dbranch_ref[...] = dmid.astype(BF)
    sums_ref[2:3] = row_sums(dbranch_ref[...])[:1]
    datt_ref[...] = dg(w_out_ref[...], dbranch_ref[...], 0, 0).astype(BF)
    inner = att_ref[...] * datt_ref[...].astype(F)
    delta_ref[...] = jnp.sum(inner.reshape(HEADS, width // HEADS, tokens), axis=1)

    @pl.loop(0, width // step)
    def _(j):
        rows = pl.ds(pl.multiple_of(j * step, step), step)
        g_out_ref[rows, :] = dg(dbranch_ref[rows, :], attb_ref[...], 1, 1).astype(BF)

    @pl.loop(0, hidden // step)
    def _(j):
        for copy in stores(j):
            copy.wait()


def middle_kernel(*refs):
    x_ref, cot_ref, scalars_ref, att_ref, w_out_in, w_up_in, w_down_in = refs[:7]
    outputs = refs[7:17]
    w_out_ref, w_up_ref, w_down_ref = refs[17:20]
    scratch, in_sem = refs[20:30], refs[30]
    loads = [
        pltpu.make_async_copy(source, target, in_sem.at[k])
        for k, (source, target) in enumerate(
            ((w_out_in, w_out_ref), (w_up_in, w_up_ref), (w_down_in, w_down_ref))
        )
    ]
    for copy in loads:
        copy.start()
    middle_body(
        x_ref, cot_ref, scalars_ref, att_ref, w_out_ref, w_up_ref, w_down_ref, *outputs, *scratch,
        *refs[31:], loads[0].wait, loads[1].wait,
        [(loads[2].wait, w_up_ref.shape[0] // 256, lambda t: t)],
    )


def middle(x, cot, scalars, att, w_out, w_up, w_down, cols, bias_up):
    width, tokens = x.shape
    hidden = w_up.shape[0]
    full = (width, tokens)
    weights = [w_out.shape, w_up.shape, w_down.shape]
    return pl.pallas_call(
        middle_kernel,
        name="middle",
        out_shape=(
            shape((tokens, width), BF),
            shape(full, F),
            shape(full, BF),
            shape((HEADS, tokens), F),
            shape(w_out.shape, BF),
            shape(w_up.shape, BF),
            shape(w_down.shape, BF),
            shape((SUM_ROWS, width), F),
        ),
        in_specs=[VM, VM, SM, VM] + [ANY] * 3 + [VM] * 2,
        out_specs=(VM,) * 5 + (ANY, ANY, VM),
        scratch_shapes=[pltpu.VMEM(s, BF) for s in weights + weights[1:]]
        + [
            pltpu.VMEM(full, F),
            pltpu.VMEM(full, F),
            pltpu.VMEM(full, BF),
            pltpu.VMEM(full, BF),
            pltpu.VMEM(full, F),
            pltpu.VMEM(full, F),
            pltpu.VMEM(full, BF),
            pltpu.VMEM(full, BF),
            pltpu.SemaphoreType.DMA((3,)),
            pltpu.SemaphoreType.DMA((hidden // 256,)),
            pltpu.SemaphoreType.DMA((hidden // 256,)),
        ],
        compiler_params=pltpu.CompilerParams(vmem_limit_bytes=LIMIT),
    )(x, cot, scalars, att, w_out, w_up, w_down, cols, bias_up)


def finish_kernel(
    x_ref, h_ref, dq_ref, dkv_ref, w_ref, cols_ref, dmid_ref, gx_ref, g_ref, sums_ref, err_ref
):
    width, tokens = x_ref.shape
    step = 256
    blocks = width // step
    err_ref[...] = jnp.zeros_like(err_ref)
    for ref, count, base in ((dq_ref, blocks, 0), (dkv_ref, 2 * blocks, blocks)):

        @pl.loop(0, count)
        def _(j):
            rows = pl.ds(pl.multiple_of(j * step, step), step)
            to = pl.ds(pl.multiple_of((j + base) * step, step), step)
            g_ref[to, :] = dg(ref[rows, :], h_ref[...], 1, 1).astype(BF)
            err_ref[...] += dg(w_ref[to, :], ref[rows, :], 0, 0)

    normed, inverse = normalize(x_ref[...].astype(F))
    err = err_ref[...]
    sums_ref[...] = jnp.zeros_like(sums_ref)
    sums_ref[0:1] = row_sums(dq_ref[...])[:1]
    sums_ref[1:2] = row_sums(dkv_ref[pl.ds(width, width), :])[:1]
    sums_ref[4:5] = row_sums(err * normed)[:1]
    sums_ref[5:6] = row_sums(err)[:1]
    grad = dmid_ref[...] + norm_back(err, normed, inverse, cols_ref[:, GAIN_ONE])
    gx_ref[...] = grad.T.astype(BF)


def finish(x, h, dq, dkv, w, cols, dmid):
    width, tokens = x.shape
    return pl.pallas_call(
        finish_kernel,
        name="finish",
        out_shape=(shape((tokens, width), BF), shape(w.shape, BF), shape((SUM_ROWS, width), F)),
        in_specs=[VM] * 7,
        out_specs=(VM, VM, VM),
        scratch_shapes=[pltpu.VMEM(x.shape, F)],
        compiler_params=pltpu.CompilerParams(vmem_limit_bytes=LIMIT),
    )(x, h, dq, dkv, w, cols, dmid)


class Place:
    def __init__(self, images):
        self.images = images
        self.depth = images // 2
        self.img = lax.axis_index("img")
        self.band = lax.axis_index("band")
        self.z, self.y = self.img // 2, self.img % 2
        self.x, self.c = self.band // 2, self.band % 2
        self.partner = (self.img, self.band + 1 - 2 * self.c)
        self.across_x = (self.img, self.band + 2 - 4 * self.x)
        self.across_y = (self.img + 1 - 2 * self.y, self.band)
        self.z_peers = [self.along_z(k) for k in range(1, self.depth)]

    def along_z(self, k):
        z = lax.rem(self.z + k, self.depth)
        return (2 * z + self.y, self.band), z


def greet(peers):
    barrier = pltpu.get_barrier_semaphore()
    for peer in peers:
        pl.semaphore_signal(barrier, inc=1, device_id=peer, device_id_type=MESH)
    pl.semaphore_wait(barrier, len(peers))


def send(src, dst, send_sem, recv_sem, peer):
    copy = pltpu.make_async_remote_copy(
        src_ref=src,
        dst_ref=dst,
        send_sem=send_sem,
        recv_sem=recv_sem,
        device_id=peer,
        device_id_type=MESH,
    )
    copy.start()
    return copy


def comm_params(collective_id):
    return pltpu.CompilerParams(
        collective_id=collective_id, has_side_effects=True, vmem_limit_bytes=LIMIT
    )


class Spread:
    def __init__(self, at, make, order, part, parts, source, ref, local_sem):
        depth, near, c = at.depth, at.depth // 2, at.c
        rows, half = ref.shape[2] // 2, ref.shape[3] // 2
        rows = pl.ds(pl.multiple_of(c * rows, 16), rows)
        size = half // parts
        lanes = pl.ds(pl.multiple_of(at.x * half + part * size, 128), size)
        both = [pl.ds(x * half + part * size, size) for x in range(2)]
        if parts == 1:
            both = [slice(None)]
        low, high = pl.ds(0, near), pl.ds(near, depth - near)

        def same(index, peer):
            if len(index) == 4:
                return [make(ref.at[index], ref.at[index], peer)]
            return [make(ref.at[index + (l,)], ref.at[index + (l,)], peer) for l in both]

        piece = ref.at[at.z, at.y, rows, lanes]
        source = source.at[:, pl.ds(part * size, size)]
        self.keep = pltpu.make_async_copy(source, piece, local_sem)
        z_first = []
        if order != "xyz":
            z_first = [make(source, piece, peer) for peer, _ in at.z_peers]
        if order == "mixed":
            self.stages = [
                z_first,
                same((low, at.y, rows, lanes), at.across_x)
                + same((high, at.y, rows, lanes), at.across_y),
                same((low, at.y, rows), at.across_y)
                + same((high, slice(None), rows, lanes), at.across_x),
            ]
        elif order == "zxy":
            self.stages = [
                z_first,
                same((slice(None), at.y, rows, lanes), at.across_x),
                same((slice(None), at.y, rows), at.across_y),
            ]
        else:
            last = [same((at.z, slice(None), rows), peer) for peer, _ in at.z_peers]
            self.stages = [
                [make(source, piece, at.across_x)],
                same((at.z, at.y, rows), at.across_y),
                sum(last, []),
            ]
        self.stages.append(same((slice(None), slice(None), rows), at.partner))

    def start(self):
        self.keep.start()
        for copy in self.stages[0]:
            copy.start()

    def step(self, k):
        if k == 1:
            self.keep.wait()
        for copy in self.stages[k - 1]:
            copy.wait_recv()
        for copy in self.stages[k]:
            copy.start()

    def wait(self):
        for copy in self.stages[-1]:
            copy.wait_recv()

    def end(self):
        for stage in self.stages:
            for copy in stage:
                copy.wait_send()


def kv_rows(ref, b, h):
    part = ref.shape[2] // 2
    heads = part // HEAD_DIM
    first = pl.multiple_of(h % heads * HEAD_DIM, 16)
    second = pl.multiple_of(part + h % heads * HEAD_DIM, 16)
    at = ref.at[b, h // heads]
    return at.at[pl.ds(first, HEAD_DIM)], at.at[pl.ds(second, HEAD_DIM)]


def front_kernel(
    images, bands, scalars_ref, shard_qkv_ref, shard_out_ref, shard_up_ref, shard_down_ref,
    small_ref, tokens_ref, cot_tokens_ref,
    qkv_w_out, h_out, kv_out, x_out, x_far_out, q_ref, lse_ref, cols_ref, *rest,
):
    results, rest = rest[:8], rest[8:]
    wide_ref = shard_down_ref
    narrow_ref, x_ref, cot_ref, far_tokens_ref = rest[:4]
    rest = rest[4:]
    qkv_w_ref, out_w_ref, up_w_ref, down_w_ref, h_ref, kv_ref, att_ref, up_col_ref = rest[:8]
    theirs_ref, mine_ref, mine_wide_ref, smalls_ref, qv_col_ref, bias_ref, x_far_ref = rest[8:15]
    local_sem, send_sem, recv_sem = rest[15:18]
    middle_scratch = rest[18:]
    at = Place(images)
    width, tokens = x_ref.shape
    rows = tokens // 2
    unit = width // images
    groups = kv_ref.shape[1]
    part = width // groups
    c = at.c
    used = [0, 0]

    def make(src, dst, peer):
        k = used[0]
        used[0] += 1
        return pltpu.make_async_remote_copy(
            src_ref=src,
            dst_ref=dst,
            send_sem=send_sem.at[k],
            recv_sem=recv_sem.at[k],
            device_id=peer,
            device_id_type=MESH,
        )

    def local():
        used[1] += 1
        return local_sem.at[used[1] - 1]

    others = [(lax.rem(at.img + k, images), at.band) for k in range(1, images)]
    half = wide_ref.shape[0] // 2
    wide = wide_ref.shape[1]
    own_lanes = pl.ds(pl.multiple_of(c * wide, 128), wide)
    own_wide = pltpu.make_async_copy(
        wide_ref.at[pl.ds(pl.multiple_of(c * half, 8), half), :],
        mine_wide_ref.at[:, own_lanes],
        local(),
    )
    swap = make(narrow_ref.at[1 - c], theirs_ref, at.partner)
    swap_wide = make(
        wide_ref.at[pl.ds(pl.multiple_of((1 - c) * half, 8), half), :],
        mine_wide_ref.at[:, own_lanes],
        at.partner,
    )
    lines = pl.ds(pl.multiple_of(at.img * 16, 16), 16)
    keep_small = pltpu.make_async_copy(small_ref, smalls_ref.at[lines, :], local())
    small_copies = [make(small_ref, smalls_ref.at[lines, :], peer) for peer in others]
    sources, row = [], 0
    for ref in (qkv_w_ref, out_w_ref, up_w_ref):
        count = ref.shape[2] // 2
        sources.append(mine_ref.at[pl.ds(row, count), :])
        row += count
    sources.append(mine_wide_ref)

    def spread(ref, source, orders):
        parts = len(orders)
        return [
            Spread(at, make, orders[k], k, parts, source, ref, local()) for k in range(parts)
        ]

    s_qkv = spread(qkv_w_ref, sources[0], ("mixed",) * 3)
    (s_out,) = spread(out_w_ref, sources[1], ("mixed",))
    s_up = spread(up_w_ref, sources[2], ("mixed", "mixed", "mixed"))
    d_one, d_two = spread(down_w_ref, sources[3], ("mixed", "mixed"))
    save_w = pltpu.make_async_copy(qkv_w_ref, qkv_w_out, local())
    save_h = pltpu.make_async_copy(h_ref, h_out, local())
    save_x = pltpu.make_async_copy(x_ref, x_out, local())
    save_far = pltpu.make_async_copy(x_far_ref, x_far_out, local())
    save_kv = [
        pltpu.make_async_copy(kv_ref.at[:, g], kv_out.at[:, g], local()) for g in range(groups)
    ]
    x_lanes = [pl.ds(s * rows, rows) for s in range(2)]
    x_moves = [make(tokens_ref.at[l], far_tokens_ref.at[l], at.across_x) for l in x_lanes]
    far = at.across_x[1]
    kv_moves = [
        [
            [
                make(kv_ref.at[b, g, :, x_lanes[s]], kv_ref.at[b, g, :, x_lanes[s]], at.partner)
                for b in (at.band, far)
            ]
            for g in range(groups)
        ]
        for s in range(2)
    ]

    row = 0
    for ref in (shard_qkv_ref, shard_out_ref, shard_up_ref):
        turned = ref[...].astype(F).T.astype(BF)
        count = turned.shape[0] // 2
        for core in range(2):
            narrow_ref[core, pl.ds(row, count), :] = turned[core * count : (core + 1) * count]
        row += count
    greet([at.partner, at.across_x] + others)
    x_moves[0].start()
    x_moves[1].start()
    swap.start()
    own_wide.start()
    swap_wide.start()
    keep_small.start()
    for copy in small_copies:
        copy.start()
    fill_bias(scalars_ref, bias_ref, rows)
    swap.wait_recv()
    mine, theirs = narrow_ref[c], theirs_ref[...]
    lane_count = mine.shape[1]
    mine_ref[:, pl.ds(0, lane_count)] = jnp.where(c == 0, mine, theirs)
    mine_ref[:, pl.ds(lane_count, lane_count)] = jnp.where(c == 0, theirs, mine)
    for item in s_qkv:
        item.start()
    own_wide.wait()
    swap_wide.wait_recv()
    s_out.start()
    for item in s_up:
        item.start()
    d_two.start()
    d_one.start()

    for s in range(2):
        x_ref[:, x_lanes[s]] = tokens_ref[x_lanes[s], :].astype(F).T.astype(BF)
        cot_ref[:, x_lanes[s]] = cot_tokens_ref[x_lanes[s], :].astype(F).T.astype(BF)
    save_x.start()

    keep_small.wait()
    for copy in small_copies:
        copy.wait_recv()
    turned = smalls_ref[...].T
    qv_units, up_units = 2, up_w_ref.shape[2] // unit
    singles = 16 - qv_units - up_units
    for j in range(images):
        block = turned[:unit, 16 * j : 16 * j + 16]
        cols_ref[pl.ds(unit * j, unit), :] = block[:, :singles]
        for u in range(qv_units):
            lane = singles + u
            qv_col_ref[pl.ds(unit * (qv_units * j + u), unit), :] = block[:, lane : lane + 1]
        for u in range(up_units):
            lane = singles + qv_units + u
            up_col_ref[pl.ds(unit * (up_units * j + u), unit), :] = block[:, lane : lane + 1]

    def far_tokens(s):
        x_moves[s].wait_recv()
        x_far_ref[:, x_lanes[s]] = far_tokens_ref[x_lanes[s], :].astype(F).T.astype(BF)

    def first_norm(s, ref, side):
        normed, _ = normalize(ref[:, x_lanes[s]].astype(F))
        to = pl.ds(side * tokens + s * rows, rows)
        h_ref[:, to] = (normed * cols_ref[:, GAIN_ONE] + cols_ref[:, SHIFT_ONE]).astype(BF)

    s_qkv[0].step(1)
    s_qkv[1].step(1)
    s_qkv[0].step(2)
    s_qkv[2].step(1)
    for s in range(2):
        first_norm(s, x_ref, 0)
    s_qkv[1].step(2)
    s_qkv[0].step(3)
    s_qkv[2].step(2)
    s_out.step(1)
    far_tokens(0)
    first_norm(0, x_far_ref, 1)
    s_qkv[1].step(3)
    s_up[0].step(1)
    s_up[1].step(1)
    s_qkv[2].step(3)
    s_up[2].step(1)
    d_two.step(1)
    for item in s_qkv:
        item.wait()
    d_one.step(1)
    save_w.start()

    weights = qkv_w_ref.reshape(3 * width, width)
    scale = 1.0 / math.sqrt(HEAD_DIM)

    def project(s):
        for g in range(groups):
            for k in range(2):
                row = (1 + k) * width + g * part
                to = pl.ds(k * part, part)
                for side, band in enumerate((at.band, far)):
                    lanes = pl.ds(side * tokens + s * rows, rows)
                    out = dg(weights[pl.ds(row, part), :], h_ref[:, lanes], 1, 0)
                    if k == 1:
                        out = out + qv_col_ref[pl.ds(width + g * part, part), :]
                    kv_ref[band, g, to, x_lanes[s]] = out.astype(BF)
            for copy in kv_moves[s][g]:
                copy.start()
        for g in range(groups):
            block = pl.ds(g * part, part)
            out = dg(weights[block, :], h_ref[:, x_lanes[s]], 1, 0) + qv_col_ref[block, :]
            q_ref[block, x_lanes[s]] = (out * scale).astype(BF)

    def second_slot():
        far_tokens(1)
        first_norm(1, x_far_ref, 1)
        project(1)
        save_h.start()
        save_far.start()

    def arrive(s, g):
        for copy in kv_moves[s][g]:
            copy.wait_recv()
        if s == 1:
            save_kv[g].start()

    events = {}

    def when(j, *actions):
        events.setdefault(j, []).extend(actions)

    when(2, second_slot)
    for j in range(1, 2 * groups):
        when(j - 1, functools.partial(arrive, j // groups, j % groups))
    when(0, functools.partial(s_out.step, 2))
    when(1, functools.partial(s_up[0].step, 2))
    when(2, functools.partial(s_up[1].step, 2))
    when(3, functools.partial(s_up[2].step, 2), functools.partial(s_out.step, 3))
    when(4, functools.partial(d_two.step, 2))
    when(5, functools.partial(d_one.step, 2))
    when(6, functools.partial(s_up[0].step, 3))
    when(7, functools.partial(s_up[1].step, 3))
    project(0)
    arrive(0, 0)
    unroll = HEADS // groups

    @pl.loop(0, 2 * groups)
    def _(j):
        s, g = j // groups, j % groups
        for k in range(unroll):
            attend_step(
                s * HEADS + g * unroll + k, at.x, q_ref, kv_ref, bias_ref, att_ref, lse_ref
            )
        for when_j, actions in events.items():

            @pl.when(j == when_j)
            def _():
                for action in actions:
                    action()

    hidden = up_w_ref.shape[0] * 2 * up_w_ref.shape[2]
    blocks = hidden // 256
    quarter = blocks // 4

    def wait_out():
        s_up[2].step(3)
        s_out.wait()

    def wait_up():
        d_two.step(3)
        for item in s_up:
            item.wait()

    def wait_one():
        d_one.step(3)
        d_one.wait()

    def flat(ref):
        return ref.reshape(ref.shape[0] * 2 * ref.shape[2], ref.shape[3])

    middle_body(
        x_ref, cot_ref, scalars_ref, att_ref, flat(out_w_ref), flat(up_w_ref), flat(down_w_ref),
        cols_ref, up_col_ref, *results, *middle_scratch, wait_out, wait_up,
        [
            (d_two.wait, 2 * quarter, lambda t: t + t // quarter * quarter + quarter),
            (wait_one, 2 * quarter, lambda t: t + t // quarter * quarter),
        ],
    )
    for item in s_qkv + s_up + [s_out, d_one, d_two]:
        item.end()
    for copy in [save_w, save_h, save_x, save_far] + save_kv:
        copy.wait()
    for copy in [swap, swap_wide] + small_copies + x_moves:
        copy.wait_send()
    for copy in sum(sum(kv_moves, []), []):
        copy.wait_send()


def front(images, bands, scalars, shards, small, tokens_by_slot, cot_by_slot):
    depth = images // 2
    tokens, width = tokens_by_slot.shape
    groups = GROUPS_OF_HEADS
    widths = [item.shape[1] for item in shards[:3]]
    hidden = images * widths[2]
    full = (width, tokens)
    part = shards[0].shape[0]
    narrow = (2, sum(widths) // 2, part)
    wide = shards[3].shape
    kv = (bands, groups, 2 * width // groups, tokens)
    weights = [(depth, 2, w, width) for w in widths]
    weights.append((depth, 2, wide[0], 4 * wide[1]))
    return pl.pallas_call(
        functools.partial(front_kernel, images, bands),
        name="front",
        out_shape=(
            shape(weights[0], BF),
            shape((width, 2 * tokens), BF),
            shape(kv, BF),
            shape(full, BF),
            shape(full, BF),
            shape(full, BF),
            shape((2 * HEADS, tokens // 2), F),
            shape((width, COLUMNS), F),
            shape((tokens, width), BF),
            shape(full, F),
            shape(full, BF),
            shape((HEADS, tokens), F),
            shape((width, width), BF),
            shape((hidden, width), BF),
            shape((width, hidden), BF),
            shape((SUM_ROWS, width), F),
        ),
        in_specs=[SM] + [VM] * 7,
        out_specs=(ANY,) * 5 + (VM,) * 8 + (ANY, ANY, VM),
        scratch_shapes=[pltpu.VMEM(s, BF) for s in (narrow, full, full, (tokens, width))]
        + [pltpu.VMEM(s, BF) for s in weights]
        + [
            pltpu.VMEM((width, 2 * tokens), BF),
            pltpu.VMEM(kv, BF),
            pltpu.VMEM(full, F),
            pltpu.VMEM((hidden, 1), F),
            pltpu.VMEM(narrow[1:], BF),
            pltpu.VMEM((narrow[1], 2 * narrow[2]), BF),
            pltpu.VMEM((wide[0] // 2, 2 * wide[1]), BF),
            pltpu.VMEM((16 * images, 128), F),
            pltpu.VMEM((2 * width, 1), F),
            pltpu.VMEM((8, tokens // 2), F),
            pltpu.VMEM(full, BF),
            pltpu.SemaphoreType.DMA((24,)),
            pltpu.SemaphoreType.DMA((FRONT_COPIES,)),
            pltpu.SemaphoreType.DMA((FRONT_COPIES,)),
            pltpu.VMEM((hidden, width), BF),
            pltpu.VMEM((width, hidden), BF),
            pltpu.VMEM(full, F),
            pltpu.VMEM(full, F),
            pltpu.VMEM(full, BF),
            pltpu.VMEM(full, BF),
            pltpu.VMEM(full, F),
            pltpu.VMEM(full, F),
            pltpu.VMEM(full, BF),
            pltpu.VMEM(full, BF),
            pltpu.SemaphoreType.DMA((hidden // 256,)),
            pltpu.SemaphoreType.DMA((hidden // 256,)),
        ],
        compiler_params=comm_params(0),
    )(scalars, *shards, small, tokens_by_slot, cot_by_slot)


def share_kernel(images, kv_ref, all_ref, local_sem, send_sem, recv_sem):
    at = Place(images)
    greet([at.partner, at.across_x])
    rows = kv_ref.shape[1] // 2
    mine = pltpu.make_async_copy(kv_ref, all_ref.at[at.band], local_sem)
    mine.start()
    copies = []
    for s in range(2):
        lanes = pl.ds(s * rows, rows)
        copies.append(
            send(
                kv_ref.at[:, lanes],
                all_ref.at[at.band, :, lanes],
                send_sem.at[s],
                recv_sem.at[s],
                at.across_x,
            )
        )
    near = send(kv_ref, all_ref.at[at.band], send_sem.at[2], recv_sem.at[2], at.partner)
    passed = []
    for s in range(2):
        copies[s].wait_recv()
        part = all_ref.at[at.across_x[1], :, pl.ds(s * rows, rows)]
        passed.append(send(part, part, send_sem.at[3 + s], recv_sem.at[3 + s], at.partner))
    for copy in passed + [near]:
        copy.wait()
    for copy in copies:
        copy.wait_send()
    mine.wait()


def share(images, bands, kv):
    return pl.pallas_call(
        functools.partial(share_kernel, images),
        name="share",
        out_shape=shape((bands,) + kv.shape, BF),
        in_specs=[VM],
        out_specs=ANY,
        scratch_shapes=[
            pltpu.SemaphoreType.DMA,
            pltpu.SemaphoreType.DMA((5,)),
            pltpu.SemaphoreType.DMA((5,)),
        ],
        compiler_params=comm_params(1),
    )(kv)


def add_rows(total_ref, other_ref, step):
    @pl.loop(0, total_ref.shape[0] // step)
    def _(j):
        rows = pl.ds(pl.multiple_of(j * step, step), step)
        total_ref[rows, :] = (
            total_ref[rows, :].astype(F) + other_ref[rows, :].astype(F)
        ).astype(total_ref.dtype)


def unshare_kernel(images, dkv_ref, sum_ref, near_ref, far_ref, send_sem, recv_sem):
    at = Place(images)
    greet([at.partner, at.across_x])
    mate, far = at.partner[1], at.across_x[1]
    far_mate = at.band + 2 - 4 * at.x + 1 - 2 * at.c
    one = send(dkv_ref.at[far_mate], near_ref.at[0], send_sem.at[0], recv_sem.at[0], at.partner)
    two = send(dkv_ref.at[mate], near_ref.at[1], send_sem.at[1], recv_sem.at[1], at.partner)
    one.wait_recv()
    add_rows(near_ref.at[0], dkv_ref.at[far], 64)
    three = send(near_ref.at[0], far_ref, send_sem.at[2], recv_sem.at[2], at.across_x)
    two.wait_recv()
    add_rows(near_ref.at[1], dkv_ref.at[at.band], 64)
    three.wait_recv()
    sum_ref[...] = near_ref[1]
    add_rows(sum_ref, far_ref, 64)
    for copy in (one, two, three):
        copy.wait_send()


def unshare(images, dkv):
    block = dkv.shape[1:]
    return pl.pallas_call(
        functools.partial(unshare_kernel, images),
        name="unshare",
        out_shape=shape(block, BF),
        in_specs=[VM],
        out_specs=VM,
        scratch_shapes=[
            pltpu.VMEM((2,) + block, BF),
            pltpu.VMEM(block, BF),
            pltpu.SemaphoreType.DMA((3,)),
            pltpu.SemaphoreType.DMA((3,)),
        ],
        compiler_params=comm_params(2),
    )(dkv)


def accumulate(total, other):
    total[...] = total[...] + other[...]


class Reduction:
    def __init__(self, at, make, order, start, size, ref, one, other, bufs, total):
        depth, near = at.depth, at.depth // 2
        half = ref.shape[3] // 2
        self.at, self.near, self.one, self.other, self.order = at, near, one, other, order

        def lanes_of(x):
            return pl.ds(pl.multiple_of(x * half + start, 128), size)

        self.lanes, self.both = lanes_of(at.x), [lanes_of(x) for x in range(2)]
        self.total = total.at[:, pl.ds(start, size)]
        far = lanes_of(1 - at.x)
        upper = depth - near
        if order == "mixed":
            two_x, two_y, three, four = bufs
            self.two_x, self.two_y = two_x, two_y
            low, high = pl.ds(0, near), pl.ds(near, upper)
            self.first = [make(one.at[low, :, :, far], two_x, at.across_x)] + [
                make(one.at[high, 1 - at.y, :, self.both[x]], two_y.at[x], at.across_y)
                for x in range(2)
            ]
            self.second = [
                make(two_x.at[:, 1 - at.y], three.at[low], at.across_y),
                make(two_y.at[1 - at.x], three.at[high], at.across_x),
            ]
        else:
            two, three, four = bufs
            self.two = two
            self.first = [
                make(one.at[:, 1 - at.y, :, self.both[x]], two.at[x], at.across_y)
                for x in range(2)
            ]
            self.second = [make(two.at[1 - at.x], three, at.across_x)]
        self.three, self.four = three, four
        self.third = [
            make(three.at[z], four.at[k], peer) for k, (peer, z) in enumerate(at.z_peers)
        ]

    def step_one(self):
        for lanes in self.both:

            @pl.loop(0, 2 * self.at.depth)
            def _(j):
                accumulate(
                    self.one.at[j // 2, j % 2, :, lanes],
                    self.other.at[j // 2, j % 2, :, lanes],
                )

        for copy in self.first:
            copy.start()

    def step_two(self):
        at = self.at
        if self.order == "mixed":
            self.first[0].wait_recv()

            @pl.loop(0, 2 * self.near)
            def _(j):
                accumulate(
                    self.two_x.at[j // 2, j % 2], self.one.at[j // 2, j % 2, :, self.lanes]
                )

            self.second[0].start()
            for x in range(2):
                self.first[1 + x].wait_recv()

                @pl.loop(0, at.depth - self.near)
                def _(j):
                    accumulate(
                        self.two_y.at[x, j], self.one.at[self.near + j, at.y, :, self.both[x]]
                    )

            self.second[1].start()
        else:
            for x in range(2):
                self.first[x].wait_recv()

                @pl.loop(0, at.depth)
                def _(j):
                    accumulate(self.two.at[x, j], self.one.at[j, at.y, :, self.both[x]])

            self.second[0].start()

    def step_three(self):
        at = self.at
        for copy in self.second:
            copy.wait_recv()
        if self.order == "mixed":

            @pl.loop(0, self.near)
            def _(j):
                accumulate(self.three.at[j], self.two_x.at[j, at.y])

            @pl.loop(0, at.depth - self.near)
            def _(j):
                accumulate(self.three.at[self.near + j], self.two_y.at[at.x, j])

        else:

            @pl.loop(0, at.depth)
            def _(j):
                accumulate(self.three.at[j], self.two.at[at.x, j])

        for copy in self.third:
            copy.start()

    def step_four(self):
        for copy in self.third:
            copy.wait_recv()
        total = self.three[self.at.z].astype(F)
        for k in range(len(self.third)):
            total = total + self.four[k].astype(F)
        self.total[...] = total

    def end(self):
        for copy in self.first + self.second + self.third:
            copy.wait_send()


def reduction_buffers(order, depth, rows, size):
    near = depth // 2
    if order == "mixed":
        first = [(near, 2, rows, size), (2, depth - near, rows, size)]
    else:
        first = [(2, depth, rows, size)]
    return [pltpu.VMEM(s, BF) for s in first + [(depth, rows, size), (depth - 1, rows, size)]]


BACK_ORDERS = (
    (("mixed", 1), ("mixed", 1)),
    (("mixed", 1), ("mixed", 1), ("mixed", 1)),
    (("mixed", 1),),
    (("mixed", 2), ("yx", 1)),
)


def lane_parts(orders, half):
    unit = half // sum(share for _, share in orders)
    parts, start = [], 0
    for order, share in orders:
        parts.append((order, start, share * unit))
        start += share * unit
    return parts


def back_kernel(
    images, bands, scalars_ref, q_ref, delta_ref, lse_ref, datt_ref, cols_ref, sums_ref,
    kv_in, x_in, x_far_in, h_in, dmid_in, w_in, g_out_ref, g_up_ref, g_down_ref,
    gx_ref, o_qkv_ref, o_out_ref, o_up_ref, o_down_ref, total_ref,
    p_down_ref, p_up_ref, p_out_ref, p_qkv_ref,
    kv_ref, x_ref, x_far_ref, h_ref, dmid_ref, w_ref,
    bias_ref, dq_ref, dwide_ref, dkv_ref, near_ref, g_qkv_ref, err_ref, err_far_ref, err_in_ref,
    small_ref, small_in_ref, small_z_ref, *rest,
):
    at = Place(images)
    depth = at.depth
    local_sem, send_sem, recv_sem = rest[-3:]
    rest = list(rest[:-3])
    used = [0, 0]

    def make(src, dst, peer):
        k = used[0]
        used[0] += 1
        return pltpu.make_async_remote_copy(
            src_ref=src,
            dst_ref=dst,
            send_sem=send_sem.at[k],
            recv_sem=recv_sem.at[k],
            device_id=peer,
            device_id_type=MESH,
        )

    def load(src, dst):
        used[1] += 1
        return pltpu.make_async_copy(src, dst, local_sem.at[used[1] - 1])

    width, tokens = x_ref.shape
    rows = tokens // 2
    unroll = 4
    groups = HEADS // unroll
    part = width // groups

    def four_d(ref):
        return ref.reshape(depth, 2, ref.shape[0] // images, ref.shape[1])

    sources = (four_d(g_down_ref), four_d(g_up_ref), four_d(g_out_ref), g_qkv_ref)
    targets = (p_down_ref, p_up_ref, p_out_ref, p_qkv_ref)
    swaps, owns, moves, ends = [], [], [], []
    for m in range(4):
        one, total, away = rest[:3]
        rest = rest[3:]
        block, lanes = sources[m].shape[2] // 2, sources[m].shape[3]
        near_rows = pl.ds(pl.multiple_of(at.c * block, 16), block)
        far_rows = pl.ds(pl.multiple_of((1 - at.c) * block, 16), block)
        parts = lane_parts(BACK_ORDERS[m], lanes // 2)
        if m < 3:
            other = rest.pop(0)
            owns.append(load(sources[m].at[:, :, near_rows, :], one))
            swaps.append([make(sources[m].at[:, :, far_rows, :], other, at.partner)])
        else:
            other = sources[m].at[:, :, near_rows, :]
            for _, start, size in parts:
                both = [pl.ds(x * (lanes // 2) + start, size) for x in range(2)]
                swaps.append(
                    [
                        make(sources[m].at[:, :, far_rows, l], one.at[:, :, :, l], at.partner)
                        for l in both
                    ]
                )
        moves.append([])
        for order, start, size in parts:
            count = 4 if order == "mixed" else 3
            moves[m].append(
                Reduction(
                    at, make, order, start, size, sources[m], one, other, rest[:count], total
                )
            )
            rest = rest[count:]
        ends.append((total, away, targets[m], make(away, targets[m].at[at.c], at.partner)))
    down, up, out, qkv = moves

    def deliver(m):
        total_ref, away, target, copy = ends[m]
        total = total_ref[...]
        size = total.shape[1] // 2
        low, high = total[:, :size], total[:, size:]
        target[at.c] = jnp.where(at.c == 0, low, high)
        away[...] = jnp.where(at.c == 0, high, low)
        copy.start()

    mate, far = at.partner[1], at.across_x[1]
    far_mate = at.across_x[1] + 1 - 2 * at.c
    one = [make(dkv_ref.at[far_mate, g], near_ref.at[0, g], at.partner) for g in range(groups)]
    two = [make(dkv_ref.at[mate, g], near_ref.at[1, g], at.partner) for g in range(groups)]
    err_moves = [make(err_far_ref.at[s], err_in_ref.at[s], at.across_x) for s in range(2)]
    small_steps = [
        make(small_ref.at[k], small_in_ref.at[k], peer)
        for k, peer in enumerate((at.partner, at.across_x, at.across_y))
    ]
    small_last = [
        make(small_z_ref.at[at.z], small_z_ref.at[at.z], peer) for peer, _ in at.z_peers
    ]

    kv_loads = [load(kv_in.at[:, g], kv_ref.at[:, g]) for g in range(groups)]
    late_loads = [
        load(h_in, h_ref),
        load(w_in, w_ref),
        load(x_in, x_ref),
        load(x_far_in, x_far_ref),
        load(dmid_in, dmid_ref),
    ]
    kv_loads[0].start()
    owns[0].start()
    greet([at.partner, at.across_x, at.across_y] + [peer for peer, _ in at.z_peers])
    for m in range(3):
        swaps[m][0].start()
    for copy in owns[1:] + kv_loads[1:] + late_loads:
        copy.start()
    fill_bias(scalars_ref, bias_ref, rows)

    sides = [pl.ds(side * tokens, tokens) for side in range(2)]

    def share_one(g):
        one[g].start()
        two[g].start()

    def share_two(g):
        for copy, side, band in ((one[g], 1, far), (two[g], 0, at.band)):
            copy.wait_recv()
            for half in range(2):
                block = pl.ds(half * part, part)
                to = pl.ds(half * width + g * part, part)
                value = (
                    near_ref[1 - side, g, block, :].astype(F)
                    + dkv_ref[band, g, block, :].astype(F)
                ).astype(BF)
                dwide_ref[to, sides[side]] = value

    events = {}

    def when(j, *actions):
        events.setdefault(j, []).extend(actions)

    def received(m):
        owns[m].wait()
        swaps[m][0].wait_recv()

    for g in range(1, groups):
        when(2 * g - 1, kv_loads[g].wait)
    when(0, down[1].step_one)
    when(0, lambda: received(1), up[0].step_one)
    when(1, up[1].step_one, lambda: share_one(0))
    when(2, up[2].step_one, down[0].step_two, lambda: share_two(0))
    when(3, lambda: received(2), out[0].step_one, down[1].step_two, lambda: share_one(1))
    when(4, up[0].step_two, down[0].step_three, lambda: share_two(1))
    when(5, up[1].step_two, down[1].step_three, lambda: share_one(2))
    when(6, up[2].step_two, up[0].step_three, lambda: share_two(2))
    when(7, lambda: share_one(3), out[0].step_two, up[1].step_three)
    received(0)
    down[0].step_one()
    kv_loads[0].wait()

    @pl.loop(0, 2 * groups)
    def _(j):
        g, s = j // 2, j % 2
        lanes = pl.ds(pl.multiple_of(s * rows, rows), rows)
        for k in range(unroll):

            def put_key(b, values):
                dkv_ref[b, g, pl.ds(k * HEAD_DIM, HEAD_DIM), lanes] = values

            def put_value(b, values):
                dkv_ref[b, g, pl.ds(part + k * HEAD_DIM, HEAD_DIM), lanes] = values

            attend_back_step(
                s * HEADS + g * unroll + k,
                at.x, q_ref, kv_ref, delta_ref, lse_ref, datt_ref, bias_ref, dq_ref,
                put_key, put_value,
            )
        for when_j, actions in events.items():

            @pl.when(j == when_j)
            def _():
                for action in actions:
                    action()

    chunk = width // 2
    g_flat = g_qkv_ref.reshape(3 * width, width)
    parts = lane_parts(BACK_ORDERS[3], width // 2)

    def weight_grad(part, source_ref, first, count, tokens_at):
        _, start, size = parts[part]
        lanes = [pl.ds(x * (width // 2) + start, size) for x in range(2)]

        @pl.loop(0, count)
        def _(j):
            block = pl.ds(pl.multiple_of(j * chunk, 128), chunk)
            to = pl.ds(pl.multiple_of((first + j) * chunk, 128), chunk)
            both = jnp.concatenate([h_ref[l, tokens_at] for l in lanes], axis=0)
            result = dg(source_ref[block, :], both, 1, 1).astype(BF)
            g_flat[to, lanes[0]] = result[:, :size]
            g_flat[to, lanes[1]] = result[:, size:]

    def back_through(side):
        err_ref[...] = jnp.zeros_like(err_ref)

        @pl.loop(0, 4)
        def _(j):
            block = pl.ds(pl.multiple_of(j * chunk, 128), chunk)
            source = pl.ds(pl.multiple_of((2 + j) * chunk, 128), chunk)
            err_ref[...] += dg(w_ref[source, :], dwide_ref[block, sides[side]], 0, 0)

    def start_swap(part):
        for copy in swaps[3 + part]:
            copy.start()

    def first_sum(part):
        for copy in swaps[3 + part]:
            copy.wait_recv()
        qkv[part].step_one()

    for copy in late_loads:
        copy.wait()
    for p in range(2):
        weight_grad(p, dq_ref, 0, 2, sides[0])
    share_two(groups - 1)
    weight_grad(0, dwide_ref, 2, 4, slice(None))
    start_swap(0)
    up[2].step_three()
    out[0].step_three()
    back_through(1)
    err_far = err_ref[...]
    for s in range(2):
        err_far_ref[s] = err_far[:, s * rows : (s + 1) * rows].astype(BF)
    first_sum(0)
    err_moves[0].start()
    weight_grad(1, dwide_ref, 2, 4, slice(None))
    start_swap(1)
    normed_far, _ = normalize(x_far_ref[...].astype(F))
    gain_row = row_sums(err_ref[...] * normed_far)[:1]
    shift_row = row_sums(err_ref[...])[:1]
    first_sum(1)
    back_through(0)

    @pl.loop(0, 2)
    def _(j):
        block = pl.ds(pl.multiple_of(j * chunk, 128), chunk)
        err_ref[...] += dg(w_ref[block, :], dq_ref[block, :], 0, 0)

    small_ref[0] = sums_ref[...]
    small_ref[0, 0:1] = row_sums(dq_ref[...])[:1]
    small_ref[0, 1:2] = row_sums(dwide_ref[pl.ds(width, width), :])[:1]
    normed, _ = normalize(x_ref[...].astype(F))
    small_ref[0, 4:5] = gain_row + row_sums(err_ref[...] * normed)[:1]
    small_ref[0, 5:6] = shift_row + row_sums(err_ref[...])[:1]
    small_steps[0].start()
    qkv[0].step_two()
    for item in down:
        item.step_four()
    deliver(0)
    small_steps[0].wait_recv()
    small_ref[1] = small_ref[0] + small_in_ref[0]
    small_steps[1].start()
    qkv[1].step_two()
    err_moves[1].start()
    qkv[0].step_three()
    small_steps[1].wait_recv()
    small_ref[2] = small_ref[1] + small_in_ref[1]
    small_steps[2].start()
    for item in up:
        item.step_four()
    deliver(1)
    small_steps[2].wait_recv()
    small_z_ref[at.z] = small_ref[2] + small_in_ref[2]
    for copy in small_last:
        copy.start()
    out[0].step_four()
    deliver(2)
    qkv[1].step_three()

    def finish_slot(s):
        err_moves[s].wait_recv()
        lanes = slice(s * rows, (s + 1) * rows)
        err = err_ref[:, lanes] + err_in_ref[s].astype(F)
        normed, inverse = normalize(x_ref[:, lanes].astype(F))
        grad = dmid_ref[:, lanes] + norm_back(err, normed, inverse, cols_ref[:, GAIN_ONE])
        gx_ref[lanes, :] = grad.T.astype(BF)

    finish_slot(0)
    qkv[0].step_four()
    for copy in small_last:
        copy.wait_recv()
    total = small_z_ref[0]
    for k in range(1, depth):
        total = total + small_z_ref[k]
    total_ref[...] = total
    qkv[1].step_four()
    deliver(3)
    finish_slot(1)
    for m, ref in enumerate((o_down_ref, o_up_ref, o_out_ref, o_qkv_ref)):
        ends[m][3].wait()
        whole = jnp.concatenate([targets[m][k] for k in range(2)], axis=0)
        ref[...] = whole if m == 0 else whole.T
        for item in moves[m]:
            item.end()
    for copy in sum(swaps, []) + one + two + err_moves + small_steps + small_last:
        copy.wait_send()


def back(
    images, bands, scalars, q, kv, delta, lse, datt, x, x_far, h, dmid, w, cols, grads, sums
):
    depth = images // 2
    width, tokens = x.shape
    g_out, g_up, g_down = grads
    groups = HEADS // 4
    results, placed, buffers = [], [], []
    for m, item in enumerate((g_down, g_up, g_out, w)):
        block, lanes = item.shape[0] // images // 2, item.shape[1]
        placing = (lanes // 4, 2 * block) if m else (2 * block, lanes // 4)
        results.append(shape(placing, F))
        placed.append(pltpu.VMEM((2, block, lanes // 4), F))
        buffers += [
            pltpu.VMEM((depth, 2, block, lanes), BF),
            pltpu.VMEM((block, lanes // 2), F),
            pltpu.VMEM((block, lanes // 4), F),
        ]
        if m < 3:
            buffers.append(pltpu.VMEM((depth, 2, block, lanes), BF))
        for order, _, size in lane_parts(BACK_ORDERS[m], lanes // 2):
            buffers += reduction_buffers(order, depth, block, size)
    small = (SUM_ROWS, width)
    return pl.pallas_call(
        functools.partial(back_kernel, images, bands),
        name="back",
        out_shape=(shape((tokens, width), BF), results[3], results[2], results[1], results[0], shape(small, F)),
        in_specs=[SM] + [VM] * 6 + [ANY] * 9,
        out_specs=(VM,) * 6,
        scratch_shapes=placed
        + [
            pltpu.VMEM(kv.shape, BF),
            pltpu.VMEM((width, tokens), BF),
            pltpu.VMEM((width, tokens), BF),
            pltpu.VMEM((width, 2 * tokens), BF),
            pltpu.VMEM((width, tokens), F),
            pltpu.VMEM(w.shape, BF),
            pltpu.VMEM((8, tokens // 2), F),
            pltpu.VMEM((width, tokens), BF),
            pltpu.VMEM((2 * width, 2 * tokens), BF),
            pltpu.VMEM((bands, groups, 2 * width // groups, tokens), BF),
            pltpu.VMEM((2, groups, 2 * width // groups, tokens), BF),
            pltpu.VMEM((depth, 2, w.shape[0] // images, width), BF),
            pltpu.VMEM((width, tokens), F),
            pltpu.VMEM((2, width, tokens // 2), BF),
            pltpu.VMEM((2, width, tokens // 2), BF),
            pltpu.VMEM((3,) + small, F),
            pltpu.VMEM((3,) + small, F),
            pltpu.VMEM((depth,) + small, F),
        ]
        + buffers
        + [
            pltpu.SemaphoreType.DMA((16,)),
            pltpu.SemaphoreType.DMA((BACK_COPIES,)),
            pltpu.SemaphoreType.DMA((BACK_COPIES,)),
        ],
        compiler_params=comm_params(3),
    )(
        scalars, q, delta, lse, datt, cols, sums, kv, x, x_far, h, dmid, w, g_out, g_up, g_down
    )


def body(
    tokens,
    slot_kind,
    w_qkv,
    w_out,
    w_up,
    w_down,
    bias_qv,
    bias_out,
    bias_up,
    bias_down,
    gain_one,
    shift_one,
    gain_two,
    shift_two,
    cotangent,
):
    rows, slots, width = tokens.shape[1:]
    count = rows * slots
    images, bands = lax.axis_size("img"), lax.axis_size("band")
    band = lax.axis_index("band")
    smalls = (bias_qv, bias_out, bias_up, bias_down, gain_one, shift_one, gain_two, shift_two)
    sizes = [item.shape[0] for item in smalls]
    own = (w_qkv, w_out, w_up)
    widths = [item.shape[1] for item in own]
    direct = images % 4 == 0 and all(w % 32 == 0 for w in widths + [w_down.shape[1]])
    direct = direct and bias_qv.shape[0] == 2 * (width // images) <= 256
    direct = direct and bias_up.shape[0] == 4 * (width // images)

    def by_slot(values):
        return values[0].transpose(1, 0, 2).reshape(count, width)

    def turn(values):
        return by_slot(values).T

    def turn_back(values):
        return values.reshape(slots, rows, width).transpose(1, 0, 2)[None]

    scalars = slot_kind
    single = (bias_out, bias_down, gain_one, shift_one, gain_two, shift_two)
    if direct:
        unit = width // images
        units = [jnp.stack(single), jnp.zeros((4, unit), BF)]
        units += [bias_qv.reshape(-1, unit), bias_up.reshape(-1, unit)]
        small = jnp.pad(jnp.concatenate(units), ((0, 0), (0, 128 - unit))).astype(F)
        full_qkv, h, all_kv, x, x_far, q, lse, cols, *rest = front(
            images, bands, scalars, (*own, w_down.T), small, by_slot(tokens), by_slot(cotangent)
        )
        full_qkv = full_qkv.reshape(-1, width)
    else:
        scalars = jnp.concatenate([slot_kind, jnp.full((1, 1), band // 2, jnp.int32)], axis=1)
        x, cot = turn(tokens), turn(cotangent)
        full_qkv, full_out, full_up, full_down = (
            lax.all_gather(lax.all_gather(item, "band", axis=0, tiled=True).T, "img", tiled=True)
            for item in (*own, w_down)
        )
        whole = [lax.all_gather(item, "img", tiled=True).astype(F) for item in single]
        cols = jnp.stack(whole + [whole[0]] * (COLUMNS - len(whole)), axis=1)
        c_qv = lax.all_gather(bias_qv, "img", tiled=True).astype(F)[:, None]
        c_up = lax.all_gather(bias_up, "img", tiled=True).astype(F)[:, None]
        bias = jnp.concatenate([c_qv[:width], jnp.zeros((width, 1), F), c_qv[width:]])
        h, qkv = project(x, full_qkv, cols, bias)
        q = qkv[:width]
        all_kv = share(images, bands, qkv[width:])
        all_kv = all_kv.reshape(bands, 2, GROUPS_OF_HEADS, -1, count).transpose(0, 2, 1, 3, 4)
        all_kv = all_kv.reshape(bands, GROUPS_OF_HEADS, -1, count)
        att, lse = attend(scalars, q, all_kv)
        rest = middle(x, cot, scalars, att, full_out, full_up, full_down, cols, c_up)
    out, dmid, datt, delta, g_out, g_up, g_down, sums = rest
    if direct:
        gx, *matrices, turned, total = back(
            images, bands, scalars, q, all_kv, delta, lse, datt, x, x_far, h, dmid,
            full_qkv, cols, (g_out, g_up, g_down), sums,
        )
        matrices.append(turned.T)
    else:
        dq, dkv = attend_back(scalars, q, all_kv, delta, lse, datt)
        dkv = unshare(images, dkv)
        gx, g_qkv, sums_one = finish(x, h, dq, dkv, full_qkv, cols, dmid)
        matrices = [
            lax.psum_scatter(
                lax.psum_scatter(item, "img", scatter_dimension=0, tiled=True),
                "band",
                scatter_dimension=1,
                tiled=True,
            )
            .astype(F)
            .T
            for item in (g_qkv, g_out, g_up, g_down)
        ]
        total = lax.psum(sums + sums_one, ("img", "band"))
    own_small = lax.axis_index("img")
    flat = total.reshape(-1)
    starts = [0, 2, UP_ROW, 3, 4, 5, 6, 7]
    small = [
        lax.dynamic_slice(flat, (start * width + own_small * size,), (size,))
        for start, size in zip(starts, sizes)
    ]
    return (turn_back(out), turn_back(gx), *matrices, *small)


def solution(mesh):
    data, weight, vector = P("img", "band", None, None), P("band", "img"), P("img")
    return jax.shard_map(
        body,
        mesh=mesh,
        in_specs=(data, P("img", None)) + (weight,) * 4 + (vector,) * 8 + (data,),
        out_specs=(data, data) + (weight,) * 4 + (vector,) * 8,
        check_vma=False,
    )
```

```python
import functools
import math

import jax
import jax.numpy as jnp
from jax import lax
from jax.experimental import pallas as pl
from jax.experimental.pallas import tpu as pltpu
from jax.sharding import PartitionSpec as P

HEADS = 16
HEAD_DIM = 48
EPSILON = 1e-06
MASKED = -1e30
BF = jnp.bfloat16
F = jnp.float32
MESH = pl.DeviceIdType.MESH
VM = pl.BlockSpec(memory_space=pltpu.VMEM)
SM = pl.BlockSpec(memory_space=pltpu.SMEM)
ANY = pl.BlockSpec(memory_space=pl.ANY)
LIMIT = 67043328
SUM_ROWS, UP_ROW = 16, 8
COLUMNS = 10
BIAS_OUT, BIAS_DOWN, GAIN_ONE, SHIFT_ONE, GAIN_TWO, SHIFT_TWO = (slice(k, k + 1) for k in range(6))
GROUPS_OF_HEADS = 4
FRONT_COPIES, BACK_COPIES = 128, 128


def dg(left, right, left_dim, right_dim):
    return lax.dot_general(
        left, right, (((left_dim,), (right_dim,)), ((), ())), preferred_element_type=F
    )


def shape(dims, dtype):
    return jax.ShapeDtypeStruct(tuple(dims), dtype)


def row_sums(values):
    ones = jnp.ones((8, values.shape[1]), BF)
    if values.dtype == BF:
        return dg(ones, values, 1, 1)
    high = values.astype(BF)
    low = (values - high.astype(F)).astype(BF)
    return dg(ones, high, 1, 1) + dg(ones, low, 1, 1)


def normalize(values):
    average = jnp.mean(values, axis=0, keepdims=True)
    centered = values - average
    variance = jnp.mean(centered * centered, axis=0, keepdims=True)
    inverse = lax.rsqrt(variance + EPSILON)
    return centered * inverse, inverse


def norm_back(error, normed, inverse, gain):
    f = gain * error
    mean_f = jnp.mean(f, axis=0, keepdims=True)
    mean_fn = jnp.mean(f * normed, axis=0, keepdims=True)
    return (f - mean_f - normed * mean_fn) * inverse


def project_kernel(x_ref, w_ref, cols_ref, bias_ref, h_ref, qkv_ref):
    width = x_ref.shape[0]
    normed, _ = normalize(x_ref[...].astype(F))
    h_ref[...] = (normed * cols_ref[:, GAIN_ONE] + cols_ref[:, SHIFT_ONE]).astype(BF)
    scale = 1.0 / math.sqrt(HEAD_DIM)
    step = 256

    @pl.loop(0, 3 * width // step)
    def _(j):
        rows = pl.ds(pl.multiple_of(j * step, step), step)
        out = dg(w_ref[rows, :], h_ref[...], 1, 0) + bias_ref[rows, :]
        qkv_ref[rows, :] = (out * jnp.where(j < width // step, scale, 1.0)).astype(BF)


def project(x, w, cols, bias):
    width, tokens = x.shape
    return pl.pallas_call(
        project_kernel,
        name="project",
        out_shape=(shape((width, tokens), BF), shape((3 * width, tokens), BF)),
        in_specs=[VM] * 4,
        out_specs=(VM, VM),
        compiler_params=pltpu.CompilerParams(vmem_limit_bytes=LIMIT),
    )(x, w, cols, bias)


def fill_bias(scalars_ref, bias_ref, rows):
    lane_half = lax.broadcasted_iota(jnp.int32, (1, rows), 1) // (rows // 2)
    for s in range(2):
        small = scalars_ref[0, s] == 2
        for other in range(2):
            for half in range(2):
                keep = jnp.logical_and(other == 0, lane_half == half)
                masked = jnp.where(small, MASKED, 0.0)
                bias_ref[pl.ds(4 * s + 2 * other + half, 1), :] = jnp.where(
                    keep, jnp.zeros((1, rows), F), jnp.full((1, rows), masked, F)
                )


def add_bias(scores, bias_ref, s, other):
    rows = scores.shape[0]
    at = 4 * s + 2 * other
    return jnp.concatenate(
        [
            scores[: rows // 2] + bias_ref[pl.ds(at, 1), :],
            scores[rows // 2 :] + bias_ref[pl.ds(at + 1, 1), :],
        ],
        axis=0,
    )


def head_slices(i, rows):
    s, h = i // HEADS, i % HEADS
    lanes = pl.ds(pl.multiple_of(s * rows, rows), rows)
    first = pl.ds(pl.multiple_of(h * HEAD_DIM, 16), HEAD_DIM)
    second = pl.ds(pl.multiple_of(HEADS * HEAD_DIM + h * HEAD_DIM, 16), HEAD_DIM)
    return s, lanes, first, second


def attend_step(i, chip_x, q_ref, kv_ref, bias_ref, out_ref, lse_ref):
    bands = kv_ref.shape[0]
    rows = q_ref.shape[1] // 2
    s, lanes, first, second = head_slices(i, rows)
    q = q_ref[first, lanes]
    scores = []
    maximum = None
    for b in range(bands):
        other = jnp.where(chip_x == b // 2, 0, 1)
        keys, _ = kv_rows(kv_ref, b, i % HEADS)
        part = add_bias(dg(keys[:, lanes], q, 0, 0), bias_ref, s, other)
        scores.append(part)
        top = jnp.max(part, axis=0, keepdims=True)
        maximum = top if maximum is None else jnp.maximum(maximum, top)
    total, acc = 0.0, 0.0
    for b in range(bands):
        weight = jnp.exp(scores[b] - maximum)
        total = total + jnp.sum(weight, axis=0, keepdims=True)
        _, values = kv_rows(kv_ref, b, i % HEADS)
        acc = acc + dg(values[:, lanes], weight.astype(BF), 1, 0)
    out_ref[first, lanes] = acc / total
    lse_ref[pl.ds(i, 1), :] = maximum + jnp.log(total)


def attend_kernel(unroll, scalars_ref, q_ref, kv_ref, out_ref, lse_ref, bias_ref):
    fill_bias(scalars_ref, bias_ref, q_ref.shape[1] // 2)

    @pl.loop(0, 2 * HEADS // unroll)
    def _(j):
        for k in range(unroll):
            attend_step(
                j * unroll + k, scalars_ref[0, 2], q_ref, kv_ref, bias_ref, out_ref, lse_ref
            )


def attend(scalars, q, kv):
    width, tokens = q.shape
    return pl.pallas_call(
        functools.partial(attend_kernel, 4),
        name="attend",
        out_shape=(shape((width, tokens), F), shape((2 * HEADS, tokens // 2), F)),
        in_specs=[SM, VM, VM],
        out_specs=(VM, VM),
        scratch_shapes=[pltpu.VMEM((8, tokens // 2), F)],
        compiler_params=pltpu.CompilerParams(vmem_limit_bytes=LIMIT),
    )(scalars, q, kv)


def attend_back_step(
    i, chip_x, q_ref, kv_ref, delta_ref, lse_ref, dout_ref, bias_ref, dq_ref, put_key, put_value
):
    bands = kv_ref.shape[0]
    rows = q_ref.shape[1] // 2
    s, lanes, first, second = head_slices(i, rows)
    q = q_ref[first, lanes]
    dout = dout_ref[first, lanes]
    delta = delta_ref[pl.ds(i % HEADS, 1), lanes]
    lse = lse_ref[pl.ds(i, 1), :]
    dq = 0.0
    for b in range(bands):
        other = jnp.where(chip_x == b // 2, 0, 1)
        k, v = (ref[:, lanes] for ref in kv_rows(kv_ref, b, i % HEADS))
        scores = add_bias(dg(k, q, 0, 0), bias_ref, s, other)
        dweight = dg(v, dout, 0, 0)
        weight = jnp.exp(scores - lse)
        dscores = (weight * (dweight - delta)).astype(BF)
        dq = dq + dg(k, dscores, 1, 0)
        put_key(b, dg(q, dscores, 1, 1).astype(BF))
        put_value(b, dg(dout, weight.astype(BF), 1, 1).astype(BF))
    dq_ref[first, lanes] = (dq * (1.0 / math.sqrt(HEAD_DIM))).astype(BF)


def attend_back_kernel(
    unroll, scalars_ref, q_ref, kv_ref, delta_ref, lse_ref, dout_ref, dq_ref, dkv_ref, bias_ref
):
    fill_bias(scalars_ref, bias_ref, q_ref.shape[1] // 2)

    @pl.loop(0, 2 * HEADS // unroll)
    def _(j):
        for k in range(unroll):
            i = j * unroll + k
            _, lanes, first, second = head_slices(i, q_ref.shape[1] // 2)

            def put_key(b, values):
                dkv_ref[b, first, lanes] = values

            def put_value(b, values):
                dkv_ref[b, second, lanes] = values

            attend_back_step(
                i, scalars_ref[0, 2], q_ref, kv_ref, delta_ref, lse_ref, dout_ref, bias_ref, dq_ref,
                put_key, put_value,
            )


def attend_back(scalars, q, kv, delta, lse, dout):
    return pl.pallas_call(
        functools.partial(attend_back_kernel, 4),
        name="attend_back",
        out_shape=(shape(q.shape, BF), shape((kv.shape[0], 2 * q.shape[0], q.shape[1]), BF)),
        in_specs=[SM] + [VM] * 5,
        out_specs=(VM, VM),
        scratch_shapes=[pltpu.VMEM((8, q.shape[1] // 2), F)],
        compiler_params=pltpu.CompilerParams(vmem_limit_bytes=LIMIT),
    )(scalars, q, kv, delta, lse, dout)


def middle_body(
    x_ref, cot_ref, scalars_ref, att_ref, w_out_ref, w_up_ref, w_down_ref, cols_ref, bias_up_ref,
    out_ref, dmid_ref, datt_ref, delta_ref, g_out_ref, g_up_out, g_down_out, sums_ref,
    g_up_ref, g_down_ref,
    mid_ref, norm_ref, h_ref, dmlp_ref, mlp_ref, err_ref, attb_ref, dbranch_ref,
    up_sem, down_sem, wait_out, wait_up, passes,
):
    width, tokens = x_ref.shape
    hidden = w_up_ref.shape[0]
    step = 256
    first_slot = lax.broadcasted_iota(jnp.int32, (1, tokens), 1) < tokens // 2
    valid = jnp.where(
        first_slot,
        jnp.where(scalars_ref[0, 0] > 0, 1.0, 0.0),
        jnp.where(scalars_ref[0, 1] > 0, 1.0, 0.0),
    )
    attb_ref[...] = att_ref[...].astype(BF)
    dmlp_ref[...] = (cot_ref[...].astype(F) * valid).astype(BF)
    sums_ref[...] = jnp.zeros_like(sums_ref)
    mlp_ref[...] = jnp.zeros_like(mlp_ref)
    err_ref[...] = jnp.zeros_like(err_ref)
    wait_out()

    @pl.loop(0, width // step)
    def _(j):
        rows = pl.ds(pl.multiple_of(j * step, step), step)
        mid_ref[rows, :] = (
            dg(w_out_ref[rows, :], attb_ref[...], 1, 0)
            + cols_ref[rows, BIAS_OUT]
            + x_ref[rows, :].astype(F)
        )

    normed, inverse = normalize(mid_ref[...])
    norm_ref[...] = normed
    h_ref[...] = (normed * cols_ref[:, GAIN_TWO] + cols_ref[:, SHIFT_TWO]).astype(BF)
    wait_up()

    def stores(j):
        rows = pl.ds(pl.multiple_of(j * step, step), step)
        return (
            pltpu.make_async_copy(g_up_ref.at[rows, :], g_up_out.at[rows, :], up_sem.at[j]),
            pltpu.make_async_copy(g_down_ref.at[:, rows], g_down_out.at[:, rows], down_sem.at[j]),
        )

    def block(j):
        rows = pl.ds(pl.multiple_of(j * step, step), step)
        pre = dg(w_up_ref[rows, :], h_ref[...], 1, 0) + bias_up_ref[rows, :]
        phi = 0.5 + 0.5 * lax.erf(pre * math.sqrt(0.5))
        act = (pre * phi).astype(BF)
        slope = phi + pre * jnp.exp(pre * pre * -0.5) * (1.0 / math.sqrt(2.0 * math.pi))
        mlp_ref[...] += dg(w_down_ref[:, rows], act, 1, 0)
        dact = dg(w_down_ref[:, rows], dmlp_ref[...], 0, 0)
        dhid = (slope * dact).astype(BF)
        g_down_ref[:, rows] = dg(dmlp_ref[...], act, 1, 1).astype(BF)
        g_up_ref[rows, :] = dg(dhid, h_ref[...], 1, 1).astype(BF)
        per = width // step
        lanes = pl.ds(pl.multiple_of(j % per * step, step), step)
        sums_ref[pl.ds(UP_ROW + j // per, 1), lanes] = row_sums(dhid)[:1]
        err_ref[...] += dg(w_up_ref[rows, :], dhid, 0, 0)
        for copy in stores(j):
            copy.start()

    for wait, count, place in passes:
        wait()

        @pl.loop(0, count)
        def _(t):
            block(place(t))

    out = (mid_ref[...] + mlp_ref[...] + cols_ref[:, BIAS_DOWN]) * valid
    out_ref[...] = out.T.astype(BF)
    err = err_ref[...]
    sums_ref[3:4] = row_sums(dmlp_ref[...])[:1]
    sums_ref[6:7] = row_sums(err * norm_ref[...])[:1]
    sums_ref[7:8] = row_sums(err)[:1]
    dmid = cot_ref[...].astype(F) * valid + norm_back(
        err, norm_ref[...], inverse, cols_ref[:, GAIN_TWO]
    )
    dmid_ref[...] = dmid
    dbranch_ref[...] = dmid.astype(BF)
    sums_ref[2:3] = row_sums(dbranch_ref[...])[:1]
    datt_ref[...] = dg(w_out_ref[...], dbranch_ref[...], 0, 0).astype(BF)
    inner = att_ref[...] * datt_ref[...].astype(F)
    delta_ref[...] = jnp.sum(inner.reshape(HEADS, width // HEADS, tokens), axis=1)

    @pl.loop(0, width // step)
    def _(j):
        rows = pl.ds(pl.multiple_of(j * step, step), step)
        g_out_ref[rows, :] = dg(dbranch_ref[rows, :], attb_ref[...], 1, 1).astype(BF)

    @pl.loop(0, hidden // step)
    def _(j):
        for copy in stores(j):
            copy.wait()


def middle_kernel(*refs):
    x_ref, cot_ref, scalars_ref, att_ref, w_out_in, w_up_in, w_down_in = refs[:7]
    outputs = refs[7:17]
    w_out_ref, w_up_ref, w_down_ref = refs[17:20]
    scratch, in_sem = refs[20:30], refs[30]
    loads = [
        pltpu.make_async_copy(source, target, in_sem.at[k])
        for k, (source, target) in enumerate(
            ((w_out_in, w_out_ref), (w_up_in, w_up_ref), (w_down_in, w_down_ref))
        )
    ]
    for copy in loads:
        copy.start()
    middle_body(
        x_ref, cot_ref, scalars_ref, att_ref, w_out_ref, w_up_ref, w_down_ref, *outputs, *scratch,
        *refs[31:], loads[0].wait, loads[1].wait,
        [(loads[2].wait, w_up_ref.shape[0] // 256, lambda t: t)],
    )


def middle(x, cot, scalars, att, w_out, w_up, w_down, cols, bias_up):
    width, tokens = x.shape
    hidden = w_up.shape[0]
    full = (width, tokens)
    weights = [w_out.shape, w_up.shape, w_down.shape]
    return pl.pallas_call(
        middle_kernel,
        name="middle",
        out_shape=(
            shape((tokens, width), BF),
            shape(full, F),
            shape(full, BF),
            shape((HEADS, tokens), F),
            shape(w_out.shape, BF),
            shape(w_up.shape, BF),
            shape(w_down.shape, BF),
            shape((SUM_ROWS, width), F),
        ),
        in_specs=[VM, VM, SM, VM] + [ANY] * 3 + [VM] * 2,
        out_specs=(VM,) * 5 + (ANY, ANY, VM),
        scratch_shapes=[pltpu.VMEM(s, BF) for s in weights + weights[1:]]
        + [
            pltpu.VMEM(full, F),
            pltpu.VMEM(full, F),
            pltpu.VMEM(full, BF),
            pltpu.VMEM(full, BF),
            pltpu.VMEM(full, F),
            pltpu.VMEM(full, F),
            pltpu.VMEM(full, BF),
            pltpu.VMEM(full, BF),
            pltpu.SemaphoreType.DMA((3,)),
            pltpu.SemaphoreType.DMA((hidden // 256,)),
            pltpu.SemaphoreType.DMA((hidden // 256,)),
        ],
        compiler_params=pltpu.CompilerParams(vmem_limit_bytes=LIMIT),
    )(x, cot, scalars, att, w_out, w_up, w_down, cols, bias_up)


def finish_kernel(
    x_ref, h_ref, dq_ref, dkv_ref, w_ref, cols_ref, dmid_ref, gx_ref, g_ref, sums_ref, err_ref
):
    width, tokens = x_ref.shape
    step = 256
    blocks = width // step
    err_ref[...] = jnp.zeros_like(err_ref)
    for ref, count, base in ((dq_ref, blocks, 0), (dkv_ref, 2 * blocks, blocks)):

        @pl.loop(0, count)
        def _(j):
            rows = pl.ds(pl.multiple_of(j * step, step), step)
            to = pl.ds(pl.multiple_of((j + base) * step, step), step)
            g_ref[to, :] = dg(ref[rows, :], h_ref[...], 1, 1).astype(BF)
            err_ref[...] += dg(w_ref[to, :], ref[rows, :], 0, 0)

    normed, inverse = normalize(x_ref[...].astype(F))
    err = err_ref[...]
    sums_ref[...] = jnp.zeros_like(sums_ref)
    sums_ref[0:1] = row_sums(dq_ref[...])[:1]
    sums_ref[1:2] = row_sums(dkv_ref[pl.ds(width, width), :])[:1]
    sums_ref[4:5] = row_sums(err * normed)[:1]
    sums_ref[5:6] = row_sums(err)[:1]
    grad = dmid_ref[...] + norm_back(err, normed, inverse, cols_ref[:, GAIN_ONE])
    gx_ref[...] = grad.T.astype(BF)


def finish(x, h, dq, dkv, w, cols, dmid):
    width, tokens = x.shape
    return pl.pallas_call(
        finish_kernel,
        name="finish",
        out_shape=(shape((tokens, width), BF), shape(w.shape, BF), shape((SUM_ROWS, width), F)),
        in_specs=[VM] * 7,
        out_specs=(VM, VM, VM),
        scratch_shapes=[pltpu.VMEM(x.shape, F)],
        compiler_params=pltpu.CompilerParams(vmem_limit_bytes=LIMIT),
    )(x, h, dq, dkv, w, cols, dmid)


class Place:
    def __init__(self, images):
        self.images = images
        self.depth = images // 2
        self.img = lax.axis_index("img")
        self.band = lax.axis_index("band")
        self.z, self.y = self.img // 2, self.img % 2
        self.x, self.c = self.band // 2, self.band % 2
        self.partner = (self.img, self.band + 1 - 2 * self.c)
        self.across_x = (self.img, self.band + 2 - 4 * self.x)
        self.across_y = (self.img + 1 - 2 * self.y, self.band)
        self.z_peers = [self.along_z(k) for k in range(1, self.depth)]

    def along_z(self, k):
        z = lax.rem(self.z + k, self.depth)
        return (2 * z + self.y, self.band), z


def greet(peers):
    barrier = pltpu.get_barrier_semaphore()
    for peer in peers:
        pl.semaphore_signal(barrier, inc=1, device_id=peer, device_id_type=MESH)
    pl.semaphore_wait(barrier, len(peers))


def send(src, dst, send_sem, recv_sem, peer):
    copy = pltpu.make_async_remote_copy(
        src_ref=src,
        dst_ref=dst,
        send_sem=send_sem,
        recv_sem=recv_sem,
        device_id=peer,
        device_id_type=MESH,
    )
    copy.start()
    return copy


def comm_params(collective_id):
    return pltpu.CompilerParams(
        collective_id=collective_id, has_side_effects=True, vmem_limit_bytes=LIMIT
    )


class Spread:
    def __init__(self, at, make, order, part, parts, source, ref, local_sem):
        depth, near, c = at.depth, at.depth // 2, at.c
        rows, half = ref.shape[2] // 2, ref.shape[3] // 2
        rows = pl.ds(pl.multiple_of(c * rows, 16), rows)
        size = half // parts
        lanes = pl.ds(pl.multiple_of(at.x * half + part * size, 128), size)
        both = [pl.ds(x * half + part * size, size) for x in range(2)]
        if parts == 1:
            both = [slice(None)]
        low, high = pl.ds(0, near), pl.ds(near, depth - near)

        def same(index, peer):
            if len(index) == 4:
                return [make(ref.at[index], ref.at[index], peer)]
            return [make(ref.at[index + (l,)], ref.at[index + (l,)], peer) for l in both]

        piece = ref.at[at.z, at.y, rows, lanes]
        source = source.at[:, pl.ds(part * size, size)]
        self.keep = pltpu.make_async_copy(source, piece, local_sem)
        z_first = []
        if order != "xyz":
            z_first = [make(source, piece, peer) for peer, _ in at.z_peers]
        if order == "mixed":
            self.stages = [
                z_first,
                same((low, at.y, rows, lanes), at.across_x)
                + same((high, at.y, rows, lanes), at.across_y),
                same((low, at.y, rows), at.across_y)
                + same((high, slice(None), rows, lanes), at.across_x),
            ]
        elif order == "zxy":
            self.stages = [
                z_first,
                same((slice(None), at.y, rows, lanes), at.across_x),
                same((slice(None), at.y, rows), at.across_y),
            ]
        else:
            last = [same((at.z, slice(None), rows), peer) for peer, _ in at.z_peers]
            self.stages = [
                [make(source, piece, at.across_x)],
                same((at.z, at.y, rows), at.across_y),
                sum(last, []),
            ]
        self.stages.append(same((slice(None), slice(None), rows), at.partner))

    def start(self):
        self.keep.start()
        for copy in self.stages[0]:
            copy.start()

    def step(self, k):
        if k == 1:
            self.keep.wait()
        for copy in self.stages[k - 1]:
            copy.wait_recv()
        for copy in self.stages[k]:
            copy.start()

    def wait(self):
        for copy in self.stages[-1]:
            copy.wait_recv()

    def end(self):
        for stage in self.stages:
            for copy in stage:
                copy.wait_send()


def kv_rows(ref, b, h):
    part = ref.shape[2] // 2
    heads = part // HEAD_DIM
    first = pl.multiple_of(h % heads * HEAD_DIM, 16)
    second = pl.multiple_of(part + h % heads * HEAD_DIM, 16)
    at = ref.at[b, h // heads]
    return at.at[pl.ds(first, HEAD_DIM)], at.at[pl.ds(second, HEAD_DIM)]


def front_kernel(
    images, bands, scalars_ref, shard_qkv_ref, shard_out_ref, shard_up_ref, shard_down_ref,
    small_ref, tokens_ref, cot_tokens_ref,
    qkv_w_out, h_out, kv_out, x_out, x_far_out, q_ref, lse_ref, cols_ref, *rest,
):
    results, rest = rest[:8], rest[8:]
    wide_ref = shard_down_ref
    narrow_ref, x_ref, cot_ref, far_tokens_ref = rest[:4]
    rest = rest[4:]
    qkv_w_ref, out_w_ref, up_w_ref, down_w_ref, h_ref, kv_ref, att_ref, up_col_ref = rest[:8]
    theirs_ref, mine_ref, mine_wide_ref, smalls_ref, qv_col_ref, bias_ref, x_far_ref = rest[8:15]
    local_sem, send_sem, recv_sem = rest[15:18]
    middle_scratch = rest[18:]
    at = Place(images)
    width, tokens = x_ref.shape
    rows = tokens // 2
    unit = width // images
    groups = kv_ref.shape[1]
    part = width // groups
    c = at.c
    used = [0, 0]

    def make(src, dst, peer):
        k = used[0]
        used[0] += 1
        return pltpu.make_async_remote_copy(
            src_ref=src,
            dst_ref=dst,
            send_sem=send_sem.at[k],
            recv_sem=recv_sem.at[k],
            device_id=peer,
            device_id_type=MESH,
        )

    def local():
        used[1] += 1
        return local_sem.at[used[1] - 1]

    others = [(lax.rem(at.img + k, images), at.band) for k in range(1, images)]
    half = wide_ref.shape[0] // 2
    wide = wide_ref.shape[1]
    own_lanes = pl.ds(pl.multiple_of(c * wide, 128), wide)
    own_wide = pltpu.make_async_copy(
        wide_ref.at[pl.ds(pl.multiple_of(c * half, 8), half), :],
        mine_wide_ref.at[:, own_lanes],
        local(),
    )
    swap = make(narrow_ref.at[1 - c], theirs_ref, at.partner)
    swap_wide = make(
        wide_ref.at[pl.ds(pl.multiple_of((1 - c) * half, 8), half), :],
        mine_wide_ref.at[:, own_lanes],
        at.partner,
    )
    lines = pl.ds(pl.multiple_of(at.img * 16, 16), 16)
    keep_small = pltpu.make_async_copy(small_ref, smalls_ref.at[lines, :], local())
    small_copies = [make(small_ref, smalls_ref.at[lines, :], peer) for peer in others]
    sources, row = [], 0
    for ref in (qkv_w_ref, out_w_ref, up_w_ref):
        count = ref.shape[2] // 2
        sources.append(mine_ref.at[pl.ds(row, count), :])
        row += count
    sources.append(mine_wide_ref)

    def spread(ref, source, orders):
        parts = len(orders)
        return [
            Spread(at, make, orders[k], k, parts, source, ref, local()) for k in range(parts)
        ]

    s_qkv = spread(qkv_w_ref, sources[0], ("mixed",) * 3)
    (s_out,) = spread(out_w_ref, sources[1], ("mixed",))
    s_up = spread(up_w_ref, sources[2], ("mixed", "mixed", "mixed"))
    d_one, d_two = spread(down_w_ref, sources[3], ("mixed", "mixed"))
    save_w = pltpu.make_async_copy(qkv_w_ref, qkv_w_out, local())
    save_h = pltpu.make_async_copy(h_ref, h_out, local())
    save_x = pltpu.make_async_copy(x_ref, x_out, local())
    save_far = pltpu.make_async_copy(x_far_ref, x_far_out, local())
    save_kv = [
        pltpu.make_async_copy(kv_ref.at[:, g], kv_out.at[:, g], local()) for g in range(groups)
    ]
    x_lanes = [pl.ds(s * rows, rows) for s in range(2)]
    x_moves = [make(tokens_ref.at[l], far_tokens_ref.at[l], at.across_x) for l in x_lanes]
    far = at.across_x[1]
    kv_moves = [
        [
            [
                make(kv_ref.at[b, g, :, x_lanes[s]], kv_ref.at[b, g, :, x_lanes[s]], at.partner)
                for b in (at.band, far)
            ]
            for g in range(groups)
        ]
        for s in range(2)
    ]

    row = 0
    for ref in (shard_qkv_ref, shard_out_ref, shard_up_ref):
        turned = ref[...].astype(F).T.astype(BF)
        count = turned.shape[0] // 2
        for core in range(2):
            narrow_ref[core, pl.ds(row, count), :] = turned[core * count : (core + 1) * count]
        row += count
    greet([at.partner, at.across_x] + others)
    x_moves[0].start()
    x_moves[1].start()
    swap.start()
    own_wide.start()
    swap_wide.start()
    keep_small.start()
    for copy in small_copies:
        copy.start()
    fill_bias(scalars_ref, bias_ref, rows)
    swap.wait_recv()
    mine, theirs = narrow_ref[c], theirs_ref[...]
    lane_count = mine.shape[1]
    mine_ref[:, pl.ds(0, lane_count)] = jnp.where(c == 0, mine, theirs)
    mine_ref[:, pl.ds(lane_count, lane_count)] = jnp.where(c == 0, theirs, mine)
    for item in s_qkv:
        item.start()
    own_wide.wait()
    swap_wide.wait_recv()
    s_out.start()
    for item in s_up:
        item.start()
    d_two.start()
    d_one.start()

    for s in range(2):
        x_ref[:, x_lanes[s]] = tokens_ref[x_lanes[s], :].astype(F).T.astype(BF)
        cot_ref[:, x_lanes[s]] = cot_tokens_ref[x_lanes[s], :].astype(F).T.astype(BF)
    save_x.start()

    keep_small.wait()
    for copy in small_copies:
        copy.wait_recv()
    turned = smalls_ref[...].T
    qv_units, up_units = 2, up_w_ref.shape[2] // unit
    singles = 16 - qv_units - up_units
    for j in range(images):
        block = turned[:unit, 16 * j : 16 * j + 16]
        cols_ref[pl.ds(unit * j, unit), :] = block[:, :singles]
        for u in range(qv_units):
            lane = singles + u
            qv_col_ref[pl.ds(unit * (qv_units * j + u), unit), :] = block[:, lane : lane + 1]
        for u in range(up_units):
            lane = singles + qv_units + u
            up_col_ref[pl.ds(unit * (up_units * j + u), unit), :] = block[:, lane : lane + 1]

    def far_tokens(s):
        x_moves[s].wait_recv()
        x_far_ref[:, x_lanes[s]] = far_tokens_ref[x_lanes[s], :].astype(F).T.astype(BF)

    def first_norm(s, ref, side):
        normed, _ = normalize(ref[:, x_lanes[s]].astype(F))
        to = pl.ds(side * tokens + s * rows, rows)
        h_ref[:, to] = (normed * cols_ref[:, GAIN_ONE] + cols_ref[:, SHIFT_ONE]).astype(BF)

    s_qkv[0].step(1)
    s_qkv[1].step(1)
    s_qkv[0].step(2)
    s_qkv[2].step(1)
    for s in range(2):
        first_norm(s, x_ref, 0)
    s_qkv[1].step(2)
    s_qkv[0].step(3)
    s_qkv[2].step(2)
    s_out.step(1)
    far_tokens(0)
    first_norm(0, x_far_ref, 1)
    s_qkv[1].step(3)
    s_up[0].step(1)
    s_up[1].step(1)
    s_qkv[2].step(3)
    s_up[2].step(1)
    d_two.step(1)
    for item in s_qkv:
        item.wait()
    d_one.step(1)
    save_w.start()

    weights = qkv_w_ref.reshape(3 * width, width)
    scale = 1.0 / math.sqrt(HEAD_DIM)

    def project(s):
        for g in range(groups):
            for k in range(2):
                row = (1 + k) * width + g * part
                to = pl.ds(k * part, part)
                for side, band in enumerate((at.band, far)):
                    lanes = pl.ds(side * tokens + s * rows, rows)
                    out = dg(weights[pl.ds(row, part), :], h_ref[:, lanes], 1, 0)
                    if k == 1:
                        out = out + qv_col_ref[pl.ds(width + g * part, part), :]
                    kv_ref[band, g, to, x_lanes[s]] = out.astype(BF)
            for copy in kv_moves[s][g]:
                copy.start()
        for g in range(groups):
            block = pl.ds(g * part, part)
            out = dg(weights[block, :], h_ref[:, x_lanes[s]], 1, 0) + qv_col_ref[block, :]
            q_ref[block, x_lanes[s]] = (out * scale).astype(BF)

    def second_slot():
        far_tokens(1)
        first_norm(1, x_far_ref, 1)
        project(1)
        save_h.start()
        save_far.start()

    def arrive(s, g):
        for copy in kv_moves[s][g]:
            copy.wait_recv()
        if s == 1:
            save_kv[g].start()

    events = {}

    def when(j, *actions):
        events.setdefault(j, []).extend(actions)

    when(2, second_slot)
    for j in range(1, 2 * groups):
        when(j - 1, functools.partial(arrive, j // groups, j % groups))
    when(0, functools.partial(s_up[0].step, 2))
    when(1, functools.partial(s_up[1].step, 2))
    when(2, functools.partial(s_up[2].step, 2), functools.partial(s_out.step, 3))
    when(3, functools.partial(d_two.step, 2))
    when(4, functools.partial(d_one.step, 2))
    when(5, functools.partial(s_up[0].step, 3))
    when(6, functools.partial(s_up[1].step, 3))
    when(7, functools.partial(s_up[2].step, 3))
    s_out.step(2)
    project(0)
    arrive(0, 0)
    unroll = HEADS // groups

    @pl.loop(0, 2 * groups)
    def _(j):
        s, g = j // groups, j % groups
        for k in range(unroll):
            attend_step(
                s * HEADS + g * unroll + k, at.x, q_ref, kv_ref, bias_ref, att_ref, lse_ref
            )
        for when_j, actions in events.items():

            @pl.when(j == when_j)
            def _():
                for action in actions:
                    action()

    hidden = up_w_ref.shape[0] * 2 * up_w_ref.shape[2]
    blocks = hidden // 256
    quarter = blocks // 4

    def wait_out():
        s_out.wait()

    def wait_up():
        d_two.step(3)
        for item in s_up:
            item.wait()

    def wait_one():
        d_one.step(3)
        d_one.wait()

    def flat(ref):
        return ref.reshape(ref.shape[0] * 2 * ref.shape[2], ref.shape[3])

    middle_body(
        x_ref, cot_ref, scalars_ref, att_ref, flat(out_w_ref), flat(up_w_ref), flat(down_w_ref),
        cols_ref, up_col_ref, *results, *middle_scratch, wait_out, wait_up,
        [
            (d_two.wait, 2 * quarter, lambda t: t + t // quarter * quarter + quarter),
            (wait_one, 2 * quarter, lambda t: t + t // quarter * quarter),
        ],
    )
    for item in s_qkv + s_up + [s_out, d_one, d_two]:
        item.end()
    for copy in [save_w, save_h, save_x, save_far] + save_kv:
        copy.wait()
    for copy in [swap, swap_wide] + small_copies + x_moves:
        copy.wait_send()
    for copy in sum(sum(kv_moves, []), []):
        copy.wait_send()


def front(images, bands, scalars, shards, small, tokens_by_slot, cot_by_slot):
    depth = images // 2
    tokens, width = tokens_by_slot.shape
    groups = GROUPS_OF_HEADS
    widths = [item.shape[1] for item in shards[:3]]
    hidden = images * widths[2]
    full = (width, tokens)
    part = shards[0].shape[0]
    narrow = (2, sum(widths) // 2, part)
    wide = shards[3].shape
    kv = (bands, groups, 2 * width // groups, tokens)
    weights = [(depth, 2, w, width) for w in widths]
    weights.append((depth, 2, wide[0], 4 * wide[1]))
    return pl.pallas_call(
        functools.partial(front_kernel, images, bands),
        name="front",
        out_shape=(
            shape(weights[0], BF),
            shape((width, 2 * tokens), BF),
            shape(kv, BF),
            shape(full, BF),
            shape(full, BF),
            shape(full, BF),
            shape((2 * HEADS, tokens // 2), F),
            shape((width, COLUMNS), F),
            shape((tokens, width), BF),
            shape(full, F),
            shape(full, BF),
            shape((HEADS, tokens), F),
            shape((width, width), BF),
            shape((hidden, width), BF),
            shape((width, hidden), BF),
            shape((SUM_ROWS, width), F),
        ),
        in_specs=[SM] + [VM] * 7,
        out_specs=(ANY,) * 5 + (VM,) * 8 + (ANY, ANY, VM),
        scratch_shapes=[pltpu.VMEM(s, BF) for s in (narrow, full, full, (tokens, width))]
        + [pltpu.VMEM(s, BF) for s in weights]
        + [
            pltpu.VMEM((width, 2 * tokens), BF),
            pltpu.VMEM(kv, BF),
            pltpu.VMEM(full, F),
            pltpu.VMEM((hidden, 1), F),
            pltpu.VMEM(narrow[1:], BF),
            pltpu.VMEM((narrow[1], 2 * narrow[2]), BF),
            pltpu.VMEM((wide[0] // 2, 2 * wide[1]), BF),
            pltpu.VMEM((16 * images, 128), F),
            pltpu.VMEM((2 * width, 1), F),
            pltpu.VMEM((8, tokens // 2), F),
            pltpu.VMEM(full, BF),
            pltpu.SemaphoreType.DMA((24,)),
            pltpu.SemaphoreType.DMA((FRONT_COPIES,)),
            pltpu.SemaphoreType.DMA((FRONT_COPIES,)),
            pltpu.VMEM((hidden, width), BF),
            pltpu.VMEM((width, hidden), BF),
            pltpu.VMEM(full, F),
            pltpu.VMEM(full, F),
            pltpu.VMEM(full, BF),
            pltpu.VMEM(full, BF),
            pltpu.VMEM(full, F),
            pltpu.VMEM(full, F),
            pltpu.VMEM(full, BF),
            pltpu.VMEM(full, BF),
            pltpu.SemaphoreType.DMA((hidden // 256,)),
            pltpu.SemaphoreType.DMA((hidden // 256,)),
        ],
        compiler_params=comm_params(0),
    )(scalars, *shards, small, tokens_by_slot, cot_by_slot)


def share_kernel(images, kv_ref, all_ref, local_sem, send_sem, recv_sem):
    at = Place(images)
    greet([at.partner, at.across_x])
    rows = kv_ref.shape[1] // 2
    mine = pltpu.make_async_copy(kv_ref, all_ref.at[at.band], local_sem)
    mine.start()
    copies = []
    for s in range(2):
        lanes = pl.ds(s * rows, rows)
        copies.append(
            send(
                kv_ref.at[:, lanes],
                all_ref.at[at.band, :, lanes],
                send_sem.at[s],
                recv_sem.at[s],
                at.across_x,
            )
        )
    near = send(kv_ref, all_ref.at[at.band], send_sem.at[2], recv_sem.at[2], at.partner)
    passed = []
    for s in range(2):
        copies[s].wait_recv()
        part = all_ref.at[at.across_x[1], :, pl.ds(s * rows, rows)]
        passed.append(send(part, part, send_sem.at[3 + s], recv_sem.at[3 + s], at.partner))
    for copy in passed + [near]:
        copy.wait()
    for copy in copies:
        copy.wait_send()
    mine.wait()


def share(images, bands, kv):
    return pl.pallas_call(
        functools.partial(share_kernel, images),
        name="share",
        out_shape=shape((bands,) + kv.shape, BF),
        in_specs=[VM],
        out_specs=ANY,
        scratch_shapes=[
            pltpu.SemaphoreType.DMA,
            pltpu.SemaphoreType.DMA((5,)),
            pltpu.SemaphoreType.DMA((5,)),
        ],
        compiler_params=comm_params(1),
    )(kv)


def add_rows(total_ref, other_ref, step):
    @pl.loop(0, total_ref.shape[0] // step)
    def _(j):
        rows = pl.ds(pl.multiple_of(j * step, step), step)
        total_ref[rows, :] = (
            total_ref[rows, :].astype(F) + other_ref[rows, :].astype(F)
        ).astype(total_ref.dtype)


def unshare_kernel(images, dkv_ref, sum_ref, near_ref, far_ref, send_sem, recv_sem):
    at = Place(images)
    greet([at.partner, at.across_x])
    mate, far = at.partner[1], at.across_x[1]
    far_mate = at.band + 2 - 4 * at.x + 1 - 2 * at.c
    one = send(dkv_ref.at[far_mate], near_ref.at[0], send_sem.at[0], recv_sem.at[0], at.partner)
    two = send(dkv_ref.at[mate], near_ref.at[1], send_sem.at[1], recv_sem.at[1], at.partner)
    one.wait_recv()
    add_rows(near_ref.at[0], dkv_ref.at[far], 64)
    three = send(near_ref.at[0], far_ref, send_sem.at[2], recv_sem.at[2], at.across_x)
    two.wait_recv()
    add_rows(near_ref.at[1], dkv_ref.at[at.band], 64)
    three.wait_recv()
    sum_ref[...] = near_ref[1]
    add_rows(sum_ref, far_ref, 64)
    for copy in (one, two, three):
        copy.wait_send()


def unshare(images, dkv):
    block = dkv.shape[1:]
    return pl.pallas_call(
        functools.partial(unshare_kernel, images),
        name="unshare",
        out_shape=shape(block, BF),
        in_specs=[VM],
        out_specs=VM,
        scratch_shapes=[
            pltpu.VMEM((2,) + block, BF),
            pltpu.VMEM(block, BF),
            pltpu.SemaphoreType.DMA((3,)),
            pltpu.SemaphoreType.DMA((3,)),
        ],
        compiler_params=comm_params(2),
    )(dkv)


def accumulate(total, other):
    total[...] = total[...] + other[...]


class Reduction:
    def __init__(self, at, make, order, start, size, ref, one, other, bufs, total):
        depth, near = at.depth, at.depth // 2
        half = ref.shape[3] // 2
        self.at, self.near, self.one, self.other, self.order = at, near, one, other, order

        def lanes_of(x):
            return pl.ds(pl.multiple_of(x * half + start, 128), size)

        self.lanes, self.both = lanes_of(at.x), [lanes_of(x) for x in range(2)]
        self.total = total.at[:, pl.ds(start, size)]
        far = lanes_of(1 - at.x)
        upper = depth - near
        if order == "mixed":
            two_x, two_y, three, four = bufs
            self.two_x, self.two_y = two_x, two_y
            low, high = pl.ds(0, near), pl.ds(near, upper)
            self.first = [make(one.at[low, :, :, far], two_x, at.across_x)] + [
                make(one.at[high, 1 - at.y, :, self.both[x]], two_y.at[x], at.across_y)
                for x in range(2)
            ]
            self.second = [
                make(two_x.at[:, 1 - at.y], three.at[low], at.across_y),
                make(two_y.at[1 - at.x], three.at[high], at.across_x),
            ]
        else:
            two, three, four = bufs
            self.two = two
            self.first = [
                make(one.at[:, 1 - at.y, :, self.both[x]], two.at[x], at.across_y)
                for x in range(2)
            ]
            self.second = [make(two.at[1 - at.x], three, at.across_x)]
        self.three, self.four = three, four
        self.third = [
            make(three.at[z], four.at[k], peer) for k, (peer, z) in enumerate(at.z_peers)
        ]

    def step_one(self):
        for lanes in self.both:

            @pl.loop(0, 2 * self.at.depth)
            def _(j):
                accumulate(
                    self.one.at[j // 2, j % 2, :, lanes],
                    self.other.at[j // 2, j % 2, :, lanes],
                )

        for copy in self.first:
            copy.start()

    def step_two(self):
        at = self.at
        if self.order == "mixed":
            self.first[0].wait_recv()

            @pl.loop(0, 2 * self.near)
            def _(j):
                accumulate(
                    self.two_x.at[j // 2, j % 2], self.one.at[j // 2, j % 2, :, self.lanes]
                )

            self.second[0].start()
            for x in range(2):
                self.first[1 + x].wait_recv()

                @pl.loop(0, at.depth - self.near)
                def _(j):
                    accumulate(
                        self.two_y.at[x, j], self.one.at[self.near + j, at.y, :, self.both[x]]
                    )

            self.second[1].start()
        else:
            for x in range(2):
                self.first[x].wait_recv()

                @pl.loop(0, at.depth)
                def _(j):
                    accumulate(self.two.at[x, j], self.one.at[j, at.y, :, self.both[x]])

            self.second[0].start()

    def step_three(self):
        at = self.at
        for copy in self.second:
            copy.wait_recv()
        if self.order == "mixed":

            @pl.loop(0, self.near)
            def _(j):
                accumulate(self.three.at[j], self.two_x.at[j, at.y])

            @pl.loop(0, at.depth - self.near)
            def _(j):
                accumulate(self.three.at[self.near + j], self.two_y.at[at.x, j])

        else:

            @pl.loop(0, at.depth)
            def _(j):
                accumulate(self.three.at[j], self.two.at[at.x, j])

        for copy in self.third:
            copy.start()

    def step_four(self):
        for copy in self.third:
            copy.wait_recv()
        total = self.three[self.at.z].astype(F)
        for k in range(len(self.third)):
            total = total + self.four[k].astype(F)
        self.total[...] = total

    def end(self):
        for copy in self.first + self.second + self.third:
            copy.wait_send()


def reduction_buffers(order, depth, rows, size):
    near = depth // 2
    if order == "mixed":
        first = [(near, 2, rows, size), (2, depth - near, rows, size)]
    else:
        first = [(2, depth, rows, size)]
    return [pltpu.VMEM(s, BF) for s in first + [(depth, rows, size), (depth - 1, rows, size)]]


BACK_ORDERS = (
    (("mixed", 1), ("mixed", 1)),
    (("mixed", 1), ("mixed", 1), ("mixed", 1)),
    (("mixed", 1),),
    (("mixed", 2), ("yx", 1)),
)


def lane_parts(orders, half):
    unit = half // sum(share for _, share in orders)
    parts, start = [], 0
    for order, share in orders:
        parts.append((order, start, share * unit))
        start += share * unit
    return parts


def back_kernel(
    images, bands, scalars_ref, q_ref, delta_ref, lse_ref, datt_ref, cols_ref, sums_ref,
    kv_in, x_in, x_far_in, h_in, dmid_in, w_in, g_out_ref, g_up_ref, g_down_ref,
    gx_ref, o_qkv_ref, o_out_ref, o_up_ref, o_down_ref, total_ref,
    p_down_ref, p_up_ref, p_out_ref, p_qkv_ref,
    kv_ref, x_ref, x_far_ref, h_ref, dmid_ref, w_ref,
    bias_ref, dq_ref, dwide_ref, dkv_ref, near_ref, g_qkv_ref, err_ref, err_far_ref, err_in_ref,
    small_ref, small_in_ref, small_z_ref, *rest,
):
    at = Place(images)
    depth = at.depth
    local_sem, send_sem, recv_sem = rest[-3:]
    rest = list(rest[:-3])
    used = [0, 0]

    def make(src, dst, peer):
        k = used[0]
        used[0] += 1
        return pltpu.make_async_remote_copy(
            src_ref=src,
            dst_ref=dst,
            send_sem=send_sem.at[k],
            recv_sem=recv_sem.at[k],
            device_id=peer,
            device_id_type=MESH,
        )

    def load(src, dst):
        used[1] += 1
        return pltpu.make_async_copy(src, dst, local_sem.at[used[1] - 1])

    width, tokens = x_ref.shape
    rows = tokens // 2
    unroll = 4
    groups = HEADS // unroll
    part = width // groups

    def four_d(ref):
        return ref.reshape(depth, 2, ref.shape[0] // images, ref.shape[1])

    sources = (four_d(g_down_ref), four_d(g_up_ref), four_d(g_out_ref), g_qkv_ref)
    targets = (p_down_ref, p_up_ref, p_out_ref, p_qkv_ref)
    swaps, owns, moves, ends = [], [], [], []
    for m in range(4):
        one, total, away = rest[:3]
        rest = rest[3:]
        block, lanes = sources[m].shape[2] // 2, sources[m].shape[3]
        near_rows = pl.ds(pl.multiple_of(at.c * block, 16), block)
        far_rows = pl.ds(pl.multiple_of((1 - at.c) * block, 16), block)
        parts = lane_parts(BACK_ORDERS[m], lanes // 2)
        if m < 3:
            other = rest.pop(0)
            owns.append(load(sources[m].at[:, :, near_rows, :], one))
            swaps.append([make(sources[m].at[:, :, far_rows, :], other, at.partner)])
        else:
            other = sources[m].at[:, :, near_rows, :]
            for _, start, size in parts:
                both = [pl.ds(x * (lanes // 2) + start, size) for x in range(2)]
                swaps.append(
                    [
                        make(sources[m].at[:, :, far_rows, l], one.at[:, :, :, l], at.partner)
                        for l in both
                    ]
                )
        moves.append([])
        for order, start, size in parts:
            count = 4 if order == "mixed" else 3
            moves[m].append(
                Reduction(
                    at, make, order, start, size, sources[m], one, other, rest[:count], total
                )
            )
            rest = rest[count:]
        ends.append((total, away, targets[m], make(away, targets[m].at[at.c], at.partner)))
    down, up, out, qkv = moves

    def deliver(m):
        total_ref, away, target, copy = ends[m]
        total = total_ref[...]
        size = total.shape[1] // 2
        low, high = total[:, :size], total[:, size:]
        target[at.c] = jnp.where(at.c == 0, low, high)
        away[...] = jnp.where(at.c == 0, high, low)
        copy.start()

    mate, far = at.partner[1], at.across_x[1]
    far_mate = at.across_x[1] + 1 - 2 * at.c
    one = [make(dkv_ref.at[far_mate, g], near_ref.at[0, g], at.partner) for g in range(groups)]
    two = [make(dkv_ref.at[mate, g], near_ref.at[1, g], at.partner) for g in range(groups)]
    err_moves = [make(err_far_ref.at[s], err_in_ref.at[s], at.across_x) for s in range(2)]
    small_steps = [
        make(small_ref.at[k], small_in_ref.at[k], peer)
        for k, peer in enumerate((at.partner, at.across_x, at.across_y))
    ]
    small_last = [
        make(small_z_ref.at[at.z], small_z_ref.at[at.z], peer) for peer, _ in at.z_peers
    ]

    kv_loads = [load(kv_in.at[:, g], kv_ref.at[:, g]) for g in range(groups)]
    late_loads = [
        load(h_in, h_ref),
        load(w_in, w_ref),
        load(x_in, x_ref),
        load(x_far_in, x_far_ref),
        load(dmid_in, dmid_ref),
    ]
    kv_loads[0].start()
    owns[0].start()
    greet([at.partner, at.across_x, at.across_y] + [peer for peer, _ in at.z_peers])
    for m in range(3):
        swaps[m][0].start()
    for copy in owns[1:] + kv_loads[1:] + late_loads:
        copy.start()
    fill_bias(scalars_ref, bias_ref, rows)

    sides = [pl.ds(side * tokens, tokens) for side in range(2)]

    def share_one(g):
        one[g].start()
        two[g].start()

    def share_two(g):
        for copy, side, band in ((one[g], 1, far), (two[g], 0, at.band)):
            copy.wait_recv()
            for half in range(2):
                block = pl.ds(half * part, part)
                to = pl.ds(half * width + g * part, part)
                value = (
                    near_ref[1 - side, g, block, :].astype(F)
                    + dkv_ref[band, g, block, :].astype(F)
                ).astype(BF)
                dwide_ref[to, sides[side]] = value

    events = {}

    def when(j, *actions):
        events.setdefault(j, []).extend(actions)

    def received(m):
        owns[m].wait()
        swaps[m][0].wait_recv()

    for g in range(1, groups):
        when(2 * g - 1, kv_loads[g].wait)
    when(0, down[1].step_one)
    when(0, lambda: received(1), up[0].step_one)
    when(1, up[1].step_one, lambda: share_one(0))
    when(2, up[2].step_one, down[0].step_two, lambda: share_two(0))
    when(3, lambda: received(2), out[0].step_one, down[1].step_two, lambda: share_one(1))
    when(4, up[0].step_two, down[0].step_three, lambda: share_two(1))
    when(5, up[1].step_two, down[1].step_three, lambda: share_one(2))
    when(6, up[2].step_two, up[0].step_three, lambda: share_two(2))
    when(7, lambda: share_one(3), out[0].step_two, up[1].step_three)
    received(0)
    down[0].step_one()
    kv_loads[0].wait()

    @pl.loop(0, 2 * groups)
    def _(j):
        g, s = j // 2, j % 2
        lanes = pl.ds(pl.multiple_of(s * rows, rows), rows)
        for k in range(unroll):

            def put_key(b, values):
                dkv_ref[b, g, pl.ds(k * HEAD_DIM, HEAD_DIM), lanes] = values

            def put_value(b, values):
                dkv_ref[b, g, pl.ds(part + k * HEAD_DIM, HEAD_DIM), lanes] = values

            attend_back_step(
                s * HEADS + g * unroll + k,
                at.x, q_ref, kv_ref, delta_ref, lse_ref, datt_ref, bias_ref, dq_ref,
                put_key, put_value,
            )
        for when_j, actions in events.items():

            @pl.when(j == when_j)
            def _():
                for action in actions:
                    action()

    chunk = width // 2
    g_flat = g_qkv_ref.reshape(3 * width, width)
    parts = lane_parts(BACK_ORDERS[3], width // 2)

    def weight_grad(part, source_ref, first, count, tokens_at):
        _, start, size = parts[part]
        lanes = [pl.ds(x * (width // 2) + start, size) for x in range(2)]

        @pl.loop(0, count)
        def _(j):
            block = pl.ds(pl.multiple_of(j * chunk, 128), chunk)
            to = pl.ds(pl.multiple_of((first + j) * chunk, 128), chunk)
            both = jnp.concatenate([h_ref[l, tokens_at] for l in lanes], axis=0)
            result = dg(source_ref[block, :], both, 1, 1).astype(BF)
            g_flat[to, lanes[0]] = result[:, :size]
            g_flat[to, lanes[1]] = result[:, size:]

    def back_through(side):
        err_ref[...] = jnp.zeros_like(err_ref)

        @pl.loop(0, 4)
        def _(j):
            block = pl.ds(pl.multiple_of(j * chunk, 128), chunk)
            source = pl.ds(pl.multiple_of((2 + j) * chunk, 128), chunk)
            err_ref[...] += dg(w_ref[source, :], dwide_ref[block, sides[side]], 0, 0)

    def start_swap(part):
        for copy in swaps[3 + part]:
            copy.start()

    def first_sum(part):
        for copy in swaps[3 + part]:
            copy.wait_recv()
        qkv[part].step_one()

    for copy in late_loads:
        copy.wait()
    for p in range(2):
        weight_grad(p, dq_ref, 0, 2, sides[0])
    share_two(groups - 1)
    weight_grad(0, dwide_ref, 2, 4, slice(None))
    start_swap(0)
    up[2].step_three()
    out[0].step_three()
    back_through(1)
    err_far = err_ref[...]
    for s in range(2):
        err_far_ref[s] = err_far[:, s * rows : (s + 1) * rows].astype(BF)
    first_sum(0)
    err_moves[0].start()
    weight_grad(1, dwide_ref, 2, 4, slice(None))
    start_swap(1)
    normed_far, _ = normalize(x_far_ref[...].astype(F))
    gain_row = row_sums(err_ref[...] * normed_far)[:1]
    shift_row = row_sums(err_ref[...])[:1]
    first_sum(1)
    back_through(0)

    @pl.loop(0, 2)
    def _(j):
        block = pl.ds(pl.multiple_of(j * chunk, 128), chunk)
        err_ref[...] += dg(w_ref[block, :], dq_ref[block, :], 0, 0)

    small_ref[0] = sums_ref[...]
    small_ref[0, 0:1] = row_sums(dq_ref[...])[:1]
    small_ref[0, 1:2] = row_sums(dwide_ref[pl.ds(width, width), :])[:1]
    normed, _ = normalize(x_ref[...].astype(F))
    small_ref[0, 4:5] = gain_row + row_sums(err_ref[...] * normed)[:1]
    small_ref[0, 5:6] = shift_row + row_sums(err_ref[...])[:1]
    small_steps[0].start()
    qkv[0].step_two()
    for item in down:
        item.step_four()
    deliver(0)
    small_steps[0].wait_recv()
    small_ref[1] = small_ref[0] + small_in_ref[0]
    small_steps[1].start()
    qkv[1].step_two()
    err_moves[1].start()
    qkv[0].step_three()
    small_steps[1].wait_recv()
    small_ref[2] = small_ref[1] + small_in_ref[1]
    small_steps[2].start()
    for item in up:
        item.step_four()
    deliver(1)
    small_steps[2].wait_recv()
    small_z_ref[at.z] = small_ref[2] + small_in_ref[2]
    for copy in small_last:
        copy.start()
    out[0].step_four()
    deliver(2)
    qkv[1].step_three()

    def finish_slot(s):
        err_moves[s].wait_recv()
        lanes = slice(s * rows, (s + 1) * rows)
        err = err_ref[:, lanes] + err_in_ref[s].astype(F)
        normed, inverse = normalize(x_ref[:, lanes].astype(F))
        grad = dmid_ref[:, lanes] + norm_back(err, normed, inverse, cols_ref[:, GAIN_ONE])
        gx_ref[lanes, :] = grad.T.astype(BF)

    finish_slot(0)
    qkv[0].step_four()
    for copy in small_last:
        copy.wait_recv()
    total = small_z_ref[0]
    for k in range(1, depth):
        total = total + small_z_ref[k]
    total_ref[...] = total
    qkv[1].step_four()
    deliver(3)
    finish_slot(1)
    for m, ref in enumerate((o_down_ref, o_up_ref, o_out_ref, o_qkv_ref)):
        ends[m][3].wait()
        whole = jnp.concatenate([targets[m][k] for k in range(2)], axis=0)
        ref[...] = whole if m == 0 else whole.T
        for item in moves[m]:
            item.end()
    for copy in sum(swaps, []) + one + two + err_moves + small_steps + small_last:
        copy.wait_send()


def back(
    images, bands, scalars, q, kv, delta, lse, datt, x, x_far, h, dmid, w, cols, grads, sums
):
    depth = images // 2
    width, tokens = x.shape
    g_out, g_up, g_down = grads
    groups = HEADS // 4
    results, placed, buffers = [], [], []
    for m, item in enumerate((g_down, g_up, g_out, w)):
        block, lanes = item.shape[0] // images // 2, item.shape[1]
        placing = (lanes // 4, 2 * block) if m else (2 * block, lanes // 4)
        results.append(shape(placing, F))
        placed.append(pltpu.VMEM((2, block, lanes // 4), F))
        buffers += [
            pltpu.VMEM((depth, 2, block, lanes), BF),
            pltpu.VMEM((block, lanes // 2), F),
            pltpu.VMEM((block, lanes // 4), F),
        ]
        if m < 3:
            buffers.append(pltpu.VMEM((depth, 2, block, lanes), BF))
        for order, _, size in lane_parts(BACK_ORDERS[m], lanes // 2):
            buffers += reduction_buffers(order, depth, block, size)
    small = (SUM_ROWS, width)
    return pl.pallas_call(
        functools.partial(back_kernel, images, bands),
        name="back",
        out_shape=(shape((tokens, width), BF), results[3], results[2], results[1], results[0], shape(small, F)),
        in_specs=[SM] + [VM] * 6 + [ANY] * 9,
        out_specs=(VM,) * 6,
        scratch_shapes=placed
        + [
            pltpu.VMEM(kv.shape, BF),
            pltpu.VMEM((width, tokens), BF),
            pltpu.VMEM((width, tokens), BF),
            pltpu.VMEM((width, 2 * tokens), BF),
            pltpu.VMEM((width, tokens), F),
            pltpu.VMEM(w.shape, BF),
            pltpu.VMEM((8, tokens // 2), F),
            pltpu.VMEM((width, tokens), BF),
            pltpu.VMEM((2 * width, 2 * tokens), BF),
            pltpu.VMEM((bands, groups, 2 * width // groups, tokens), BF),
            pltpu.VMEM((2, groups, 2 * width // groups, tokens), BF),
            pltpu.VMEM((depth, 2, w.shape[0] // images, width), BF),
            pltpu.VMEM((width, tokens), F),
            pltpu.VMEM((2, width, tokens // 2), BF),
            pltpu.VMEM((2, width, tokens // 2), BF),
            pltpu.VMEM((3,) + small, F),
            pltpu.VMEM((3,) + small, F),
            pltpu.VMEM((depth,) + small, F),
        ]
        + buffers
        + [
            pltpu.SemaphoreType.DMA((16,)),
            pltpu.SemaphoreType.DMA((BACK_COPIES,)),
            pltpu.SemaphoreType.DMA((BACK_COPIES,)),
        ],
        compiler_params=comm_params(3),
    )(
        scalars, q, delta, lse, datt, cols, sums, kv, x, x_far, h, dmid, w, g_out, g_up, g_down
    )


def body(
    tokens,
    slot_kind,
    w_qkv,
    w_out,
    w_up,
    w_down,
    bias_qv,
    bias_out,
    bias_up,
    bias_down,
    gain_one,
    shift_one,
    gain_two,
    shift_two,
    cotangent,
):
    rows, slots, width = tokens.shape[1:]
    count = rows * slots
    images, bands = lax.axis_size("img"), lax.axis_size("band")
    band = lax.axis_index("band")
    smalls = (bias_qv, bias_out, bias_up, bias_down, gain_one, shift_one, gain_two, shift_two)
    sizes = [item.shape[0] for item in smalls]
    own = (w_qkv, w_out, w_up)
    widths = [item.shape[1] for item in own]
    direct = images % 4 == 0 and all(w % 32 == 0 for w in widths + [w_down.shape[1]])
    direct = direct and bias_qv.shape[0] == 2 * (width // images) <= 256
    direct = direct and bias_up.shape[0] == 4 * (width // images)

    def by_slot(values):
        return values[0].transpose(1, 0, 2).reshape(count, width)

    def turn(values):
        return by_slot(values).T

    def turn_back(values):
        return values.reshape(slots, rows, width).transpose(1, 0, 2)[None]

    scalars = slot_kind
    single = (bias_out, bias_down, gain_one, shift_one, gain_two, shift_two)
    if direct:
        unit = width // images
        units = [jnp.stack(single), jnp.zeros((4, unit), BF)]
        units += [bias_qv.reshape(-1, unit), bias_up.reshape(-1, unit)]
        small = jnp.pad(jnp.concatenate(units), ((0, 0), (0, 128 - unit))).astype(F)
        full_qkv, h, all_kv, x, x_far, q, lse, cols, *rest = front(
            images, bands, scalars, (*own, w_down.T), small, by_slot(tokens), by_slot(cotangent)
        )
        full_qkv = full_qkv.reshape(-1, width)
    else:
        scalars = jnp.concatenate([slot_kind, jnp.full((1, 1), band // 2, jnp.int32)], axis=1)
        x, cot = turn(tokens), turn(cotangent)
        full_qkv, full_out, full_up, full_down = (
            lax.all_gather(lax.all_gather(item, "band", axis=0, tiled=True).T, "img", tiled=True)
            for item in (*own, w_down)
        )
        whole = [lax.all_gather(item, "img", tiled=True).astype(F) for item in single]
        cols = jnp.stack(whole + [whole[0]] * (COLUMNS - len(whole)), axis=1)
        c_qv = lax.all_gather(bias_qv, "img", tiled=True).astype(F)[:, None]
        c_up = lax.all_gather(bias_up, "img", tiled=True).astype(F)[:, None]
        bias = jnp.concatenate([c_qv[:width], jnp.zeros((width, 1), F), c_qv[width:]])
        h, qkv = project(x, full_qkv, cols, bias)
        q = qkv[:width]
        all_kv = share(images, bands, qkv[width:])
        all_kv = all_kv.reshape(bands, 2, GROUPS_OF_HEADS, -1, count).transpose(0, 2, 1, 3, 4)
        all_kv = all_kv.reshape(bands, GROUPS_OF_HEADS, -1, count)
        att, lse = attend(scalars, q, all_kv)
        rest = middle(x, cot, scalars, att, full_out, full_up, full_down, cols, c_up)
    out, dmid, datt, delta, g_out, g_up, g_down, sums = rest
    if direct:
        gx, *matrices, turned, total = back(
            images, bands, scalars, q, all_kv, delta, lse, datt, x, x_far, h, dmid,
            full_qkv, cols, (g_out, g_up, g_down), sums,
        )
        matrices.append(turned.T)
    else:
        dq, dkv = attend_back(scalars, q, all_kv, delta, lse, datt)
        dkv = unshare(images, dkv)
        gx, g_qkv, sums_one = finish(x, h, dq, dkv, full_qkv, cols, dmid)
        matrices = [
            lax.psum_scatter(
                lax.psum_scatter(item, "img", scatter_dimension=0, tiled=True),
                "band",
                scatter_dimension=1,
                tiled=True,
            )
            .astype(F)
            .T
            for item in (g_qkv, g_out, g_up, g_down)
        ]
        total = lax.psum(sums + sums_one, ("img", "band"))
    own_small = lax.axis_index("img")
    flat = total.reshape(-1)
    starts = [0, 2, UP_ROW, 3, 4, 5, 6, 7]
    small = [
        lax.dynamic_slice(flat, (start * width + own_small * size,), (size,))
        for start, size in zip(starts, sizes)
    ]
    return (turn_back(out), turn_back(gx), *matrices, *small)


def solution(mesh):
    data, weight, vector = P("img", "band", None, None), P("band", "img"), P("img")
    return jax.shard_map(
        body,
        mesh=mesh,
        in_specs=(data, P("img", None)) + (weight,) * 4 + (vector,) * 8 + (data,),
        out_specs=(data, data) + (weight,) * 4 + (vector,) * 8,
        check_vma=False,
    )
```
